32 devices in a mesh: dp: 4 (over y, core), expert: 8 (over z, x).
Axes of the slice: x: 2, y: 2, z: 4, core: 2. Of those that a mesh axis runs over, the one named last changes fastest.
Arguments:
- tokens: bfloat16 [4096, 1024], P(('dp', 'expert')), may hold values from -6 to 6
- norm_gain: bfloat16 [1024], P('dp'), may hold values from 0.25 to 1.75
- qkv_weight: bfloat16 [1024, 3072], P('dp'), may hold values from -0.1875 to 0.1875
- out_weight: bfloat16 [1024, 1024], P('dp'), may hold values from -3 to 3
- centroids: bfloat16 [8, 1024], P(None, 'dp'), may hold values from -0.09375 to 0.09375
- expert_gain: bfloat16 [8, 2, 1024], P('expert', None, 'dp'), may hold values from 0.25 to 1.75
- expert_in: bfloat16 [8, 2, 4096, 1024], P('expert', None, 'dp'), may hold values from -0.1875 to 0.1875
- expert_out: bfloat16 [8, 2, 4096, 1024], P('expert', None, 'dp'), may hold values from -0.09375 to 0.09375
- routes: int32 [4096, 1], P(('dp', 'expert')), may hold values from 0 to 7; in each aligned block of 128 rows (0 to 127, 128 to 255, ...) at most 24 rows name the same one
- cotangent: bfloat16 [4096, 1024], P(('dp', 'expert')), may hold values from -6 to 6
Outputs:
- block_out: bfloat16 [4096, 1024], P(('dp', 'expert'))
- grad_tokens: float32 [4096, 1024], P(('dp', 'expert'))
- grad_norm_gain: float32 [1024], P('dp')
- grad_qkv: float32 [1024, 3072], P('dp')
- grad_out_weight: float32 [1024, 1024], P('dp')
- grad_centroids: float32 [8, 1024], P(None, 'dp')
- grad_expert_gain: float32 [8, 2, 1024], P('expert', None, 'dp')
- grad_expert_in: float32 [8, 2, 4096, 1024], P('expert', None, 'dp')
- grad_expert_out: float32 [8, 2, 4096, 1024], P('expert', None, 'dp')
The draws below stay inside these ranges and needn't reach their ends.
Inputs may be any that keep to these rules, and one draw needn't show every extreme that they name: `routes`: in each aligned block of 128 rows (the rows of one device) no expert is named by more than 24 rows, a bound that some block reaches.
All inputs are finite; a program needn't handle non-finite values.
Results may differ from the reference program's by a relative error of at most 0.04.
Values may be sent and summed in bfloat16 or wider, within the bound.
A program may use at most 256 MiB of HBM per device.

```python
import math
from functools import partial
import jax
import jax.numpy as jnp
import numpy as np
from jax import lax

D = 1024
HEADS = 16
HEAD = 64
FF = 4096
BLOCK = 256
TOK_DEV = 128
SEQ = 1024
SEQS = 4
TOKENS = 4096
EXPERTS = 8
CAP = 24


def steps_of(rng, dims, shards, low, high):
    factor_of, own = 1.0, jax.random.fold_in(rng, 6)
    for axis_at, blocks in shards:
        draws = jnp.exp(jax.random.uniform(jax.random.fold_in(own, axis_at), (blocks,), jnp.float32, low / len(shards), high / len(shards)))
        factor_of = factor_of * jnp.repeat(draws, dims[axis_at] // blocks).reshape([-1 if axis == axis_at else 1 for axis in range(len(dims))])
    return factor_of


def assign_block(key, own, number, rows, amount, top, reach, skew):
    order = jax.random.permutation(key, amount)
    crowded, ordinary = portions_of(amount, rows * top, reach, skew, True), portions_of(amount, rows * top, reach, skew, False)
    places = jnp.arange(amount)

    def named(sizes, turn):
        used = int((sizes > 0).sum())
        fixed = max(1, used // 4)
        shifted = fixed + (places - fixed + turn * (used - fixed)) % max(1, amount - fixed)
        return jnp.zeros((amount,), jnp.int32).at[order[jnp.where(places < fixed, places, shifted)]].set(jnp.asarray(sizes, jnp.int32))

    sizes = jnp.where(number % 4 == 0, named(crowded, number // 4), named(ordinary, number - number // 4 - 1))
    mixed = jax.random.permutation(jax.random.fold_in(own, 3), amount)
    source_of, receiver = mixed[0:amount // 2 * 2:2], mixed[1:amount // 2 * 2:2]
    margin = jnp.minimum(sizes[source_of] - 1, reach - sizes[receiver]) // 2
    margin = jnp.where((source_of == order[0]) | (receiver == order[0]) | (sizes[receiver] == 0), 0, jnp.maximum(margin, 0))
    shifted = jax.random.randint(jax.random.fold_in(own, 4), (amount // 2,), 0, 1 << 20) % (margin + 1)
    sizes = sizes.at[source_of].add(-shifted).at[receiver].add(shifted)
    items = jnp.searchsorted(jnp.cumsum(sizes), jnp.arange(rows * top), side="right").astype(jnp.int32)
    grid = items.reshape(top, rows).T
    grid = grid[jax.random.permutation(jax.random.fold_in(own, 1), rows)]
    turn = jax.random.randint(jax.random.fold_in(own, 2), (rows, 1), 0, top)
    return jnp.take_along_axis(grid, (jnp.arange(top)[None, :] + turn) % top, axis=1)


def portions_of(number_of, total, bound, lean, full):
    weights = [(1 << 20) // math.isqrt(standing ** lean) + 1 for standing in range(1, number_of + 1)]
    largest = bound if full else min(bound, max(-(-total // number_of), total * weights[0] // sum(weights)))
    least = 1 if total - largest >= number_of - 1 else 0
    counts, rest = [largest] + [least] * (number_of - 1), total - largest - least * (number_of - 1)
    while rest > 0:
        movable = [i for i in range(1, number_of) if counts[i] < largest] or [i for i in range(1, number_of) if counts[i] < bound]
        pool, budget = sum([weights[i] for i in movable]), rest
        for i in movable:
            more = min(bound - counts[i], max(1, budget * weights[i] // pool), rest)
            counts[i] = counts[i] + more
            rest = rest - more
    return np.array(counts)


def gaussian(stream_key, shape, deviation, reach, cuts=(), kind=jnp.bfloat16):
    entries = jax.random.normal(stream_key, shape, jnp.float32) * deviation
    if len(cuts) > 0:
        entries = steps_of(stream_key, shape, cuts, -0.22, 0.18) * entries
    return jnp.clip(entries, min=-reach, max=reach).astype(kind)


def setup_inputs(seed: int = 0) -> dict:
    key_of = jax.random.split(jax.random.key(seed), 11)
    tokens = gaussian(key_of[0], (TOKENS, D), 1.0, 6.0, ((0, 32),))
    norm_gain = jnp.clip(1.0 + 0.15 * jax.random.normal(key_of[1], (D,), jnp.float32), 0.25, 1.75).astype(jnp.bfloat16)
    qkv_weight = gaussian(key_of[2], (D, 3 * D), D ** -0.5, 0.1875, ((0, 4),))
    out_weight = gaussian(key_of[3], (D, D), 4 ** -0.5, 3.0, ((0, 4),))
    centroids = gaussian(key_of[4], (EXPERTS, D), (4 * D) ** -0.5, 0.09375, ((1, 4),))
    expert_gain = jnp.clip(1.0 + 0.15 * jax.random.normal(key_of[5], (EXPERTS, 2, D), jnp.float32), 0.25, 1.75).astype(jnp.bfloat16)
    expert_in = gaussian(key_of[6], (EXPERTS, 2, FF, D), D ** -0.5, 0.1875, ((0, 8), (2, 4)))
    expert_out = gaussian(key_of[7], (EXPERTS, 2, FF, D), FF ** -0.5, 0.09375, ((0, 8), (2, 4)))
    routes_keys = jax.random.split(jax.random.fold_in(key_of[8], 1), TOKENS // TOK_DEV)
    routes_turns = jax.random.permutation(jax.random.fold_in(key_of[8], 3), TOKENS // TOK_DEV)
    routes = jax.vmap(lambda own, number: assign_block(jax.random.fold_in(key_of[8], 2), own, number, TOK_DEV, EXPERTS, 1, CAP, 1))(routes_keys, routes_turns).reshape((TOKENS, 1))
    cotangent = gaussian(key_of[9], (TOKENS, D), 1.0, 6.0, ((0, 32),))
    return dict(tokens=tokens, norm_gain=norm_gain, qkv_weight=qkv_weight, out_weight=out_weight, centroids=centroids, expert_gain=expert_gain, expert_in=expert_in, expert_out=expert_out, routes=routes, cotangent=cotangent)


EPS = 1e-05
HIGH = lax.Precision.HIGHEST

@jax.custom_vjp
def low(v):
    return lax.optimization_barrier(v.astype(jnp.bfloat16)).astype(jnp.float32)

@jax.custom_vjp
def low_back(v):
    return v

def low_keep(v):
    return (low(v), None)

def low_pass(kept, grad):
    return (grad,)

def back_keep(v):
    return (v, None)

def back_low(kept, grad):
    return (low(grad),)
low.defvjp(low_keep, low_pass)
low_back.defvjp(back_keep, back_low)

def rounded_both(values):
    return low_back(low(values))

def layer_norm(values, gain_row):
    center = values - lax.optimization_barrier(jnp.mean(values, axis=-1, keepdims=True))
    spread = lax.optimization_barrier(jnp.mean(center * center, axis=-1, keepdims=True))
    return center * lax.rsqrt(spread + EPS) * gain_row

def attend_sequence(members):
    queries, keyset, values = members
    query_rows = min(512, SEQ)
    starts = jnp.arange(SEQ // query_rows, dtype=jnp.int32) * query_rows
    key_block = jnp.arange(SEQ, dtype=jnp.int32) // BLOCK

    @jax.checkpoint
    def one_block(element):
        query_part, offset = element
        scores = jnp.einsum('qhd,khd->hqk', query_part, keyset, precision=HIGH) * HEAD ** (-0.5)
        scores = low_back(scores)
        query_block = (offset + jnp.arange(query_rows, dtype=jnp.int32)) // BLOCK
        visible = key_block[None, :] <= query_block[:, None]
        scores = jnp.where(visible[None], scores, -1e+30)
        weights = jax.nn.softmax(scores, axis=-1)
        return jnp.einsum('hqk,khd->qhd', low(weights), values, precision=HIGH)
    blocks = queries.reshape(SEQ // query_rows, query_rows, HEADS, HEAD)
    return lax.map(one_block, (blocks, starts)).reshape(SEQ, HEADS, HEAD)

def expert_rows(members):
    row_block, gains, first_weight, second_weight = members
    expert_state = row_block
    total_change = jnp.zeros_like(row_block)
    for sublayer in range(2):
        normed = low(layer_norm(expert_state, gains[sublayer]))
        hidden_pre = low_back(jnp.dot(normed, first_weight[sublayer].T, precision=HIGH))
        hidden = low(jax.nn.gelu(hidden_pre, approximate=False))
        change = low_back(jnp.dot(hidden, second_weight[sublayer], precision=HIGH))
        expert_state = expert_state + change
        total_change = total_change + change
    return rounded_both(total_change)

def forward(tokens, norm_gain, qkv_weight, out_weight, centroids, expert_gain, expert_in, expert_out, route_ids, target, blocks_count):
    normed = low(layer_norm(tokens, norm_gain))
    projected = jnp.dot(normed, qkv_weight, precision=HIGH)
    queries = rounded_both(projected[:, :D])
    keyset = rounded_both(projected[:, D:2 * D])
    values = rounded_both(projected[:, 2 * D:])
    layout = (SEQS, SEQ, HEADS, HEAD)
    mixed = lax.map(attend_sequence, (queries.reshape(layout), keyset.reshape(layout), values.reshape(layout)))
    mixed = rounded_both(mixed.reshape(TOKENS, D))
    attended = low_back(jnp.dot(mixed, out_weight, precision=HIGH))
    residual = tokens + attended
    gate_value = jax.nn.sigmoid(lax.optimization_barrier(jnp.sum(residual * centroids[route_ids], axis=-1)))
    sent = rounded_both(residual)
    slot_rows = jnp.zeros((EXPERTS * blocks_count * CAP, D), jnp.float32).at[target].set(sent)
    slot_rows = slot_rows.reshape(EXPERTS, blocks_count * CAP, D)
    branch = lax.map(jax.checkpoint(expert_rows), (slot_rows, expert_gain, expert_in, expert_out))
    branch_rows = branch.reshape(EXPERTS * blocks_count * CAP, D)[target]
    return residual + gate_value[:, None] * branch_rows

def reference(tokens, norm_gain, qkv_weight, out_weight, centroids, expert_gain, expert_in, expert_out, routes, cotangent):
    blocks_count = TOKENS // TOK_DEV
    route_ids = routes[:, 0].astype(jnp.int32)
    by_block = route_ids.reshape(blocks_count, TOK_DEV)
    chosen = (by_block[:, :, None] == jnp.arange(EXPERTS, dtype=jnp.int32)[None, None, :]).astype(jnp.int32)
    slot_index = lax.optimization_barrier(jnp.sum((jnp.cumsum(chosen, axis=1) - 1) * chosen, axis=-1))
    block_index = jnp.arange(blocks_count, dtype=jnp.int32)[:, None]
    target = ((by_block * blocks_count + block_index) * CAP + slot_index).reshape(TOKENS).astype(jnp.int32)
    primals = (tokens.astype(jnp.float32), norm_gain.astype(jnp.float32), qkv_weight.astype(jnp.float32), out_weight.astype(jnp.float32), centroids.astype(jnp.float32), expert_gain.astype(jnp.float32), expert_in.astype(jnp.float32), expert_out.astype(jnp.float32))
    function = partial(forward, route_ids=route_ids, target=target, blocks_count=blocks_count)
    result, pullback = jax.vjp(function, *primals)
    grads = pullback(cotangent.astype(jnp.float32))
    return (result.astype(jnp.bfloat16), grads[0], grads[1], grads[2], grads[3], grads[4], grads[5], grads[6], grads[7])
```

```python
from functools import partial

import jax
import jax.numpy as jnp
from jax import lax
from jax.experimental import pallas as pl
from jax.experimental.pallas import tpu as pltpu
from jax.sharding import PartitionSpec as P

HEADS = 16
HEAD = 64
BLOCK = 256


EPS = 1e-05
NEGATIVE = -1e30
HIGH = lax.Precision.HIGHEST


def normalize(inputs, gain_row):
    centered = inputs - jnp.mean(inputs, axis=-1, keepdims=True)
    inverse = lax.rsqrt(jnp.mean(centered * centered, axis=-1, keepdims=True) + EPS)
    unit_rows = centered * inverse
    return (unit_rows, inverse, unit_rows * gain_row)


def norm_backward(grad_normed, unit_rows, inverse, gain_row):
    grad_unit = grad_normed * gain_row
    first_mean = jnp.mean(grad_unit, axis=-1, keepdims=True)
    second_mean = jnp.mean(grad_unit * unit_rows, axis=-1, keepdims=True)
    grad_input = inverse * (grad_unit - first_mean - unit_rows * second_mean)
    return (grad_input, jnp.sum(grad_normed * unit_rows, axis=0))


def split_heads(matrix):
    return matrix.reshape(matrix.shape[0], HEADS, HEAD)


def exact_gelu(inputs):
    return jax.nn.gelu(inputs, approximate=False)


def keep_state(current):
    return current


def row_product(left_rows, right_matrix, offset, amount):
    return jnp.dot(left_rows, right_matrix, preferred_element_type=jnp.float32)


def fetch_dense(norm_gain, qkv_weight, out_weight, centroids, expert_gain):
    return (
        lax.all_gather(norm_gain, "dp", axis=0, tiled=True),
        lax.all_gather(qkv_weight, "dp", axis=0, tiled=True),
        lax.all_gather(out_weight, "dp", axis=0, tiled=True),
        lax.all_gather(centroids, "dp", axis=1, tiled=True),
        lax.all_gather(expert_gain, "dp", axis=2, tiled=True),
    )


def spread_rows(rows_low):
    return lax.all_gather(rows_low, "dp", axis=0, tiled=True)


def sum_rows(term, amount):
    return lax.psum_scatter(
        term(jnp.int32(0), amount * lax.axis_size("dp")).astype(jnp.bfloat16),
        "dp",
        scatter_dimension=0,
        tiled=True,
    ).astype(jnp.float32)


def send_slots(rows_low, target, experts, capacity):
    buffer_rows = (
        jnp.zeros((experts * capacity, rows_low.shape[1]), rows_low.dtype).at[target].set(rows_low)
    )
    return buffer_rows.reshape(experts, capacity, rows_low.shape[1])


BF = jnp.bfloat16
F32 = jnp.float32
NT = (((1,), (1,)), ((), ()))
TILE = 256


def mean_last(v):
    return jnp.mean(v, axis=-1, keepdims=True)


def dp_peers():
    me = lax.axis_index("dp")
    sibling = me + 1 - 2 * lax.rem(me, 2)
    across = lax.rem(me + 2, 4)
    return sibling, across


def greet(axis_targets):
    barrier = pltpu.get_barrier_semaphore()
    for target in axis_targets:
        pl.semaphore_signal(barrier, inc=1, device_id=target, device_id_type=pl.DeviceIdType.MESH)
    pl.semaphore_wait(barrier, len(axis_targets))


def expert_kernel(
    z0_ref, dbr_ref, gain_ref, w1_hbm, w2_hbm,
    branch_ref, gstate_ref, ggain_ref, n_out, h_out, df_out, du_out,
    w1, w2, x, hid, gpr, unit_s, inv_s, state, total, own, far, f1, f3, ssum, rf1, rf3, rss,
    send_sem, recv_sem, copy_sem,
):
    half = z0_ref.shape[0] // 2
    pair_rows = 2 * half
    width = z0_ref.shape[1]
    tiles = width // TILE
    sibling, across = dp_peers()

    loads = []
    for i, (src, dst) in enumerate(
        [(w1_hbm.at[0, 0], w1.at[0]), (w2_hbm.at[0, 0], w2.at[0]),
         (w1_hbm.at[0, 1], w1.at[1]), (w2_hbm.at[0, 1], w2.at[1])]
    ):
        cp = pltpu.make_async_copy(src, dst, copy_sem.at[i])
        cp.start()
        loads.append(cp)
    greet([{"dp": sibling}, {"dp": across}])

    def rows_of(h, r):
        return pl.ds((h * 4 + r) * half, half)

    def remote(src, dst, kind, p, h, peer):
        i = (p * 2 + h) * 6 + kind
        return pltpu.make_async_remote_copy(
            src_ref=src, dst_ref=dst, send_sem=send_sem.at[i], recv_sem=recv_sem.at[i],
            device_id={"dp": peer}, device_id_type=pl.DeviceIdType.MESH,
        )

    def copy_of(kind, p, h):
        q = p * 2 + h
        if kind == 0:
            return remote(x.at[p, rows_of(h, 0)], x.at[p, rows_of(h, 1)], 0, p, h, sibling)
        if kind == 1:
            return remote(x.at[p, rows_of(h, 0)], x.at[p, rows_of(h, 2)], 1, p, h, across)
        if kind == 2:
            return remote(x.at[p, rows_of(h, 2)], x.at[p, rows_of(h, 3)], 2, p, h, sibling)
        if kind == 3:
            return remote(f1.at[q], rf1.at[q], 3, p, h, sibling)
        if kind == 4:
            return remote(f3.at[q], rf3.at[q], 4, p, h, sibling)
        return remote(ssum.at[q], rss.at[q], 5, p, h, across)

    layer_of = (0, 1, 1, 0)

    def start_rows(p, h):
        k = layer_of[p]
        rs = pl.ds(h * half, half)
        if p < 2:
            z = state[rs, :]
            center = z - mean_last(z)
            inverse = lax.rsqrt(mean_last(center * center) + EPS)
            unit = center * inverse
            unit_s[k, rs, :] = unit
            inv_s[k, rs, :] = jnp.broadcast_to(inverse, (half, 128))
            x[p, rows_of(h, 0), :] = (unit * gain_ref[pl.ds(k, 1), :]).astype(BF)
        else:
            x[p, rows_of(h, 0), :] = (dbr_ref[rs, :].astype(F32) + state[rs, :]).astype(BF)
        copy_of(1, p, h).start()
        copy_of(0, p, h).start()

    def compute(p, h, pair):
        k = layer_of[p]
        base = pl.ds((h * 2 + pair) * pair_rows, pair_rows)
        first, second = (w1, w2) if p < 2 else (w2, w1)
        q = p * 2 + h

        def up(t, c):
            cols = pl.ds(pl.multiple_of(t * TILE, TILE), TILE)
            pre = lax.dot_general(x[p, base, :], first[k, cols, :], NT, preferred_element_type=F32)
            if p < 2:
                cdf = 0.5 * (1.0 + lax.erf(pre * (0.5 ** 0.5)))
                pdf = jnp.exp(-0.5 * pre * pre) * 0.3989422804014327
                hid[k, base, cols] = (pre * cdf).astype(BF)
                gpr[k, base, cols] = cdf + pre * pdf
            else:
                hid[2 + k, base, cols] = (pre * gpr[k, base, cols]).astype(BF)
            return c

        lax.fori_loop(0, tiles, up, 0)
        slot = k if p < 2 else 2 + k

        def down(t, c):
            cols = pl.ds(pl.multiple_of(t * TILE, TILE), TILE)
            res = jnp.dot(hid[slot, base, :], second[k, :, cols], preferred_element_type=F32)
            if pair == 0:
                own[h, :, cols] = res[:half]
                f1[q, :, cols] = res[half:].astype(BF)
            else:
                far[:, cols] = res[:half]
                f3[q, :, cols] = res[half:].astype(BF)
            return c

        lax.fori_loop(0, tiles, down, 0)
        if pair == 0:
            copy_of(3, p, h).start()
        else:
            copy_of(4, p, h).start()
            copy_of(4, p, h).wait_recv()
            ssum[q] = (far[...] + rf3[q].astype(F32)).astype(BF)
            copy_of(5, p, h).start()

    def finish(p, h):
        k = layer_of[p]
        q = p * 2 + h
        rs = pl.ds(h * half, half)
        copy_of(3, p, h).wait_recv()
        copy_of(5, p, h).wait_recv()
        got = own[h] + rf1[q].astype(F32) + rss[q].astype(F32)
        if p == 0:
            state[rs, :] = state[rs, :] + got
            total[rs, :] = got
        elif p == 1:
            branch_ref[rs, :] = (total[rs, :] + got).astype(BF)
            state[rs, :] = jnp.zeros((half, width), F32)
        else:
            unit = unit_s[k, rs, :]
            part = jnp.sum(got * unit, axis=0, keepdims=True)
            if h == 0:
                ggain_ref[pl.ds(k, 1), :] = part
            else:
                ggain_ref[pl.ds(k, 1), :] = ggain_ref[pl.ds(k, 1), :] + part
            a = got * gain_ref[pl.ds(k, 1), :]
            back = inv_s[k, rs, :][:, :1] * (a - mean_last(a) - unit * mean_last(a * unit))
            if p == 2:
                state[rs, :] = state[rs, :] + back
            else:
                gstate_ref[rs, :] = (state[rs, :] + back).astype(BF)

    def relay(p, h):
        copy_of(1, p, h).wait_recv()
        copy_of(2, p, h).start()

    stores = []

    def store(i, src, dst):
        cp = pltpu.make_async_copy(src, dst, copy_sem.at[4 + i])
        cp.start()
        stores.append(cp)

    state[...] = z0_ref[...].astype(F32)
    start_rows(0, 0)
    start_rows(0, 1)
    loads[0].wait()
    loads[1].wait()
    for p in range(4):
        if p == 0:
            copy_of(0, p, 0).wait_recv()
            compute(p, 0, 0)
        relay(p, 0)
        copy_of(2, p, 0).wait_recv()
        compute(p, 0, 1)
        copy_of(0, p, 1).wait_recv()
        compute(p, 1, 0)
        relay(p, 1)
        copy_of(2, p, 1).wait_recv()
        compute(p, 1, 1)
        finish(p, 0)
        if p == 0:
            loads[2].wait()
            loads[3].wait()
        if p < 3:
            start_rows(p + 1, 0)
            copy_of(0, p + 1, 0).wait_recv()
            compute(p + 1, 0, 0)
        finish(p, 1)
        if p < 3:
            start_rows(p + 1, 1)
        k = layer_of[p]
        if p < 2:
            store(p * 2, x.at[p], n_out.at[k])
            store(p * 2 + 1, hid.at[k], h_out.at[k])
        else:
            store(p * 2, x.at[p], df_out.at[k])
            store(p * 2 + 1, hid.at[2 + k], du_out.at[k])
    for p in range(4):
        for h in range(2):
            for kind in range(6):
                copy_of(kind, p, h).wait_send()
    for cp in stores:
        cp.wait()


def expert_block(z0, dbr, gains, expert_in, expert_out):
    rows, width = z0.shape
    half = rows // 2
    hidden = expert_in.shape[2]
    everything = 4 * rows
    any_spec = pl.BlockSpec(memory_space=pl.ANY)
    vmem_spec = pl.BlockSpec(memory_space=pltpu.VMEM)
    big = jax.ShapeDtypeStruct((2, everything, width), BF)
    V = pltpu.VMEM
    return pl.pallas_call(
        expert_kernel,
        out_shape=(
            jax.ShapeDtypeStruct((rows, width), BF),
            jax.ShapeDtypeStruct((rows, width), BF),
            jax.ShapeDtypeStruct((2, width), F32),
            big, big, big, big,
        ),
        in_specs=[vmem_spec] * 3 + [any_spec] * 2,
        out_specs=(vmem_spec, vmem_spec, vmem_spec, any_spec, any_spec, any_spec, any_spec),
        scratch_shapes=[
            V((2, hidden, width), BF), V((2, hidden, width), BF),
            V((4, everything, width), BF), V((4, everything, hidden), BF), V((2, everything, hidden), F32),
            V((2, rows, width), F32), V((2, rows, 128), F32), V((rows, width), F32), V((rows, width), F32),
            V((2, half, width), F32), V((half, width), F32),
        ]
        + [V((8, half, width), BF)] * 6
        + [pltpu.SemaphoreType.DMA((48,)), pltpu.SemaphoreType.DMA((48,)), pltpu.SemaphoreType.DMA((12,))],
        compiler_params=pltpu.CompilerParams(
            collective_id=1, has_side_effects=True, vmem_limit_bytes=58 * 1024 * 1024
        ),
        cost_estimate=pl.CostEstimate(
            flops=16 * everything * hidden * width, bytes_accessed=24 * 1024 * 1024, transcendentals=0
        ),
        name="expert_block",
    )(z0, dbr, gains, expert_in, expert_out)


def on_device_split(
    tokens,
    norm_gain,
    qkv_weight,
    out_weight,
    centroids,
    expert_gain,
    expert_in,
    expert_out,
    routes,
    cotangent,
):
    model_width = tokens.shape[1]
    local_rows = tokens.shape[0]
    experts = lax.axis_size("expert")
    capacity = max(2, 3 * local_rows // (2 * experts))
    slot_total = experts * capacity
    first_pos = lax.axis_index("expert") * local_rows
    scale = HEAD ** (-0.5)
    gain_full, qkv_full, out_full, centroid_full, expert_gain_full = fetch_dense(
        norm_gain, qkv_weight, out_weight, centroids, expert_gain
    )
    inputs = tokens.astype(jnp.float32)
    unit_attn, inverse_attn, normed_attn = normalize(inputs, gain_full.astype(jnp.float32))
    normed_low = normed_attn.astype(jnp.bfloat16)
    projected = jnp.dot(normed_low, qkv_full, preferred_element_type=jnp.float32).astype(
        jnp.bfloat16
    )
    queries = projected[:, :model_width]
    keyset = projected[:, model_width : 2 * model_width]
    values = projected[:, 2 * model_width :]
    query_heads = split_heads(queries)
    key_heads = split_heads(keyset)
    value_heads = split_heads(values)
    query_block = (first_pos + jnp.arange(local_rows, dtype=jnp.int32)) // BLOCK
    last_block = (first_pos + local_rows - 1) // BLOCK
    start_state = (
        jnp.zeros((local_rows, HEADS, HEAD), jnp.float32),
        jnp.full((HEADS, local_rows), NEGATIVE, jnp.float32),
        jnp.zeros((HEADS, local_rows), jnp.float32),
    )
    key_piece = lax.all_gather(keyset, "expert", axis=0, tiled=True)
    value_piece = lax.all_gather(values, "expert", axis=0, tiled=True)
    amount = key_piece.shape[0]

    def update(current):
        accumulated, highest, totals = current
        scores = (
            jnp.einsum(
                "qhd,khd->hqk",
                query_heads,
                split_heads(key_piece),
                preferred_element_type=jnp.float32,
            )
            * scale
        )
        piece_block = jnp.arange(amount, dtype=jnp.int32) // BLOCK
        visible = (piece_block[None, :] <= query_block[:, None])[None]
        scores = jnp.where(visible, scores, NEGATIVE)
        new_high = jnp.maximum(highest, jnp.max(scores, axis=-1))
        factor = jnp.exp(highest - new_high)
        weights = jnp.where(visible, jnp.exp(scores - new_high[:, :, None]), 0.0)
        totals = jnp.sum(weights, axis=-1)
        accumulated = accumulated * factor.T[:, :, None] + jnp.einsum(
            "hqk,khd->qhd",
            weights.astype(jnp.bfloat16),
            split_heads(value_piece),
            preferred_element_type=jnp.float32,
        )
        return (accumulated, new_high, totals)

    accumulated, highest, totals = lax.cond(
        jnp.int32(0) // BLOCK <= last_block, update, keep_state, start_state
    )
    mixed_heads = accumulated / totals.T[:, :, None]
    log_total = (highest + jnp.log(totals)).T
    mixed_low = mixed_heads.reshape(local_rows, model_width).astype(jnp.bfloat16)
    residual = inputs + jnp.dot(mixed_low, out_full, preferred_element_type=jnp.float32)
    route_ids = routes[:, 0]
    chosen = route_ids[:, None] == jnp.arange(experts, dtype=jnp.int32)[None, :]
    centroid_rows = jnp.dot(
        chosen.astype(jnp.bfloat16), centroid_full, preferred_element_type=jnp.float32
    )
    gate_value = jax.nn.sigmoid(jnp.sum(residual * centroid_rows, axis=-1))
    chosen_int = chosen.astype(jnp.int32)
    slot_index = jnp.sum((jnp.cumsum(chosen_int, axis=0) - 1) * chosen_int, axis=-1)
    target = route_ids * capacity + slot_index
    arrived = lax.all_to_all(
        send_slots(residual.astype(jnp.bfloat16), target, experts, capacity),
        "expert",
        split_axis=0,
        concat_axis=0,
        tiled=True,
    )
    gains_here = expert_gain_full[0].astype(jnp.float32)
    grad_out = cotangent.astype(jnp.float32)
    grad_branch = (gate_value[:, None] * grad_out).astype(jnp.bfloat16)
    branch_grads = lax.all_to_all(
        send_slots(grad_branch, target, experts, capacity),
        "expert",
        split_axis=0,
        concat_axis=0,
        tiled=True,
    )
    branch_low, state_low, expert_gain_grad, n_rows, h_rows, df_rows, du_rows = expert_block(
        arrived.reshape(slot_total, model_width),
        branch_grads.reshape(slot_total, model_width),
        gains_here,
        expert_in,
        expert_out,
    )
    expert_gain_grad = expert_gain_grad[None]
    grad_expert_out = jnp.einsum("krf,krd->kfd", h_rows, df_rows, preferred_element_type=jnp.float32)[None]
    grad_expert_in = jnp.einsum("krf,krd->kfd", du_rows, n_rows, preferred_element_type=jnp.float32)[None]
    returned = lax.all_to_all(
        branch_low.reshape(experts, capacity, model_width),
        "expert",
        split_axis=0,
        concat_axis=0,
        tiled=True,
    )
    branch_tok = returned.reshape(slot_total, model_width)[target].astype(jnp.float32)
    block_out = (residual + gate_value[:, None] * branch_tok).astype(jnp.bfloat16)
    grad_logit = jnp.sum(grad_out * branch_tok, axis=-1) * gate_value * (1.0 - gate_value)
    grad_centroid = jnp.dot(
        chosen.astype(jnp.float32).T, grad_logit[:, None] * residual, precision=HIGH
    )
    grad_resid = grad_out + grad_logit[:, None] * centroid_rows
    came_back = lax.all_to_all(
        state_low.reshape(experts, capacity, model_width),
        "expert",
        split_axis=0,
        concat_axis=0,
        tiled=True,
    )
    grad_resid = grad_resid + came_back.reshape(slot_total, model_width)[target].astype(jnp.float32)
    grad_attended = grad_resid.astype(jnp.bfloat16)
    grad_out_weight = jnp.einsum(
        "rd,re->de", mixed_low, grad_attended, preferred_element_type=jnp.float32
    )
    grad_mixed = jnp.einsum(
        "re,de->rd", grad_attended, out_full, preferred_element_type=jnp.float32
    ).astype(jnp.bfloat16)
    grad_heads = split_heads(grad_mixed)
    delta_rows = jnp.sum(grad_heads.astype(jnp.float32) * mixed_heads, axis=-1)
    zero_heads = jnp.zeros((local_rows, HEADS, HEAD), jnp.float32)
    running = (zero_heads, zero_heads, zero_heads)
    offset = jnp.int32(0)
    fold_key_piece = lax.all_gather(keyset, "expert", axis=0, tiled=True)
    fold_value_piece = lax.all_gather(values, "expert", axis=0, tiled=True)
    query_piece = lax.all_gather(queries, "expert", axis=0, tiled=True)
    grad_piece = lax.all_gather(grad_mixed, "expert", axis=0, tiled=True)
    log_piece = lax.all_gather(log_total.astype(jnp.bfloat16), "expert", axis=0, tiled=True).astype(
        jnp.float32
    )
    delta_piece = lax.all_gather(
        delta_rows.astype(jnp.bfloat16), "expert", axis=0, tiled=True
    ).astype(jnp.float32)
    fold_amount = fold_key_piece.shape[0]
    piece_block = jnp.arange(fold_amount, dtype=jnp.int32) // BLOCK

    def to_queries(current):
        grad_query, grad_key, grad_value = current
        piece_keys = split_heads(fold_key_piece)
        scores = (
            jnp.einsum("qhd,khd->hqk", query_heads, piece_keys, preferred_element_type=jnp.float32)
            * scale
        )
        visible = (piece_block[None, :] <= query_block[:, None])[None]
        weights = jnp.where(visible, jnp.exp(scores - log_total.T[:, :, None]), 0.0)
        grad_weights = jnp.einsum(
            "qhd,khd->hqk",
            grad_heads,
            split_heads(fold_value_piece),
            preferred_element_type=jnp.float32,
        )
        grad_scores = (weights * (grad_weights - delta_rows.T[:, :, None])).astype(jnp.bfloat16)
        grad_query = (
            jnp.einsum("hqk,khd->qhd", grad_scores, piece_keys, preferred_element_type=jnp.float32)
            * scale
        )
        return (grad_query, grad_key, grad_value)

    def to_keys(current):
        grad_query, grad_key, grad_value = current
        piece_queries = split_heads(query_piece)
        piece_grads = split_heads(grad_piece)
        scores = (
            jnp.einsum("qhd,khd->hqk", piece_queries, key_heads, preferred_element_type=jnp.float32)
            * scale
        )
        visible = (query_block[None, :] <= piece_block[:, None])[None]
        weights = jnp.where(visible, jnp.exp(scores - log_piece.T[:, :, None]), 0.0)
        grad_weights = jnp.einsum(
            "qhd,khd->hqk", piece_grads, value_heads, preferred_element_type=jnp.float32
        )
        grad_scores = (weights * (grad_weights - delta_piece.T[:, :, None])).astype(jnp.bfloat16)
        grad_key = (
            grad_key
            + jnp.einsum(
                "hqk,qhd->khd", grad_scores, piece_queries, preferred_element_type=jnp.float32
            )
            * scale
        )
        grad_value = grad_value + jnp.einsum(
            "hqk,qhd->khd",
            weights.astype(jnp.bfloat16),
            piece_grads,
            preferred_element_type=jnp.float32,
        )
        return (grad_query, grad_key, grad_value)

    running = lax.cond(offset // BLOCK <= last_block, to_queries, keep_state, running)
    grad_query, grad_key, grad_value = lax.cond(
        query_block[0] <= (offset + fold_amount - 1) // BLOCK, to_keys, keep_state, running
    )
    grad_qkv_rows = jnp.concatenate(
        [
            grad_query.reshape(local_rows, model_width),
            grad_key.reshape(local_rows, model_width),
            grad_value.reshape(local_rows, model_width),
        ],
        axis=1,
    ).astype(jnp.bfloat16)
    grad_qkv = jnp.einsum(
        "rd,re->de", normed_low, grad_qkv_rows, preferred_element_type=jnp.float32
    )
    grad_normed_attn = jnp.einsum(
        "re,de->rd", grad_qkv_rows, qkv_full, preferred_element_type=jnp.float32
    )
    grad_input_attn, attn_gain_grad = norm_backward(
        grad_normed_attn, unit_attn, inverse_attn, gain_full.astype(jnp.float32)
    )
    grad_tokens = grad_resid + grad_input_attn
    gain_share, qkv_share, out_share, centroid_share, expert_gain_share = (
        lax.psum_scatter(
            attn_gain_grad.astype(jnp.bfloat16), "dp", scatter_dimension=0, tiled=True
        ).astype(jnp.float32),
        lax.psum_scatter(
            grad_qkv.astype(jnp.bfloat16), "dp", scatter_dimension=0, tiled=True
        ).astype(jnp.float32),
        lax.psum_scatter(
            grad_out_weight.astype(jnp.bfloat16), "dp", scatter_dimension=0, tiled=True
        ).astype(jnp.float32),
        lax.psum_scatter(
            grad_centroid.astype(jnp.bfloat16), "dp", scatter_dimension=1, tiled=True
        ).astype(jnp.float32),
        lax.psum_scatter(
            expert_gain_grad.astype(jnp.bfloat16), "dp", scatter_dimension=2, tiled=True
        ).astype(jnp.float32),
    )
    gain_total, qkv_total, out_total, centroid_total = (
        lax.psum(gain_share.astype(jnp.bfloat16), "expert").astype(jnp.float32),
        lax.psum(qkv_share.astype(jnp.bfloat16), "expert").astype(jnp.float32),
        lax.psum(out_share.astype(jnp.bfloat16), "expert").astype(jnp.float32),
        lax.psum(centroid_share.astype(jnp.bfloat16), "expert").astype(jnp.float32),
    )
    return (
        block_out,
        grad_tokens,
        gain_total,
        qkv_total,
        out_total,
        centroid_total,
        expert_gain_share,
        grad_expert_in,
        grad_expert_out,
    )


def on_device(
    tokens,
    norm_gain,
    qkv_weight,
    out_weight,
    centroids,
    expert_gain,
    expert_in,
    expert_out,
    routes,
    cotangent,
):
    model_width = tokens.shape[1]
    local_rows = tokens.shape[0]
    experts = lax.axis_size("expert")
    capacity = max(2, 3 * local_rows // (2 * experts))
    slot_total = experts * capacity
    first_pos = lax.axis_index("expert") * local_rows
    scale = HEAD ** (-0.5)
    gain_full, qkv_full, out_full, centroid_full, expert_gain_full = fetch_dense(
        norm_gain, qkv_weight, out_weight, centroids, expert_gain
    )
    inputs = tokens.astype(jnp.float32)
    unit_attn, inverse_attn, normed_attn = normalize(inputs, gain_full.astype(jnp.float32))
    normed_low = normed_attn.astype(jnp.bfloat16)
    projected = jnp.dot(normed_low, qkv_full, preferred_element_type=jnp.float32).astype(
        jnp.bfloat16
    )
    queries = projected[:, :model_width]
    keyset = projected[:, model_width : 2 * model_width]
    values = projected[:, 2 * model_width :]
    query_heads = split_heads(queries)
    key_heads = split_heads(keyset)
    value_heads = split_heads(values)
    query_block = (first_pos + jnp.arange(local_rows, dtype=jnp.int32)) // BLOCK
    last_block = (first_pos + local_rows - 1) // BLOCK
    start_state = (
        jnp.zeros((local_rows, HEADS, HEAD), jnp.float32),
        jnp.full((HEADS, local_rows), NEGATIVE, jnp.float32),
        jnp.zeros((HEADS, local_rows), jnp.float32),
    )
    key_piece = lax.all_gather(keyset, "expert", axis=0, tiled=True)
    value_piece = lax.all_gather(values, "expert", axis=0, tiled=True)
    amount = key_piece.shape[0]

    def update(current):
        accumulated, highest, totals = current
        scores = (
            jnp.einsum(
                "qhd,khd->hqk",
                query_heads,
                split_heads(key_piece),
                preferred_element_type=jnp.float32,
            )
            * scale
        )
        piece_block = jnp.arange(amount, dtype=jnp.int32) // BLOCK
        visible = (piece_block[None, :] <= query_block[:, None])[None]
        scores = jnp.where(visible, scores, NEGATIVE)
        new_high = jnp.maximum(highest, jnp.max(scores, axis=-1))
        factor = jnp.exp(highest - new_high)
        weights = jnp.where(visible, jnp.exp(scores - new_high[:, :, None]), 0.0)
        totals = jnp.sum(weights, axis=-1)
        accumulated = accumulated * factor.T[:, :, None] + jnp.einsum(
            "hqk,khd->qhd",
            weights.astype(jnp.bfloat16),
            split_heads(value_piece),
            preferred_element_type=jnp.float32,
        )
        return (accumulated, new_high, totals)

    accumulated, highest, totals = lax.cond(
        jnp.int32(0) // BLOCK <= last_block, update, keep_state, start_state
    )
    mixed_heads = accumulated / totals.T[:, :, None]
    log_total = (highest + jnp.log(totals)).T
    mixed_low = mixed_heads.reshape(local_rows, model_width).astype(jnp.bfloat16)
    residual = inputs + jnp.dot(mixed_low, out_full, preferred_element_type=jnp.float32)
    route_ids = routes[:, 0]
    chosen = route_ids[:, None] == jnp.arange(experts, dtype=jnp.int32)[None, :]
    centroid_rows = jnp.dot(
        chosen.astype(jnp.bfloat16), centroid_full, preferred_element_type=jnp.float32
    )
    gate_value = jax.nn.sigmoid(jnp.sum(residual * centroid_rows, axis=-1))
    chosen_int = chosen.astype(jnp.int32)
    slot_index = jnp.sum((jnp.cumsum(chosen_int, axis=0) - 1) * chosen_int, axis=-1)
    target = route_ids * capacity + slot_index
    arrived = lax.all_to_all(
        send_slots(residual.astype(jnp.bfloat16), target, experts, capacity),
        "expert",
        split_axis=0,
        concat_axis=0,
        tiled=True,
    )
    expert_state = arrived.reshape(slot_total, model_width).astype(jnp.float32)
    gains_here = expert_gain_full[0].astype(jnp.float32)
    total_change = jnp.zeros_like(expert_state)
    stored = []
    for sublayer in range(2):
        unit_rows, inverse, normed = normalize(expert_state, gains_here[sublayer])
        normed_rows = normed.astype(jnp.bfloat16)
        first_full, second_full = (expert_in[0, sublayer], expert_out[0, sublayer])
        left_rows = spread_rows(normed_rows)
        hidden_pre = jnp.einsum(
            "rd,fd->rf", left_rows, first_full, preferred_element_type=jnp.float32
        )
        hidden_act, slope_pull = jax.vjp(exact_gelu, hidden_pre)
        hidden_low = hidden_act.astype(jnp.bfloat16)
        change = sum_rows(partial(row_product, hidden_low, second_full), slot_total)
        expert_state = expert_state + change
        total_change = total_change + change
        stored.append((unit_rows, inverse, left_rows, hidden_low, slope_pull))
    branch_low = total_change.astype(jnp.bfloat16)
    returned = lax.all_to_all(
        branch_low.reshape(experts, capacity, model_width),
        "expert",
        split_axis=0,
        concat_axis=0,
        tiled=True,
    )
    branch_tok = returned.reshape(slot_total, model_width)[target].astype(jnp.float32)
    block_out = (residual + gate_value[:, None] * branch_tok).astype(jnp.bfloat16)
    gain_full, qkv_full, out_full, centroid_full, expert_gain_full = fetch_dense(
        norm_gain, qkv_weight, out_weight, centroids, expert_gain
    )
    gains_here = expert_gain_full[0].astype(jnp.float32)
    grad_out = cotangent.astype(jnp.float32)
    grad_logit = jnp.sum(grad_out * branch_tok, axis=-1) * gate_value * (1.0 - gate_value)
    grad_centroid = jnp.dot(
        chosen.astype(jnp.float32).T, grad_logit[:, None] * residual, precision=HIGH
    )
    grad_resid = grad_out + grad_logit[:, None] * centroid_rows
    grad_branch = (gate_value[:, None] * grad_out).astype(jnp.bfloat16)
    branch_grads = lax.all_to_all(
        send_slots(grad_branch, target, experts, capacity),
        "expert",
        split_axis=0,
        concat_axis=0,
        tiled=True,
    )
    grad_change = branch_grads.reshape(slot_total, model_width).astype(jnp.float32)
    grad_state = jnp.zeros_like(grad_change)
    gain_grads = [None, None]
    first_grads = [None, None]
    second_grads = [None, None]
    for sublayer in (1, 0):
        unit_rows, inverse, left_rows, hidden_low, slope_pull = stored[sublayer]
        grad_rows_low = (grad_change + grad_state).astype(jnp.bfloat16)
        first_full, second_full = (expert_in[0, sublayer], expert_out[0, sublayer])
        grad_rows = spread_rows(grad_rows_low)
        grad_hidden = jnp.einsum(
            "rd,fd->rf", grad_rows, second_full, preferred_element_type=jnp.float32
        )
        grad_pre = slope_pull(grad_hidden)[0].astype(jnp.bfloat16)
        grad_first = jnp.einsum(
            "rf,rd->fd", grad_pre, left_rows, preferred_element_type=jnp.float32
        )
        grad_second = jnp.einsum(
            "rf,rd->fd", hidden_low, grad_rows, preferred_element_type=jnp.float32
        )
        grad_normed = sum_rows(partial(row_product, grad_pre, first_full), slot_total)
        grad_input, gain_grad = norm_backward(grad_normed, unit_rows, inverse, gains_here[sublayer])
        grad_state = grad_state + grad_input
        gain_grads[sublayer] = gain_grad
        first_grads[sublayer] = grad_first
        second_grads[sublayer] = grad_second
    came_back = lax.all_to_all(
        grad_state.astype(jnp.bfloat16).reshape(experts, capacity, model_width),
        "expert",
        split_axis=0,
        concat_axis=0,
        tiled=True,
    )
    grad_resid = grad_resid + came_back.reshape(slot_total, model_width)[target].astype(jnp.float32)
    grad_attended = grad_resid.astype(jnp.bfloat16)
    grad_out_weight = jnp.einsum(
        "rd,re->de", mixed_low, grad_attended, preferred_element_type=jnp.float32
    )
    grad_mixed = jnp.einsum(
        "re,de->rd", grad_attended, out_full, preferred_element_type=jnp.float32
    ).astype(jnp.bfloat16)
    grad_heads = split_heads(grad_mixed)
    delta_rows = jnp.sum(grad_heads.astype(jnp.float32) * mixed_heads, axis=-1)
    zero_heads = jnp.zeros((local_rows, HEADS, HEAD), jnp.float32)
    running = (zero_heads, zero_heads, zero_heads)
    offset = jnp.int32(0)
    fold_key_piece = lax.all_gather(keyset, "expert", axis=0, tiled=True)
    fold_value_piece = lax.all_gather(values, "expert", axis=0, tiled=True)
    query_piece = lax.all_gather(queries, "expert", axis=0, tiled=True)
    grad_piece = lax.all_gather(grad_mixed, "expert", axis=0, tiled=True)
    log_piece = lax.all_gather(log_total.astype(jnp.bfloat16), "expert", axis=0, tiled=True).astype(
        jnp.float32
    )
    delta_piece = lax.all_gather(
        delta_rows.astype(jnp.bfloat16), "expert", axis=0, tiled=True
    ).astype(jnp.float32)
    fold_amount = fold_key_piece.shape[0]
    piece_block = jnp.arange(fold_amount, dtype=jnp.int32) // BLOCK

    def to_queries(current):
        grad_query, grad_key, grad_value = current
        piece_keys = split_heads(fold_key_piece)
        scores = (
            jnp.einsum("qhd,khd->hqk", query_heads, piece_keys, preferred_element_type=jnp.float32)
            * scale
        )
        visible = (piece_block[None, :] <= query_block[:, None])[None]
        weights = jnp.where(visible, jnp.exp(scores - log_total.T[:, :, None]), 0.0)
        grad_weights = jnp.einsum(
            "qhd,khd->hqk",
            grad_heads,
            split_heads(fold_value_piece),
            preferred_element_type=jnp.float32,
        )
        grad_scores = (weights * (grad_weights - delta_rows.T[:, :, None])).astype(jnp.bfloat16)
        grad_query = (
            jnp.einsum("hqk,khd->qhd", grad_scores, piece_keys, preferred_element_type=jnp.float32)
            * scale
        )
        return (grad_query, grad_key, grad_value)

    def to_keys(current):
        grad_query, grad_key, grad_value = current
        piece_queries = split_heads(query_piece)
        piece_grads = split_heads(grad_piece)
        scores = (
            jnp.einsum("qhd,khd->hqk", piece_queries, key_heads, preferred_element_type=jnp.float32)
            * scale
        )
        visible = (query_block[None, :] <= piece_block[:, None])[None]
        weights = jnp.where(visible, jnp.exp(scores - log_piece.T[:, :, None]), 0.0)
        grad_weights = jnp.einsum(
            "qhd,khd->hqk", piece_grads, value_heads, preferred_element_type=jnp.float32
        )
        grad_scores = (weights * (grad_weights - delta_piece.T[:, :, None])).astype(jnp.bfloat16)
        grad_key = (
            grad_key
            + jnp.einsum(
                "hqk,qhd->khd", grad_scores, piece_queries, preferred_element_type=jnp.float32
            )
            * scale
        )
        grad_value = grad_value + jnp.einsum(
            "hqk,qhd->khd",
            weights.astype(jnp.bfloat16),
            piece_grads,
            preferred_element_type=jnp.float32,
        )
        return (grad_query, grad_key, grad_value)

    running = lax.cond(offset // BLOCK <= last_block, to_queries, keep_state, running)
    grad_query, grad_key, grad_value = lax.cond(
        query_block[0] <= (offset + fold_amount - 1) // BLOCK, to_keys, keep_state, running
    )
    grad_qkv_rows = jnp.concatenate(
        [
            grad_query.reshape(local_rows, model_width),
            grad_key.reshape(local_rows, model_width),
            grad_value.reshape(local_rows, model_width),
        ],
        axis=1,
    ).astype(jnp.bfloat16)
    grad_qkv = jnp.einsum(
        "rd,re->de", normed_low, grad_qkv_rows, preferred_element_type=jnp.float32
    )
    grad_normed_attn = jnp.einsum(
        "re,de->rd", grad_qkv_rows, qkv_full, preferred_element_type=jnp.float32
    )
    grad_input_attn, attn_gain_grad = norm_backward(
        grad_normed_attn, unit_attn, inverse_attn, gain_full.astype(jnp.float32)
    )
    grad_tokens = grad_resid + grad_input_attn
    expert_gain_grad = jnp.stack(gain_grads)[None]
    gain_share, qkv_share, out_share, centroid_share, expert_gain_share = (
        lax.psum_scatter(
            attn_gain_grad.astype(jnp.bfloat16), "dp", scatter_dimension=0, tiled=True
        ).astype(jnp.float32),
        lax.psum_scatter(
            grad_qkv.astype(jnp.bfloat16), "dp", scatter_dimension=0, tiled=True
        ).astype(jnp.float32),
        lax.psum_scatter(
            grad_out_weight.astype(jnp.bfloat16), "dp", scatter_dimension=0, tiled=True
        ).astype(jnp.float32),
        lax.psum_scatter(
            grad_centroid.astype(jnp.bfloat16), "dp", scatter_dimension=1, tiled=True
        ).astype(jnp.float32),
        lax.psum_scatter(
            expert_gain_grad.astype(jnp.bfloat16), "dp", scatter_dimension=2, tiled=True
        ).astype(jnp.float32),
    )
    gain_total, qkv_total, out_total, centroid_total = (
        lax.psum(gain_share.astype(jnp.bfloat16), "expert").astype(jnp.float32),
        lax.psum(qkv_share.astype(jnp.bfloat16), "expert").astype(jnp.float32),
        lax.psum(out_share.astype(jnp.bfloat16), "expert").astype(jnp.float32),
        lax.psum(centroid_share.astype(jnp.bfloat16), "expert").astype(jnp.float32),
    )
    grad_expert_in = jnp.stack(first_grads)[None]
    grad_expert_out = jnp.stack(second_grads)[None]
    return (
        block_out,
        grad_tokens,
        gain_total,
        qkv_total,
        out_total,
        centroid_total,
        expert_gain_share,
        grad_expert_in,
        grad_expert_out,
    )


def solution(mesh):
    in_specs = (
        P(("dp", "expert"), None),
        P("dp"),
        P("dp", None),
        P("dp", None),
        P(None, "dp"),
        P("expert", None, "dp"),
        P("expert", None, "dp", None),
        P("expert", None, "dp", None),
        P(("dp", "expert"), None),
        P(("dp", "expert"), None),
    )
    out_specs = (
        P(("dp", "expert"), None),
        P(("dp", "expert"), None),
        P("dp"),
        P("dp", None),
        P("dp", None),
        P(None, "dp"),
        P("expert", None, "dp"),
        P("expert", None, "dp", None),
        P("expert", None, "dp", None),
    )
    split = mesh.shape["dp"] == 4 and mesh.shape["expert"] == 8
    return jax.shard_map(
        on_device_split if split else on_device, mesh=mesh, in_specs=in_specs, out_specs=out_specs, check_vma=False
    )
```

```python
from functools import partial

import jax
import jax.numpy as jnp
from jax import lax
from jax.experimental import pallas as pl
from jax.experimental.pallas import tpu as pltpu
from jax.sharding import PartitionSpec as P

HEADS = 16
HEAD = 64
BLOCK = 256


EPS = 1e-05
NEGATIVE = -1e30
HIGH = lax.Precision.HIGHEST


def normalize(inputs, gain_row):
    centered = inputs - jnp.mean(inputs, axis=-1, keepdims=True)
    inverse = lax.rsqrt(jnp.mean(centered * centered, axis=-1, keepdims=True) + EPS)
    unit_rows = centered * inverse
    return (unit_rows, inverse, unit_rows * gain_row)


def norm_backward(grad_normed, unit_rows, inverse, gain_row):
    grad_unit = grad_normed * gain_row
    first_mean = jnp.mean(grad_unit, axis=-1, keepdims=True)
    second_mean = jnp.mean(grad_unit * unit_rows, axis=-1, keepdims=True)
    grad_input = inverse * (grad_unit - first_mean - unit_rows * second_mean)
    return (grad_input, jnp.sum(grad_normed * unit_rows, axis=0))


def split_heads(matrix):
    return matrix.reshape(matrix.shape[0], HEADS, HEAD)


def exact_gelu(inputs):
    return jax.nn.gelu(inputs, approximate=False)


def keep_state(current):
    return current


def row_product(left_rows, right_matrix, offset, amount):
    return jnp.dot(left_rows, right_matrix, preferred_element_type=jnp.float32)


def fetch_dense(norm_gain, qkv_weight, out_weight, centroids, expert_gain):
    return (
        lax.all_gather(norm_gain, "dp", axis=0, tiled=True),
        lax.all_gather(qkv_weight, "dp", axis=0, tiled=True),
        lax.all_gather(out_weight, "dp", axis=0, tiled=True),
        lax.all_gather(centroids, "dp", axis=1, tiled=True),
        lax.all_gather(expert_gain, "dp", axis=2, tiled=True),
    )


def spread_rows(rows_low):
    return lax.all_gather(rows_low, "dp", axis=0, tiled=True)


def sum_rows(term, amount):
    return lax.psum_scatter(
        term(jnp.int32(0), amount * lax.axis_size("dp")).astype(jnp.bfloat16),
        "dp",
        scatter_dimension=0,
        tiled=True,
    ).astype(jnp.float32)


def send_slots(rows_low, target, experts, capacity):
    buffer_rows = (
        jnp.zeros((experts * capacity, rows_low.shape[1]), rows_low.dtype).at[target].set(rows_low)
    )
    return buffer_rows.reshape(experts, capacity, rows_low.shape[1])


BF = jnp.bfloat16
F32 = jnp.float32
NT = (((1,), (1,)), ((), ()))
TN = (((0,), (0,)), ((), ()))
TILE = 256
MESH_ID = pl.DeviceIdType.MESH


def mean_last(v):
    return jnp.mean(v, axis=-1, keepdims=True)


def dp_peers():
    me = lax.axis_index("dp")
    sibling = me + 1 - 2 * lax.rem(me, 2)
    across = lax.rem(me + 2, 4)
    diagonal = lax.rem(sibling + 2, 4)
    return me, sibling, across, diagonal


def expert_peers():
    me = lax.axis_index("expert")
    z, x = me // 2, lax.rem(me, 2)
    beside = me + 1 - 2 * x
    near = z + 1 - 2 * lax.rem(z, 2)
    low, high = lax.rem(z, 2), z // 2
    inner = low + high - 2 * low * high
    flip, turn = 3 - z, lax.rem(z + 2, 4)
    second = inner * flip + (1 - inner) * turn
    third = inner * turn + (1 - inner) * flip
    return me, z, x, beside, (near, second, third)


def greet(targets):
    barrier = pltpu.get_barrier_semaphore()
    for target in targets:
        pl.semaphore_signal(barrier, inc=1, device_id=target, device_id_type=MESH_ID)
    pl.semaphore_wait(barrier, len(targets))


def others(n, me):
    return [lax.rem(me + d, n) for d in range(1, n)]


def push(src, dst, send, recv, target):
    return pltpu.make_async_remote_copy(
        src_ref=src, dst_ref=dst, send_sem=send, recv_sem=recv, device_id=target, device_id_type=MESH_ID
    )


def spread_plan(own_src, slots, send, recv):
    me, z, x, beside, zs = expert_peers()

    def first(i):
        if i == 0:
            return push(own_src, slots.at[me], send.at[0], recv.at[me], {"expert": beside})
        return push(own_src, slots.at[me], send.at[i], recv.at[me], {"expert": 2 * zs[i - 1] + x})

    def arrival(zz, xx):
        s = 2 * zz + xx
        return push(slots.at[s], slots.at[s], send.at[0], recv.at[s], {"expert": beside})

    def passed(i):
        s = 2 * zs[i] + x
        return push(slots.at[s], slots.at[s], send.at[4 + i], recv.at[s], {"expert": beside})

    return first, arrival, passed


def lane_masks(rows):
    lane = lax.broadcasted_iota(jnp.int32, (rows, 128), 1)
    return lane < HEAD


def front_kernel(
    tok, small, wqkv, wout,
    olow, normed_out, qkv_out, mixed_out, lse_out, wout_full, small_full,
    held, wblk, normed, qkv, mixed, lse, mixed_low, gain, bounce, smalls,
    tok_send, tok_recv, w_send, w_recv, o_send, o_recv, copy_sem,
):
    j, sibling, across, diagonal = dp_peers()
    e, z, x, beside, zs = expert_peers()
    rows, width = tok.shape
    shard = wqkv.shape[0]
    lanes = 128

    def mine(s):
        return pl.ds(pl.multiple_of(s * shard, shard), shard)

    mycols = pl.ds(pl.multiple_of(e * lanes, lanes), lanes)
    own_tok = pltpu.make_async_copy(tok, held.at[e], copy_sem.at[0])
    own_tok.start()
    own_w = [
        pltpu.make_async_copy(
            wqkv.at[:, pl.ds(pl.multiple_of(i * width + e * lanes, lanes), lanes)],
            wblk.at[mine(j), pl.ds(i * lanes, lanes)],
            copy_sem.at[1 + i],
        )
        for i in range(3)
    ]
    for cp in own_w:
        cp.start()
    own_out = pltpu.make_async_copy(wout, bounce, copy_sem.at[4])
    own_out.start()
    smalls[j] = small[...]
    greet([{"expert": p} for p in others(8, e)] + [{"dp": p} for p in (sibling, across, diagonal)])

    first, arrival, passed = spread_plan(tok, held, tok_send, tok_recv)
    for i in (1, 2, 3, 0):
        first(i).start()
    for cp in own_w:
        cp.wait()

    def w_copy(kind):
        if kind == 0:
            return push(wblk.at[mine(j)], wblk.at[mine(j)], w_send.at[0], w_recv.at[j], {"dp": sibling})
        if kind == 1:
            return push(wblk.at[mine(j)], wblk.at[mine(j)], w_send.at[1], w_recv.at[j], {"dp": across})
        return push(wblk.at[mine(across)], wblk.at[mine(across)], w_send.at[2], w_recv.at[across], {"dp": sibling})

    def w_arrival(s):
        return push(wblk.at[mine(s)], wblk.at[mine(s)], w_send.at[0], w_recv.at[s], {"dp": sibling})

    def s_copy(i):
        return push(small, smalls.at[j], w_send.at[3 + i], w_recv.at[4 + j], {"dp": (sibling, across, diagonal)[i]})

    def s_arrival(s):
        return push(small, smalls.at[s], w_send.at[3], w_recv.at[4 + s], {"dp": sibling})

    def out_copy(kind):
        if kind == 0:
            return push(wout, wout_full.at[mine(j)], w_send.at[6], w_recv.at[8 + j], {"dp": sibling})
        if kind == 1:
            return push(wout, wout_full.at[mine(j)], w_send.at[7], w_recv.at[8 + j], {"dp": across})
        return push(wout_full.at[mine(across)], wout_full.at[mine(across)], w_send.at[8], w_recv.at[8 + across], {"dp": sibling})

    def out_arrival(s):
        return push(wout, wout_full.at[mine(s)], w_send.at[6], w_recv.at[8 + s], {"dp": sibling})

    for i in range(3):
        s_copy(i).start()
    w_copy(1).start()
    w_copy(0).start()
    out_copy(1).start()
    out_copy(0).start()
    own_out.wait()
    keep_out = pltpu.make_async_copy(bounce, wout_full.at[mine(j)], copy_sem.at[4])
    keep_out.start()
    for s in (sibling, across, diagonal):
        s_arrival(s).wait_recv()
    gain[...] = jnp.concatenate([smalls[s, 0:1, :] for s in range(4)], axis=1).astype(F32)
    w_arrival(across).wait_recv()
    w_copy(2).start()
    w_arrival(sibling).wait_recv()
    w_arrival(diagonal).wait_recv()

    def project(zz):
        base = zz * 2 * rows
        for xx in range(2):
            def norm_rows(t, c):
                rs = pl.ds(pl.multiple_of(t * 64, 64), 64)
                v = held[2 * zz + xx, rs, :].astype(F32)
                center = v - mean_last(v)
                inverse = lax.rsqrt(mean_last(center * center) + EPS)
                at = pl.ds(pl.multiple_of(base + xx * rows + t * 64, 64), 64)
                normed[at, :] = (center * inverse * gain[...]).astype(BF)
                return c
            lax.fori_loop(0, rows // 64, norm_rows, 0)
        at = pl.ds(pl.multiple_of(base, 2 * rows), 2 * rows)
        qkv[at, :] = jnp.dot(normed[at, :], wblk[...], preferred_element_type=F32).astype(BF)

    own_tok.wait()
    arrival(z, 1 - x).wait_recv()
    project(z)
    for i in range(2):
        arrival(zs[i], x).wait_recv()
        passed(i).start()
    arrival(zs[0], 1 - x).wait_recv()
    project(zs[0])
    out_arrival(across).wait_recv()
    out_copy(2).start()
    arrival(zs[2], x).wait_recv()
    passed(2).start()
    arrival(zs[1], 1 - x).wait_recv()
    project(zs[1])
    arrival(zs[2], 1 - x).wait_recv()
    project(zs[2])
    stores = [
        pltpu.make_async_copy(normed, normed_out, copy_sem.at[0]),
        pltpu.make_async_copy(qkv, qkv_out, copy_sem.at[1]),
    ]
    for cp in stores:
        cp.start()

    def o_copy(dest):
        return push(mixed_low.at[pl.ds(dest * rows, rows)], olow.at[:, mycols], o_send.at[dest], o_recv.at[e], {"expert": dest})

    def o_own(dest):
        return pltpu.make_async_copy(mixed_low.at[pl.ds(dest * rows, rows)], olow.at[:, mycols], copy_sem.at[5])

    left = lane_masks(2 * rows)
    for b in (3, 2, 1, 0):
        qs = qkv[pl.ds(b * 2 * rows, 2 * rows), 0:lanes]
        keys = qkv[0 : (b + 1) * 2 * rows, lanes : 2 * lanes]
        vals = qkv[0 : (b + 1) * 2 * rows, 2 * lanes : 3 * lanes]
        outs, logs = [], []
        for h in range(2):
            mask = left if h == 0 else jnp.logical_not(left)
            q_h = jnp.where(mask, qs.astype(F32) * (HEAD ** -0.5), 0.0).astype(BF)
            sc = lax.dot_general(q_h, keys, NT, preferred_element_type=F32)
            top = jnp.max(sc, axis=-1, keepdims=True)
            pr = jnp.exp(sc - top)
            tot = jnp.sum(pr, axis=-1, keepdims=True)
            outs.append(jnp.dot(pr.astype(BF), vals, preferred_element_type=F32) / tot)
            logs.append(top + jnp.log(tot))
        at = pl.ds(b * 2 * rows, 2 * rows)
        res = jnp.where(left, outs[0], outs[1])
        mixed[at, :] = res
        mixed_low[at, :] = res.astype(BF)
        lse[at, :] = jnp.where(left, logs[0], logs[1])
        for dest in (2 * b, 2 * b + 1):
            @pl.when(dest != e)
            def _():
                o_copy(dest).start()

            @pl.when(dest == e)
            def _():
                o_own(dest).start()
    more = [
        pltpu.make_async_copy(mixed, mixed_out, copy_sem.at[2]),
        pltpu.make_async_copy(lse, lse_out, copy_sem.at[3]),
        pltpu.make_async_copy(smalls, small_full, copy_sem.at[6]),
    ]
    for cp in more:
        cp.start()
    for dest in range(8):
        @pl.when(dest != e)
        def _():
            push(mixed_low.at[pl.ds(0, rows)], olow.at[:, pl.ds(dest * lanes, lanes)], o_send.at[dest], o_recv.at[dest], {"expert": dest}).wait_recv()
            o_copy(dest).wait_send()

        @pl.when(dest == e)
        def _():
            o_own(dest).wait()
    for s in (sibling, diagonal):
        out_arrival(s).wait_recv()
    for i in range(4):
        first(i).wait_send()
    for i in range(3):
        passed(i).wait_send()
        w_copy(i).wait_send()
        s_copy(i).wait_send()
        out_copy(i).wait_send()
    keep_out.wait()
    for cp in stores + more:
        cp.wait()


def front_block(tokens, small, qkv_weight, out_weight):
    rows, width = tokens.shape
    seq = 8 * rows
    shard = qkv_weight.shape[0]
    any_spec = pl.BlockSpec(memory_space=pl.ANY)
    vmem_spec = pl.BlockSpec(memory_space=pltpu.VMEM)
    V = pltpu.VMEM
    D = pltpu.SemaphoreType.DMA
    S = jax.ShapeDtypeStruct
    return pl.pallas_call(
        front_kernel,
        out_shape=(
            S((rows, width), BF), S((seq, width), BF), S((seq, 384), BF), S((seq, 128), F32), S((seq, 128), F32),
            S((width, width), BF), S((4,) + small.shape, BF),
        ),
        in_specs=[any_spec, vmem_spec, any_spec, any_spec],
        out_specs=(any_spec,) * 7,
        scratch_shapes=[
            V((8, rows, width), BF), V((width, 384), BF), V((seq, width), BF), V((seq, 384), BF),
            V((seq, 128), F32), V((seq, 128), F32), V((seq, 128), BF), V((1, width), F32), V((shard, width), BF),
            V((4,) + small.shape, BF),
            D((7,)), D((8,)), D((9,)), D((12,)), D((8,)), D((8,)), D((8,)),
        ],
        compiler_params=pltpu.CompilerParams(collective_id=2, has_side_effects=True, vmem_limit_bytes=56 * 1024 * 1024),
        name="front_block",
    )(tokens, small, qkv_weight, out_weight)


def expert_kernel(
    zslots, dslots, olow, gain_ref, w1_hbm, w2_hbm,
    returned, came_back, olow_full, ggain_ref, n_out, h_out, df_out, du_out,
    w1, w2, x, hid, gpr, unit_s, inv_s, state, total, grad_in, own, far, f1, f3, ssum, rf1, rf3, rss,
    zland, dland, bsend, gsend,
    send_sem, recv_sem, a_send, a_recv, g_send, g_recv, copy_sem, own_sem,
):
    cap, width = zslots.shape[1:]
    half = 4 * cap
    pair_rows = 2 * half
    tiles = width // TILE
    j, sibling, across, diagonal = dp_peers()
    e, zpos, xpos, beside, zs = expert_peers()

    loads = []
    for i, (src, dst) in enumerate(
        [(w1_hbm.at[0, 0], w1.at[0]), (w2_hbm.at[0, 0], w2.at[0]),
         (w1_hbm.at[0, 1], w1.at[1]), (w2_hbm.at[0, 1], w2.at[1])]
    ):
        cp = pltpu.make_async_copy(src, dst, copy_sem.at[i])
        cp.start()
        loads.append(cp)
    own_z = pltpu.make_async_copy(zslots.at[e], zland.at[e], own_sem.at[0])
    own_d = pltpu.make_async_copy(dslots.at[e], dland.at[e], own_sem.at[1])
    own_z.start()
    own_d.start()
    greet([{"expert": p} for p in others(8, e)] + [{"dp": sibling}, {"dp": across}])

    def swap(src, dst, which, dest):
        return push(src.at[dest], dst.at[e], a_send.at[which * 8 + dest], a_recv.at[which * 8 + e], {"expert": dest})

    def swap_arrival(src, dst, which, source):
        return push(src.at[source], dst.at[source], a_send.at[which * 8 + source], a_recv.at[which * 8 + source], {"expert": source})

    peers = others(8, e)
    for dest in peers:
        swap(zslots, zland, 0, dest).start()
    for dest in peers:
        swap(dslots, dland, 1, dest).start()
    first, arrival, passed = spread_plan(olow, olow_full, g_send, g_recv)
    own_o = pltpu.make_async_copy(olow, olow_full.at[e], copy_sem.at[12])
    own_o.start()

    def rows_of(h, r):
        return pl.ds((h * 4 + r) * half, half)

    def remote(src, dst, kind, p, h, peer):
        i = (p * 2 + h) * 6 + kind
        return push(src, dst, send_sem.at[i], recv_sem.at[i], {"dp": peer})

    def copy_of(kind, p, h):
        q = p * 2 + h
        if kind == 0:
            return remote(x.at[p, rows_of(h, 0)], x.at[p, rows_of(h, 1)], 0, p, h, sibling)
        if kind == 1:
            return remote(x.at[p, rows_of(h, 0)], x.at[p, rows_of(h, 2)], 1, p, h, across)
        if kind == 2:
            return remote(x.at[p, rows_of(h, 2)], x.at[p, rows_of(h, 3)], 2, p, h, sibling)
        if kind == 3:
            return remote(f1.at[q], rf1.at[q], 3, p, h, sibling)
        if kind == 4:
            return remote(f3.at[q], rf3.at[q], 4, p, h, sibling)
        return remote(ssum.at[q], rss.at[q], 5, p, h, across)

    layer_of = (0, 1, 1, 0)

    def start_rows(p, h):
        k = layer_of[p]
        rs = pl.ds(h * half, half)
        if p < 2:
            v = state[rs, :]
            center = v - mean_last(v)
            inverse = lax.rsqrt(mean_last(center * center) + EPS)
            unit = center * inverse
            unit_s[k, rs, :] = unit
            inv_s[k, rs, :] = jnp.broadcast_to(inverse, (half, 128))
            x[p, rows_of(h, 0), :] = (unit * gain_ref[pl.ds(k, 1), :]).astype(BF)
        else:
            x[p, rows_of(h, 0), :] = (grad_in[rs, :] + state[rs, :]).astype(BF)
        copy_of(1, p, h).start()
        copy_of(0, p, h).start()

    def compute(p, h, pair):
        k = layer_of[p]
        base = pl.ds((h * 2 + pair) * pair_rows, pair_rows)
        left_w, right_w = (w1, w2) if p < 2 else (w2, w1)
        q = p * 2 + h

        def up(t, c):
            cols = pl.ds(pl.multiple_of(t * TILE, TILE), TILE)
            pre = lax.dot_general(x[p, base, :], left_w[k, cols, :], NT, preferred_element_type=F32)
            if p < 2:
                cdf = 0.5 * (1.0 + lax.erf(pre * (0.5 ** 0.5)))
                pdf = jnp.exp(-0.5 * pre * pre) * 0.3989422804014327
                hid[k, base, cols] = (pre * cdf).astype(BF)
                gpr[k, base, cols] = cdf + pre * pdf
            else:
                hid[2 + k, base, cols] = (pre * gpr[k, base, cols]).astype(BF)
            return c

        lax.fori_loop(0, tiles, up, 0)
        slot = k if p < 2 else 2 + k

        def down(t, c):
            cols = pl.ds(pl.multiple_of(t * TILE, TILE), TILE)
            res = jnp.dot(hid[slot, base, :], right_w[k, :, cols], preferred_element_type=F32)
            if pair == 0:
                own[h, :, cols] = res[:half]
                f1[q, :, cols] = res[half:].astype(BF)
            else:
                far[:, cols] = res[:half]
                f3[q, :, cols] = res[half:].astype(BF)
            return c

        lax.fori_loop(0, tiles, down, 0)
        if pair == 0:
            copy_of(3, p, h).start()
        else:
            copy_of(4, p, h).start()
            copy_of(4, p, h).wait_recv()
            ssum[q] = (far[...] + rf3[q].astype(F32)).astype(BF)
            copy_of(5, p, h).start()

    def give_back(buf, dst, which, h):
        for dest in range(4 * h, 4 * h + 4):
            @pl.when(dest != e)
            def _():
                swap(buf, dst, which, dest).start()

            @pl.when(dest == e)
            def _():
                pltpu.make_async_copy(buf.at[dest], dst.at[dest], own_sem.at[which]).start()

    def finish(p, h):
        k = layer_of[p]
        q = p * 2 + h
        rs = pl.ds(h * half, half)
        copy_of(3, p, h).wait_recv()
        copy_of(5, p, h).wait_recv()
        got = own[h] + rf1[q].astype(F32) + rss[q].astype(F32)
        if p == 0:
            state[rs, :] = state[rs, :] + got
            total[rs, :] = got
        elif p == 1:
            total[rs, :] = total[rs, :] + got
            for i in range(4):
                bsend[4 * h + i] = total[pl.ds(h * half + i * cap, cap), :].astype(BF)
            state[rs, :] = jnp.zeros((half, width), F32)
            give_back(bsend, returned, 2, h)
        else:
            unit = unit_s[k, rs, :]
            part = jnp.sum(got * unit, axis=0, keepdims=True)
            if h == 0:
                ggain_ref[pl.ds(k, 1), :] = part
            else:
                ggain_ref[pl.ds(k, 1), :] = ggain_ref[pl.ds(k, 1), :] + part
            a = got * gain_ref[pl.ds(k, 1), :]
            back = inv_s[k, rs, :][:, :1] * (a - mean_last(a) - unit * mean_last(a * unit))
            state[rs, :] = state[rs, :] + back
            if p == 3:
                for i in range(4):
                    gsend[4 * h + i] = state[pl.ds(h * half + i * cap, cap), :].astype(BF)
                give_back(gsend, came_back, 3, h)

    def relay(p, h):
        copy_of(1, p, h).wait_recv()
        copy_of(2, p, h).start()

    stores = []

    def store(i, src, dst):
        cp = pltpu.make_async_copy(src, dst, copy_sem.at[4 + i])
        cp.start()
        stores.append(cp)

    def landed(buf, src, own_copy, which, h, out):
        for source in range(4 * h, 4 * h + 4):
            @pl.when(source != e)
            def _():
                swap_arrival(src, buf, which, source).wait_recv()

            @pl.when(source == e)
            def _():
                own_copy.wait()
        for source in range(4 * h, 4 * h + 4):
            out[pl.ds(source * cap, cap), :] = buf[source].astype(F32)

    landed(zland, zslots, own_z, 0, 0, state)
    start_rows(0, 0)
    landed(zland, zslots, own_z, 0, 1, state)
    start_rows(0, 1)
    loads[0].wait()
    loads[1].wait()
    for p in range(4):
        if p == 0:
            copy_of(0, p, 0).wait_recv()
            compute(p, 0, 0)
            for i in (1, 2, 3, 0):
                first(i).start()
        relay(p, 0)
        copy_of(2, p, 0).wait_recv()
        compute(p, 0, 1)
        copy_of(0, p, 1).wait_recv()
        compute(p, 1, 0)
        relay(p, 1)
        copy_of(2, p, 1).wait_recv()
        compute(p, 1, 1)
        if p == 1:
            for i in range(3):
                arrival(zs[i], xpos).wait_recv()
                passed(i).start()
            landed(dland, dslots, own_d, 1, 0, grad_in)
            landed(dland, dslots, own_d, 1, 1, grad_in)
        finish(p, 0)
        if p == 0:
            loads[2].wait()
            loads[3].wait()
        if p < 3:
            start_rows(p + 1, 0)
            copy_of(0, p + 1, 0).wait_recv()
            compute(p + 1, 0, 0)
        finish(p, 1)
        if p < 3:
            start_rows(p + 1, 1)
        k = layer_of[p]
        if p < 2:
            store(p * 2, x.at[p], n_out.at[k])
            store(p * 2 + 1, hid.at[k], h_out.at[k])
        else:
            store(p * 2, x.at[p], df_out.at[k])
            store(p * 2 + 1, hid.at[2 + k], du_out.at[k])
    own_o.wait()
    for s in range(4):
        arrival(s, 1 - xpos).wait_recv()
    for i in range(4):
        first(i).wait_send()
    for i in range(3):
        passed(i).wait_send()
    for p in range(4):
        for h in range(2):
            for kind in range(6):
                copy_of(kind, p, h).wait_send()
    for cp in stores:
        cp.wait()
    for dest in peers:
        swap(zslots, zland, 0, dest).wait_send()
        swap(dslots, dland, 1, dest).wait_send()
        swap(bsend, returned, 2, dest).wait_send()
        swap(gsend, came_back, 3, dest).wait_send()
        swap_arrival(bsend, returned, 2, dest).wait_recv()
        swap_arrival(gsend, came_back, 3, dest).wait_recv()
    pltpu.make_async_copy(bsend.at[0], returned.at[0], own_sem.at[2]).wait()
    pltpu.make_async_copy(gsend.at[0], came_back.at[0], own_sem.at[3]).wait()


def expert_block(zslots, dslots, olow, gains, expert_in, expert_out):
    sources, cap, width = zslots.shape
    rows = sources * cap
    half = rows // 2
    hidden = expert_in.shape[2]
    everything = 4 * rows
    any_spec = pl.BlockSpec(memory_space=pl.ANY)
    vmem_spec = pl.BlockSpec(memory_space=pltpu.VMEM)
    S = jax.ShapeDtypeStruct
    big = S((2, everything, width), BF)
    V = pltpu.VMEM
    D = pltpu.SemaphoreType.DMA
    return pl.pallas_call(
        expert_kernel,
        out_shape=(
            S(zslots.shape, BF), S(zslots.shape, BF), S((8,) + olow.shape, BF), S((2, width), F32),
            big, big, big, big,
        ),
        in_specs=[any_spec] * 3 + [vmem_spec] + [any_spec] * 2,
        out_specs=(any_spec, any_spec, any_spec, vmem_spec, any_spec, any_spec, any_spec, any_spec),
        scratch_shapes=[
            V((2, hidden, width), BF), V((2, hidden, width), BF),
            V((4, everything, width), BF), V((4, everything, hidden), BF), V((2, everything, hidden), F32),
            V((2, rows, width), F32), V((2, rows, 128), F32), V((rows, width), F32), V((rows, width), F32),
            V((rows, width), F32), V((2, half, width), F32), V((half, width), F32),
        ]
        + [V((8, half, width), BF)] * 6
        + [V(zslots.shape, BF)] * 4
        + [D((48,)), D((48,)), D((32,)), D((32,)), D((7,)), D((8,)), D((13,)), D((4,))],
        compiler_params=pltpu.CompilerParams(
            collective_id=1, has_side_effects=True, vmem_limit_bytes=60 * 1024 * 1024
        ),
        name="expert_block",
    )(zslots, dslots, olow, gains, expert_in, expert_out)


def back_kernel(
    gmix, gatt, qkv_hbm, mixed_hbm, lse_rows, normed_hbm, olow_hbm, cent,
    dq_land, gq_land, go_land, gc_land,
    dom, dam, qkv, mixed, normed, olow, delta, dq_acc, dqkv,
    part, f1, f3, ssum, rf1, rf3, rss, gq_own, go_own, cland, csum, cdp,
    h_send, h_recv, d_send, d_recv, p_send, p_recv, gq_send, gq_recv, go_send, go_recv, c_send, c_recv, copy_sem,
):
    j, sibling, across, diagonal = dp_peers()
    e, zpos, xpos, beside, zs = expert_peers()
    rows, width = gmix.shape
    blk = 2 * rows
    lanes = 128
    shard = width // 4
    loads = [
        pltpu.make_async_copy(src, dst, copy_sem.at[i])
        for i, (src, dst) in enumerate([(qkv_hbm, qkv), (mixed_hbm, mixed), (olow_hbm, olow), (normed_hbm, normed)])
    ]
    for cp in loads:
        cp.start()
    peers = others(8, e)
    greet([{"expert": p} for p in peers] + [{"dp": p} for p in (sibling, across, diagonal)])

    def cols_of(s):
        return pl.ds(pl.multiple_of(s * lanes, lanes), lanes)

    def rows_of(s):
        return pl.ds(pl.multiple_of(s * rows, rows), rows)

    def head_copy(src, dst, which, dest):
        return push(src.at[:, cols_of(dest)], dst.at[rows_of(e)], h_send.at[which * 8 + dest], h_recv.at[which * 8 + e], {"expert": dest})

    def head_arrival(src, dst, which, source):
        return push(src.at[:, cols_of(source)], dst.at[rows_of(source)], h_send.at[which * 8 + source], h_recv.at[which * 8 + source], {"expert": source})

    for dest in peers:
        head_copy(gmix, dom, 0, dest).start()
    for dest in peers:
        head_copy(gatt, dam, 1, dest).start()
    for dest in peers:
        push(cent.at[dest], cland.at[e], c_send.at[dest], c_recv.at[e], {"expert": dest}).start()
    dom[rows_of(e), :] = gmix[:, cols_of(e)]
    dam[rows_of(e), :] = gatt[:, cols_of(e)]
    cland[e] = cent[e]

    def dp_sum_start(buf, n, t):
        def block(s):
            return buf[0:n, pl.ds(pl.multiple_of(s * shard, shard), shard)]
        f3[t, 0:n, :] = block(diagonal).astype(BF)
        f1[t, 0:n, :] = block(sibling).astype(BF)
        dp_copy(1, n, t).start()
        dp_copy(0, n, t).start()
        dp_copy(1, n, t).wait_recv()
        ssum[t, 0:n, :] = (block(across) + rf3[t, 0:n, :].astype(F32)).astype(BF)
        dp_copy(2, n, t).start()

    def dp_copy(kind, n, t):
        at = pl.ds(0, n)
        if kind == 0:
            return push(f1.at[t, at], rf1.at[t, at], p_send.at[t * 3], p_recv.at[t * 3], {"dp": sibling})
        if kind == 1:
            return push(f3.at[t, at], rf3.at[t, at], p_send.at[t * 3 + 1], p_recv.at[t * 3 + 1], {"dp": sibling})
        return push(ssum.at[t, at], rss.at[t, at], p_send.at[t * 3 + 2], p_recv.at[t * 3 + 2], {"dp": across})

    def dp_sum_end(buf, n, t):
        dp_copy(0, n, t).wait_recv()
        dp_copy(2, n, t).wait_recv()
        return buf[0:n, pl.ds(pl.multiple_of(j * shard, shard), shard)] + rf1[t, 0:n, :].astype(F32) + rss[t, 0:n, :].astype(F32)

    for cp in loads[:2]:
        cp.wait()
    for source in peers:
        head_arrival(gmix, dom, 0, source).wait_recv()
    left_row = lax.broadcasted_iota(jnp.int32, (8, 128), 1) < HEAD
    row_id = lax.broadcasted_iota(jnp.int32, (8, 128), 0)
    pick = jnp.where((row_id == 0) == left_row, 1.0, 0.0).astype(F32)
    delta[...] = lax.dot_general(pick, dom[...].astype(F32) * mixed[...], NT, precision=HIGH, preferred_element_type=F32)

    for source in peers:
        push(cent.at[source], cland.at[source], c_send.at[source], c_recv.at[source], {"expert": source}).wait_recv()
    csum[0] = jnp.sum(cland[...], axis=0)

    def c_copy(i):
        s = (sibling, across, diagonal)[i]
        return push(csum.at[0, :, pl.ds(pl.multiple_of(s * shard, shard), shard)], cdp.at[j], c_send.at[8 + i], c_recv.at[8 + j], {"dp": s})

    def c_arrival(s):
        return push(csum.at[0, :, pl.ds(0, shard)], cdp.at[s], c_send.at[8], c_recv.at[8 + s], {"dp": sibling})

    for i in range(3):
        c_copy(i).start()
    cdp[j] = csum[0, :, pl.ds(pl.multiple_of(j * shard, shard), shard)]

    left = lane_masks(blk)
    dq_acc[...] = jnp.zeros_like(dq_acc)

    def d_copy(dest):
        return push(dqkv.at[pl.ds(dest * rows, rows)], dq_land.at[e], d_send.at[dest], d_recv.at[e], {"expert": dest})

    for b in range(4):
        at = pl.ds(b * blk, blk)
        tail = pl.ds(b * blk, 8 * rows - b * blk)
        qs = qkv[tail, 0:lanes]
        dos = dom[tail, :]
        keys = qkv[at, lanes : 2 * lanes].astype(F32) * (HEAD ** -0.5)
        vals = qkv[at, 2 * lanes : 3 * lanes]
        dks, dvs = [], []
        for h in range(2):
            mask = left if h == 0 else jnp.logical_not(left)
            k_h = jnp.where(mask, keys, 0.0).astype(BF)
            v_h = jnp.where(mask, vals.astype(F32), 0.0).astype(BF)
            sc = lax.dot_general(k_h, qs, NT, preferred_element_type=F32)
            pr = jnp.exp(sc - lse_rows[h : h + 1, tail])
            dp = lax.dot_general(v_h, dos, NT, preferred_element_type=F32)
            ds = (pr * (dp - delta[h : h + 1, tail])).astype(BF)
            dvs.append(jnp.dot(pr.astype(BF), dos, preferred_element_type=F32))
            dks.append(jnp.dot(ds, qs, preferred_element_type=F32))
            dq_acc[tail, :] += lax.dot_general(ds, k_h, TN, preferred_element_type=F32)
        dqkv[at, 0:lanes] = dq_acc[at, :].astype(BF)
        dqkv[at, lanes : 2 * lanes] = (jnp.where(left, dks[0], dks[1]) * (HEAD ** -0.5)).astype(BF)
        dqkv[at, 2 * lanes : 3 * lanes] = jnp.where(left, dvs[0], dvs[1]).astype(BF)
        for dest in (2 * b, 2 * b + 1):
            @pl.when(dest != e)
            def _():
                d_copy(dest).start()

            @pl.when(dest == e)
            def _():
                pltpu.make_async_copy(dqkv.at[pl.ds(dest * rows, rows)], dq_land.at[dest], copy_sem.at[4]).start()
        if b == 0:
            loads[2].wait()
            for source in peers:
                head_arrival(gatt, dam, 1, source).wait_recv()
            part[0:lanes, :] = lax.dot_general(dam[...], olow[...], TN, preferred_element_type=F32)
            dp_sum_start(part, lanes, 0)
        if b == 1:
            go_own[...] = dp_sum_end(part, lanes, 0).T.astype(BF)
            go_first, go_arrival, go_passed = spread_plan(go_own, go_land, go_send, go_recv)
            for i in (1, 2, 3, 0):
                go_first(i).start()
            own_go = pltpu.make_async_copy(go_own, go_land.at[e], copy_sem.at[5])
            own_go.start()
            for s in (sibling, across, diagonal):
                c_arrival(s).wait_recv()
            csum[1, :, 0:shard] = jnp.sum(cdp[...], axis=0)
            for dest in peers:
                push(csum.at[1, :, pl.ds(0, shard)], gc_land.at[e], c_send.at[12 + dest], c_recv.at[12 + e], {"expert": dest}).start()
            own_gc = pltpu.make_async_copy(csum.at[1, :, pl.ds(0, shard)], gc_land.at[e], copy_sem.at[6])
            own_gc.start()
    loads[3].wait()
    part[...] = lax.dot_general(dqkv[...], normed[...], TN, preferred_element_type=F32)
    dp_sum_start(part, 3 * lanes, 1)
    for i in range(3):
        go_arrival(zs[i], xpos).wait_recv()
        go_passed(i).start()
    gq_own[...] = dp_sum_end(part, 3 * lanes, 1).T.astype(BF)
    gq_first, gq_arrival, gq_passed = spread_plan(gq_own, gq_land, gq_send, gq_recv)
    for i in (1, 2, 3, 0):
        gq_first(i).start()
    own_gq = pltpu.make_async_copy(gq_own, gq_land.at[e], copy_sem.at[7])
    own_gq.start()
    for i in range(3):
        gq_arrival(zs[i], xpos).wait_recv()
        gq_passed(i).start()
    for s in range(4):
        go_arrival(s, 1 - xpos).wait_recv()
        gq_arrival(s, 1 - xpos).wait_recv()
    for source in range(8):
        @pl.when(source != e)
        def _():
            push(dqkv.at[pl.ds(0, rows)], dq_land.at[source], d_send.at[source], d_recv.at[source], {"expert": source}).wait_recv()
            d_copy(source).wait_send()
            push(csum.at[1, :, pl.ds(0, shard)], gc_land.at[source], c_send.at[12 + source], c_recv.at[12 + source], {"expert": source}).wait()

        @pl.when(source == e)
        def _():
            pltpu.make_async_copy(dqkv.at[pl.ds(0, rows)], dq_land.at[source], copy_sem.at[4]).wait()
    for dest in peers:
        head_copy(gmix, dom, 0, dest).wait_send()
        head_copy(gatt, dam, 1, dest).wait_send()
        push(cent.at[dest], cland.at[e], c_send.at[dest], c_recv.at[e], {"expert": dest}).wait_send()
    for i in range(3):
        c_copy(i).wait_send()
        dp_copy(i, lanes, 0).wait_send()
        dp_copy(i, 3 * lanes, 1).wait_send()
        go_passed(i).wait_send()
        gq_passed(i).wait_send()
    for i in range(4):
        go_first(i).wait_send()
        gq_first(i).wait_send()
    for cp in (own_go, own_gc, own_gq):
        cp.wait()


def back_block(gmix, gatt, qkv, mixed, lse_rows, normed, olow_full, cent):
    rows, width = gmix.shape
    seq = 8 * rows
    shard = width // 4
    any_spec = pl.BlockSpec(memory_space=pl.ANY)
    vmem_spec = pl.BlockSpec(memory_space=pltpu.VMEM)
    S = jax.ShapeDtypeStruct
    V = pltpu.VMEM
    D = pltpu.SemaphoreType.DMA
    return pl.pallas_call(
        back_kernel,
        out_shape=(S((8, rows, 384), BF), S((8, shard, 384), BF), S((8, shard, 128), BF), S((8, 1, shard), F32)),
        in_specs=[vmem_spec, vmem_spec, any_spec, any_spec, vmem_spec, any_spec, any_spec, vmem_spec],
        out_specs=(any_spec,) * 4,
        scratch_shapes=[
            V((seq, 128), BF), V((seq, 128), BF), V((seq, 384), BF), V((seq, 128), F32), V((seq, width), BF), V((seq, width), BF),
            V((8, seq), F32), V((seq, 128), F32), V((seq, 384), BF),
            V((384, width), F32),
        ]
        + [V((2, 384, shard), BF)] * 6
        + [
            V((shard, 384), BF), V((shard, 128), BF), V((8, 1, width), F32), V((2, 1, width), F32), V((4, 1, shard), F32),
            D((16,)), D((16,)), D((8,)), D((8,)), D((6,)), D((6,)), D((7,)), D((8,)), D((7,)), D((8,)), D((20,)), D((20,)), D((8,)),
        ],
        compiler_params=pltpu.CompilerParams(collective_id=3, has_side_effects=True, vmem_limit_bytes=56 * 1024 * 1024),
        name="back_block",
    )(gmix, gatt, qkv, mixed, lse_rows, normed, olow_full, cent)


def on_device_split(
    tokens,
    norm_gain,
    qkv_weight,
    out_weight,
    centroids,
    expert_gain,
    expert_in,
    expert_out,
    routes,
    cotangent,
):
    rows, width = tokens.shape
    experts = lax.axis_size("expert")
    capacity = max(2, 3 * rows // (2 * experts))
    slots = experts * capacity
    shard = width // 4
    around = [(s, (s + 2) % 4) for s in range(4)]
    beside = [(s, s ^ 1) for s in range(4)]
    w_near = jnp.stack([qkv_weight, lax.ppermute(qkv_weight, "dp", around)])
    w_far = lax.ppermute(w_near, "dp", beside)
    small = jnp.concatenate(
        [norm_gain[None], expert_gain[0], jnp.zeros((5, shard), BF), centroids], axis=0
    )
    olow, normed_all, qkv, mixed, lse, wout_full, small_full = front_block(tokens, small, qkv_weight, out_weight)
    gains = small_full[:, 1:3].transpose(1, 0, 2).reshape(2, width).astype(F32)
    centroid_full = small_full[:, 8:16].transpose(1, 0, 2).reshape(8, width)
    inputs = tokens.astype(F32)
    residual = inputs + jnp.dot(olow, wout_full, preferred_element_type=F32)
    route_ids = routes[:, 0]
    chosen = (route_ids[:, None] == jnp.arange(experts, dtype=jnp.int32)[None, :]).astype(BF)
    centroid_rows = jnp.dot(chosen, centroid_full, preferred_element_type=F32)
    gate = jax.nn.sigmoid(jnp.sum(residual * centroid_rows, axis=-1))
    before = jnp.tril(jnp.ones((rows, rows), BF), -1)
    rank = jnp.sum(jnp.dot(before, chosen, preferred_element_type=F32) * chosen.astype(F32), axis=-1)
    target = route_ids * capacity + rank.astype(jnp.int32)
    place = (jnp.arange(slots, dtype=jnp.int32)[:, None] == target[None, :]).astype(BF)
    grad_out = cotangent.astype(F32)
    sent = jnp.concatenate([residual.astype(BF), (gate[:, None] * grad_out).astype(BF)], axis=1)
    spread = jnp.dot(place, sent, preferred_element_type=F32).astype(BF)
    returned, came_back, olow_full, gain_part, n_rows, h_rows, df_rows, du_rows = expert_block(
        spread[:, :width].reshape(experts, capacity, width),
        spread[:, width:].reshape(experts, capacity, width),
        olow,
        gains,
        expert_in,
        expert_out,
    )
    grad_expert_out = jnp.einsum("krf,krd->kfd", h_rows, df_rows, preferred_element_type=F32)[None]
    grad_expert_in = jnp.einsum("krf,krd->kfd", du_rows, n_rows, preferred_element_type=F32)[None]
    expert_gain_share = lax.psum_scatter(gain_part[None], "dp", scatter_dimension=2, tiled=True)
    branch_tok = lax.dot_general(place, returned.reshape(slots, width), TN, preferred_element_type=F32)
    block_out = (residual + gate[:, None] * branch_tok).astype(BF)
    grad_logit = jnp.sum(grad_out * branch_tok, axis=-1) * gate * (1.0 - gate)
    grad_centroid = jnp.dot(chosen.astype(F32).T, grad_logit[:, None] * residual, precision=HIGH)
    back_rows = lax.dot_general(place, came_back.reshape(slots, width), TN, preferred_element_type=F32)
    grad_resid = grad_out + grad_logit[:, None] * centroid_rows + back_rows
    grad_attended = grad_resid.astype(BF)
    grad_mixed = lax.dot_general(grad_attended, wout_full, NT, preferred_element_type=F32).astype(BF)
    lse_rows = jnp.pad(lse[:, ::HEAD].T, ((0, 6), (0, 0)))
    dq_land, gq_land, go_land, gc_land = back_block(
        grad_mixed, grad_attended, qkv, mixed, lse_rows, normed_all,
        olow_full.reshape(experts * rows, width), grad_centroid[:, None, :],
    )
    dqkv = dq_land.reshape(8, rows, 3, 128).transpose(1, 2, 0, 3).reshape(rows, 3 * width)
    pieces = jnp.concatenate([w_near, w_far])
    order = lax.axis_index("dp") ^ jnp.array([0, 2, 1, 3], jnp.int32)
    grad_pieces = lax.dot_general(pieces, dqkv, (((2,), (1,)), ((), ())), preferred_element_type=F32)
    grad_normed = jnp.take(grad_pieces, jnp.argsort(order), axis=0).reshape(width, rows).T
    gain_full = small_full[:, 0].reshape(1, width).astype(F32)
    unit, inverse, _ = normalize(inputs, gain_full)
    grad_input, _ = norm_backward(grad_normed, unit, inverse, gain_full)
    grad_tokens = grad_resid + grad_input
    grad_qkv = gq_land.reshape(8, shard, 3, 128).transpose(1, 2, 0, 3).reshape(shard, 3 * width).astype(F32)
    grad_out_weight = go_land.transpose(1, 0, 2).reshape(shard, width).astype(F32)
    grad_norm_gain = jnp.sum(grad_qkv * qkv_weight.astype(F32), axis=1) / norm_gain.astype(F32)
    return (
        block_out,
        grad_tokens,
        grad_norm_gain,
        grad_qkv,
        grad_out_weight,
        gc_land[:, 0],
        expert_gain_share,
        grad_expert_in,
        grad_expert_out,
    )


def on_device(
    tokens,
    norm_gain,
    qkv_weight,
    out_weight,
    centroids,
    expert_gain,
    expert_in,
    expert_out,
    routes,
    cotangent,
):
    model_width = tokens.shape[1]
    local_rows = tokens.shape[0]
    experts = lax.axis_size("expert")
    capacity = max(2, 3 * local_rows // (2 * experts))
    slot_total = experts * capacity
    first_pos = lax.axis_index("expert") * local_rows
    scale = HEAD ** (-0.5)
    gain_full, qkv_full, out_full, centroid_full, expert_gain_full = fetch_dense(
        norm_gain, qkv_weight, out_weight, centroids, expert_gain
    )
    inputs = tokens.astype(jnp.float32)
    unit_attn, inverse_attn, normed_attn = normalize(inputs, gain_full.astype(jnp.float32))
    normed_low = normed_attn.astype(jnp.bfloat16)
    projected = jnp.dot(normed_low, qkv_full, preferred_element_type=jnp.float32).astype(
        jnp.bfloat16
    )
    queries = projected[:, :model_width]
    keyset = projected[:, model_width : 2 * model_width]
    values = projected[:, 2 * model_width :]
    query_heads = split_heads(queries)
    key_heads = split_heads(keyset)
    value_heads = split_heads(values)
    query_block = (first_pos + jnp.arange(local_rows, dtype=jnp.int32)) // BLOCK
    last_block = (first_pos + local_rows - 1) // BLOCK
    start_state = (
        jnp.zeros((local_rows, HEADS, HEAD), jnp.float32),
        jnp.full((HEADS, local_rows), NEGATIVE, jnp.float32),
        jnp.zeros((HEADS, local_rows), jnp.float32),
    )
    key_piece = lax.all_gather(keyset, "expert", axis=0, tiled=True)
    value_piece = lax.all_gather(values, "expert", axis=0, tiled=True)
    amount = key_piece.shape[0]

    def update(current):
        accumulated, highest, totals = current
        scores = (
            jnp.einsum(
                "qhd,khd->hqk",
                query_heads,
                split_heads(key_piece),
                preferred_element_type=jnp.float32,
            )
            * scale
        )
        piece_block = jnp.arange(amount, dtype=jnp.int32) // BLOCK
        visible = (piece_block[None, :] <= query_block[:, None])[None]
        scores = jnp.where(visible, scores, NEGATIVE)
        new_high = jnp.maximum(highest, jnp.max(scores, axis=-1))
        factor = jnp.exp(highest - new_high)
        weights = jnp.where(visible, jnp.exp(scores - new_high[:, :, None]), 0.0)
        totals = jnp.sum(weights, axis=-1)
        accumulated = accumulated * factor.T[:, :, None] + jnp.einsum(
            "hqk,khd->qhd",
            weights.astype(jnp.bfloat16),
            split_heads(value_piece),
            preferred_element_type=jnp.float32,
        )
        return (accumulated, new_high, totals)

    accumulated, highest, totals = lax.cond(
        jnp.int32(0) // BLOCK <= last_block, update, keep_state, start_state
    )
    mixed_heads = accumulated / totals.T[:, :, None]
    log_total = (highest + jnp.log(totals)).T
    mixed_low = mixed_heads.reshape(local_rows, model_width).astype(jnp.bfloat16)
    residual = inputs + jnp.dot(mixed_low, out_full, preferred_element_type=jnp.float32)
    route_ids = routes[:, 0]
    chosen = route_ids[:, None] == jnp.arange(experts, dtype=jnp.int32)[None, :]
    centroid_rows = jnp.dot(
        chosen.astype(jnp.bfloat16), centroid_full, preferred_element_type=jnp.float32
    )
    gate_value = jax.nn.sigmoid(jnp.sum(residual * centroid_rows, axis=-1))
    chosen_int = chosen.astype(jnp.int32)
    slot_index = jnp.sum((jnp.cumsum(chosen_int, axis=0) - 1) * chosen_int, axis=-1)
    target = route_ids * capacity + slot_index
    arrived = lax.all_to_all(
        send_slots(residual.astype(jnp.bfloat16), target, experts, capacity),
        "expert",
        split_axis=0,
        concat_axis=0,
        tiled=True,
    )
    expert_state = arrived.reshape(slot_total, model_width).astype(jnp.float32)
    gains_here = expert_gain_full[0].astype(jnp.float32)
    total_change = jnp.zeros_like(expert_state)
    stored = []
    for sublayer in range(2):
        unit_rows, inverse, normed = normalize(expert_state, gains_here[sublayer])
        normed_rows = normed.astype(jnp.bfloat16)
        first_full, second_full = (expert_in[0, sublayer], expert_out[0, sublayer])
        left_rows = spread_rows(normed_rows)
        hidden_pre = jnp.einsum(
            "rd,fd->rf", left_rows, first_full, preferred_element_type=jnp.float32
        )
        hidden_act, slope_pull = jax.vjp(exact_gelu, hidden_pre)
        hidden_low = hidden_act.astype(jnp.bfloat16)
        change = sum_rows(partial(row_product, hidden_low, second_full), slot_total)
        expert_state = expert_state + change
        total_change = total_change + change
        stored.append((unit_rows, inverse, left_rows, hidden_low, slope_pull))
    branch_low = total_change.astype(jnp.bfloat16)
    returned = lax.all_to_all(
        branch_low.reshape(experts, capacity, model_width),
        "expert",
        split_axis=0,
        concat_axis=0,
        tiled=True,
    )
    branch_tok = returned.reshape(slot_total, model_width)[target].astype(jnp.float32)
    block_out = (residual + gate_value[:, None] * branch_tok).astype(jnp.bfloat16)
    gain_full, qkv_full, out_full, centroid_full, expert_gain_full = fetch_dense(
        norm_gain, qkv_weight, out_weight, centroids, expert_gain
    )
    gains_here = expert_gain_full[0].astype(jnp.float32)
    grad_out = cotangent.astype(jnp.float32)
    grad_logit = jnp.sum(grad_out * branch_tok, axis=-1) * gate_value * (1.0 - gate_value)
    grad_centroid = jnp.dot(
        chosen.astype(jnp.float32).T, grad_logit[:, None] * residual, precision=HIGH
    )
    grad_resid = grad_out + grad_logit[:, None] * centroid_rows
    grad_branch = (gate_value[:, None] * grad_out).astype(jnp.bfloat16)
    branch_grads = lax.all_to_all(
        send_slots(grad_branch, target, experts, capacity),
        "expert",
        split_axis=0,
        concat_axis=0,
        tiled=True,
    )
    grad_change = branch_grads.reshape(slot_total, model_width).astype(jnp.float32)
    grad_state = jnp.zeros_like(grad_change)
    gain_grads = [None, None]
    first_grads = [None, None]
    second_grads = [None, None]
    for sublayer in (1, 0):
        unit_rows, inverse, left_rows, hidden_low, slope_pull = stored[sublayer]
        grad_rows_low = (grad_change + grad_state).astype(jnp.bfloat16)
        first_full, second_full = (expert_in[0, sublayer], expert_out[0, sublayer])
        grad_rows = spread_rows(grad_rows_low)
        grad_hidden = jnp.einsum(
            "rd,fd->rf", grad_rows, second_full, preferred_element_type=jnp.float32
        )
        grad_pre = slope_pull(grad_hidden)[0].astype(jnp.bfloat16)
        grad_first = jnp.einsum(
            "rf,rd->fd", grad_pre, left_rows, preferred_element_type=jnp.float32
        )
        grad_second = jnp.einsum(
            "rf,rd->fd", hidden_low, grad_rows, preferred_element_type=jnp.float32
        )
        grad_normed = sum_rows(partial(row_product, grad_pre, first_full), slot_total)
        grad_input, gain_grad = norm_backward(grad_normed, unit_rows, inverse, gains_here[sublayer])
        grad_state = grad_state + grad_input
        gain_grads[sublayer] = gain_grad
        first_grads[sublayer] = grad_first
        second_grads[sublayer] = grad_second
    came_back = lax.all_to_all(
        grad_state.astype(jnp.bfloat16).reshape(experts, capacity, model_width),
        "expert",
        split_axis=0,
        concat_axis=0,
        tiled=True,
    )
    grad_resid = grad_resid + came_back.reshape(slot_total, model_width)[target].astype(jnp.float32)
    grad_attended = grad_resid.astype(jnp.bfloat16)
    grad_out_weight = jnp.einsum(
        "rd,re->de", mixed_low, grad_attended, preferred_element_type=jnp.float32
    )
    grad_mixed = jnp.einsum(
        "re,de->rd", grad_attended, out_full, preferred_element_type=jnp.float32
    ).astype(jnp.bfloat16)
    grad_heads = split_heads(grad_mixed)
    delta_rows = jnp.sum(grad_heads.astype(jnp.float32) * mixed_heads, axis=-1)
    zero_heads = jnp.zeros((local_rows, HEADS, HEAD), jnp.float32)
    running = (zero_heads, zero_heads, zero_heads)
    offset = jnp.int32(0)
    fold_key_piece = lax.all_gather(keyset, "expert", axis=0, tiled=True)
    fold_value_piece = lax.all_gather(values, "expert", axis=0, tiled=True)
    query_piece = lax.all_gather(queries, "expert", axis=0, tiled=True)
    grad_piece = lax.all_gather(grad_mixed, "expert", axis=0, tiled=True)
    log_piece = lax.all_gather(log_total.astype(jnp.bfloat16), "expert", axis=0, tiled=True).astype(
        jnp.float32
    )
    delta_piece = lax.all_gather(
        delta_rows.astype(jnp.bfloat16), "expert", axis=0, tiled=True
    ).astype(jnp.float32)
    fold_amount = fold_key_piece.shape[0]
    piece_block = jnp.arange(fold_amount, dtype=jnp.int32) // BLOCK

    def to_queries(current):
        grad_query, grad_key, grad_value = current
        piece_keys = split_heads(fold_key_piece)
        scores = (
            jnp.einsum("qhd,khd->hqk", query_heads, piece_keys, preferred_element_type=jnp.float32)
            * scale
        )
        visible = (piece_block[None, :] <= query_block[:, None])[None]
        weights = jnp.where(visible, jnp.exp(scores - log_total.T[:, :, None]), 0.0)
        grad_weights = jnp.einsum(
            "qhd,khd->hqk",
            grad_heads,
            split_heads(fold_value_piece),
            preferred_element_type=jnp.float32,
        )
        grad_scores = (weights * (grad_weights - delta_rows.T[:, :, None])).astype(jnp.bfloat16)
        grad_query = (
            jnp.einsum("hqk,khd->qhd", grad_scores, piece_keys, preferred_element_type=jnp.float32)
            * scale
        )
        return (grad_query, grad_key, grad_value)

    def to_keys(current):
        grad_query, grad_key, grad_value = current
        piece_queries = split_heads(query_piece)
        piece_grads = split_heads(grad_piece)
        scores = (
            jnp.einsum("qhd,khd->hqk", piece_queries, key_heads, preferred_element_type=jnp.float32)
            * scale
        )
        visible = (query_block[None, :] <= piece_block[:, None])[None]
        weights = jnp.where(visible, jnp.exp(scores - log_piece.T[:, :, None]), 0.0)
        grad_weights = jnp.einsum(
            "qhd,khd->hqk", piece_grads, value_heads, preferred_element_type=jnp.float32
        )
        grad_scores = (weights * (grad_weights - delta_piece.T[:, :, None])).astype(jnp.bfloat16)
        grad_key = (
            grad_key
            + jnp.einsum(
                "hqk,qhd->khd", grad_scores, piece_queries, preferred_element_type=jnp.float32
            )
            * scale
        )
        grad_value = grad_value + jnp.einsum(
            "hqk,qhd->khd",
            weights.astype(jnp.bfloat16),
            piece_grads,
            preferred_element_type=jnp.float32,
        )
        return (grad_query, grad_key, grad_value)

    running = lax.cond(offset // BLOCK <= last_block, to_queries, keep_state, running)
    grad_query, grad_key, grad_value = lax.cond(
        query_block[0] <= (offset + fold_amount - 1) // BLOCK, to_keys, keep_state, running
    )
    grad_qkv_rows = jnp.concatenate(
        [
            grad_query.reshape(local_rows, model_width),
            grad_key.reshape(local_rows, model_width),
            grad_value.reshape(local_rows, model_width),
        ],
        axis=1,
    ).astype(jnp.bfloat16)
    grad_qkv = jnp.einsum(
        "rd,re->de", normed_low, grad_qkv_rows, preferred_element_type=jnp.float32
    )
    grad_normed_attn = jnp.einsum(
        "re,de->rd", grad_qkv_rows, qkv_full, preferred_element_type=jnp.float32
    )
    grad_input_attn, attn_gain_grad = norm_backward(
        grad_normed_attn, unit_attn, inverse_attn, gain_full.astype(jnp.float32)
    )
    grad_tokens = grad_resid + grad_input_attn
    expert_gain_grad = jnp.stack(gain_grads)[None]
    gain_share, qkv_share, out_share, centroid_share, expert_gain_share = (
        lax.psum_scatter(
            attn_gain_grad.astype(jnp.bfloat16), "dp", scatter_dimension=0, tiled=True
        ).astype(jnp.float32),
        lax.psum_scatter(
            grad_qkv.astype(jnp.bfloat16), "dp", scatter_dimension=0, tiled=True
        ).astype(jnp.float32),
        lax.psum_scatter(
            grad_out_weight.astype(jnp.bfloat16), "dp", scatter_dimension=0, tiled=True
        ).astype(jnp.float32),
        lax.psum_scatter(
            grad_centroid.astype(jnp.bfloat16), "dp", scatter_dimension=1, tiled=True
        ).astype(jnp.float32),
        lax.psum_scatter(
            expert_gain_grad.astype(jnp.bfloat16), "dp", scatter_dimension=2, tiled=True
        ).astype(jnp.float32),
    )
    gain_total, qkv_total, out_total, centroid_total = (
        lax.psum(gain_share.astype(jnp.bfloat16), "expert").astype(jnp.float32),
        lax.psum(qkv_share.astype(jnp.bfloat16), "expert").astype(jnp.float32),
        lax.psum(out_share.astype(jnp.bfloat16), "expert").astype(jnp.float32),
        lax.psum(centroid_share.astype(jnp.bfloat16), "expert").astype(jnp.float32),
    )
    grad_expert_in = jnp.stack(first_grads)[None]
    grad_expert_out = jnp.stack(second_grads)[None]
    return (
        block_out,
        grad_tokens,
        gain_total,
        qkv_total,
        out_total,
        centroid_total,
        expert_gain_share,
        grad_expert_in,
        grad_expert_out,
    )


def solution(mesh):
    in_specs = (
        P(("dp", "expert"), None),
        P("dp"),
        P("dp", None),
        P("dp", None),
        P(None, "dp"),
        P("expert", None, "dp"),
        P("expert", None, "dp", None),
        P("expert", None, "dp", None),
        P(("dp", "expert"), None),
        P(("dp", "expert"), None),
    )
    out_specs = (
        P(("dp", "expert"), None),
        P(("dp", "expert"), None),
        P("dp"),
        P("dp", None),
        P("dp", None),
        P(None, "dp"),
        P("expert", None, "dp"),
        P("expert", None, "dp", None),
        P("expert", None, "dp", None),
    )
    split = mesh.shape["dp"] == 4 and mesh.shape["expert"] == 8
    return jax.shard_map(
        on_device_split if split else on_device, mesh=mesh, in_specs=in_specs, out_specs=out_specs, check_vma=False
    )
```

```python
from functools import partial

import jax
import jax.numpy as jnp
from jax import lax
from jax.experimental import pallas as pl
from jax.experimental.pallas import tpu as pltpu
from jax.sharding import PartitionSpec as P

HEADS = 16
HEAD = 64
BLOCK = 256


EPS = 1e-05
NEGATIVE = -1e30
HIGH = lax.Precision.HIGHEST


def normalize(inputs, gain_row):
    centered = inputs - jnp.mean(inputs, axis=-1, keepdims=True)
    inverse = lax.rsqrt(jnp.mean(centered * centered, axis=-1, keepdims=True) + EPS)
    unit_rows = centered * inverse
    return (unit_rows, inverse, unit_rows * gain_row)


def norm_backward(grad_normed, unit_rows, inverse, gain_row):
    grad_unit = grad_normed * gain_row
    first_mean = jnp.mean(grad_unit, axis=-1, keepdims=True)
    second_mean = jnp.mean(grad_unit * unit_rows, axis=-1, keepdims=True)
    grad_input = inverse * (grad_unit - first_mean - unit_rows * second_mean)
    return (grad_input, jnp.sum(grad_normed * unit_rows, axis=0))


def split_heads(matrix):
    return matrix.reshape(matrix.shape[0], HEADS, HEAD)


def exact_gelu(inputs):
    return jax.nn.gelu(inputs, approximate=False)


def keep_state(current):
    return current


def row_product(left_rows, right_matrix, offset, amount):
    return jnp.dot(left_rows, right_matrix, preferred_element_type=jnp.float32)


def fetch_dense(norm_gain, qkv_weight, out_weight, centroids, expert_gain):
    return (
        lax.all_gather(norm_gain, "dp", axis=0, tiled=True),
        lax.all_gather(qkv_weight, "dp", axis=0, tiled=True),
        lax.all_gather(out_weight, "dp", axis=0, tiled=True),
        lax.all_gather(centroids, "dp", axis=1, tiled=True),
        lax.all_gather(expert_gain, "dp", axis=2, tiled=True),
    )


def spread_rows(rows_low):
    return lax.all_gather(rows_low, "dp", axis=0, tiled=True)


def sum_rows(term, amount):
    return lax.psum_scatter(
        term(jnp.int32(0), amount * lax.axis_size("dp")).astype(jnp.bfloat16),
        "dp",
        scatter_dimension=0,
        tiled=True,
    ).astype(jnp.float32)


def send_slots(rows_low, target, experts, capacity):
    buffer_rows = (
        jnp.zeros((experts * capacity, rows_low.shape[1]), rows_low.dtype).at[target].set(rows_low)
    )
    return buffer_rows.reshape(experts, capacity, rows_low.shape[1])


BF = jnp.bfloat16
F32 = jnp.float32
NT = (((1,), (1,)), ((), ()))
TN = (((0,), (0,)), ((), ()))
TILE = 256
MESH_ID = pl.DeviceIdType.MESH


def mean_last(v):
    return jnp.mean(v, axis=-1, keepdims=True)


def dp_peers():
    me = lax.axis_index("dp")
    sibling = me + 1 - 2 * lax.rem(me, 2)
    across = lax.rem(me + 2, 4)
    diagonal = lax.rem(sibling + 2, 4)
    return me, sibling, across, diagonal


def expert_peers():
    me = lax.axis_index("expert")
    z, x = me // 2, lax.rem(me, 2)
    beside = me + 1 - 2 * x
    near = z + 1 - 2 * lax.rem(z, 2)
    low, high = lax.rem(z, 2), z // 2
    inner = low + high - 2 * low * high
    flip, turn = 3 - z, lax.rem(z + 2, 4)
    second = inner * flip + (1 - inner) * turn
    third = inner * turn + (1 - inner) * flip
    return me, z, x, beside, (near, second, third)


def greet(targets):
    barrier = pltpu.get_barrier_semaphore()
    for target in targets:
        pl.semaphore_signal(barrier, inc=1, device_id=target, device_id_type=MESH_ID)
    pl.semaphore_wait(barrier, len(targets))


def others(n, me):
    return [lax.rem(me + d, n) for d in range(1, n)]


def push(src, dst, send, recv, target):
    return pltpu.make_async_remote_copy(
        src_ref=src, dst_ref=dst, send_sem=send, recv_sem=recv, device_id=target, device_id_type=MESH_ID
    )


class Spread:
    def __init__(self, own_src, slots, send, recv, chunks):
        self.me, self.z, self.x, self.beside, self.zs = expert_peers()
        self.own_src, self.slots, self.send, self.recv, self.chunks = own_src, slots, send, recv, chunks
        self.part = own_src.shape[0] // chunks

    def rows(self, c):
        return pl.ds(c * self.part, self.part)

    def own(self, way, c):
        peer = self.beside if way == 0 else 2 * (self.z + (1 if way == 1 else -1)) + self.x
        return push(
            self.own_src.at[self.rows(c)], self.slots.at[self.me, self.rows(c)],
            self.send.at[way * self.chunks + c], self.recv.at[self.me * self.chunks + c], {"expert": peer},
        )

    def slot(self, s, c, base, peer):
        block = self.slots.at[s, self.rows(c)]
        return push(block, block, self.send.at[base * self.chunks + c], self.recv.at[s * self.chunks + c], {"expert": peer})

    def own_all(self, act):
        for way in range(3):
            for c in range(self.chunks):
                if way == 0:
                    act(self.own(way, c))
                else:
                    @pl.when(self.z < 3 if way == 1 else self.z > 0)
                    def _():
                        act(self.own(way, c))

    def start(self):
        self.own_all(lambda cp: cp.start())

    def each(self, d, act):
        for sign in (-1, 1):
            zz = self.z + sign * d
            onward = self.z - sign

            @pl.when(jnp.logical_and(zz >= 0, zz <= 3))
            def _():
                s = 2 * zz + self.x
                for c in range(self.chunks):
                    act(s, zz, onward, c)

    def step(self, d):
        def act(s, zz, onward, c):
            self.slot(s, c, 0, self.beside).wait_recv()

            @pl.when(jnp.logical_and(onward >= 0, onward <= 3))
            def _():
                self.slot(s, c, 7 + zz, 2 * onward + self.x).start()

            self.slot(s, c, 3 + zz, self.beside).start()

        self.each(d, act)

    def wait_beside(self, zz):
        for c in range(self.chunks):
            self.slot(2 * zz + 1 - self.x, c, 0, self.beside).wait_recv()

    def drain(self):
        self.own_all(lambda cp: cp.wait_send())

        def act(s, zz, onward, c):
            @pl.when(jnp.logical_and(onward >= 0, onward <= 3))
            def _():
                self.slot(s, c, 7 + zz, 2 * onward + self.x).wait_send()

            self.slot(s, c, 3 + zz, self.beside).wait_send()

        for d in (1, 2, 3):
            self.each(d, act)


class Weights:
    def __init__(self, src, first, rows, full, send, recv, copy):
        self.j, self.sibling, self.across, self.diagonal = dp_peers()
        self.src, self.full, self.send, self.recv = src.at[pl.ds(first, rows)], full, send, recv
        self.keep = pltpu.make_async_copy(self.src, full.at[self.j], copy)

    def copy(self, kind):
        if kind == 2:
            block = self.full.at[self.across]
            return push(block, block, self.send.at[2], self.recv.at[self.across], {"dp": self.sibling})
        peer = self.sibling if kind == 0 else self.across
        return push(self.src, self.full.at[self.j], self.send.at[kind], self.recv.at[self.j], {"dp": peer})

    def start(self):
        self.copy(1).start()
        self.copy(0).start()
        self.keep.start()

    def arrival(self, s):
        return push(self.src, self.full.at[s], self.send.at[0], self.recv.at[s], {"dp": self.sibling})

    def relay(self):
        self.arrival(self.across).wait_recv()
        self.copy(2).start()

    def drain(self):
        self.arrival(self.sibling).wait_recv()
        self.arrival(self.diagonal).wait_recv()
        for kind in range(3):
            self.copy(kind).wait_send()
        self.keep.wait()


def lane_masks(rows):
    lane = lax.broadcasted_iota(jnp.int32, (rows, 128), 1)
    return lane < HEAD


def front_kernel(
    tok, small, wqkv, wout,
    olow, normed_out, qkv_out, mixed_out, lse_out, wout_full, small_full, wfirst,
    held, wblk, normed, qkv, mixed, lse, mixed_low, gain, bounce, smalls,
    tok_send, tok_recv, w_send, w_recv, o_send, o_recv, copy_sem, q_send, q_recv,
):
    j, sibling, across, diagonal = dp_peers()
    e, z, x, beside, zs = expert_peers()
    rows, width = tok.shape
    shard = wqkv.shape[0]
    lanes = 128

    def mine(s):
        return pl.ds(pl.multiple_of(s * shard, shard), shard)

    mycols = pl.ds(pl.multiple_of(e * lanes, lanes), lanes)
    own_tok = pltpu.make_async_copy(tok, held.at[e], copy_sem.at[0])
    own_tok.start()
    own_w = [
        pltpu.make_async_copy(
            wqkv.at[:, pl.ds(pl.multiple_of(i * width + e * lanes, lanes), lanes)],
            wblk.at[mine(j), pl.ds(i * lanes, lanes)],
            copy_sem.at[1 + i],
        )
        for i in range(3)
    ]
    for cp in own_w:
        cp.start()
    own_out = pltpu.make_async_copy(wout, bounce, copy_sem.at[4])
    own_out.start()
    smalls[j] = small[...]
    greet([{"expert": p} for p in others(8, e)] + [{"dp": p} for p in (sibling, across, diagonal)])

    toks = Spread(tok, held, tok_send, tok_recv, 2)
    toks.start()
    later = Weights(wqkv, 0, shard // 2, wfirst, q_send, q_recv, copy_sem.at[7])
    for cp in own_w:
        cp.wait()

    def w_copy(kind):
        if kind == 0:
            return push(wblk.at[mine(j)], wblk.at[mine(j)], w_send.at[0], w_recv.at[j], {"dp": sibling})
        if kind == 1:
            return push(wblk.at[mine(j)], wblk.at[mine(j)], w_send.at[1], w_recv.at[j], {"dp": across})
        return push(wblk.at[mine(across)], wblk.at[mine(across)], w_send.at[2], w_recv.at[across], {"dp": sibling})

    def w_arrival(s):
        return push(wblk.at[mine(s)], wblk.at[mine(s)], w_send.at[0], w_recv.at[s], {"dp": sibling})

    def s_copy(i):
        return push(small, smalls.at[j], w_send.at[3 + i], w_recv.at[4 + j], {"dp": (sibling, across, diagonal)[i]})

    def s_arrival(s):
        return push(small, smalls.at[s], w_send.at[3], w_recv.at[4 + s], {"dp": sibling})

    def out_copy(kind):
        if kind == 0:
            return push(wout, wout_full.at[mine(j)], w_send.at[6], w_recv.at[8 + j], {"dp": sibling})
        if kind == 1:
            return push(wout, wout_full.at[mine(j)], w_send.at[7], w_recv.at[8 + j], {"dp": across})
        return push(wout_full.at[mine(across)], wout_full.at[mine(across)], w_send.at[8], w_recv.at[8 + across], {"dp": sibling})

    def out_arrival(s):
        return push(wout, wout_full.at[mine(s)], w_send.at[6], w_recv.at[8 + s], {"dp": sibling})

    for i in range(3):
        s_copy(i).start()
    w_copy(1).start()
    w_copy(0).start()
    out_copy(1).start()
    out_copy(0).start()
    later.start()
    own_out.wait()
    keep_out = pltpu.make_async_copy(bounce, wout_full.at[mine(j)], copy_sem.at[4])
    keep_out.start()
    for s in (sibling, across, diagonal):
        s_arrival(s).wait_recv()
    gain[...] = jnp.concatenate([smalls[s, 0:1, :] for s in range(4)], axis=1).astype(F32)
    w_arrival(across).wait_recv()
    w_copy(2).start()
    w_arrival(sibling).wait_recv()
    w_arrival(diagonal).wait_recv()

    def project(zz):
        base = zz * 2 * rows
        for xx in range(2):
            def norm_rows(t, c):
                rs = pl.ds(pl.multiple_of(t * 64, 64), 64)
                v = held[2 * zz + xx, rs, :].astype(F32)
                center = v - mean_last(v)
                inverse = lax.rsqrt(mean_last(center * center) + EPS)
                at = pl.ds(pl.multiple_of(base + xx * rows + t * 64, 64), 64)
                normed[at, :] = (center * inverse * gain[...]).astype(BF)
                return c
            lax.fori_loop(0, rows // 64, norm_rows, 0)
        at = pl.ds(pl.multiple_of(base, 2 * rows), 2 * rows)
        qkv[at, :] = jnp.dot(normed[at, :], wblk[...], preferred_element_type=F32).astype(BF)

    own_tok.wait()
    toks.step(1)
    toks.wait_beside(z)
    project(z)
    toks.step(2)
    toks.wait_beside(zs[0])
    project(zs[0])
    toks.step(3)
    out_arrival(across).wait_recv()
    out_copy(2).start()
    toks.wait_beside(zs[1])
    project(zs[1])
    toks.wait_beside(zs[2])
    project(zs[2])
    stores = [
        pltpu.make_async_copy(normed, normed_out, copy_sem.at[0]),
        pltpu.make_async_copy(qkv, qkv_out, copy_sem.at[1]),
    ]
    for cp in stores:
        cp.start()

    def o_copy(dest):
        return push(mixed_low.at[pl.ds(dest * rows, rows)], olow.at[:, mycols], o_send.at[dest], o_recv.at[e], {"expert": dest})

    def o_own(dest):
        return pltpu.make_async_copy(mixed_low.at[pl.ds(dest * rows, rows)], olow.at[:, mycols], copy_sem.at[5])

    left = lane_masks(2 * rows)
    for b in (3, 2, 1, 0):
        qs = qkv[pl.ds(b * 2 * rows, 2 * rows), 0:lanes]
        keys = qkv[0 : (b + 1) * 2 * rows, lanes : 2 * lanes]
        vals = qkv[0 : (b + 1) * 2 * rows, 2 * lanes : 3 * lanes]
        outs, logs = [], []
        for h in range(2):
            mask = left if h == 0 else jnp.logical_not(left)
            q_h = jnp.where(mask, qs.astype(F32) * (HEAD ** -0.5), 0.0).astype(BF)
            sc = lax.dot_general(q_h, keys, NT, preferred_element_type=F32)
            top = jnp.max(sc, axis=-1, keepdims=True)
            pr = jnp.exp(sc - top)
            tot = jnp.sum(pr, axis=-1, keepdims=True)
            outs.append(jnp.dot(pr.astype(BF), vals, preferred_element_type=F32) / tot)
            logs.append(top + jnp.log(tot))
        at = pl.ds(b * 2 * rows, 2 * rows)
        res = jnp.where(left, outs[0], outs[1])
        mixed[at, :] = res
        mixed_low[at, :] = res.astype(BF)
        lse[at, :] = jnp.where(left, logs[0], logs[1])
        for dest in (2 * b, 2 * b + 1):
            @pl.when(dest != e)
            def _():
                o_copy(dest).start()

            @pl.when(dest == e)
            def _():
                o_own(dest).start()
    more = [
        pltpu.make_async_copy(mixed, mixed_out, copy_sem.at[2]),
        pltpu.make_async_copy(lse, lse_out, copy_sem.at[3]),
        pltpu.make_async_copy(smalls, small_full, copy_sem.at[6]),
    ]
    for cp in more:
        cp.start()
    for dest in range(8):
        @pl.when(dest != e)
        def _():
            push(mixed_low.at[pl.ds(0, rows)], olow.at[:, pl.ds(dest * lanes, lanes)], o_send.at[dest], o_recv.at[dest], {"expert": dest}).wait_recv()
            o_copy(dest).wait_send()

        @pl.when(dest == e)
        def _():
            o_own(dest).wait()
    later.relay()
    for s in (sibling, diagonal):
        out_arrival(s).wait_recv()
    toks.drain()
    later.drain()
    for i in range(3):
        w_copy(i).wait_send()
        s_copy(i).wait_send()
        out_copy(i).wait_send()
    keep_out.wait()
    for cp in stores + more:
        cp.wait()


def front_block(tokens, small, qkv_weight, out_weight):
    rows, width = tokens.shape
    seq = 8 * rows
    shard = qkv_weight.shape[0]
    any_spec = pl.BlockSpec(memory_space=pl.ANY)
    vmem_spec = pl.BlockSpec(memory_space=pltpu.VMEM)
    V = pltpu.VMEM
    D = pltpu.SemaphoreType.DMA
    S = jax.ShapeDtypeStruct
    return pl.pallas_call(
        front_kernel,
        out_shape=(
            S((rows, width), BF), S((seq, width), BF), S((seq, 384), BF), S((seq, 128), F32), S((seq, 128), F32),
            S((width, width), BF), S((4,) + small.shape, BF), S((4, shard // 2, 3 * width), BF),
        ),
        in_specs=[any_spec, vmem_spec, any_spec, any_spec],
        out_specs=(any_spec,) * 8,
        scratch_shapes=[
            V((8, rows, width), BF), V((width, 384), BF), V((seq, width), BF), V((seq, 384), BF),
            V((seq, 128), F32), V((seq, 128), F32), V((seq, 128), BF), V((1, width), F32), V((shard, width), BF),
            V((4,) + small.shape, BF),
            D((22,)), D((16,)), D((9,)), D((12,)), D((8,)), D((8,)), D((8,)), D((3,)), D((4,)),
        ],
        compiler_params=pltpu.CompilerParams(collective_id=2, has_side_effects=True, vmem_limit_bytes=56 * 1024 * 1024),
        name="front_block",
    )(tokens, small, qkv_weight, out_weight)


def expert_kernel(
    zslots, dslots, olow, gain_ref, w1_hbm, w2_hbm,
    returned, came_back, olow_full, ggain_ref, n_out, h_out, df_out, du_out,
    w1, w2, x, hid, gpr, unit_s, inv_s, state, total, grad_in, own, far, f1, f3, ssum, rf1, rf3, rss,
    zland, dland, bsend, gsend, ggain, gland,
    send_sem, recv_sem, a_send, a_recv, g_send, g_recv, copy_sem, own_sem, e_send, e_recv,
):
    cap, width = zslots.shape[1:]
    half = 4 * cap
    pair_rows = 2 * half
    tiles = width // TILE
    j, sibling, across, diagonal = dp_peers()
    e, zpos, xpos, beside, zs = expert_peers()

    loads = []
    for i, (src, dst) in enumerate(
        [(w1_hbm.at[0, 0], w1.at[0]), (w2_hbm.at[0, 0], w2.at[0]),
         (w1_hbm.at[0, 1], w1.at[1]), (w2_hbm.at[0, 1], w2.at[1])]
    ):
        cp = pltpu.make_async_copy(src, dst, copy_sem.at[i])
        cp.start()
        loads.append(cp)
    zx = (zpos, zs[0], lax.rem(zpos + 2, 4), 3 - zpos)

    def peer_at(q):
        return 2 * zx[q // 2] + q % 2

    def seat(q):
        return 2 * (q // 2) + xpos

    greet([{"expert": p} for p in others(8, e)] + [{"dp": p} for p in (sibling, across, diagonal)])

    def swap(src, dst, which, q):
        peer = peer_at(q)
        if which < 2:
            return push(src.at[peer], dst.at[seat(q)], a_send.at[which * 8 + q], a_recv.at[which * 8 + seat(q)], {"expert": peer})
        return push(src.at[q], dst.at[e], a_send.at[which * 8 + q], a_recv.at[which * 8 + seat(q)], {"expert": peer})

    def swap_arrival(src, dst, which, q):
        peer = peer_at(q)
        if which < 2:
            return push(src.at[peer], dst.at[q], a_send.at[which * 8 + q], a_recv.at[which * 8 + q], {"expert": peer})
        return push(src.at[q], dst.at[peer], a_send.at[which * 8 + q], a_recv.at[which * 8 + q], {"expert": peer})

    def swap_own(src, dst, which):
        if which < 2:
            return pltpu.make_async_copy(src.at[e], dst.at[xpos], own_sem.at[which])
        return pltpu.make_async_copy(src.at[xpos], dst.at[e], own_sem.at[which])

    def for_places(h, act, mine):
        for q in range(4 * h, 4 * h + 4):
            if q >= 2:
                act(q)
            else:
                @pl.when(xpos != q)
                def _():
                    act(q)

                @pl.when(xpos == q)
                def _():
                    mine()

    for which, (src, dst) in enumerate([(zslots, zland), (dslots, dland)]):
        for h in (1, 0):
            for_places(h, lambda q: swap(src, dst, which, q).start(), lambda: swap_own(src, dst, which).start())
    olows = Spread(olow, olow_full, g_send, g_recv, 1)
    own_o = pltpu.make_async_copy(olow, olow_full.at[e], copy_sem.at[12])
    own_o.start()

    def rows_of(h, r):
        return pl.ds((h * 4 + r) * half, half)

    def remote(src, dst, kind, p, h, peer):
        i = (p * 2 + h) * 6 + kind
        return push(src, dst, send_sem.at[i], recv_sem.at[i], {"dp": peer})

    def copy_of(kind, p, h):
        q = p * 2 + h
        if kind == 0:
            return remote(x.at[p, rows_of(h, 0)], x.at[p, rows_of(h, 1)], 0, p, h, sibling)
        if kind == 1:
            return remote(x.at[p, rows_of(h, 0)], x.at[p, rows_of(h, 2)], 1, p, h, across)
        if kind == 2:
            return remote(x.at[p, rows_of(h, 2)], x.at[p, rows_of(h, 3)], 2, p, h, sibling)
        if kind == 3:
            return remote(f1.at[q], rf1.at[q], 3, p, h, sibling)
        if kind == 4:
            return remote(f3.at[q], rf3.at[q], 4, p, h, sibling)
        return remote(ssum.at[q], rss.at[q], 5, p, h, across)

    layer_of = (0, 1, 1, 0)

    def start_rows(p, h):
        k = layer_of[p]
        rs = pl.ds(h * half, half)
        if p < 2:
            v = state[rs, :]
            center = v - mean_last(v)
            inverse = lax.rsqrt(mean_last(center * center) + EPS)
            unit = center * inverse
            unit_s[k, rs, :] = unit
            inv_s[k, rs, :] = jnp.broadcast_to(inverse, (half, 128))
            x[p, rows_of(h, 0), :] = (unit * gain_ref[pl.ds(k, 1), :]).astype(BF)
        else:
            x[p, rows_of(h, 0), :] = (grad_in[rs, :] + state[rs, :]).astype(BF)
        copy_of(1, p, h).start()
        copy_of(0, p, h).start()

    def compute(p, h, pair):
        k = layer_of[p]
        base = pl.ds((h * 2 + pair) * pair_rows, pair_rows)
        left_w, right_w = (w1, w2) if p < 2 else (w2, w1)
        q = p * 2 + h

        def up(t, c):
            cols = pl.ds(pl.multiple_of(t * TILE, TILE), TILE)
            pre = lax.dot_general(x[p, base, :], left_w[k, cols, :], NT, preferred_element_type=F32)
            if p < 2:
                cdf = 0.5 * (1.0 + lax.erf(pre * (0.5 ** 0.5)))
                pdf = jnp.exp(-0.5 * pre * pre) * 0.3989422804014327
                hid[k, base, cols] = (pre * cdf).astype(BF)
                gpr[k, base, cols] = cdf + pre * pdf
            else:
                hid[2 + k, base, cols] = (pre * gpr[k, base, cols]).astype(BF)
            return c

        lax.fori_loop(0, tiles, up, 0)
        slot = k if p < 2 else 2 + k

        def down(t, c):
            cols = pl.ds(pl.multiple_of(t * TILE, TILE), TILE)
            res = jnp.dot(hid[slot, base, :], right_w[k, :, cols], preferred_element_type=F32)
            if pair == 0:
                own[h, :, cols] = res[:half]
                f1[q, :, cols] = res[half:].astype(BF)
            else:
                far[h, :, cols] = res[:half]
                f3[q, :, cols] = res[half:].astype(BF)
                remote(f3.at[q, :, cols], rf3.at[q, :, cols], 4, p, h, sibling).start()
            return c

        lax.fori_loop(0, tiles, down, 0)
        if pair == 0:
            copy_of(3, p, h).start()

    def send_sum(p, h):
        q = p * 2 + h
        copy_of(4, p, h).wait_recv()
        ssum[q] = (far[h] + rf3[q].astype(F32)).astype(BF)
        copy_of(5, p, h).start()

    def give_back(buf, dst, which, h):
        for_places(h, lambda q: swap(buf, dst, which, q).start(), lambda: swap_own(buf, dst, which).start())

    def finish(p, h):
        k = layer_of[p]
        q = p * 2 + h
        rs = pl.ds(h * half, half)
        copy_of(3, p, h).wait_recv()
        copy_of(5, p, h).wait_recv()
        got = own[h] + rf1[q].astype(F32) + rss[q].astype(F32)
        if p == 0:
            state[rs, :] = state[rs, :] + got
            total[rs, :] = got
        elif p == 1:
            total[rs, :] = total[rs, :] + got
            for i in range(4):
                bsend[4 * h + i] = total[pl.ds(h * half + i * cap, cap), :].astype(BF)
            state[rs, :] = jnp.zeros((half, width), F32)
            give_back(bsend, returned, 2, h)
        else:
            unit = unit_s[k, rs, :]
            part = jnp.sum(got * unit, axis=0, keepdims=True)
            if h == 0:
                ggain[pl.ds(k, 1), :] = part
            else:
                ggain[pl.ds(k, 1), :] = ggain[pl.ds(k, 1), :] + part
            a = got * gain_ref[pl.ds(k, 1), :]
            back = inv_s[k, rs, :][:, :1] * (a - mean_last(a) - unit * mean_last(a * unit))
            state[rs, :] = state[rs, :] + back
            if p == 3:
                for i in range(4):
                    gsend[4 * h + i] = state[pl.ds(h * half + i * cap, cap), :].astype(BF)
                give_back(gsend, came_back, 3, h)

    def relay(p, h):
        copy_of(1, p, h).wait_recv()
        copy_of(2, p, h).start()

    stores = []

    def store(i, src, dst):
        cp = pltpu.make_async_copy(src, dst, copy_sem.at[4 + i])
        cp.start()
        stores.append(cp)

    def landed(src, buf, which, h, out):
        for_places(h, lambda q: swap_arrival(src, buf, which, q).wait_recv(), lambda: swap_own(src, buf, which).wait())
        for q in range(4 * h, 4 * h + 4):
            out[pl.ds(q * cap, cap), :] = buf[q].astype(F32)

    def gain_copy(i):
        s = (sibling, across, diagonal)[i]
        return push(ggain.at[:, pl.ds(pl.multiple_of(s * shard, shard), shard)], gland.at[j], e_send.at[i], e_recv.at[j], {"dp": s})

    shard = width // 4
    landed(zslots, zland, 0, 0, state)
    start_rows(0, 0)
    loads[0].wait()
    loads[1].wait()
    copy_of(0, 0, 0).wait_recv()
    compute(0, 0, 0)
    landed(zslots, zland, 0, 1, state)
    start_rows(0, 1)
    for p in range(4):
        relay(p, 0)
        copy_of(2, p, 0).wait_recv()
        compute(p, 0, 1)
        send_sum(p, 0)
        if p == 0:
            olows.start()
        relay(p, 1)
        copy_of(0, p, 1).wait_recv()
        compute(p, 1, 0)
        copy_of(2, p, 1).wait_recv()
        compute(p, 1, 1)
        if p == 1:
            landed(dslots, dland, 1, 0, grad_in)
            landed(dslots, dland, 1, 1, grad_in)
        finish(p, 0)
        if p < 3:
            start_rows(p + 1, 0)
        send_sum(p, 1)
        if p < 3:
            olows.step(p + 1)
        if p == 0:
            loads[2].wait()
            loads[3].wait()
        if p < 3:
            copy_of(0, p + 1, 0).wait_recv()
            compute(p + 1, 0, 0)
        finish(p, 1)
        if p < 3:
            start_rows(p + 1, 1)
        k = layer_of[p]
        if p < 2:
            store(p * 2, x.at[p], n_out.at[k])
            store(p * 2 + 1, hid.at[k], h_out.at[k])
        else:
            store(p * 2, x.at[p], df_out.at[k])
            store(p * 2 + 1, hid.at[2 + k], du_out.at[k])
    for i in range(3):
        gain_copy(i).start()
    gland[j] = ggain[:, pl.ds(pl.multiple_of(j * shard, shard), shard)]
    own_o.wait()
    for zz in range(4):
        olows.wait_beside(zz)
    olows.drain()
    for p in range(4):
        for h in range(2):
            for kind in range(6):
                copy_of(kind, p, h).wait_send()
    for cp in stores:
        cp.wait()
    for i in range(3):
        push(ggain.at[:, pl.ds(0, shard)], gland.at[(sibling, across, diagonal)[i]], e_send.at[0], e_recv.at[(sibling, across, diagonal)[i]], {"dp": sibling}).wait_recv()
        gain_copy(i).wait_send()
    ggain_ref[...] = jnp.sum(gland[...], axis=0)
    for h in range(2):
        for which, (src, dst) in enumerate([(zslots, zland), (dslots, dland), (bsend, returned), (gsend, came_back)]):
            for_places(h, lambda q: swap(src, dst, which, q).wait_send(), lambda: None)
            if which >= 2:
                for_places(h, lambda q: swap_arrival(src, dst, which, q).wait_recv(), lambda: swap_own(src, dst, which).wait())


def expert_block(zslots, dslots, olow, gains, expert_in, expert_out):
    sources, cap, width = zslots.shape
    rows = sources * cap
    half = rows // 2
    hidden = expert_in.shape[2]
    everything = 4 * rows
    any_spec = pl.BlockSpec(memory_space=pl.ANY)
    vmem_spec = pl.BlockSpec(memory_space=pltpu.VMEM)
    S = jax.ShapeDtypeStruct
    big = S((2, everything, width), BF)
    V = pltpu.VMEM
    D = pltpu.SemaphoreType.DMA
    return pl.pallas_call(
        expert_kernel,
        out_shape=(
            S(zslots.shape, BF), S(zslots.shape, BF), S((8,) + olow.shape, BF), S((2, width // 4), F32),
            big, big, big, big,
        ),
        in_specs=[any_spec] * 3 + [vmem_spec] + [any_spec] * 2,
        out_specs=(any_spec, any_spec, any_spec, vmem_spec, any_spec, any_spec, any_spec, any_spec),
        scratch_shapes=[
            V((2, hidden, width), BF), V((2, hidden, width), BF),
            V((4, everything, width), BF), V((4, everything, hidden), BF), V((2, everything, hidden), F32),
            V((2, rows, width), F32), V((2, rows, 128), F32), V((rows, width), F32), V((rows, width), F32),
            V((rows, width), F32), V((2, half, width), F32), V((2, half, width), F32),
        ]
        + [V((8, half, width), BF)] * 6
        + [V(zslots.shape, BF)] * 4
        + [V((2, width), F32), V((4, 2, width // 4), F32)]
        + [D((48,)), D((48,)), D((32,)), D((32,)), D((11,)), D((8,)), D((13,)), D((4,)), D((3,)), D((4,))],
        compiler_params=pltpu.CompilerParams(
            collective_id=1, has_side_effects=True, vmem_limit_bytes=60 * 1024 * 1024
        ),
        name="expert_block",
    )(zslots, dslots, olow, gains, expert_in, expert_out)


def back_kernel(
    gmix, gatt, qkv_hbm, mixed_hbm, lse_rows, normed_hbm, olow_hbm, cent, wqkv,
    dq_land, gq_land, go_land, gc_land, wsecond,
    dom, dam, qkv, mixed, normed, olow, delta, dq_acc, dqkv,
    part, f1, f3, ssum, rf1, rf3, rss, gq_own, go_own, cland, csum, cdp,
    h_send, h_recv, d_send, d_recv, p_send, p_recv, gq_send, gq_recv, go_send, go_recv, c_send, c_recv, copy_sem, q_send, q_recv,
):
    j, sibling, across, diagonal = dp_peers()
    e, zpos, xpos, beside, zs = expert_peers()
    rows, width = gmix.shape
    blk = 2 * rows
    lanes = 128
    shard = width // 4
    loads = [
        pltpu.make_async_copy(src, dst, copy_sem.at[i])
        for i, (src, dst) in enumerate([(qkv_hbm, qkv), (mixed_hbm, mixed), (olow_hbm, olow), (normed_hbm, normed)])
    ]
    for cp in loads:
        cp.start()
    peers = others(8, e)
    greet([{"expert": p} for p in peers] + [{"dp": p} for p in (sibling, across, diagonal)])

    def cols_of(s):
        return pl.ds(pl.multiple_of(s * lanes, lanes), lanes)

    def rows_of(s):
        return pl.ds(pl.multiple_of(s * rows, rows), rows)

    def head_copy(src, dst, which, dest):
        return push(src.at[:, cols_of(dest)], dst.at[rows_of(e)], h_send.at[which * 8 + dest], h_recv.at[which * 8 + e], {"expert": dest})

    def head_arrival(src, dst, which, source):
        return push(src.at[:, cols_of(source)], dst.at[rows_of(source)], h_send.at[which * 8 + source], h_recv.at[which * 8 + source], {"expert": source})

    for dest in peers:
        head_copy(gmix, dom, 0, dest).start()
    for dest in peers:
        head_copy(gatt, dam, 1, dest).start()
    for dest in peers:
        push(cent.at[dest], cland.at[e], c_send.at[dest], c_recv.at[e], {"expert": dest}).start()
    later = Weights(wqkv, shard // 2, shard // 2, wsecond, q_send, q_recv, copy_sem.at[8])
    later.start()
    dom[rows_of(e), :] = gmix[:, cols_of(e)]
    dam[rows_of(e), :] = gatt[:, cols_of(e)]
    cland[e] = cent[e]

    def dp_sum_start(buf, n, t):
        def block(s):
            return buf[0:n, pl.ds(pl.multiple_of(s * shard, shard), shard)]
        f3[t, 0:n, :] = block(diagonal).astype(BF)
        f1[t, 0:n, :] = block(sibling).astype(BF)
        dp_copy(1, n, t).start()
        dp_copy(0, n, t).start()
        dp_copy(1, n, t).wait_recv()
        ssum[t, 0:n, :] = (block(across) + rf3[t, 0:n, :].astype(F32)).astype(BF)
        dp_copy(2, n, t).start()

    def dp_copy(kind, n, t):
        at = pl.ds(0, n)
        if kind == 0:
            return push(f1.at[t, at], rf1.at[t, at], p_send.at[t * 3], p_recv.at[t * 3], {"dp": sibling})
        if kind == 1:
            return push(f3.at[t, at], rf3.at[t, at], p_send.at[t * 3 + 1], p_recv.at[t * 3 + 1], {"dp": sibling})
        return push(ssum.at[t, at], rss.at[t, at], p_send.at[t * 3 + 2], p_recv.at[t * 3 + 2], {"dp": across})

    def dp_sum_end(buf, n, t):
        dp_copy(0, n, t).wait_recv()
        dp_copy(2, n, t).wait_recv()
        return buf[0:n, pl.ds(pl.multiple_of(j * shard, shard), shard)] + rf1[t, 0:n, :].astype(F32) + rss[t, 0:n, :].astype(F32)

    for cp in loads[:2]:
        cp.wait()
    for source in peers:
        head_arrival(gmix, dom, 0, source).wait_recv()
    left_row = lax.broadcasted_iota(jnp.int32, (8, 128), 1) < HEAD
    row_id = lax.broadcasted_iota(jnp.int32, (8, 128), 0)
    pick = jnp.where((row_id == 0) == left_row, 1.0, 0.0).astype(F32)
    delta[...] = lax.dot_general(pick, dom[...].astype(F32) * mixed[...], NT, precision=HIGH, preferred_element_type=F32)

    for source in peers:
        push(cent.at[source], cland.at[source], c_send.at[source], c_recv.at[source], {"expert": source}).wait_recv()
    csum[0] = jnp.sum(cland[...], axis=0)

    def c_copy(i):
        s = (sibling, across, diagonal)[i]
        return push(csum.at[0, :, pl.ds(pl.multiple_of(s * shard, shard), shard)], cdp.at[j], c_send.at[8 + i], c_recv.at[8 + j], {"dp": s})

    def c_arrival(s):
        return push(csum.at[0, :, pl.ds(0, shard)], cdp.at[s], c_send.at[8], c_recv.at[8 + s], {"dp": sibling})

    for i in range(3):
        c_copy(i).start()
    cdp[j] = csum[0, :, pl.ds(pl.multiple_of(j * shard, shard), shard)]

    left = lane_masks(blk)
    dq_acc[...] = jnp.zeros_like(dq_acc)

    def d_copy(dest):
        return push(dqkv.at[pl.ds(dest * rows, rows)], dq_land.at[e], d_send.at[dest], d_recv.at[e], {"expert": dest})

    for b in range(4):
        at = pl.ds(b * blk, blk)
        tail = pl.ds(b * blk, 8 * rows - b * blk)
        qs = qkv[tail, 0:lanes]
        dos = dom[tail, :]
        keys = qkv[at, lanes : 2 * lanes].astype(F32) * (HEAD ** -0.5)
        vals = qkv[at, 2 * lanes : 3 * lanes]
        dks, dvs = [], []
        for h in range(2):
            mask = left if h == 0 else jnp.logical_not(left)
            k_h = jnp.where(mask, keys, 0.0).astype(BF)
            v_h = jnp.where(mask, vals.astype(F32), 0.0).astype(BF)
            sc = lax.dot_general(k_h, qs, NT, preferred_element_type=F32)
            pr = jnp.exp(sc - lse_rows[h : h + 1, tail])
            dp = lax.dot_general(v_h, dos, NT, preferred_element_type=F32)
            ds = (pr * (dp - delta[h : h + 1, tail])).astype(BF)
            dvs.append(jnp.dot(pr.astype(BF), dos, preferred_element_type=F32))
            dks.append(jnp.dot(ds, qs, preferred_element_type=F32))
            dq_acc[tail, :] += lax.dot_general(ds, k_h, TN, preferred_element_type=F32)
        dqkv[at, 0:lanes] = dq_acc[at, :].astype(BF)
        dqkv[at, lanes : 2 * lanes] = (jnp.where(left, dks[0], dks[1]) * (HEAD ** -0.5)).astype(BF)
        dqkv[at, 2 * lanes : 3 * lanes] = jnp.where(left, dvs[0], dvs[1]).astype(BF)
        for dest in (2 * b, 2 * b + 1):
            @pl.when(dest != e)
            def _():
                d_copy(dest).start()

            @pl.when(dest == e)
            def _():
                pltpu.make_async_copy(dqkv.at[pl.ds(dest * rows, rows)], dq_land.at[dest], copy_sem.at[4]).start()
        if b == 0:
            loads[2].wait()
            for source in peers:
                head_arrival(gatt, dam, 1, source).wait_recv()
            part[0:lanes, :] = lax.dot_general(dam[...], olow[...], TN, preferred_element_type=F32)
            dp_sum_start(part, lanes, 0)
        if b == 1:
            go_own[...] = dp_sum_end(part, lanes, 0).T.astype(BF)
            gos = Spread(go_own, go_land, go_send, go_recv, 1)
            gos.start()
            own_go = pltpu.make_async_copy(go_own, go_land.at[e], copy_sem.at[5])
            own_go.start()
            for s in (sibling, across, diagonal):
                c_arrival(s).wait_recv()
            csum[1, :, 0:shard] = jnp.sum(cdp[...], axis=0)
            for dest in peers:
                push(csum.at[1, :, pl.ds(0, shard)], gc_land.at[e], c_send.at[12 + dest], c_recv.at[12 + e], {"expert": dest}).start()
            own_gc = pltpu.make_async_copy(csum.at[1, :, pl.ds(0, shard)], gc_land.at[e], copy_sem.at[6])
            own_gc.start()
    loads[3].wait()
    part[...] = lax.dot_general(dqkv[...], normed[...], TN, preferred_element_type=F32)
    dp_sum_start(part, 3 * lanes, 1)
    gos.step(1)
    gq_own[...] = dp_sum_end(part, 3 * lanes, 1).T.astype(BF)
    gqs = Spread(gq_own, gq_land, gq_send, gq_recv, 2)
    gqs.start()
    own_gq = pltpu.make_async_copy(gq_own, gq_land.at[e], copy_sem.at[7])
    own_gq.start()
    gos.step(2)
    later.relay()
    gqs.step(1)
    gos.step(3)
    gqs.step(2)
    gqs.step(3)
    for zz in range(4):
        gos.wait_beside(zz)
        gqs.wait_beside(zz)
    gos.drain()
    gqs.drain()
    later.drain()
    for source in range(8):
        @pl.when(source != e)
        def _():
            push(dqkv.at[pl.ds(0, rows)], dq_land.at[source], d_send.at[source], d_recv.at[source], {"expert": source}).wait_recv()
            d_copy(source).wait_send()
            push(csum.at[1, :, pl.ds(0, shard)], gc_land.at[source], c_send.at[12 + source], c_recv.at[12 + source], {"expert": source}).wait()

        @pl.when(source == e)
        def _():
            pltpu.make_async_copy(dqkv.at[pl.ds(0, rows)], dq_land.at[source], copy_sem.at[4]).wait()
    for dest in peers:
        head_copy(gmix, dom, 0, dest).wait_send()
        head_copy(gatt, dam, 1, dest).wait_send()
        push(cent.at[dest], cland.at[e], c_send.at[dest], c_recv.at[e], {"expert": dest}).wait_send()
    for i in range(3):
        c_copy(i).wait_send()
        dp_copy(i, lanes, 0).wait_send()
        dp_copy(i, 3 * lanes, 1).wait_send()
    for cp in (own_go, own_gc, own_gq):
        cp.wait()


def back_block(gmix, gatt, qkv, mixed, lse_rows, normed, olow_full, cent, qkv_weight):
    rows, width = gmix.shape
    seq = 8 * rows
    shard = width // 4
    any_spec = pl.BlockSpec(memory_space=pl.ANY)
    vmem_spec = pl.BlockSpec(memory_space=pltpu.VMEM)
    S = jax.ShapeDtypeStruct
    V = pltpu.VMEM
    D = pltpu.SemaphoreType.DMA
    return pl.pallas_call(
        back_kernel,
        out_shape=(
            S((8, rows, 384), BF), S((8, shard, 384), BF), S((8, shard, 128), BF), S((8, 1, shard), F32),
            S((4, shard // 2, 3 * width), BF),
        ),
        in_specs=[vmem_spec, vmem_spec, any_spec, any_spec, vmem_spec, any_spec, any_spec, vmem_spec, any_spec],
        out_specs=(any_spec,) * 5,
        scratch_shapes=[
            V((seq, 128), BF), V((seq, 128), BF), V((seq, 384), BF), V((seq, 128), F32), V((seq, width), BF), V((seq, width), BF),
            V((8, seq), F32), V((seq, 128), F32), V((seq, 384), BF),
            V((384, width), F32),
        ]
        + [V((2, 384, shard), BF)] * 6
        + [
            V((shard, 384), BF), V((shard, 128), BF), V((8, 1, width), F32), V((2, 1, width), F32), V((4, 1, shard), F32),
            D((16,)), D((16,)), D((8,)), D((8,)), D((6,)), D((6,)), D((22,)), D((16,)), D((11,)), D((8,)), D((20,)), D((20,)), D((9,)), D((3,)), D((4,)),
        ],
        compiler_params=pltpu.CompilerParams(collective_id=3, has_side_effects=True, vmem_limit_bytes=56 * 1024 * 1024),
        name="back_block",
    )(gmix, gatt, qkv, mixed, lse_rows, normed, olow_full, cent, qkv_weight)


def final_kernel(
    dq_land, wfirst, wsecond, tok, gain_col, gres, gq_land, go_land, wqkv,
    gtok, gqkv, gout, ggain,
    dqkv, dnorm, small_sum,
):
    rows, width = tok.shape
    shard = wqkv.shape[0]
    half = shard // 2
    for s in range(8):
        for i in range(3):
            at = pl.ds(i * width + s * 128, 128)
            dqkv[:, at] = dq_land[s, :, pl.ds(i * 128, 128)]
            gqkv[:, at] = gq_land[s, :, pl.ds(i * 128, 128)].astype(F32)
        gout[:, pl.ds(s * 128, 128)] = go_land[s].astype(F32)
    for s in range(4):
        for side, w in enumerate((wfirst, wsecond)):
            dnorm[:, pl.ds(s * shard + side * half, half)] = lax.dot_general(dqkv[...], w[s], NT, preferred_element_type=F32)
    gain = jnp.concatenate([gain_col[s : s + 1, :] for s in range(4)], axis=1)

    def norm_rows(t, c):
        at = pl.ds(pl.multiple_of(t * 32, 32), 32)
        v = tok[at, :].astype(F32)
        center = v - mean_last(v)
        inverse = lax.rsqrt(mean_last(center * center) + EPS)
        unit = center * inverse
        a = dnorm[at, :] * gain
        gtok[at, :] = gres[at, :] + inverse * (a - mean_last(a) - unit * mean_last(a * unit))
        return c

    lax.fori_loop(0, rows // 32, norm_rows, 0)
    small_sum[...] = jnp.zeros_like(small_sum)

    def add(t, c):
        at = pl.ds(pl.multiple_of(t * 256, 256), 256)
        prod = gqkv[:, at] * wqkv[:, at].astype(F32)
        small_sum[...] += prod[:, :128] + prod[:, 128:]
        return c

    lax.fori_loop(0, 3 * width // 256, add, 0)
    ggain[...] = lax.dot_general(jnp.ones((8, 128), F32), small_sum[...], NT, precision=HIGH, preferred_element_type=F32)


def final_block(dq_land, wfirst, wsecond, tokens, gain_col, grad_resid, gq_land, go_land, qkv_weight):
    rows, width = tokens.shape
    shard = width // 4
    vmem_spec = pl.BlockSpec(memory_space=pltpu.VMEM)
    S = jax.ShapeDtypeStruct
    V = pltpu.VMEM
    return pl.pallas_call(
        final_kernel,
        out_shape=(S((rows, width), F32), S((shard, 3 * width), F32), S((shard, width), F32), S((8, shard), F32)),
        in_specs=[vmem_spec] * 9,
        out_specs=(vmem_spec,) * 4,
        scratch_shapes=[V((rows, 3 * width), BF), V((rows, width), F32), V((shard, 128), F32)],
        compiler_params=pltpu.CompilerParams(vmem_limit_bytes=48 * 1024 * 1024),
        name="final_block",
    )(dq_land, wfirst, wsecond, tokens, gain_col, grad_resid, gq_land, go_land, qkv_weight)


def on_device_split(
    tokens,
    norm_gain,
    qkv_weight,
    out_weight,
    centroids,
    expert_gain,
    expert_in,
    expert_out,
    routes,
    cotangent,
):
    rows, width = tokens.shape
    experts = lax.axis_size("expert")
    capacity = max(2, 3 * rows // (2 * experts))
    slots = experts * capacity
    shard = width // 4
    small = jnp.concatenate(
        [norm_gain[None], expert_gain[0], jnp.zeros((5, shard), BF), centroids], axis=0
    )
    olow, normed_all, qkv, mixed, lse, wout_full, small_full, wfirst = front_block(tokens, small, qkv_weight, out_weight)
    gains = small_full[:, 1:3].transpose(1, 0, 2).reshape(2, width).astype(F32)
    centroid_full = small_full[:, 8:16].transpose(1, 0, 2).reshape(8, width)
    inputs = tokens.astype(F32)
    residual = inputs + jnp.dot(olow, wout_full, preferred_element_type=F32)
    route_ids = routes[:, 0]
    chosen = (route_ids[:, None] == jnp.arange(experts, dtype=jnp.int32)[None, :]).astype(BF)
    centroid_rows = jnp.dot(chosen, centroid_full, preferred_element_type=F32)
    gate = jax.nn.sigmoid(jnp.sum(residual * centroid_rows, axis=-1))
    before = jnp.tril(jnp.ones((rows, rows), BF), -1)
    rank = jnp.sum(jnp.dot(before, chosen, preferred_element_type=F32) * chosen.astype(F32), axis=-1)
    target = route_ids * capacity + rank.astype(jnp.int32)
    place = (jnp.arange(slots, dtype=jnp.int32)[:, None] == target[None, :]).astype(BF)
    grad_out = cotangent.astype(F32)
    sent = jnp.concatenate([residual.astype(BF), (gate[:, None] * grad_out).astype(BF)], axis=1)
    spread = jnp.dot(place, sent, preferred_element_type=F32).astype(BF)
    returned, came_back, olow_full, gain_part, n_rows, h_rows, df_rows, du_rows = expert_block(
        spread[:, :width].reshape(experts, capacity, width),
        spread[:, width:].reshape(experts, capacity, width),
        olow,
        gains,
        expert_in,
        expert_out,
    )
    grad_expert_out = jnp.einsum("krf,krd->kfd", h_rows, df_rows, preferred_element_type=F32)[None]
    grad_expert_in = jnp.einsum("krf,krd->kfd", du_rows, n_rows, preferred_element_type=F32)[None]
    branch_tok = lax.dot_general(place, returned.reshape(slots, width), TN, preferred_element_type=F32)
    block_out = (residual + gate[:, None] * branch_tok).astype(BF)
    grad_logit = jnp.sum(grad_out * branch_tok, axis=-1) * gate * (1.0 - gate)
    grad_centroid = jnp.dot(chosen.astype(F32).T, grad_logit[:, None] * residual, precision=HIGH)
    back_rows = lax.dot_general(place, came_back.reshape(slots, width), TN, preferred_element_type=F32)
    grad_resid = grad_out + grad_logit[:, None] * centroid_rows + back_rows
    grad_attended = grad_resid.astype(BF)
    grad_mixed = lax.dot_general(grad_attended, wout_full, NT, preferred_element_type=F32).astype(BF)
    lse_rows = jnp.pad(lse[:, ::HEAD].T, ((0, 6), (0, 0)))
    dq_land, gq_land, go_land, gc_land, wsecond = back_block(
        grad_mixed, grad_attended, qkv, mixed, lse_rows, normed_all,
        olow_full.reshape(experts * rows, width), grad_centroid[:, None, :], qkv_weight,
    )
    gain_col = small_full[:, 0].astype(F32)
    grad_tokens, grad_qkv, grad_out_weight, gain_sums = final_block(
        dq_land, wfirst, wsecond, tokens, gain_col, grad_resid, gq_land, go_land, qkv_weight
    )
    grad_norm_gain = gain_sums[0] / norm_gain.astype(F32)
    return (
        block_out,
        grad_tokens,
        grad_norm_gain,
        grad_qkv,
        grad_out_weight,
        gc_land[:, 0],
        gain_part[None],
        grad_expert_in,
        grad_expert_out,
    )


def on_device(
    tokens,
    norm_gain,
    qkv_weight,
    out_weight,
    centroids,
    expert_gain,
    expert_in,
    expert_out,
    routes,
    cotangent,
):
    model_width = tokens.shape[1]
    local_rows = tokens.shape[0]
    experts = lax.axis_size("expert")
    capacity = max(2, 3 * local_rows // (2 * experts))
    slot_total = experts * capacity
    first_pos = lax.axis_index("expert") * local_rows
    scale = HEAD ** (-0.5)
    gain_full, qkv_full, out_full, centroid_full, expert_gain_full = fetch_dense(
        norm_gain, qkv_weight, out_weight, centroids, expert_gain
    )
    inputs = tokens.astype(jnp.float32)
    unit_attn, inverse_attn, normed_attn = normalize(inputs, gain_full.astype(jnp.float32))
    normed_low = normed_attn.astype(jnp.bfloat16)
    projected = jnp.dot(normed_low, qkv_full, preferred_element_type=jnp.float32).astype(
        jnp.bfloat16
    )
    queries = projected[:, :model_width]
    keyset = projected[:, model_width : 2 * model_width]
    values = projected[:, 2 * model_width :]
    query_heads = split_heads(queries)
    key_heads = split_heads(keyset)
    value_heads = split_heads(values)
    query_block = (first_pos + jnp.arange(local_rows, dtype=jnp.int32)) // BLOCK
    last_block = (first_pos + local_rows - 1) // BLOCK
    start_state = (
        jnp.zeros((local_rows, HEADS, HEAD), jnp.float32),
        jnp.full((HEADS, local_rows), NEGATIVE, jnp.float32),
        jnp.zeros((HEADS, local_rows), jnp.float32),
    )
    key_piece = lax.all_gather(keyset, "expert", axis=0, tiled=True)
    value_piece = lax.all_gather(values, "expert", axis=0, tiled=True)
    amount = key_piece.shape[0]

    def update(current):
        accumulated, highest, totals = current
        scores = (
            jnp.einsum(
                "qhd,khd->hqk",
                query_heads,
                split_heads(key_piece),
                preferred_element_type=jnp.float32,
            )
            * scale
        )
        piece_block = jnp.arange(amount, dtype=jnp.int32) // BLOCK
        visible = (piece_block[None, :] <= query_block[:, None])[None]
        scores = jnp.where(visible, scores, NEGATIVE)
        new_high = jnp.maximum(highest, jnp.max(scores, axis=-1))
        factor = jnp.exp(highest - new_high)
        weights = jnp.where(visible, jnp.exp(scores - new_high[:, :, None]), 0.0)
        totals = jnp.sum(weights, axis=-1)
        accumulated = accumulated * factor.T[:, :, None] + jnp.einsum(
            "hqk,khd->qhd",
            weights.astype(jnp.bfloat16),
            split_heads(value_piece),
            preferred_element_type=jnp.float32,
        )
        return (accumulated, new_high, totals)

    accumulated, highest, totals = lax.cond(
        jnp.int32(0) // BLOCK <= last_block, update, keep_state, start_state
    )
    mixed_heads = accumulated / totals.T[:, :, None]
    log_total = (highest + jnp.log(totals)).T
    mixed_low = mixed_heads.reshape(local_rows, model_width).astype(jnp.bfloat16)
    residual = inputs + jnp.dot(mixed_low, out_full, preferred_element_type=jnp.float32)
    route_ids = routes[:, 0]
    chosen = route_ids[:, None] == jnp.arange(experts, dtype=jnp.int32)[None, :]
    centroid_rows = jnp.dot(
        chosen.astype(jnp.bfloat16), centroid_full, preferred_element_type=jnp.float32
    )
    gate_value = jax.nn.sigmoid(jnp.sum(residual * centroid_rows, axis=-1))
    chosen_int = chosen.astype(jnp.int32)
    slot_index = jnp.sum((jnp.cumsum(chosen_int, axis=0) - 1) * chosen_int, axis=-1)
    target = route_ids * capacity + slot_index
    arrived = lax.all_to_all(
        send_slots(residual.astype(jnp.bfloat16), target, experts, capacity),
        "expert",
        split_axis=0,
        concat_axis=0,
        tiled=True,
    )
    expert_state = arrived.reshape(slot_total, model_width).astype(jnp.float32)
    gains_here = expert_gain_full[0].astype(jnp.float32)
    total_change = jnp.zeros_like(expert_state)
    stored = []
    for sublayer in range(2):
        unit_rows, inverse, normed = normalize(expert_state, gains_here[sublayer])
        normed_rows = normed.astype(jnp.bfloat16)
        first_full, second_full = (expert_in[0, sublayer], expert_out[0, sublayer])
        left_rows = spread_rows(normed_rows)
        hidden_pre = jnp.einsum(
            "rd,fd->rf", left_rows, first_full, preferred_element_type=jnp.float32
        )
        hidden_act, slope_pull = jax.vjp(exact_gelu, hidden_pre)
        hidden_low = hidden_act.astype(jnp.bfloat16)
        change = sum_rows(partial(row_product, hidden_low, second_full), slot_total)
        expert_state = expert_state + change
        total_change = total_change + change
        stored.append((unit_rows, inverse, left_rows, hidden_low, slope_pull))
    branch_low = total_change.astype(jnp.bfloat16)
    returned = lax.all_to_all(
        branch_low.reshape(experts, capacity, model_width),
        "expert",
        split_axis=0,
        concat_axis=0,
        tiled=True,
    )
    branch_tok = returned.reshape(slot_total, model_width)[target].astype(jnp.float32)
    block_out = (residual + gate_value[:, None] * branch_tok).astype(jnp.bfloat16)
    gain_full, qkv_full, out_full, centroid_full, expert_gain_full = fetch_dense(
        norm_gain, qkv_weight, out_weight, centroids, expert_gain
    )
    gains_here = expert_gain_full[0].astype(jnp.float32)
    grad_out = cotangent.astype(jnp.float32)
    grad_logit = jnp.sum(grad_out * branch_tok, axis=-1) * gate_value * (1.0 - gate_value)
    grad_centroid = jnp.dot(
        chosen.astype(jnp.float32).T, grad_logit[:, None] * residual, precision=HIGH
    )
    grad_resid = grad_out + grad_logit[:, None] * centroid_rows
    grad_branch = (gate_value[:, None] * grad_out).astype(jnp.bfloat16)
    branch_grads = lax.all_to_all(
        send_slots(grad_branch, target, experts, capacity),
        "expert",
        split_axis=0,
        concat_axis=0,
        tiled=True,
    )
    grad_change = branch_grads.reshape(slot_total, model_width).astype(jnp.float32)
    grad_state = jnp.zeros_like(grad_change)
    gain_grads = [None, None]
    first_grads = [None, None]
    second_grads = [None, None]
    for sublayer in (1, 0):
        unit_rows, inverse, left_rows, hidden_low, slope_pull = stored[sublayer]
        grad_rows_low = (grad_change + grad_state).astype(jnp.bfloat16)
        first_full, second_full = (expert_in[0, sublayer], expert_out[0, sublayer])
        grad_rows = spread_rows(grad_rows_low)
        grad_hidden = jnp.einsum(
            "rd,fd->rf", grad_rows, second_full, preferred_element_type=jnp.float32
        )
        grad_pre = slope_pull(grad_hidden)[0].astype(jnp.bfloat16)
        grad_first = jnp.einsum(
            "rf,rd->fd", grad_pre, left_rows, preferred_element_type=jnp.float32
        )
        grad_second = jnp.einsum(
            "rf,rd->fd", hidden_low, grad_rows, preferred_element_type=jnp.float32
        )
        grad_normed = sum_rows(partial(row_product, grad_pre, first_full), slot_total)
        grad_input, gain_grad = norm_backward(grad_normed, unit_rows, inverse, gains_here[sublayer])
        grad_state = grad_state + grad_input
        gain_grads[sublayer] = gain_grad
        first_grads[sublayer] = grad_first
        second_grads[sublayer] = grad_second
    came_back = lax.all_to_all(
        grad_state.astype(jnp.bfloat16).reshape(experts, capacity, model_width),
        "expert",
        split_axis=0,
        concat_axis=0,
        tiled=True,
    )
    grad_resid = grad_resid + came_back.reshape(slot_total, model_width)[target].astype(jnp.float32)
    grad_attended = grad_resid.astype(jnp.bfloat16)
    grad_out_weight = jnp.einsum(
        "rd,re->de", mixed_low, grad_attended, preferred_element_type=jnp.float32
    )
    grad_mixed = jnp.einsum(
        "re,de->rd", grad_attended, out_full, preferred_element_type=jnp.float32
    ).astype(jnp.bfloat16)
    grad_heads = split_heads(grad_mixed)
    delta_rows = jnp.sum(grad_heads.astype(jnp.float32) * mixed_heads, axis=-1)
    zero_heads = jnp.zeros((local_rows, HEADS, HEAD), jnp.float32)
    running = (zero_heads, zero_heads, zero_heads)
    offset = jnp.int32(0)
    fold_key_piece = lax.all_gather(keyset, "expert", axis=0, tiled=True)
    fold_value_piece = lax.all_gather(values, "expert", axis=0, tiled=True)
    query_piece = lax.all_gather(queries, "expert", axis=0, tiled=True)
    grad_piece = lax.all_gather(grad_mixed, "expert", axis=0, tiled=True)
    log_piece = lax.all_gather(log_total.astype(jnp.bfloat16), "expert", axis=0, tiled=True).astype(
        jnp.float32
    )
    delta_piece = lax.all_gather(
        delta_rows.astype(jnp.bfloat16), "expert", axis=0, tiled=True
    ).astype(jnp.float32)
    fold_amount = fold_key_piece.shape[0]
    piece_block = jnp.arange(fold_amount, dtype=jnp.int32) // BLOCK

    def to_queries(current):
        grad_query, grad_key, grad_value = current
        piece_keys = split_heads(fold_key_piece)
        scores = (
            jnp.einsum("qhd,khd->hqk", query_heads, piece_keys, preferred_element_type=jnp.float32)
            * scale
        )
        visible = (piece_block[None, :] <= query_block[:, None])[None]
        weights = jnp.where(visible, jnp.exp(scores - log_total.T[:, :, None]), 0.0)
        grad_weights = jnp.einsum(
            "qhd,khd->hqk",
            grad_heads,
            split_heads(fold_value_piece),
            preferred_element_type=jnp.float32,
        )
        grad_scores = (weights * (grad_weights - delta_rows.T[:, :, None])).astype(jnp.bfloat16)
        grad_query = (
            jnp.einsum("hqk,khd->qhd", grad_scores, piece_keys, preferred_element_type=jnp.float32)
            * scale
        )
        return (grad_query, grad_key, grad_value)

    def to_keys(current):
        grad_query, grad_key, grad_value = current
        piece_queries = split_heads(query_piece)
        piece_grads = split_heads(grad_piece)
        scores = (
            jnp.einsum("qhd,khd->hqk", piece_queries, key_heads, preferred_element_type=jnp.float32)
            * scale
        )
        visible = (query_block[None, :] <= piece_block[:, None])[None]
        weights = jnp.where(visible, jnp.exp(scores - log_piece.T[:, :, None]), 0.0)
        grad_weights = jnp.einsum(
            "qhd,khd->hqk", piece_grads, value_heads, preferred_element_type=jnp.float32
        )
        grad_scores = (weights * (grad_weights - delta_piece.T[:, :, None])).astype(jnp.bfloat16)
        grad_key = (
            grad_key
            + jnp.einsum(
                "hqk,qhd->khd", grad_scores, piece_queries, preferred_element_type=jnp.float32
            )
            * scale
        )
        grad_value = grad_value + jnp.einsum(
            "hqk,qhd->khd",
            weights.astype(jnp.bfloat16),
            piece_grads,
            preferred_element_type=jnp.float32,
        )
        return (grad_query, grad_key, grad_value)

    running = lax.cond(offset // BLOCK <= last_block, to_queries, keep_state, running)
    grad_query, grad_key, grad_value = lax.cond(
        query_block[0] <= (offset + fold_amount - 1) // BLOCK, to_keys, keep_state, running
    )
    grad_qkv_rows = jnp.concatenate(
        [
            grad_query.reshape(local_rows, model_width),
            grad_key.reshape(local_rows, model_width),
            grad_value.reshape(local_rows, model_width),
        ],
        axis=1,
    ).astype(jnp.bfloat16)
    grad_qkv = jnp.einsum(
        "rd,re->de", normed_low, grad_qkv_rows, preferred_element_type=jnp.float32
    )
    grad_normed_attn = jnp.einsum(
        "re,de->rd", grad_qkv_rows, qkv_full, preferred_element_type=jnp.float32
    )
    grad_input_attn, attn_gain_grad = norm_backward(
        grad_normed_attn, unit_attn, inverse_attn, gain_full.astype(jnp.float32)
    )
    grad_tokens = grad_resid + grad_input_attn
    expert_gain_grad = jnp.stack(gain_grads)[None]
    gain_share, qkv_share, out_share, centroid_share, expert_gain_share = (
        lax.psum_scatter(
            attn_gain_grad.astype(jnp.bfloat16), "dp", scatter_dimension=0, tiled=True
        ).astype(jnp.float32),
        lax.psum_scatter(
            grad_qkv.astype(jnp.bfloat16), "dp", scatter_dimension=0, tiled=True
        ).astype(jnp.float32),
        lax.psum_scatter(
            grad_out_weight.astype(jnp.bfloat16), "dp", scatter_dimension=0, tiled=True
        ).astype(jnp.float32),
        lax.psum_scatter(
            grad_centroid.astype(jnp.bfloat16), "dp", scatter_dimension=1, tiled=True
        ).astype(jnp.float32),
        lax.psum_scatter(
            expert_gain_grad.astype(jnp.bfloat16), "dp", scatter_dimension=2, tiled=True
        ).astype(jnp.float32),
    )
    gain_total, qkv_total, out_total, centroid_total = (
        lax.psum(gain_share.astype(jnp.bfloat16), "expert").astype(jnp.float32),
        lax.psum(qkv_share.astype(jnp.bfloat16), "expert").astype(jnp.float32),
        lax.psum(out_share.astype(jnp.bfloat16), "expert").astype(jnp.float32),
        lax.psum(centroid_share.astype(jnp.bfloat16), "expert").astype(jnp.float32),
    )
    grad_expert_in = jnp.stack(first_grads)[None]
    grad_expert_out = jnp.stack(second_grads)[None]
    return (
        block_out,
        grad_tokens,
        gain_total,
        qkv_total,
        out_total,
        centroid_total,
        expert_gain_share,
        grad_expert_in,
        grad_expert_out,
    )


def solution(mesh):
    in_specs = (
        P(("dp", "expert"), None),
        P("dp"),
        P("dp", None),
        P("dp", None),
        P(None, "dp"),
        P("expert", None, "dp"),
        P("expert", None, "dp", None),
        P("expert", None, "dp", None),
        P(("dp", "expert"), None),
        P(("dp", "expert"), None),
    )
    out_specs = (
        P(("dp", "expert"), None),
        P(("dp", "expert"), None),
        P("dp"),
        P("dp", None),
        P("dp", None),
        P(None, "dp"),
        P("expert", None, "dp"),
        P("expert", None, "dp", None),
        P("expert", None, "dp", None),
    )
    split = mesh.shape["dp"] == 4 and mesh.shape["expert"] == 8
    return jax.shard_map(
        on_device_split if split else on_device, mesh=mesh, in_specs=in_specs, out_specs=out_specs, check_vma=False
    )
```

```python
from functools import partial

import jax
import jax.numpy as jnp
from jax import lax
from jax.experimental import pallas as pl
from jax.experimental.pallas import tpu as pltpu
from jax.sharding import PartitionSpec as P

HEADS = 16
HEAD = 64
BLOCK = 256


EPS = 1e-05
NEGATIVE = -1e30
HIGH = lax.Precision.HIGHEST


def normalize(inputs, gain_row):
    centered = inputs - jnp.mean(inputs, axis=-1, keepdims=True)
    inverse = lax.rsqrt(jnp.mean(centered * centered, axis=-1, keepdims=True) + EPS)
    unit_rows = centered * inverse
    return (unit_rows, inverse, unit_rows * gain_row)


def norm_backward(grad_normed, unit_rows, inverse, gain_row):
    grad_unit = grad_normed * gain_row
    first_mean = jnp.mean(grad_unit, axis=-1, keepdims=True)
    second_mean = jnp.mean(grad_unit * unit_rows, axis=-1, keepdims=True)
    grad_input = inverse * (grad_unit - first_mean - unit_rows * second_mean)
    return (grad_input, jnp.sum(grad_normed * unit_rows, axis=0))


def split_heads(matrix):
    return matrix.reshape(matrix.shape[0], HEADS, HEAD)


def exact_gelu(inputs):
    return jax.nn.gelu(inputs, approximate=False)


def keep_state(current):
    return current


def row_product(left_rows, right_matrix, offset, amount):
    return jnp.dot(left_rows, right_matrix, preferred_element_type=jnp.float32)


def fetch_dense(norm_gain, qkv_weight, out_weight, centroids, expert_gain):
    return (
        lax.all_gather(norm_gain, "dp", axis=0, tiled=True),
        lax.all_gather(qkv_weight, "dp", axis=0, tiled=True),
        lax.all_gather(out_weight, "dp", axis=0, tiled=True),
        lax.all_gather(centroids, "dp", axis=1, tiled=True),
        lax.all_gather(expert_gain, "dp", axis=2, tiled=True),
    )


def spread_rows(rows_low):
    return lax.all_gather(rows_low, "dp", axis=0, tiled=True)


def sum_rows(term, amount):
    return lax.psum_scatter(
        term(jnp.int32(0), amount * lax.axis_size("dp")).astype(jnp.bfloat16),
        "dp",
        scatter_dimension=0,
        tiled=True,
    ).astype(jnp.float32)


def send_slots(rows_low, target, experts, capacity):
    buffer_rows = (
        jnp.zeros((experts * capacity, rows_low.shape[1]), rows_low.dtype).at[target].set(rows_low)
    )
    return buffer_rows.reshape(experts, capacity, rows_low.shape[1])


BF = jnp.bfloat16
F32 = jnp.float32
NT = (((1,), (1,)), ((), ()))
TN = (((0,), (0,)), ((), ()))
TILE = 256
MESH_ID = pl.DeviceIdType.MESH


def mean_last(v):
    return jnp.mean(v, axis=-1, keepdims=True)


def dp_peers():
    me = lax.axis_index("dp")
    sibling = me + 1 - 2 * lax.rem(me, 2)
    across = lax.rem(me + 2, 4)
    diagonal = lax.rem(sibling + 2, 4)
    return me, sibling, across, diagonal


def expert_peers():
    me = lax.axis_index("expert")
    z, x = me // 2, lax.rem(me, 2)
    beside = me + 1 - 2 * x
    near = z + 1 - 2 * lax.rem(z, 2)
    low, high = lax.rem(z, 2), z // 2
    inner = low + high - 2 * low * high
    flip, turn = 3 - z, lax.rem(z + 2, 4)
    second = inner * flip + (1 - inner) * turn
    third = inner * turn + (1 - inner) * flip
    return me, z, x, beside, (near, second, third)


def greet(targets):
    barrier = pltpu.get_barrier_semaphore()
    for target in targets:
        pl.semaphore_signal(barrier, inc=1, device_id=target, device_id_type=MESH_ID)
    pl.semaphore_wait(barrier, len(targets))


def others(n, me):
    return [lax.rem(me + d, n) for d in range(1, n)]


def push(src, dst, send, recv, target):
    return pltpu.make_async_remote_copy(
        src_ref=src, dst_ref=dst, send_sem=send, recv_sem=recv, device_id=target, device_id_type=MESH_ID
    )


class Spread:
    def __init__(self, own_src, slots, send, recv, chunks):
        self.me, self.z, self.x, self.beside, self.zs = expert_peers()
        self.own_src, self.slots, self.send, self.recv, self.chunks = own_src, slots, send, recv, chunks
        self.part = own_src.shape[0] // chunks

    def rows(self, c):
        return pl.ds(c * self.part, self.part)

    def own(self, way, c):
        peer = self.beside if way == 0 else 2 * (self.z + (1 if way == 1 else -1)) + self.x
        return push(
            self.own_src.at[self.rows(c)], self.slots.at[self.me, self.rows(c)],
            self.send.at[way * self.chunks + c], self.recv.at[self.me * self.chunks + c], {"expert": peer},
        )

    def slot(self, s, c, base, peer):
        block = self.slots.at[s, self.rows(c)]
        return push(block, block, self.send.at[base * self.chunks + c], self.recv.at[s * self.chunks + c], {"expert": peer})

    def own_all(self, act):
        for way in range(3):
            for c in range(self.chunks):
                if way == 0:
                    act(self.own(way, c))
                else:
                    @pl.when(self.z < 3 if way == 1 else self.z > 0)
                    def _():
                        act(self.own(way, c))

    def start(self):
        self.own_all(lambda cp: cp.start())

    def each(self, d, act):
        for sign in (-1, 1):
            zz = self.z + sign * d
            onward = self.z - sign

            @pl.when(jnp.logical_and(zz >= 0, zz <= 3))
            def _():
                s = 2 * zz + self.x
                for c in range(self.chunks):
                    act(s, zz, onward, c)

    def step(self, d):
        def act(s, zz, onward, c):
            self.slot(s, c, 0, self.beside).wait_recv()

            @pl.when(jnp.logical_and(onward >= 0, onward <= 3))
            def _():
                self.slot(s, c, 7 + zz, 2 * onward + self.x).start()

            self.slot(s, c, 3 + zz, self.beside).start()

        self.each(d, act)

    def wait_beside(self, zz):
        for c in range(self.chunks):
            self.slot(2 * zz + 1 - self.x, c, 0, self.beside).wait_recv()

    def drain(self):
        self.own_all(lambda cp: cp.wait_send())

        def act(s, zz, onward, c):
            @pl.when(jnp.logical_and(onward >= 0, onward <= 3))
            def _():
                self.slot(s, c, 7 + zz, 2 * onward + self.x).wait_send()

            self.slot(s, c, 3 + zz, self.beside).wait_send()

        for d in (1, 2, 3):
            self.each(d, act)


class Weights:
    def __init__(self, src, first, rows, full, send, recv, copy):
        self.j, self.sibling, self.across, self.diagonal = dp_peers()
        self.src, self.full, self.send, self.recv = src.at[pl.ds(first, rows)], full, send, recv
        self.keep = pltpu.make_async_copy(self.src, full.at[self.j], copy)

    def copy(self, kind):
        if kind == 2:
            block = self.full.at[self.across]
            return push(block, block, self.send.at[2], self.recv.at[self.across], {"dp": self.sibling})
        peer = self.sibling if kind == 0 else self.across
        return push(self.src, self.full.at[self.j], self.send.at[kind], self.recv.at[self.j], {"dp": peer})

    def start(self):
        self.copy(1).start()
        self.copy(0).start()
        self.keep.start()

    def arrival(self, s):
        return push(self.src, self.full.at[s], self.send.at[0], self.recv.at[s], {"dp": self.sibling})

    def relay(self):
        self.arrival(self.across).wait_recv()
        self.copy(2).start()

    def drain(self):
        self.arrival(self.sibling).wait_recv()
        self.arrival(self.diagonal).wait_recv()
        for kind in range(3):
            self.copy(kind).wait_send()
        self.keep.wait()


def lane_masks(rows):
    lane = lax.broadcasted_iota(jnp.int32, (rows, 128), 1)
    return lane < HEAD


def front_kernel(
    tok, norm_gain, expert_gain, centroids, wqkv, wout,
    olow, normed_out, qkv_out, mixed_out, wout_full, wfirst, lse_rows, gain_col, gains, cent_full,
    held, wblk, normed, qkv, mixed, mixed_low, gain, bounce, small, smalls,
    tok_send, tok_recv, w_send, w_recv, o_send, o_recv, copy_sem, q_send, q_recv,
):
    j, sibling, across, diagonal = dp_peers()
    e, z, x, beside, zs = expert_peers()
    rows, width = tok.shape
    shard = wqkv.shape[0]
    lanes = 128

    def mine(s):
        return pl.ds(pl.multiple_of(s * shard, shard), shard)

    mycols = pl.ds(pl.multiple_of(e * lanes, lanes), lanes)
    own_tok = pltpu.make_async_copy(tok, held.at[e], copy_sem.at[0])
    own_tok.start()
    own_w = [
        pltpu.make_async_copy(
            wqkv.at[:, pl.ds(pl.multiple_of(i * width + e * lanes, lanes), lanes)],
            wblk.at[mine(j), pl.ds(i * lanes, lanes)],
            copy_sem.at[1 + i],
        )
        for i in range(3)
    ]
    for cp in own_w:
        cp.start()
    own_out = pltpu.make_async_copy(wout, bounce, copy_sem.at[4])
    own_out.start()
    small[...] = jnp.concatenate(
        [norm_gain[...], expert_gain[0], jnp.zeros((5, shard), BF), centroids[...]], axis=0
    )
    smalls[j] = small[...]
    greet([{"expert": p} for p in others(8, e)] + [{"dp": p} for p in (sibling, across, diagonal)])

    toks = Spread(tok, held, tok_send, tok_recv, 2)
    toks.start()
    later = Weights(wqkv, 0, shard // 2, wfirst, q_send, q_recv, copy_sem.at[7])
    for cp in own_w:
        cp.wait()

    def w_copy(kind):
        if kind == 0:
            return push(wblk.at[mine(j)], wblk.at[mine(j)], w_send.at[0], w_recv.at[j], {"dp": sibling})
        if kind == 1:
            return push(wblk.at[mine(j)], wblk.at[mine(j)], w_send.at[1], w_recv.at[j], {"dp": across})
        return push(wblk.at[mine(across)], wblk.at[mine(across)], w_send.at[2], w_recv.at[across], {"dp": sibling})

    def w_arrival(s):
        return push(wblk.at[mine(s)], wblk.at[mine(s)], w_send.at[0], w_recv.at[s], {"dp": sibling})

    def s_copy(i):
        return push(small, smalls.at[j], w_send.at[3 + i], w_recv.at[4 + j], {"dp": (sibling, across, diagonal)[i]})

    def s_arrival(s):
        return push(small, smalls.at[s], w_send.at[3], w_recv.at[4 + s], {"dp": sibling})

    def out_copy(kind):
        if kind == 0:
            return push(wout, wout_full.at[mine(j)], w_send.at[6], w_recv.at[8 + j], {"dp": sibling})
        if kind == 1:
            return push(wout, wout_full.at[mine(j)], w_send.at[7], w_recv.at[8 + j], {"dp": across})
        return push(wout_full.at[mine(across)], wout_full.at[mine(across)], w_send.at[8], w_recv.at[8 + across], {"dp": sibling})

    def out_arrival(s):
        return push(wout, wout_full.at[mine(s)], w_send.at[6], w_recv.at[8 + s], {"dp": sibling})

    for i in range(3):
        s_copy(i).start()
    w_copy(1).start()
    w_copy(0).start()
    out_copy(1).start()
    out_copy(0).start()
    later.start()
    own_out.wait()
    keep_out = pltpu.make_async_copy(bounce, wout_full.at[mine(j)], copy_sem.at[4])
    keep_out.start()
    for s in (sibling, across, diagonal):
        s_arrival(s).wait_recv()
    for s in range(4):
        at = pl.ds(s * shard, shard)
        block = smalls[s].astype(F32)
        gain[:, at] = block[0:1]
        gain_col[s : s + 1, :] = block[0:1]
        gains[:, at] = block[1:3]
        cent_full[:, at] = smalls[s, 8:16, :]
    w_arrival(across).wait_recv()
    w_copy(2).start()
    w_arrival(sibling).wait_recv()
    w_arrival(diagonal).wait_recv()

    def project(zz):
        base = zz * 2 * rows
        for xx in range(2):
            def norm_rows(t, c):
                rs = pl.ds(pl.multiple_of(t * 64, 64), 64)
                v = held[2 * zz + xx, rs, :].astype(F32)
                center = v - mean_last(v)
                inverse = lax.rsqrt(mean_last(center * center) + EPS)
                at = pl.ds(pl.multiple_of(base + xx * rows + t * 64, 64), 64)
                normed[at, :] = (center * inverse * gain[...]).astype(BF)
                return c
            lax.fori_loop(0, rows // 64, norm_rows, 0)
        at = pl.ds(pl.multiple_of(base, 2 * rows), 2 * rows)
        qkv[at, :] = jnp.dot(normed[at, :], wblk[...], preferred_element_type=F32).astype(BF)

    own_tok.wait()
    toks.step(1)
    toks.wait_beside(z)
    project(z)
    toks.step(2)
    toks.wait_beside(zs[0])
    project(zs[0])
    toks.step(3)
    out_arrival(across).wait_recv()
    out_copy(2).start()
    toks.wait_beside(zs[1])
    project(zs[1])
    toks.wait_beside(zs[2])
    project(zs[2])
    stores = [
        pltpu.make_async_copy(normed, normed_out, copy_sem.at[0]),
        pltpu.make_async_copy(qkv, qkv_out, copy_sem.at[1]),
    ]
    for cp in stores:
        cp.start()

    def o_copy(dest):
        return push(mixed_low.at[pl.ds(dest * rows, rows)], olow.at[:, mycols], o_send.at[dest], o_recv.at[e], {"expert": dest})

    def o_own(dest):
        return pltpu.make_async_copy(mixed_low.at[pl.ds(dest * rows, rows)], olow.at[:, mycols], copy_sem.at[5])

    left = lane_masks(2 * rows)
    for b in (3, 2, 1, 0):
        qs = qkv[pl.ds(b * 2 * rows, 2 * rows), 0:lanes]
        keys = qkv[0 : (b + 1) * 2 * rows, lanes : 2 * lanes]
        vals = qkv[0 : (b + 1) * 2 * rows, 2 * lanes : 3 * lanes]
        outs, logs = [], []
        for h in range(2):
            mask = left if h == 0 else jnp.logical_not(left)
            q_h = jnp.where(mask, qs.astype(F32) * (HEAD ** -0.5), 0.0).astype(BF)
            sc = lax.dot_general(q_h, keys, NT, preferred_element_type=F32)
            top = jnp.max(sc, axis=-1, keepdims=True)
            pr = jnp.exp(sc - top)
            tot = jnp.sum(pr, axis=-1, keepdims=True)
            outs.append(jnp.dot(pr.astype(BF), vals, preferred_element_type=F32) / tot)
            logs.append(top + jnp.log(tot))
        at = pl.ds(b * 2 * rows, 2 * rows)
        res = jnp.where(left, outs[0], outs[1])
        mixed[at, :] = res
        mixed_low[at, :] = res.astype(BF)
        turned = jnp.where(left, logs[0], logs[1]).T
        lse_rows[0:1, at] = turned[0:1]
        lse_rows[1:2, at] = turned[HEAD : HEAD + 1]
        for dest in (2 * b, 2 * b + 1):
            @pl.when(dest != e)
            def _():
                o_copy(dest).start()

            @pl.when(dest == e)
            def _():
                o_own(dest).start()
    more = [
        pltpu.make_async_copy(mixed, mixed_out, copy_sem.at[2]),
    ]
    for cp in more:
        cp.start()
    for dest in range(8):
        @pl.when(dest != e)
        def _():
            push(mixed_low.at[pl.ds(0, rows)], olow.at[:, pl.ds(dest * lanes, lanes)], o_send.at[dest], o_recv.at[dest], {"expert": dest}).wait_recv()
            o_copy(dest).wait_send()

        @pl.when(dest == e)
        def _():
            o_own(dest).wait()
    later.relay()
    for s in (sibling, diagonal):
        out_arrival(s).wait_recv()
    toks.drain()
    later.drain()
    for i in range(3):
        w_copy(i).wait_send()
        s_copy(i).wait_send()
        out_copy(i).wait_send()
    keep_out.wait()
    for cp in stores + more:
        cp.wait()


def front_block(tokens, norm_gain, expert_gain, centroids, qkv_weight, out_weight):
    rows, width = tokens.shape
    seq = 8 * rows
    shard = qkv_weight.shape[0]
    any_spec = pl.BlockSpec(memory_space=pl.ANY)
    vmem_spec = pl.BlockSpec(memory_space=pltpu.VMEM)
    V = pltpu.VMEM
    D = pltpu.SemaphoreType.DMA
    S = jax.ShapeDtypeStruct
    return pl.pallas_call(
        front_kernel,
        out_shape=(
            S((rows, width), BF), S((seq, width), BF), S((seq, 384), BF), S((seq, 128), F32),
            S((width, width), BF), S((4, shard // 2, 3 * width), BF),
            S((2, seq), F32), S((4, shard), F32), S((2, width), F32), S((8, width), BF),
        ),
        in_specs=[any_spec, vmem_spec, vmem_spec, vmem_spec, any_spec, any_spec],
        out_specs=(any_spec,) * 6 + (vmem_spec,) * 4,
        scratch_shapes=[
            V((8, rows, width), BF), V((width, 384), BF), V((seq, width), BF), V((seq, 384), BF),
            V((seq, 128), F32), V((seq, 128), BF), V((1, width), F32), V((shard, width), BF),
            V((16, shard), BF), V((4, 16, shard), BF),
            D((22,)), D((16,)), D((9,)), D((12,)), D((8,)), D((8,)), D((8,)), D((3,)), D((4,)),
        ],
        compiler_params=pltpu.CompilerParams(collective_id=2, has_side_effects=True, vmem_limit_bytes=56 * 1024 * 1024),
        name="front_block",
    )(tokens, norm_gain, expert_gain, centroids, qkv_weight, out_weight)


def expert_kernel(
    zslots, dslots, olow, gain_ref, w1_hbm, w2_hbm,
    returned, came_back, olow_full, ggain_ref, n_out, h_out, df_out, du_out,
    w1, w2, x, hid, gpr, unit_s, inv_s, state, total, own, f1, rf1, ssum, rss,
    zland, dland, zfar, dfar, bsend, gsend, ggain, gland,
    x_send, x_recv, f_send, f_recv, s_send, s_recv, l_send, l_recv,
    a_send, a_recv, g_send, g_recv, copy_sem, own_sem, e_send, e_recv,
):
    cap, width = zslots.shape[1:]
    quarter = 2 * cap
    pair = 2 * quarter
    chunk = 2 * pair
    tiles = width // TILE
    shard = width // 4
    j, sibling, across, diagonal = dp_peers()
    e, zpos, xpos, beside, zs = expert_peers()
    mine = pl.multiple_of((j // 2) * quarter, 16)
    theirs = pl.multiple_of((1 - j // 2) * quarter, 16)

    loads = []
    for i, (src, dst) in enumerate(
        [(w1_hbm.at[0, 0], w1.at[0]), (w2_hbm.at[0, 0], w2.at[0]),
         (w1_hbm.at[0, 1], w1.at[1]), (w2_hbm.at[0, 1], w2.at[1])]
    ):
        cp = pltpu.make_async_copy(src, dst, copy_sem.at[i])
        cp.start()
        loads.append(cp)
    zx = (zpos, zs[0], lax.rem(zpos + 2, 4), 3 - zpos)

    def peer_at(q):
        return 2 * zx[q // 2] + q % 2

    def seat(q):
        return 2 * (q // 2) + xpos

    greet([{"expert": p} for p in others(8, e)] + [{"dp": p} for p in (sibling, across, diagonal)])

    def swap(src, dst, which, q):
        peer = peer_at(q)
        if which < 2:
            return push(src.at[peer], dst.at[seat(q)], a_send.at[which * 8 + q], a_recv.at[which * 8 + seat(q)], {"expert": peer})
        return push(src.at[q], dst.at[e], a_send.at[which * 8 + q], a_recv.at[which * 8 + seat(q)], {"expert": peer})

    def swap_arrival(src, dst, which, q):
        peer = peer_at(q)
        if which < 2:
            return push(src.at[peer], dst.at[q], a_send.at[which * 8 + q], a_recv.at[which * 8 + q], {"expert": peer})
        return push(src.at[q], dst.at[peer], a_send.at[which * 8 + q], a_recv.at[which * 8 + q], {"expert": peer})

    def swap_own(src, dst, which):
        if which < 2:
            return pltpu.make_async_copy(src.at[e], dst.at[xpos], own_sem.at[which])
        return pltpu.make_async_copy(src.at[xpos], dst.at[e], own_sem.at[which])

    def for_places(c, act, here):
        for q in (2 * c, 2 * c + 1):
            if q >= 2:
                act(q)
            else:
                @pl.when(xpos != q)
                def _():
                    act(q)

                @pl.when(xpos == q)
                def _():
                    here()

    for which, (src, dst) in enumerate([(zslots, zland), (dslots, dland)]):
        for c in ((1, 2, 3, 0) if which == 0 else (3, 2, 1, 0)):
            for_places(c, lambda q: swap(src, dst, which, q).start(), lambda: swap_own(src, dst, which).start())
    olows = Spread(olow, olow_full, g_send, g_recv, 1)
    own_o = pltpu.make_async_copy(olow, olow_full.at[e], copy_sem.at[12])
    own_o.start()
    layer_of = (0, 1, 1, 0)

    def my_half(c):
        return pl.ds(c * chunk, pair)

    def x_copy(p, c):
        q = 4 * p + c
        return push(x.at[p, my_half(c)], x.at[p, pl.ds(c * chunk + pair, pair)], x_send.at[q], x_recv.at[q], {"dp": sibling})

    def f_copy(q, cols):
        return push(f1.at[q, :, cols], rf1.at[q, :, cols], f_send.at[q], f_recv.at[q], {"dp": sibling})

    def s_copy(p, c, arrives=False):
        q = 4 * p + c
        if p in (0, 2):
            return push(ssum.at[q], rss.at[q], s_send.at[q], s_recv.at[q], {"dp": across})
        at = pl.ds(mine if arrives else theirs, quarter)
        return push(ssum.at[q, at], rss.at[q, at], s_send.at[q], s_recv.at[q], {"dp": across})

    def land_copy(which, c):
        src, dst = (zland, zfar) if which == 0 else (dland, dfar)
        at = pl.ds(2 * c, 2)
        return push(src.at[at], dst.at[at], l_send.at[4 * which + c], l_recv.at[4 * which + c], {"dp": across})

    def forward(which, c):
        src, dst = (zslots, zland) if which == 0 else (dslots, dland)
        for_places(c, lambda q: swap_arrival(src, dst, which, q).wait_recv(), lambda: swap_own(src, dst, which).wait())
        land_copy(which, c).start()

    def both(buf, c):
        return jnp.concatenate([buf[2 * c].astype(F32), buf[2 * c + 1].astype(F32)], axis=0)

    def by_rows(act):
        def step(t, carry):
            act(pl.multiple_of(t * 32, 32))
            return carry
        lax.fori_loop(0, pair // 32, step, 0)

    def norm_rows(p, c, read):
        def act(t):
            v = read(t)
            center = v - mean_last(v)
            inverse = lax.rsqrt(mean_last(center * center) + EPS)
            unit = center * inverse
            rs = pl.ds(c * pair + t, 32)
            unit_s[p, rs, :] = unit
            inv_s[p, rs, :] = jnp.broadcast_to(inverse, (32, 128))
            x[p, pl.ds(c * chunk + t, 32), :] = (unit * gain_ref[pl.ds(p, 1), :]).astype(BF)
        by_rows(act)
        x_copy(p, c).start()

    def begin(c):
        land_copy(0, c).wait_recv()
        state[pl.ds(c * pair + mine, quarter), :] = both(zland, c)
        state[pl.ds(c * pair + theirs, quarter), :] = both(zfar, c)
        norm_rows(0, c, lambda t: state[pl.ds(c * pair + t, 32), :])

    def begin_back(c):
        land_copy(1, c).wait_recv()
        x[2, pl.ds(c * chunk + mine, quarter), :] = both(dland, c).astype(BF)
        x[2, pl.ds(c * chunk + theirs, quarter), :] = both(dfar, c).astype(BF)
        x_copy(2, c).start()

    def compute(p, c):
        k = layer_of[p]
        base = pl.ds(c * chunk, chunk)
        left_w, right_w = (w1, w2) if p < 2 else (w2, w1)
        q = 4 * p + c
        x_copy(p, c).wait_recv()

        def up(t, carry):
            cols = pl.ds(pl.multiple_of(t * TILE, TILE), TILE)
            pre = lax.dot_general(x[p, base, :], left_w[k, cols, :], NT, preferred_element_type=F32)
            if p < 2:
                cdf = 0.5 * (1.0 + lax.erf(pre * (0.5 ** 0.5)))
                pdf = jnp.exp(-0.5 * pre * pre) * 0.3989422804014327
                hid[k, base, cols] = (pre * cdf).astype(BF)
                gpr[k, base, cols] = cdf + pre * pdf
            else:
                hid[2 + k, base, cols] = (pre * gpr[k, base, cols]).astype(BF)
            return carry

        lax.fori_loop(0, tiles, up, 0)
        slot = k if p < 2 else 2 + k

        def down(t, carry):
            cols = pl.ds(pl.multiple_of(t * TILE, TILE), TILE)
            res = jnp.dot(hid[slot, base, :], right_w[k, :, cols], preferred_element_type=F32)
            own[c, :, cols] = res[:pair]
            f1[q, :, cols] = res[pair:].astype(BF)
            f_copy(q, cols).start()
            return carry

        lax.fori_loop(0, tiles, down, 0)

    everything = pl.ds(0, width)

    def send_sum(p, c):
        q = 4 * p + c
        f_copy(q, everything).wait_recv()

        def act(t):
            rs = pl.ds(t, 32)
            v = own[c, rs, :] + rf1[q, rs, :].astype(F32)
            own[c, rs, :] = v
            ssum[q, rs, :] = v.astype(BF)
        by_rows(act)
        s_copy(p, c).start()

    def give_back(buf, dst, which, c, v):
        for i in range(2):
            buf[2 * c + i] = v[i * cap : (i + 1) * cap].astype(BF)
        for_places(c, lambda q: swap(buf, dst, which, q).start(), lambda: swap_own(buf, dst, which).start())

    def add_gain(k, c, part):
        if c == 0:
            ggain[pl.ds(k, 1), :] = part
        else:
            ggain[pl.ds(k, 1), :] = ggain[pl.ds(k, 1), :] + part

    def norm_back(k, got, rs):
        unit = unit_s[k, rs, :]
        a = got * gain_ref[pl.ds(k, 1), :]
        back = inv_s[k, rs, :][:, :1] * (a - mean_last(a) - unit * mean_last(a * unit))
        return back, jnp.sum(got * unit, axis=0, keepdims=True)

    def finish(p, c):
        k = layer_of[p]
        q = 4 * p + c
        s_copy(p, c, True).wait_recv()
        if p == 0:
            def read(t):
                rs = pl.ds(c * pair + t, 32)
                got = own[c, pl.ds(t, 32), :] + rss[q, pl.ds(t, 32), :].astype(F32)
                total[rs, :] = got
                return state[rs, :] + got
            norm_rows(1, c, read)
        elif p == 2:
            def step(i, part):
                t = pl.multiple_of(i * 32, 32)
                rs = pl.ds(c * pair + t, 32)
                got = own[c, pl.ds(t, 32), :] + rss[q, pl.ds(t, 32), :].astype(F32)
                back, add = norm_back(1, got, rs)
                state[rs, :] = back
                at = pl.ds(c * chunk + t, 32)
                x[3, at, :] = (x[2, at, :].astype(F32) + back).astype(BF)
                return part + add
            part = lax.fori_loop(0, pair // 32, step, jnp.zeros((1, width), F32))
            x_copy(3, c).start()
            add_gain(1, c, 0.5 * part)
        else:
            at = pl.ds(mine, quarter)
            rs = pl.ds(c * pair + mine, quarter)
            got = own[c, at, :] + rss[q, at, :].astype(F32)
            if p == 1:
                give_back(bsend, returned, 2, c, total[rs, :] + got)
            else:
                back, part = norm_back(0, got, rs)
                give_back(gsend, came_back, 3, c, state[rs, :] + back)
                add_gain(0, c, part)

    stores = []

    def store(i, src, dst):
        cp = pltpu.make_async_copy(src, dst, copy_sem.at[4 + i])
        cp.start()
        stores.append(cp)

    def gain_copy(i):
        s = (sibling, across, diagonal)[i]
        return push(ggain.at[:, pl.ds(pl.multiple_of(s * shard, shard), shard)], gland.at[j], e_send.at[i], e_recv.at[j], {"dp": s})

    forward(0, 0)
    forward(0, 1)
    begin(0)
    loads[0].wait()
    loads[1].wait()
    for t in range(16):
        p, c = divmod(t, 4)
        if t == 4:
            loads[2].wait()
            loads[3].wait()
        compute(p, c)
        if t < 2:
            forward(0, t + 2)
        if 2 <= t < 6:
            forward(1, t - 2)
        if t < 3:
            begin(t + 1)
        if t >= 2:
            finish(*divmod(t - 2, 4))
        send_sum(p, c)
        if 5 <= t < 9:
            begin_back(t - 5)
        if t == 2:
            olows.start()
        if t in (5, 8, 11):
            olows.step((t - 2) // 3)
        if c == 3:
            k = layer_of[p]
            if p < 2:
                store(p * 2, x.at[p], n_out.at[k])
                store(p * 2 + 1, hid.at[k], h_out.at[k])
            else:
                store(p * 2, x.at[p], df_out.at[k])
                store(p * 2 + 1, hid.at[2 + k], du_out.at[k])
    finish(3, 2)
    finish(3, 3)
    for i in range(3):
        gain_copy(i).start()
    gland[j] = ggain[:, pl.ds(pl.multiple_of(j * shard, shard), shard)]
    own_o.wait()
    for zz in range(4):
        olows.wait_beside(zz)
    olows.drain()
    for p in range(4):
        for c in range(4):
            x_copy(p, c).wait_send()
            f_copy(4 * p + c, everything).wait_send()
            s_copy(p, c).wait_send()
    for i in range(2):
        for c in range(4):
            land_copy(i, c).wait_send()
    for cp in stores:
        cp.wait()
    for i in range(3):
        push(ggain.at[:, pl.ds(0, shard)], gland.at[(sibling, across, diagonal)[i]], e_send.at[0], e_recv.at[(sibling, across, diagonal)[i]], {"dp": sibling}).wait_recv()
        gain_copy(i).wait_send()
    ggain_ref[...] = jnp.sum(gland[...], axis=0)
    for c in range(4):
        for which, (src, dst) in enumerate([(zslots, zland), (dslots, dland), (bsend, returned), (gsend, came_back)]):
            for_places(c, lambda q: swap(src, dst, which, q).wait_send(), lambda: None)
            if which >= 2:
                for_places(c, lambda q: swap_arrival(src, dst, which, q).wait_recv(), lambda: swap_own(src, dst, which).wait())


def expert_block(zslots, dslots, olow, gains, expert_in, expert_out):
    sources, cap, width = zslots.shape
    rows = sources * cap
    pair = 4 * cap
    hidden = expert_in.shape[2]
    everything = 4 * rows
    any_spec = pl.BlockSpec(memory_space=pl.ANY)
    vmem_spec = pl.BlockSpec(memory_space=pltpu.VMEM)
    S = jax.ShapeDtypeStruct
    big = S((2, everything, width), BF)
    V = pltpu.VMEM
    D = pltpu.SemaphoreType.DMA
    return pl.pallas_call(
        expert_kernel,
        out_shape=(
            S(zslots.shape, BF), S(zslots.shape, BF), S((8,) + olow.shape, BF), S((2, width // 4), F32),
            big, big, big, big,
        ),
        in_specs=[any_spec] * 3 + [vmem_spec] + [any_spec] * 2,
        out_specs=(any_spec, any_spec, any_spec, vmem_spec, any_spec, any_spec, any_spec, any_spec),
        scratch_shapes=[
            V((2, hidden, width), BF), V((2, hidden, width), BF),
            V((4, everything, width), BF), V((4, everything, hidden), BF), V((2, everything, hidden), F32),
            V((2, 2 * rows, width), F32), V((2, 2 * rows, 128), F32), V((2 * rows, width), F32), V((2 * rows, width), F32),
            V((4, pair, width), F32),
        ]
        + [V((16, pair, width), BF)] * 4
        + [V(zslots.shape, BF)] * 6
        + [V((2, width), F32), V((4, 2, width // 4), F32)]
        + [D((16,))] * 6 + [D((8,))] * 2
        + [D((32,)), D((32,)), D((11,)), D((8,)), D((13,)), D((4,)), D((3,)), D((4,))],
        compiler_params=pltpu.CompilerParams(
            collective_id=1, has_side_effects=True, vmem_limit_bytes=62 * 1024 * 1024
        ),
        name="expert_block",
    )(zslots, dslots, olow, gains, expert_in, expert_out)


def back_kernel(
    gmix, gatt, qkv_hbm, mixed_hbm, lse_rows, normed_hbm, olow_hbm, cent, wqkv,
    dq_land, gq_land, go_land, gc_land, wsecond,
    dom, dam, qkv, mixed, normed, olow, delta, dq_acc, dqkv,
    part, f1, f3, ssum, rf1, rf3, rss, gq_own, go_own, cland, csum, cdp,
    h_send, h_recv, d_send, d_recv, p_send, p_recv, gq_send, gq_recv, go_send, go_recv, c_send, c_recv, copy_sem, q_send, q_recv,
):
    j, sibling, across, diagonal = dp_peers()
    e, zpos, xpos, beside, zs = expert_peers()
    rows, width = gmix.shape
    blk = 2 * rows
    lanes = 128
    shard = width // 4
    loads = [
        pltpu.make_async_copy(src, dst, copy_sem.at[i])
        for i, (src, dst) in enumerate([(qkv_hbm, qkv), (mixed_hbm, mixed), (olow_hbm, olow), (normed_hbm, normed)])
    ]
    for cp in loads:
        cp.start()
    peers = others(8, e)
    greet([{"expert": p} for p in peers] + [{"dp": p} for p in (sibling, across, diagonal)])

    def cols_of(s):
        return pl.ds(pl.multiple_of(s * lanes, lanes), lanes)

    def rows_of(s):
        return pl.ds(pl.multiple_of(s * rows, rows), rows)

    def head_copy(src, dst, which, dest):
        return push(src.at[:, cols_of(dest)], dst.at[rows_of(e)], h_send.at[which * 8 + dest], h_recv.at[which * 8 + e], {"expert": dest})

    def head_arrival(src, dst, which, source):
        return push(src.at[:, cols_of(source)], dst.at[rows_of(source)], h_send.at[which * 8 + source], h_recv.at[which * 8 + source], {"expert": source})

    for dest in peers:
        head_copy(gmix, dom, 0, dest).start()
    for dest in peers:
        head_copy(gatt, dam, 1, dest).start()
    for dest in peers:
        push(cent.at[dest], cland.at[e], c_send.at[dest], c_recv.at[e], {"expert": dest}).start()
    later = Weights(wqkv, shard // 2, shard // 2, wsecond, q_send, q_recv, copy_sem.at[8])
    later.start()
    dom[rows_of(e), :] = gmix[:, cols_of(e)]
    dam[rows_of(e), :] = gatt[:, cols_of(e)]
    cland[e] = cent[e]

    def dp_sum_start(buf, n, t):
        def block(s):
            return buf[0:n, pl.ds(pl.multiple_of(s * shard, shard), shard)]
        f3[t, 0:n, :] = block(diagonal).astype(BF)
        f1[t, 0:n, :] = block(sibling).astype(BF)
        dp_copy(1, n, t).start()
        dp_copy(0, n, t).start()
        dp_copy(1, n, t).wait_recv()
        ssum[t, 0:n, :] = (block(across) + rf3[t, 0:n, :].astype(F32)).astype(BF)
        dp_copy(2, n, t).start()

    def dp_copy(kind, n, t):
        at = pl.ds(0, n)
        if kind == 0:
            return push(f1.at[t, at], rf1.at[t, at], p_send.at[t * 3], p_recv.at[t * 3], {"dp": sibling})
        if kind == 1:
            return push(f3.at[t, at], rf3.at[t, at], p_send.at[t * 3 + 1], p_recv.at[t * 3 + 1], {"dp": sibling})
        return push(ssum.at[t, at], rss.at[t, at], p_send.at[t * 3 + 2], p_recv.at[t * 3 + 2], {"dp": across})

    def dp_sum_end(buf, n, t):
        dp_copy(0, n, t).wait_recv()
        dp_copy(2, n, t).wait_recv()
        return buf[0:n, pl.ds(pl.multiple_of(j * shard, shard), shard)] + rf1[t, 0:n, :].astype(F32) + rss[t, 0:n, :].astype(F32)

    for cp in loads[:2]:
        cp.wait()
    for source in peers:
        head_arrival(gmix, dom, 0, source).wait_recv()
    left_row = lax.broadcasted_iota(jnp.int32, (8, 128), 1) < HEAD
    row_id = lax.broadcasted_iota(jnp.int32, (8, 128), 0)
    pick = jnp.where((row_id == 0) == left_row, 1.0, 0.0).astype(F32)
    delta[...] = lax.dot_general(pick, dom[...].astype(F32) * mixed[...], NT, precision=HIGH, preferred_element_type=F32)

    for source in peers:
        push(cent.at[source], cland.at[source], c_send.at[source], c_recv.at[source], {"expert": source}).wait_recv()
    csum[0] = jnp.sum(cland[...], axis=0)

    def c_copy(i):
        s = (sibling, across, diagonal)[i]
        return push(csum.at[0, :, pl.ds(pl.multiple_of(s * shard, shard), shard)], cdp.at[j], c_send.at[8 + i], c_recv.at[8 + j], {"dp": s})

    def c_arrival(s):
        return push(csum.at[0, :, pl.ds(0, shard)], cdp.at[s], c_send.at[8], c_recv.at[8 + s], {"dp": sibling})

    for i in range(3):
        c_copy(i).start()
    cdp[j] = csum[0, :, pl.ds(pl.multiple_of(j * shard, shard), shard)]

    left = lane_masks(blk)
    dq_acc[...] = jnp.zeros_like(dq_acc)

    def d_copy(dest):
        return push(dqkv.at[pl.ds(dest * rows, rows)], dq_land.at[e], d_send.at[dest], d_recv.at[e], {"expert": dest})

    for b in range(4):
        at = pl.ds(b * blk, blk)
        tail = pl.ds(b * blk, 8 * rows - b * blk)
        qs = qkv[tail, 0:lanes]
        dos = dom[tail, :]
        keys = qkv[at, lanes : 2 * lanes].astype(F32) * (HEAD ** -0.5)
        vals = qkv[at, 2 * lanes : 3 * lanes]
        dks, dvs = [], []
        for h in range(2):
            mask = left if h == 0 else jnp.logical_not(left)
            k_h = jnp.where(mask, keys, 0.0).astype(BF)
            v_h = jnp.where(mask, vals.astype(F32), 0.0).astype(BF)
            sc = lax.dot_general(k_h, qs, NT, preferred_element_type=F32)
            pr = jnp.exp(sc - lse_rows[h : h + 1, tail])
            dp = lax.dot_general(v_h, dos, NT, preferred_element_type=F32)
            ds = (pr * (dp - delta[h : h + 1, tail])).astype(BF)
            dvs.append(jnp.dot(pr.astype(BF), dos, preferred_element_type=F32))
            dks.append(jnp.dot(ds, qs, preferred_element_type=F32))
            dq_acc[tail, :] += lax.dot_general(ds, k_h, TN, preferred_element_type=F32)
        dqkv[at, 0:lanes] = dq_acc[at, :].astype(BF)
        dqkv[at, lanes : 2 * lanes] = (jnp.where(left, dks[0], dks[1]) * (HEAD ** -0.5)).astype(BF)
        dqkv[at, 2 * lanes : 3 * lanes] = jnp.where(left, dvs[0], dvs[1]).astype(BF)
        for dest in (2 * b, 2 * b + 1):
            @pl.when(dest != e)
            def _():
                d_copy(dest).start()

            @pl.when(dest == e)
            def _():
                pltpu.make_async_copy(dqkv.at[pl.ds(dest * rows, rows)], dq_land.at[dest], copy_sem.at[4]).start()
        if b == 0:
            loads[2].wait()
            for source in peers:
                head_arrival(gatt, dam, 1, source).wait_recv()
            part[0:lanes, :] = lax.dot_general(dam[...], olow[...], TN, preferred_element_type=F32)
            dp_sum_start(part, lanes, 0)
        if b == 1:
            go_own[...] = dp_sum_end(part, lanes, 0).T.astype(BF)
            gos = Spread(go_own, go_land, go_send, go_recv, 1)
            gos.start()
            own_go = pltpu.make_async_copy(go_own, go_land.at[e], copy_sem.at[5])
            own_go.start()
            for s in (sibling, across, diagonal):
                c_arrival(s).wait_recv()
            csum[1, :, 0:shard] = jnp.sum(cdp[...], axis=0)
            for dest in peers:
                push(csum.at[1, :, pl.ds(0, shard)], gc_land.at[e], c_send.at[12 + dest], c_recv.at[12 + e], {"expert": dest}).start()
            own_gc = pltpu.make_async_copy(csum.at[1, :, pl.ds(0, shard)], gc_land.at[e], copy_sem.at[6])
            own_gc.start()
    loads[3].wait()
    part[...] = lax.dot_general(dqkv[...], normed[...], TN, preferred_element_type=F32)
    dp_sum_start(part, 3 * lanes, 1)
    gos.step(1)
    gq_own[...] = dp_sum_end(part, 3 * lanes, 1).T.astype(BF)
    gqs = Spread(gq_own, gq_land, gq_send, gq_recv, 2)
    gqs.start()
    own_gq = pltpu.make_async_copy(gq_own, gq_land.at[e], copy_sem.at[7])
    own_gq.start()
    gos.step(2)
    later.relay()
    gqs.step(1)
    gos.step(3)
    gqs.step(2)
    gqs.step(3)
    for zz in range(4):
        gos.wait_beside(zz)
        gqs.wait_beside(zz)
    gos.drain()
    gqs.drain()
    later.drain()
    for source in range(8):
        @pl.when(source != e)
        def _():
            push(dqkv.at[pl.ds(0, rows)], dq_land.at[source], d_send.at[source], d_recv.at[source], {"expert": source}).wait_recv()
            d_copy(source).wait_send()
            push(csum.at[1, :, pl.ds(0, shard)], gc_land.at[source], c_send.at[12 + source], c_recv.at[12 + source], {"expert": source}).wait()

        @pl.when(source == e)
        def _():
            pltpu.make_async_copy(dqkv.at[pl.ds(0, rows)], dq_land.at[source], copy_sem.at[4]).wait()
    for dest in peers:
        head_copy(gmix, dom, 0, dest).wait_send()
        head_copy(gatt, dam, 1, dest).wait_send()
        push(cent.at[dest], cland.at[e], c_send.at[dest], c_recv.at[e], {"expert": dest}).wait_send()
    for i in range(3):
        c_copy(i).wait_send()
        dp_copy(i, lanes, 0).wait_send()
        dp_copy(i, 3 * lanes, 1).wait_send()
    for cp in (own_go, own_gc, own_gq):
        cp.wait()


def back_block(gmix, gatt, qkv, mixed, lse_rows, normed, olow_full, cent, qkv_weight):
    rows, width = gmix.shape
    seq = 8 * rows
    shard = width // 4
    any_spec = pl.BlockSpec(memory_space=pl.ANY)
    vmem_spec = pl.BlockSpec(memory_space=pltpu.VMEM)
    S = jax.ShapeDtypeStruct
    V = pltpu.VMEM
    D = pltpu.SemaphoreType.DMA
    return pl.pallas_call(
        back_kernel,
        out_shape=(
            S((8, rows, 384), BF), S((8, shard, 384), BF), S((8, shard, 128), BF), S((8, 1, shard), F32),
            S((4, shard // 2, 3 * width), BF),
        ),
        in_specs=[vmem_spec, vmem_spec, any_spec, any_spec, vmem_spec, any_spec, any_spec, vmem_spec, any_spec],
        out_specs=(any_spec,) * 5,
        scratch_shapes=[
            V((seq, 128), BF), V((seq, 128), BF), V((seq, 384), BF), V((seq, 128), F32), V((seq, width), BF), V((seq, width), BF),
            V((8, seq), F32), V((seq, 128), F32), V((seq, 384), BF),
            V((384, width), F32),
        ]
        + [V((2, 384, shard), BF)] * 6
        + [
            V((shard, 384), BF), V((shard, 128), BF), V((8, 1, width), F32), V((2, 1, width), F32), V((4, 1, shard), F32),
            D((16,)), D((16,)), D((8,)), D((8,)), D((6,)), D((6,)), D((22,)), D((16,)), D((11,)), D((8,)), D((20,)), D((20,)), D((9,)), D((3,)), D((4,)),
        ],
        compiler_params=pltpu.CompilerParams(collective_id=3, has_side_effects=True, vmem_limit_bytes=56 * 1024 * 1024),
        name="back_block",
    )(gmix, gatt, qkv, mixed, lse_rows, normed, olow_full, cent, qkv_weight)


def final_kernel(
    dq_hbm, wfirst, wsecond, tok_hbm, gain_col, gres_hbm, gq_hbm, go_hbm, wqkv_hbm, gc_land, gain_part,
    n_hbm, h_hbm, df_hbm, du_hbm,
    gtok_hbm, gqkv_hbm, gout_hbm, gnorm, gcent, ggain, gein, geout,
    n, h, df, du, tile_in, tile_out, dq_land, w, tok, gres, gq_land, go_land, wqkv,
    dqkv, dnorm, gtok, gqkv, gout, small_sum,
    load_sem, tile_sem, store_sem,
):
    rows, width = tok.shape
    shard = wqkv.shape[0]
    half = shard // 2
    tiles = width // TILE

    def load(i, src, dst):
        cp = pltpu.make_async_copy(src, dst, load_sem.at[i])
        cp.start()
        return cp

    pairs = []
    for i, (src, dst) in enumerate([(du_hbm, du), (n_hbm, n), (h_hbm, h), (df_hbm, df)]):
        pairs.append([load(2 * i + k, src.at[k], dst.at[k]) for k in range(2)])
    first = [load(8, dq_hbm, dq_land), load(9, gq_hbm, gq_land), load(10, go_hbm, go_land), load(11, wqkv_hbm, wqkv)]
    rest = [load(12, tok_hbm, tok), load(13, gres_hbm, gres)]
    for s in range(4):
        rest.append(load(14 + 2 * s, wfirst.at[s], w.at[s, pl.ds(0, half)]))
        rest.append(load(15 + 2 * s, wsecond.at[s], w.at[s, pl.ds(half, half)]))

    def tile_copy(stage, out, base, k, t):
        at = pl.ds(pl.multiple_of(t * TILE, TILE), TILE)
        return pltpu.make_async_copy(stage.at[k, at], out.at[k, at], tile_sem.at[(base + k) * tiles + t])

    for base, left, right, stage, out, waits in (
        (0, du, n, tile_in, gein, pairs[:2]), (2, h, df, tile_out, geout, pairs[2:]),
    ):
        for k in range(2):
            for pair in waits:
                pair[k].wait()

            def tile(t, c):
                at = pl.ds(pl.multiple_of(t * TILE, TILE), TILE)
                stage[k, at, :] = lax.dot_general(left[k, :, at], right[k], TN, preferred_element_type=F32)
                tile_copy(stage, out, base, k, t).start()
                return c

            lax.fori_loop(0, tiles, tile, 0)
    for cp in first:
        cp.wait()
    for s in range(8):
        for i in range(3):
            at = pl.ds(i * width + s * 128, 128)
            dqkv[:, at] = dq_land[s, :, pl.ds(i * 128, 128)]
            gqkv[:, at] = gq_land[s, :, pl.ds(i * 128, 128)].astype(F32)
        gout[:, pl.ds(s * 128, 128)] = go_land[s].astype(F32)
    stores = [
        pltpu.make_async_copy(gqkv, gqkv_hbm, store_sem.at[0]),
        pltpu.make_async_copy(gout, gout_hbm, store_sem.at[1]),
    ]
    for cp in stores:
        cp.start()
    for cp in rest:
        cp.wait()
    for s in range(4):
        dnorm[:, pl.ds(s * shard, shard)] = lax.dot_general(dqkv[...], w[s], NT, preferred_element_type=F32)
    gain = jnp.concatenate([gain_col[s : s + 1, :] for s in range(4)], axis=1)

    def norm_rows(t, c):
        at = pl.ds(pl.multiple_of(t * 32, 32), 32)
        v = tok[at, :].astype(F32)
        center = v - mean_last(v)
        inverse = lax.rsqrt(mean_last(center * center) + EPS)
        unit = center * inverse
        a = dnorm[at, :] * gain
        gtok[at, :] = gres[at, :] + inverse * (a - mean_last(a) - unit * mean_last(a * unit))
        return c

    lax.fori_loop(0, rows // 32, norm_rows, 0)
    stores.append(pltpu.make_async_copy(gtok, gtok_hbm, store_sem.at[2]))
    stores[2].start()
    small_sum[...] = jnp.zeros_like(small_sum)

    def add(t, c):
        at = pl.ds(pl.multiple_of(t * 256, 256), 256)
        prod = gqkv[:, at] * wqkv[:, at].astype(F32)
        small_sum[...] += prod[:, :128] + prod[:, 128:]
        return c

    lax.fori_loop(0, 3 * width // 256, add, 0)
    own_gain = gain_col[pl.ds(lax.axis_index("dp"), 1), :]
    sums = lax.dot_general(jnp.ones((8, 128), F32), small_sum[...], NT, precision=HIGH, preferred_element_type=F32)
    gnorm[...] = sums[0:1] / own_gain
    for s in range(8):
        gcent[s : s + 1, :] = gc_land[s]
    ggain[...] = gain_part[...]
    for cp in stores:
        cp.wait()
    for k in range(2):
        for t in range(tiles):
            tile_copy(tile_in, gein, 0, k, t).wait()
            tile_copy(tile_out, geout, 2, k, t).wait()


def final_block(dq_land, wfirst, wsecond, tokens, gain_col, grad_resid, gq_land, go_land, qkv_weight, gc_land, gain_part, n, h, df, du):
    rows, width = tokens.shape
    shard = width // 4
    hidden = h.shape[2]
    any_spec = pl.BlockSpec(memory_space=pl.ANY)
    vmem_spec = pl.BlockSpec(memory_space=pltpu.VMEM)
    S = jax.ShapeDtypeStruct
    V = pltpu.VMEM
    D = pltpu.SemaphoreType.DMA
    return pl.pallas_call(
        final_kernel,
        out_shape=(
            S((rows, width), F32), S((shard, 3 * width), F32), S((shard, width), F32), S((1, shard), F32),
            S((8, shard), F32), S((2, shard), F32), S((2, hidden, width), F32), S((2, hidden, width), F32),
        ),
        in_specs=[any_spec] * 4 + [vmem_spec] + [any_spec] * 4 + [vmem_spec] * 2 + [any_spec] * 4,
        out_specs=(any_spec,) * 3 + (vmem_spec,) * 3 + (any_spec,) * 2,
        scratch_shapes=[V(n.shape, BF), V(h.shape, BF), V(df.shape, BF), V(du.shape, BF)]
        + [V((2, hidden, width), F32)] * 2
        + [
            V(dq_land.shape, BF), V((4, shard, 3 * width), BF), V((rows, width), BF), V((rows, width), F32),
            V(gq_land.shape, BF), V(go_land.shape, BF), V((shard, 3 * width), BF),
            V((rows, 3 * width), BF), V((rows, width), F32), V((rows, width), F32),
            V((shard, 3 * width), F32), V((shard, width), F32), V((shard, 128), F32),
            D((22,)), D((16,)), D((3,)),
        ],
        compiler_params=pltpu.CompilerParams(vmem_limit_bytes=58 * 1024 * 1024),
        name="final_block",
    )(dq_land, wfirst, wsecond, tokens, gain_col, grad_resid, gq_land, go_land, qkv_weight, gc_land, gain_part, n, h, df, du)


def on_device_split(
    tokens,
    norm_gain,
    qkv_weight,
    out_weight,
    centroids,
    expert_gain,
    expert_in,
    expert_out,
    routes,
    cotangent,
):
    rows, width = tokens.shape
    experts = lax.axis_size("expert")
    capacity = max(2, 3 * rows // (2 * experts))
    slots = experts * capacity
    shard = width // 4
    olow, normed_all, qkv, mixed, wout_full, wfirst, lse_rows, gain_col, gains, centroid_full = front_block(
        tokens, norm_gain[None], expert_gain, centroids, qkv_weight, out_weight
    )
    inputs = tokens.astype(F32)
    residual = inputs + jnp.dot(olow, wout_full, preferred_element_type=F32)
    route_ids = routes[:, 0]
    chosen = (route_ids[:, None] == jnp.arange(experts, dtype=jnp.int32)[None, :]).astype(BF)
    centroid_rows = jnp.dot(chosen, centroid_full, preferred_element_type=F32)
    gate = jax.nn.sigmoid(jnp.sum(residual * centroid_rows, axis=-1))
    before = jnp.tril(jnp.ones((rows, rows), BF), -1)
    rank = jnp.sum(jnp.dot(before, chosen, preferred_element_type=F32) * chosen.astype(F32), axis=-1)
    target = route_ids * capacity + rank.astype(jnp.int32)
    place = (jnp.arange(slots, dtype=jnp.int32)[:, None] == target[None, :]).astype(BF)
    grad_out = cotangent.astype(F32)
    sent = jnp.concatenate([residual.astype(BF), (gate[:, None] * grad_out).astype(BF)], axis=1)
    spread = jnp.dot(place, sent, preferred_element_type=F32).astype(BF)
    returned, came_back, olow_full, gain_part, n_rows, h_rows, df_rows, du_rows = expert_block(
        spread[:, :width].reshape(experts, capacity, width),
        spread[:, width:].reshape(experts, capacity, width),
        olow,
        gains,
        expert_in,
        expert_out,
    )
    branch_tok = lax.dot_general(place, returned.reshape(slots, width), TN, preferred_element_type=F32)
    block_out = (residual + gate[:, None] * branch_tok).astype(BF)
    grad_logit = jnp.sum(grad_out * branch_tok, axis=-1) * gate * (1.0 - gate)
    grad_centroid = jnp.dot(chosen.astype(F32).T, grad_logit[:, None] * residual, precision=HIGH)
    back_rows = lax.dot_general(place, came_back.reshape(slots, width), TN, preferred_element_type=F32)
    grad_resid = grad_out + grad_logit[:, None] * centroid_rows + back_rows
    grad_attended = grad_resid.astype(BF)
    grad_mixed = lax.dot_general(grad_attended, wout_full, NT, preferred_element_type=F32).astype(BF)
    dq_land, gq_land, go_land, gc_land, wsecond = back_block(
        grad_mixed, grad_attended, qkv, mixed, lse_rows, normed_all,
        olow_full.reshape(experts * rows, width), grad_centroid[:, None, :], qkv_weight,
    )
    grad_tokens, grad_qkv, grad_out_weight, grad_norm_gain, grad_centroids, grad_gain, grad_expert_in, grad_expert_out = final_block(
        dq_land, wfirst, wsecond, tokens, gain_col, grad_resid, gq_land, go_land, qkv_weight, gc_land, gain_part,
        n_rows, h_rows, df_rows, du_rows,
    )
    return (
        block_out,
        grad_tokens,
        grad_norm_gain[0],
        grad_qkv,
        grad_out_weight,
        grad_centroids,
        grad_gain[None],
        grad_expert_in[None],
        grad_expert_out[None],
    )


def on_device(
    tokens,
    norm_gain,
    qkv_weight,
    out_weight,
    centroids,
    expert_gain,
    expert_in,
    expert_out,
    routes,
    cotangent,
):
    model_width = tokens.shape[1]
    local_rows = tokens.shape[0]
    experts = lax.axis_size("expert")
    capacity = max(2, 3 * local_rows // (2 * experts))
    slot_total = experts * capacity
    first_pos = lax.axis_index("expert") * local_rows
    scale = HEAD ** (-0.5)
    gain_full, qkv_full, out_full, centroid_full, expert_gain_full = fetch_dense(
        norm_gain, qkv_weight, out_weight, centroids, expert_gain
    )
    inputs = tokens.astype(jnp.float32)
    unit_attn, inverse_attn, normed_attn = normalize(inputs, gain_full.astype(jnp.float32))
    normed_low = normed_attn.astype(jnp.bfloat16)
    projected = jnp.dot(normed_low, qkv_full, preferred_element_type=jnp.float32).astype(
        jnp.bfloat16
    )
    queries = projected[:, :model_width]
    keyset = projected[:, model_width : 2 * model_width]
    values = projected[:, 2 * model_width :]
    query_heads = split_heads(queries)
    key_heads = split_heads(keyset)
    value_heads = split_heads(values)
    query_block = (first_pos + jnp.arange(local_rows, dtype=jnp.int32)) // BLOCK
    last_block = (first_pos + local_rows - 1) // BLOCK
    start_state = (
        jnp.zeros((local_rows, HEADS, HEAD), jnp.float32),
        jnp.full((HEADS, local_rows), NEGATIVE, jnp.float32),
        jnp.zeros((HEADS, local_rows), jnp.float32),
    )
    key_piece = lax.all_gather(keyset, "expert", axis=0, tiled=True)
    value_piece = lax.all_gather(values, "expert", axis=0, tiled=True)
    amount = key_piece.shape[0]

    def update(current):
        accumulated, highest, totals = current
        scores = (
            jnp.einsum(
                "qhd,khd->hqk",
                query_heads,
                split_heads(key_piece),
                preferred_element_type=jnp.float32,
            )
            * scale
        )
        piece_block = jnp.arange(amount, dtype=jnp.int32) // BLOCK
        visible = (piece_block[None, :] <= query_block[:, None])[None]
        scores = jnp.where(visible, scores, NEGATIVE)
        new_high = jnp.maximum(highest, jnp.max(scores, axis=-1))
        factor = jnp.exp(highest - new_high)
        weights = jnp.where(visible, jnp.exp(scores - new_high[:, :, None]), 0.0)
        totals = jnp.sum(weights, axis=-1)
        accumulated = accumulated * factor.T[:, :, None] + jnp.einsum(
            "hqk,khd->qhd",
            weights.astype(jnp.bfloat16),
            split_heads(value_piece),
            preferred_element_type=jnp.float32,
        )
        return (accumulated, new_high, totals)

    accumulated, highest, totals = lax.cond(
        jnp.int32(0) // BLOCK <= last_block, update, keep_state, start_state
    )
    mixed_heads = accumulated / totals.T[:, :, None]
    log_total = (highest + jnp.log(totals)).T
    mixed_low = mixed_heads.reshape(local_rows, model_width).astype(jnp.bfloat16)
    residual = inputs + jnp.dot(mixed_low, out_full, preferred_element_type=jnp.float32)
    route_ids = routes[:, 0]
    chosen = route_ids[:, None] == jnp.arange(experts, dtype=jnp.int32)[None, :]
    centroid_rows = jnp.dot(
        chosen.astype(jnp.bfloat16), centroid_full, preferred_element_type=jnp.float32
    )
    gate_value = jax.nn.sigmoid(jnp.sum(residual * centroid_rows, axis=-1))
    chosen_int = chosen.astype(jnp.int32)
    slot_index = jnp.sum((jnp.cumsum(chosen_int, axis=0) - 1) * chosen_int, axis=-1)
    target = route_ids * capacity + slot_index
    arrived = lax.all_to_all(
        send_slots(residual.astype(jnp.bfloat16), target, experts, capacity),
        "expert",
        split_axis=0,
        concat_axis=0,
        tiled=True,
    )
    expert_state = arrived.reshape(slot_total, model_width).astype(jnp.float32)
    gains_here = expert_gain_full[0].astype(jnp.float32)
    total_change = jnp.zeros_like(expert_state)
    stored = []
    for sublayer in range(2):
        unit_rows, inverse, normed = normalize(expert_state, gains_here[sublayer])
        normed_rows = normed.astype(jnp.bfloat16)
        first_full, second_full = (expert_in[0, sublayer], expert_out[0, sublayer])
        left_rows = spread_rows(normed_rows)
        hidden_pre = jnp.einsum(
            "rd,fd->rf", left_rows, first_full, preferred_element_type=jnp.float32
        )
        hidden_act, slope_pull = jax.vjp(exact_gelu, hidden_pre)
        hidden_low = hidden_act.astype(jnp.bfloat16)
        change = sum_rows(partial(row_product, hidden_low, second_full), slot_total)
        expert_state = expert_state + change
        total_change = total_change + change
        stored.append((unit_rows, inverse, left_rows, hidden_low, slope_pull))
    branch_low = total_change.astype(jnp.bfloat16)
    returned = lax.all_to_all(
        branch_low.reshape(experts, capacity, model_width),
        "expert",
        split_axis=0,
        concat_axis=0,
        tiled=True,
    )
    branch_tok = returned.reshape(slot_total, model_width)[target].astype(jnp.float32)
    block_out = (residual + gate_value[:, None] * branch_tok).astype(jnp.bfloat16)
    gain_full, qkv_full, out_full, centroid_full, expert_gain_full = fetch_dense(
        norm_gain, qkv_weight, out_weight, centroids, expert_gain
    )
    gains_here = expert_gain_full[0].astype(jnp.float32)
    grad_out = cotangent.astype(jnp.float32)
    grad_logit = jnp.sum(grad_out * branch_tok, axis=-1) * gate_value * (1.0 - gate_value)
    grad_centroid = jnp.dot(
        chosen.astype(jnp.float32).T, grad_logit[:, None] * residual, precision=HIGH
    )
    grad_resid = grad_out + grad_logit[:, None] * centroid_rows
    grad_branch = (gate_value[:, None] * grad_out).astype(jnp.bfloat16)
    branch_grads = lax.all_to_all(
        send_slots(grad_branch, target, experts, capacity),
        "expert",
        split_axis=0,
        concat_axis=0,
        tiled=True,
    )
    grad_change = branch_grads.reshape(slot_total, model_width).astype(jnp.float32)
    grad_state = jnp.zeros_like(grad_change)
    gain_grads = [None, None]
    first_grads = [None, None]
    second_grads = [None, None]
    for sublayer in (1, 0):
        unit_rows, inverse, left_rows, hidden_low, slope_pull = stored[sublayer]
        grad_rows_low = (grad_change + grad_state).astype(jnp.bfloat16)
        first_full, second_full = (expert_in[0, sublayer], expert_out[0, sublayer])
        grad_rows = spread_rows(grad_rows_low)
        grad_hidden = jnp.einsum(
            "rd,fd->rf", grad_rows, second_full, preferred_element_type=jnp.float32
        )
        grad_pre = slope_pull(grad_hidden)[0].astype(jnp.bfloat16)
        grad_first = jnp.einsum(
            "rf,rd->fd", grad_pre, left_rows, preferred_element_type=jnp.float32
        )
        grad_second = jnp.einsum(
            "rf,rd->fd", hidden_low, grad_rows, preferred_element_type=jnp.float32
        )
        grad_normed = sum_rows(partial(row_product, grad_pre, first_full), slot_total)
        grad_input, gain_grad = norm_backward(grad_normed, unit_rows, inverse, gains_here[sublayer])
        grad_state = grad_state + grad_input
        gain_grads[sublayer] = gain_grad
        first_grads[sublayer] = grad_first
        second_grads[sublayer] = grad_second
    came_back = lax.all_to_all(
        grad_state.astype(jnp.bfloat16).reshape(experts, capacity, model_width),
        "expert",
        split_axis=0,
        concat_axis=0,
        tiled=True,
    )
    grad_resid = grad_resid + came_back.reshape(slot_total, model_width)[target].astype(jnp.float32)
    grad_attended = grad_resid.astype(jnp.bfloat16)
    grad_out_weight = jnp.einsum(
        "rd,re->de", mixed_low, grad_attended, preferred_element_type=jnp.float32
    )
    grad_mixed = jnp.einsum(
        "re,de->rd", grad_attended, out_full, preferred_element_type=jnp.float32
    ).astype(jnp.bfloat16)
    grad_heads = split_heads(grad_mixed)
    delta_rows = jnp.sum(grad_heads.astype(jnp.float32) * mixed_heads, axis=-1)
    zero_heads = jnp.zeros((local_rows, HEADS, HEAD), jnp.float32)
    running = (zero_heads, zero_heads, zero_heads)
    offset = jnp.int32(0)
    fold_key_piece = lax.all_gather(keyset, "expert", axis=0, tiled=True)
    fold_value_piece = lax.all_gather(values, "expert", axis=0, tiled=True)
    query_piece = lax.all_gather(queries, "expert", axis=0, tiled=True)
    grad_piece = lax.all_gather(grad_mixed, "expert", axis=0, tiled=True)
    log_piece = lax.all_gather(log_total.astype(jnp.bfloat16), "expert", axis=0, tiled=True).astype(
        jnp.float32
    )
    delta_piece = lax.all_gather(
        delta_rows.astype(jnp.bfloat16), "expert", axis=0, tiled=True
    ).astype(jnp.float32)
    fold_amount = fold_key_piece.shape[0]
    piece_block = jnp.arange(fold_amount, dtype=jnp.int32) // BLOCK

    def to_queries(current):
        grad_query, grad_key, grad_value = current
        piece_keys = split_heads(fold_key_piece)
        scores = (
            jnp.einsum("qhd,khd->hqk", query_heads, piece_keys, preferred_element_type=jnp.float32)
            * scale
        )
        visible = (piece_block[None, :] <= query_block[:, None])[None]
        weights = jnp.where(visible, jnp.exp(scores - log_total.T[:, :, None]), 0.0)
        grad_weights = jnp.einsum(
            "qhd,khd->hqk",
            grad_heads,
            split_heads(fold_value_piece),
            preferred_element_type=jnp.float32,
        )
        grad_scores = (weights * (grad_weights - delta_rows.T[:, :, None])).astype(jnp.bfloat16)
        grad_query = (
            jnp.einsum("hqk,khd->qhd", grad_scores, piece_keys, preferred_element_type=jnp.float32)
            * scale
        )
        return (grad_query, grad_key, grad_value)

    def to_keys(current):
        grad_query, grad_key, grad_value = current
        piece_queries = split_heads(query_piece)
        piece_grads = split_heads(grad_piece)
        scores = (
            jnp.einsum("qhd,khd->hqk", piece_queries, key_heads, preferred_element_type=jnp.float32)
            * scale
        )
        visible = (query_block[None, :] <= piece_block[:, None])[None]
        weights = jnp.where(visible, jnp.exp(scores - log_piece.T[:, :, None]), 0.0)
        grad_weights = jnp.einsum(
            "qhd,khd->hqk", piece_grads, value_heads, preferred_element_type=jnp.float32
        )
        grad_scores = (weights * (grad_weights - delta_piece.T[:, :, None])).astype(jnp.bfloat16)
        grad_key = (
            grad_key
            + jnp.einsum(
                "hqk,qhd->khd", grad_scores, piece_queries, preferred_element_type=jnp.float32
            )
            * scale
        )
        grad_value = grad_value + jnp.einsum(
            "hqk,qhd->khd",
            weights.astype(jnp.bfloat16),
            piece_grads,
            preferred_element_type=jnp.float32,
        )
        return (grad_query, grad_key, grad_value)

    running = lax.cond(offset // BLOCK <= last_block, to_queries, keep_state, running)
    grad_query, grad_key, grad_value = lax.cond(
        query_block[0] <= (offset + fold_amount - 1) // BLOCK, to_keys, keep_state, running
    )
    grad_qkv_rows = jnp.concatenate(
        [
            grad_query.reshape(local_rows, model_width),
            grad_key.reshape(local_rows, model_width),
            grad_value.reshape(local_rows, model_width),
        ],
        axis=1,
    ).astype(jnp.bfloat16)
    grad_qkv = jnp.einsum(
        "rd,re->de", normed_low, grad_qkv_rows, preferred_element_type=jnp.float32
    )
    grad_normed_attn = jnp.einsum(
        "re,de->rd", grad_qkv_rows, qkv_full, preferred_element_type=jnp.float32
    )
    grad_input_attn, attn_gain_grad = norm_backward(
        grad_normed_attn, unit_attn, inverse_attn, gain_full.astype(jnp.float32)
    )
    grad_tokens = grad_resid + grad_input_attn
    expert_gain_grad = jnp.stack(gain_grads)[None]
    gain_share, qkv_share, out_share, centroid_share, expert_gain_share = (
        lax.psum_scatter(
            attn_gain_grad.astype(jnp.bfloat16), "dp", scatter_dimension=0, tiled=True
        ).astype(jnp.float32),
        lax.psum_scatter(
            grad_qkv.astype(jnp.bfloat16), "dp", scatter_dimension=0, tiled=True
        ).astype(jnp.float32),
        lax.psum_scatter(
            grad_out_weight.astype(jnp.bfloat16), "dp", scatter_dimension=0, tiled=True
        ).astype(jnp.float32),
        lax.psum_scatter(
            grad_centroid.astype(jnp.bfloat16), "dp", scatter_dimension=1, tiled=True
        ).astype(jnp.float32),
        lax.psum_scatter(
            expert_gain_grad.astype(jnp.bfloat16), "dp", scatter_dimension=2, tiled=True
        ).astype(jnp.float32),
    )
    gain_total, qkv_total, out_total, centroid_total = (
        lax.psum(gain_share.astype(jnp.bfloat16), "expert").astype(jnp.float32),
        lax.psum(qkv_share.astype(jnp.bfloat16), "expert").astype(jnp.float32),
        lax.psum(out_share.astype(jnp.bfloat16), "expert").astype(jnp.float32),
        lax.psum(centroid_share.astype(jnp.bfloat16), "expert").astype(jnp.float32),
    )
    grad_expert_in = jnp.stack(first_grads)[None]
    grad_expert_out = jnp.stack(second_grads)[None]
    return (
        block_out,
        grad_tokens,
        gain_total,
        qkv_total,
        out_total,
        centroid_total,
        expert_gain_share,
        grad_expert_in,
        grad_expert_out,
    )


def solution(mesh):
    in_specs = (
        P(("dp", "expert"), None),
        P("dp"),
        P("dp", None),
        P("dp", None),
        P(None, "dp"),
        P("expert", None, "dp"),
        P("expert", None, "dp", None),
        P("expert", None, "dp", None),
        P(("dp", "expert"), None),
        P(("dp", "expert"), None),
    )
    out_specs = (
        P(("dp", "expert"), None),
        P(("dp", "expert"), None),
        P("dp"),
        P("dp", None),
        P("dp", None),
        P(None, "dp"),
        P("expert", None, "dp"),
        P("expert", None, "dp", None),
        P("expert", None, "dp", None),
    )
    split = mesh.shape["dp"] == 4 and mesh.shape["expert"] == 8
    return jax.shard_map(
        on_device_split if split else on_device, mesh=mesh, in_specs=in_specs, out_specs=out_specs, check_vma=False
    )
```

```python
from functools import partial

import jax
import jax.numpy as jnp
from jax import lax
from jax.experimental import pallas as pl
from jax.experimental.pallas import tpu as pltpu
from jax.sharding import PartitionSpec as P

HEADS = 16
HEAD = 64
BLOCK = 256


EPS = 1e-05
NEGATIVE = -1e30
HIGH = lax.Precision.HIGHEST


def normalize(inputs, gain_row):
    centered = inputs - jnp.mean(inputs, axis=-1, keepdims=True)
    inverse = lax.rsqrt(jnp.mean(centered * centered, axis=-1, keepdims=True) + EPS)
    unit_rows = centered * inverse
    return (unit_rows, inverse, unit_rows * gain_row)


def norm_backward(grad_normed, unit_rows, inverse, gain_row):
    grad_unit = grad_normed * gain_row
    first_mean = jnp.mean(grad_unit, axis=-1, keepdims=True)
    second_mean = jnp.mean(grad_unit * unit_rows, axis=-1, keepdims=True)
    grad_input = inverse * (grad_unit - first_mean - unit_rows * second_mean)
    return (grad_input, jnp.sum(grad_normed * unit_rows, axis=0))


def split_heads(matrix):
    return matrix.reshape(matrix.shape[0], HEADS, HEAD)


def exact_gelu(inputs):
    return jax.nn.gelu(inputs, approximate=False)


def keep_state(current):
    return current


def row_product(left_rows, right_matrix, offset, amount):
    return jnp.dot(left_rows, right_matrix, preferred_element_type=jnp.float32)


def fetch_dense(norm_gain, qkv_weight, out_weight, centroids, expert_gain):
    return (
        lax.all_gather(norm_gain, "dp", axis=0, tiled=True),
        lax.all_gather(qkv_weight, "dp", axis=0, tiled=True),
        lax.all_gather(out_weight, "dp", axis=0, tiled=True),
        lax.all_gather(centroids, "dp", axis=1, tiled=True),
        lax.all_gather(expert_gain, "dp", axis=2, tiled=True),
    )


def spread_rows(rows_low):
    return lax.all_gather(rows_low, "dp", axis=0, tiled=True)


def sum_rows(term, amount):
    return lax.psum_scatter(
        term(jnp.int32(0), amount * lax.axis_size("dp")).astype(jnp.bfloat16),
        "dp",
        scatter_dimension=0,
        tiled=True,
    ).astype(jnp.float32)


def send_slots(rows_low, target, experts, capacity):
    buffer_rows = (
        jnp.zeros((experts * capacity, rows_low.shape[1]), rows_low.dtype).at[target].set(rows_low)
    )
    return buffer_rows.reshape(experts, capacity, rows_low.shape[1])


BF = jnp.bfloat16
F32 = jnp.float32
NT = (((1,), (1,)), ((), ()))
TN = (((0,), (0,)), ((), ()))
TILE = 256
MESH_ID = pl.DeviceIdType.MESH


def mean_last(v):
    return jnp.mean(v, axis=-1, keepdims=True)


def dp_peers():
    me = lax.axis_index("dp")
    sibling = me + 1 - 2 * lax.rem(me, 2)
    across = lax.rem(me + 2, 4)
    diagonal = lax.rem(sibling + 2, 4)
    return me, sibling, across, diagonal


def expert_peers():
    me = lax.axis_index("expert")
    z, x = me // 2, lax.rem(me, 2)
    beside = me + 1 - 2 * x
    near = z + 1 - 2 * lax.rem(z, 2)
    low, high = lax.rem(z, 2), z // 2
    inner = low + high - 2 * low * high
    flip, turn = 3 - z, lax.rem(z + 2, 4)
    second = inner * flip + (1 - inner) * turn
    third = inner * turn + (1 - inner) * flip
    return me, z, x, beside, (near, second, third)


def greet(targets):
    barrier = pltpu.get_barrier_semaphore()
    for target in targets:
        pl.semaphore_signal(barrier, inc=1, device_id=target, device_id_type=MESH_ID)
    pl.semaphore_wait(barrier, len(targets))


def others(n, me):
    return [lax.rem(me + d, n) for d in range(1, n)]


def push(src, dst, send, recv, target):
    return pltpu.make_async_remote_copy(
        src_ref=src, dst_ref=dst, send_sem=send, recv_sem=recv, device_id=target, device_id_type=MESH_ID
    )


class Spread:
    def __init__(self, own_src, slots, send, recv, chunks):
        self.me, self.z, self.x, self.beside, self.zs = expert_peers()
        self.own_src, self.slots, self.send, self.recv, self.chunks = own_src, slots, send, recv, chunks
        self.part = own_src.shape[0] // chunks

    def rows(self, c):
        return pl.ds(c * self.part, self.part)

    def own(self, way, c):
        peer = self.beside if way == 0 else 2 * (self.z + (1 if way == 1 else -1)) + self.x
        return push(
            self.own_src.at[self.rows(c)], self.slots.at[self.me, self.rows(c)],
            self.send.at[way * self.chunks + c], self.recv.at[self.me * self.chunks + c], {"expert": peer},
        )

    def slot(self, s, c, base, peer):
        block = self.slots.at[s, self.rows(c)]
        return push(block, block, self.send.at[base * self.chunks + c], self.recv.at[s * self.chunks + c], {"expert": peer})

    def own_all(self, act, chunks):
        for way in range(3):
            for c in chunks:
                if way == 0:
                    act(self.own(way, c))
                else:
                    @pl.when(self.z < 3 if way == 1 else self.z > 0)
                    def _():
                        act(self.own(way, c))

    def start(self):
        self.own_all(lambda cp: cp.start(), range(self.chunks))

    def start_chunk(self, c):
        self.own_all(lambda cp: cp.start(), (c,))

    def each(self, d, act):
        for sign in (-1, 1):
            zz = self.z + sign * d
            onward = self.z - sign

            @pl.when(jnp.logical_and(zz >= 0, zz <= 3))
            def _():
                s = 2 * zz + self.x
                for c in range(self.chunks):
                    act(s, zz, onward, c)

    def step(self, d):
        def act(s, zz, onward, c):
            self.slot(s, c, 0, self.beside).wait_recv()

            @pl.when(jnp.logical_and(onward >= 0, onward <= 3))
            def _():
                self.slot(s, c, 7 + zz, 2 * onward + self.x).start()

            self.slot(s, c, 3 + zz, self.beside).start()

        self.each(d, act)

    def wait_beside(self, zz):
        for c in range(self.chunks):
            self.slot(2 * zz + 1 - self.x, c, 0, self.beside).wait_recv()

    def drain(self):
        self.own_all(lambda cp: cp.wait_send(), range(self.chunks))

        def act(s, zz, onward, c):
            @pl.when(jnp.logical_and(onward >= 0, onward <= 3))
            def _():
                self.slot(s, c, 7 + zz, 2 * onward + self.x).wait_send()

            self.slot(s, c, 3 + zz, self.beside).wait_send()

        for d in (1, 2, 3):
            self.each(d, act)


class Weights:
    def __init__(self, src, first, rows, full, send, recv):
        self.j, self.sibling, self.across, self.diagonal = dp_peers()
        self.src, self.full, self.send, self.recv = src.at[pl.ds(first, rows)], full, send, recv

    def copy(self, kind):
        if kind == 2:
            block = self.full.at[self.across]
            return push(block, block, self.send.at[2], self.recv.at[self.across], {"dp": self.sibling})
        peer = self.sibling if kind == 0 else self.across
        return push(self.src, self.full.at[self.j], self.send.at[kind], self.recv.at[self.j], {"dp": peer})

    def start(self):
        self.copy(1).start()
        self.copy(0).start()

    def arrival(self, s):
        return push(self.src, self.full.at[s], self.send.at[0], self.recv.at[s], {"dp": self.sibling})

    def relay(self):
        self.arrival(self.across).wait_recv()
        self.copy(2).start()

    def drain(self):
        self.arrival(self.sibling).wait_recv()
        self.arrival(self.diagonal).wait_recv()
        for kind in range(3):
            self.copy(kind).wait_send()


def lane_masks(rows):
    lane = lax.broadcasted_iota(jnp.int32, (rows, 128), 1)
    return lane < HEAD


def front_kernel(
    tok, norm_gain, expert_gain, centroids, wqkv, wout,
    olow, normed_out, qkv_out, mixed_out, wout_full, wfirst, lse_rows, gain_col, gains, cent_full,
    held, wblk, normed, qkv, mixed, mixed_low, gain, bounce, small, smalls,
    tok_send, tok_recv, w_send, w_recv, o_send, o_recv, copy_sem, q_send, q_recv,
):
    j, sibling, across, diagonal = dp_peers()
    e, z, x, beside, zs = expert_peers()
    rows, width = tok.shape
    shard = wqkv.shape[0]
    lanes = 128

    def mine(s):
        return pl.ds(pl.multiple_of(s * shard, shard), shard)

    mycols = pl.ds(pl.multiple_of(e * lanes, lanes), lanes)
    own_tok = pltpu.make_async_copy(tok, held.at[e], copy_sem.at[0])
    own_tok.start()
    own_w = [
        pltpu.make_async_copy(
            wqkv.at[:, pl.ds(pl.multiple_of(i * width + e * lanes, lanes), lanes)],
            wblk.at[mine(j), pl.ds(i * lanes, lanes)],
            copy_sem.at[1 + i],
        )
        for i in range(3)
    ]
    for cp in own_w:
        cp.start()
    own_out = pltpu.make_async_copy(wout, bounce, copy_sem.at[4])
    own_out.start()
    small[...] = jnp.concatenate(
        [norm_gain[...], expert_gain[0], jnp.zeros((5, shard), BF), centroids[...]], axis=0
    )
    smalls[j] = small[...]
    greet([{"expert": p} for p in others(8, e)] + [{"dp": p} for p in (sibling, across, diagonal)])

    toks = Spread(tok, held, tok_send, tok_recv, 2)
    toks.start()
    later = Weights(wqkv, 0, shard // 2, wfirst, q_send, q_recv)
    for cp in own_w:
        cp.wait()

    def w_copy(kind):
        if kind == 0:
            return push(wblk.at[mine(j)], wblk.at[mine(j)], w_send.at[0], w_recv.at[j], {"dp": sibling})
        if kind == 1:
            return push(wblk.at[mine(j)], wblk.at[mine(j)], w_send.at[1], w_recv.at[j], {"dp": across})
        return push(wblk.at[mine(across)], wblk.at[mine(across)], w_send.at[2], w_recv.at[across], {"dp": sibling})

    def w_arrival(s):
        return push(wblk.at[mine(s)], wblk.at[mine(s)], w_send.at[0], w_recv.at[s], {"dp": sibling})

    def s_copy(i):
        return push(small, smalls.at[j], w_send.at[3 + i], w_recv.at[4 + j], {"dp": (sibling, across, diagonal)[i]})

    def s_arrival(s):
        return push(small, smalls.at[s], w_send.at[3], w_recv.at[4 + s], {"dp": sibling})

    def out_copy(kind):
        if kind == 0:
            return push(wout, wout_full.at[mine(j)], w_send.at[6], w_recv.at[8 + j], {"dp": sibling})
        if kind == 1:
            return push(wout, wout_full.at[mine(j)], w_send.at[7], w_recv.at[8 + j], {"dp": across})
        return push(wout_full.at[mine(across)], wout_full.at[mine(across)], w_send.at[8], w_recv.at[8 + across], {"dp": sibling})

    def out_arrival(s):
        return push(wout, wout_full.at[mine(s)], w_send.at[6], w_recv.at[8 + s], {"dp": sibling})

    for i in range(3):
        s_copy(i).start()
    w_copy(1).start()
    w_copy(0).start()
    out_copy(1).start()
    out_copy(0).start()
    later.start()
    own_out.wait()
    keep_out = pltpu.make_async_copy(bounce, wout_full.at[mine(j)], copy_sem.at[4])
    keep_out.start()
    for s in (sibling, across, diagonal):
        s_arrival(s).wait_recv()
    for s in range(4):
        at = pl.ds(s * shard, shard)
        block = smalls[s].astype(F32)
        gain[:, at] = block[0:1]
        gain_col[s : s + 1, :] = block[0:1]
        gains[:, at] = block[1:3]
        cent_full[:, at] = smalls[s, 8:16, :]
    w_arrival(across).wait_recv()
    w_copy(2).start()
    w_arrival(sibling).wait_recv()
    w_arrival(diagonal).wait_recv()

    def project(zz):
        base = zz * 2 * rows
        for xx in range(2):
            def norm_rows(t, c):
                rs = pl.ds(pl.multiple_of(t * 64, 64), 64)
                v = held[2 * zz + xx, rs, :].astype(F32)
                center = v - mean_last(v)
                inverse = lax.rsqrt(mean_last(center * center) + EPS)
                at = pl.ds(pl.multiple_of(base + xx * rows + t * 64, 64), 64)
                normed[at, :] = (center * inverse * gain[...]).astype(BF)
                return c
            lax.fori_loop(0, rows // 64, norm_rows, 0)
        at = pl.ds(pl.multiple_of(base, 2 * rows), 2 * rows)
        qkv[at, :] = jnp.dot(normed[at, :], wblk[...], preferred_element_type=F32).astype(BF)

    own_tok.wait()
    toks.step(1)
    toks.wait_beside(z)
    project(z)
    toks.step(2)
    toks.wait_beside(zs[0])
    project(zs[0])
    toks.step(3)
    out_arrival(across).wait_recv()
    out_copy(2).start()
    toks.wait_beside(zs[1])
    project(zs[1])
    toks.wait_beside(zs[2])
    project(zs[2])
    stores = [
        pltpu.make_async_copy(normed, normed_out, copy_sem.at[0]),
        pltpu.make_async_copy(qkv, qkv_out, copy_sem.at[1]),
    ]
    for cp in stores:
        cp.start()

    def o_copy(dest):
        return push(mixed_low.at[pl.ds(dest * rows, rows)], olow.at[:, mycols], o_send.at[dest], o_recv.at[e], {"expert": dest})

    def o_own(dest):
        return pltpu.make_async_copy(mixed_low.at[pl.ds(dest * rows, rows)], olow.at[:, mycols], copy_sem.at[5])

    left = lane_masks(2 * rows)
    for b in (3, 2, 1, 0):
        qs = qkv[pl.ds(b * 2 * rows, 2 * rows), 0:lanes]
        keys = qkv[0 : (b + 1) * 2 * rows, lanes : 2 * lanes]
        vals = qkv[0 : (b + 1) * 2 * rows, 2 * lanes : 3 * lanes]
        outs, logs = [], []
        for h in range(2):
            mask = left if h == 0 else jnp.logical_not(left)
            q_h = jnp.where(mask, qs.astype(F32) * (HEAD ** -0.5), 0.0).astype(BF)
            sc = lax.dot_general(q_h, keys, NT, preferred_element_type=F32)
            top = jnp.max(sc, axis=-1, keepdims=True)
            pr = jnp.exp(sc - top)
            tot = jnp.sum(pr, axis=-1, keepdims=True)
            outs.append(jnp.dot(pr.astype(BF), vals, preferred_element_type=F32) / tot)
            logs.append(top + jnp.log(tot))
        at = pl.ds(b * 2 * rows, 2 * rows)
        res = jnp.where(left, outs[0], outs[1])
        mixed[at, :] = res
        mixed_low[at, :] = res.astype(BF)
        turned = jnp.where(left, logs[0], logs[1]).T
        lse_rows[0:1, at] = turned[0:1]
        lse_rows[1:2, at] = turned[HEAD : HEAD + 1]
        for dest in (2 * b, 2 * b + 1):
            @pl.when(dest != e)
            def _():
                o_copy(dest).start()

            @pl.when(dest == e)
            def _():
                o_own(dest).start()
    more = [
        pltpu.make_async_copy(mixed, mixed_out, copy_sem.at[2]),
    ]
    for cp in more:
        cp.start()
    for dest in range(8):
        @pl.when(dest != e)
        def _():
            push(mixed_low.at[pl.ds(0, rows)], olow.at[:, pl.ds(dest * lanes, lanes)], o_send.at[dest], o_recv.at[dest], {"expert": dest}).wait_recv()
            o_copy(dest).wait_send()

        @pl.when(dest == e)
        def _():
            o_own(dest).wait()
    later.relay()
    for s in (sibling, diagonal):
        out_arrival(s).wait_recv()
    toks.drain()
    later.drain()
    for i in range(3):
        w_copy(i).wait_send()
        s_copy(i).wait_send()
        out_copy(i).wait_send()
    keep_out.wait()
    for cp in stores + more:
        cp.wait()


def front_block(tokens, norm_gain, expert_gain, centroids, qkv_weight, out_weight):
    rows, width = tokens.shape
    seq = 8 * rows
    shard = qkv_weight.shape[0]
    any_spec = pl.BlockSpec(memory_space=pl.ANY)
    vmem_spec = pl.BlockSpec(memory_space=pltpu.VMEM)
    V = pltpu.VMEM
    D = pltpu.SemaphoreType.DMA
    S = jax.ShapeDtypeStruct
    return pl.pallas_call(
        front_kernel,
        out_shape=(
            S((rows, width), BF), S((seq, width), BF), S((seq, 384), BF), S((seq, 128), F32),
            S((width, width), BF), S((4, shard // 2, 3 * width), BF),
            S((2, seq), F32), S((4, shard), F32), S((2, width), F32), S((8, width), BF),
        ),
        in_specs=[any_spec, vmem_spec, vmem_spec, vmem_spec, any_spec, any_spec],
        out_specs=(any_spec,) * 6 + (vmem_spec,) * 4,
        scratch_shapes=[
            V((8, rows, width), BF), V((width, 384), BF), V((seq, width), BF), V((seq, 384), BF),
            V((seq, 128), F32), V((seq, 128), BF), V((1, width), F32), V((shard, width), BF),
            V((16, shard), BF), V((4, 16, shard), BF),
            D((22,)), D((16,)), D((9,)), D((12,)), D((8,)), D((8,)), D((8,)), D((3,)), D((4,)),
        ],
        compiler_params=pltpu.CompilerParams(collective_id=2, has_side_effects=True, vmem_limit_bytes=56 * 1024 * 1024),
        name="front_block",
    )(tokens, norm_gain, expert_gain, centroids, qkv_weight, out_weight)


def expert_kernel(
    zslots, dslots, olow, gain_ref, w1_hbm, w2_hbm,
    returned, came_back, olow_full, ggain_ref, n_out, h_out, df_out, du_out,
    w1, w2, x, hid, gpr, unit_s, inv_s, state, total, own, f1, rf1, ssum, rss,
    zland, dland, zfar, dfar, bsend, gsend, ggain, gland, olow_held,
    x_send, x_recv, f_send, f_recv, s_send, s_recv, l_send, l_recv,
    a_send, a_recv, g_send, g_recv, copy_sem, own_sem, e_send, e_recv,
):
    cap, width = zslots.shape[1:]
    quarter = 2 * cap
    pair = 2 * quarter
    chunk = 2 * pair
    tiles = width // TILE
    shard = width // 4
    j, sibling, across, diagonal = dp_peers()
    e, zpos, xpos, beside, zs = expert_peers()
    mine = pl.multiple_of((j // 2) * quarter, 16)
    theirs = pl.multiple_of((1 - j // 2) * quarter, 16)

    loads = []
    for i, (src, dst) in enumerate(
        [(w1_hbm.at[0, 0], w1.at[0]), (w2_hbm.at[0, 0], w2.at[0]),
         (w1_hbm.at[0, 1], w1.at[1]), (w2_hbm.at[0, 1], w2.at[1])]
    ):
        cp = pltpu.make_async_copy(src, dst, copy_sem.at[i])
        cp.start()
        loads.append(cp)
    zx = (zpos, zs[0], lax.rem(zpos + 2, 4), 3 - zpos)

    def peer_at(q):
        return 2 * zx[q // 2] + q % 2

    def seat(q):
        return 2 * (q // 2) + xpos

    greet([{"expert": p} for p in others(8, e)] + [{"dp": p} for p in (sibling, across, diagonal)])

    def swap(src, dst, which, q):
        peer = peer_at(q)
        if which < 2:
            return push(src.at[peer], dst.at[seat(q)], a_send.at[which * 8 + q], a_recv.at[which * 8 + seat(q)], {"expert": peer})
        return push(src.at[q], dst.at[e], a_send.at[which * 8 + q], a_recv.at[which * 8 + seat(q)], {"expert": peer})

    def swap_arrival(src, dst, which, q):
        peer = peer_at(q)
        if which < 2:
            return push(src.at[peer], dst.at[q], a_send.at[which * 8 + q], a_recv.at[which * 8 + q], {"expert": peer})
        return push(src.at[q], dst.at[peer], a_send.at[which * 8 + q], a_recv.at[which * 8 + q], {"expert": peer})

    def swap_own(src, dst, which):
        if which < 2:
            return pltpu.make_async_copy(src.at[e], dst.at[xpos], own_sem.at[which])
        return pltpu.make_async_copy(src.at[xpos], dst.at[e], own_sem.at[which])

    def for_places(c, act, here):
        for q in (2 * c, 2 * c + 1):
            if q >= 2:
                act(q)
            else:
                @pl.when(xpos != q)
                def _():
                    act(q)

                @pl.when(xpos == q)
                def _():
                    here()

    for which, (src, dst) in enumerate([(zslots, zland), (dslots, dland)]):
        for c in ((1, 2, 3, 0) if which == 0 else (3, 2, 1, 0)):
            for_places(c, lambda q: swap(src, dst, which, q).start(), lambda: swap_own(src, dst, which).start())
    olows = Spread(olow, olow_full, g_send, g_recv, 1)
    take_o = pltpu.make_async_copy(olow, olow_held, copy_sem.at[12])
    take_o.start()
    own_o = pltpu.make_async_copy(olow_held, olow_full.at[e], copy_sem.at[12])
    layer_of = (0, 1, 1, 0)
    order = [(p, c if p < 2 else 3 - c) for p in range(4) for c in range(4)]

    def place(p, c):
        return order.index((p, c)) % 4

    def my_half(c):
        return pl.ds(c * chunk, pair)

    def x_copy(p, c):
        q = 4 * p + c
        return push(x.at[p, my_half(c)], x.at[p, pl.ds(c * chunk + pair, pair)], x_send.at[q], x_recv.at[q], {"dp": sibling})

    def f_copy(q, cols):
        return push(f1.at[q, :, cols], rf1.at[q, :, cols], f_send.at[q], f_recv.at[q], {"dp": sibling})

    def s_copy(p, c, arrives=False):
        q = 4 * p + c
        if p in (0, 2):
            return push(ssum.at[q], rss.at[q], s_send.at[q], s_recv.at[q], {"dp": across})
        at = pl.ds(mine if arrives else theirs, quarter)
        return push(ssum.at[q, at], rss.at[q, at], s_send.at[q], s_recv.at[q], {"dp": across})

    def land_copy(which, c):
        src, dst = (zland, zfar) if which == 0 else (dland, dfar)
        at = pl.ds(2 * c, 2)
        return push(src.at[at], dst.at[at], l_send.at[4 * which + c], l_recv.at[4 * which + c], {"dp": across})

    def forward(which, c):
        src, dst = (zslots, zland) if which == 0 else (dslots, dland)
        for_places(c, lambda q: swap_arrival(src, dst, which, q).wait_recv(), lambda: swap_own(src, dst, which).wait())
        land_copy(which, c).start()

    def both(buf, c):
        return jnp.concatenate([buf[2 * c].astype(F32), buf[2 * c + 1].astype(F32)], axis=0)

    def by_rows(act):
        def step(t, carry):
            act(pl.multiple_of(t * 32, 32))
            return carry
        lax.fori_loop(0, pair // 32, step, 0)

    def norm_rows(p, c, read):
        def act(t):
            v = read(t)
            center = v - mean_last(v)
            inverse = lax.rsqrt(mean_last(center * center) + EPS)
            unit = center * inverse
            rs = pl.ds(c * pair + t, 32)
            unit_s[p, rs, :] = unit
            inv_s[p, rs, :] = jnp.broadcast_to(inverse, (32, 128))
            x[p, pl.ds(c * chunk + t, 32), :] = (unit * gain_ref[pl.ds(p, 1), :]).astype(BF)
        by_rows(act)
        x_copy(p, c).start()

    def begin(c):
        land_copy(0, c).wait_recv()
        state[pl.ds(c * pair + mine, quarter), :] = both(zland, c)
        state[pl.ds(c * pair + theirs, quarter), :] = both(zfar, c)
        norm_rows(0, c, lambda t: state[pl.ds(c * pair + t, 32), :])

    def begin_back(c):
        land_copy(1, c).wait_recv()
        x[2, pl.ds(c * chunk + mine, quarter), :] = both(dland, c).astype(BF)
        x[2, pl.ds(c * chunk + theirs, quarter), :] = both(dfar, c).astype(BF)
        x_copy(2, c).start()

    def up(p, c):
        k = layer_of[p]
        base = pl.ds(c * chunk, chunk)
        left_w = w1 if p < 2 else w2
        x_copy(p, c).wait_recv()

        def gelu(t, pre):
            cols = pl.ds(pl.multiple_of(t * TILE, TILE), TILE)
            cdf = 0.5 * (1.0 + lax.erf(pre * (0.5 ** 0.5)))
            pdf = jnp.exp(-0.5 * pre * pre) * 0.3989422804014327
            hid[k, base, cols] = (pre * cdf).astype(BF)
            gpr[k, base, cols] = cdf + pre * pdf

        def product(t):
            cols = pl.ds(pl.multiple_of(t * TILE, TILE), TILE)
            return lax.dot_general(x[p, base, :], left_w[k, cols, :], NT, preferred_element_type=F32)

        def step(t, carry):
            if p < 2:
                gelu(t, product(t))
            else:
                cols = pl.ds(pl.multiple_of(t * TILE, TILE), TILE)
                hid[2 + k, base, cols] = (product(t) * gpr[k, base, cols]).astype(BF)
            return carry

        lax.fori_loop(0, tiles, step, 0)

    def down(p, c):
        k = layer_of[p]
        base = pl.ds(c * chunk, chunk)
        right_w = w2 if p < 2 else w1
        q = 4 * p + c

        def step(t, carry):
            cols = pl.ds(pl.multiple_of(t * TILE, TILE), TILE)
            res = jnp.dot(hid[k if p < 2 else 2 + k, base, :], right_w[k, :, cols], preferred_element_type=F32)
            own[place(p, c), :, cols] = res[:pair]
            f1[q, :, cols] = res[pair:].astype(BF)
            f_copy(q, cols).start()
            return carry

        lax.fori_loop(0, tiles, step, 0)

    everything = pl.ds(0, width)

    def send_sum(p, c):
        q = 4 * p + c
        f_copy(q, everything).wait_recv()

        def act(t):
            rs = pl.ds(t, 32)
            v = own[place(p, c), rs, :] + rf1[q, rs, :].astype(F32)
            own[place(p, c), rs, :] = v
            ssum[q, rs, :] = v.astype(BF)
        by_rows(act)
        s_copy(p, c).start()

    def give_back(buf, dst, which, c, v):
        for i in range(2):
            buf[2 * c + i] = v[i * cap : (i + 1) * cap].astype(BF)
        for_places(c, lambda q: swap(buf, dst, which, q).start(), lambda: swap_own(buf, dst, which).start())

    def add_gain(k, c, part):
        if c == 3:
            ggain[pl.ds(k, 1), :] = part
        else:
            ggain[pl.ds(k, 1), :] = ggain[pl.ds(k, 1), :] + part

    def norm_back(k, got, rs):
        unit = unit_s[k, rs, :]
        a = got * gain_ref[pl.ds(k, 1), :]
        back = inv_s[k, rs, :][:, :1] * (a - mean_last(a) - unit * mean_last(a * unit))
        return back, jnp.sum(got * unit, axis=0, keepdims=True)

    def finish(p, c):
        k = layer_of[p]
        q = 4 * p + c
        s_copy(p, c, True).wait_recv()
        if p == 0:
            def read(t):
                rs = pl.ds(c * pair + t, 32)
                got = own[place(p, c), pl.ds(t, 32), :] + rss[q, pl.ds(t, 32), :].astype(F32)
                total[rs, :] = got
                return state[rs, :] + got
            norm_rows(1, c, read)
        elif p == 2:
            def step(i, part):
                t = pl.multiple_of(i * 32, 32)
                rs = pl.ds(c * pair + t, 32)
                got = own[place(p, c), pl.ds(t, 32), :] + rss[q, pl.ds(t, 32), :].astype(F32)
                back, add = norm_back(1, got, rs)
                state[rs, :] = back
                at = pl.ds(c * chunk + t, 32)
                x[3, at, :] = (x[2, at, :].astype(F32) + back).astype(BF)
                return part + add
            part = lax.fori_loop(0, pair // 32, step, jnp.zeros((1, width), F32))
            x_copy(3, c).start()
            add_gain(1, c, 0.5 * part)
        else:
            at = pl.ds(mine, quarter)
            rs = pl.ds(c * pair + mine, quarter)
            got = own[place(p, c), at, :] + rss[q, at, :].astype(F32)
            if p == 1:
                give_back(bsend, returned, 2, c, total[rs, :] + got)
            else:
                back, part = norm_back(0, got, rs)
                give_back(gsend, came_back, 3, c, state[rs, :] + back)
                add_gain(0, c, part)

    stores = []

    def store(i, src, dst):
        cp = pltpu.make_async_copy(src, dst, copy_sem.at[4 + i])
        cp.start()
        stores.append(cp)

    def gain_copy(i):
        s = (sibling, across, diagonal)[i]
        return push(ggain.at[:, pl.ds(pl.multiple_of(s * shard, shard), shard)], gland.at[j], e_send.at[i], e_recv.at[j], {"dp": s})

    forward(0, 0)
    forward(0, 1)
    begin(0)
    loads[0].wait()
    loads[1].wait()
    for t, (p, c) in enumerate(order):
        if t == 4:
            loads[2].wait()
            loads[3].wait()
        up(p, c)
        if t > 0:
            send_sum(*order[t - 1])
        if t < 2:
            forward(0, t + 2)
        down(p, c)
        if 2 <= t < 6:
            forward(1, 5 - t)
        if t < 3:
            begin(t + 1)
        if t >= 2:
            finish(*order[t - 2])
        if 5 <= t < 9:
            begin_back(8 - t)
        if t == 2:
            olows.start()
            take_o.wait()
            own_o.start()
        if t in (5, 8, 11):
            olows.step((t - 2) // 3)
        if t % 4 == 3:
            k = layer_of[p]
            if p < 2:
                store(p * 2, x.at[p], n_out.at[k])
                store(p * 2 + 1, hid.at[k], h_out.at[k])
            else:
                store(p * 2, x.at[p], df_out.at[k])
                store(p * 2 + 1, hid.at[2 + k], du_out.at[k])
    send_sum(*order[15])
    finish(*order[14])
    finish(*order[15])
    for i in range(3):
        gain_copy(i).start()
    gland[j] = ggain[:, pl.ds(pl.multiple_of(j * shard, shard), shard)]
    own_o.wait()
    for zz in range(4):
        olows.wait_beside(zz)
    olows.drain()
    for p in range(4):
        for c in range(4):
            x_copy(p, c).wait_send()
            f_copy(4 * p + c, everything).wait_send()
            s_copy(p, c).wait_send()
    for i in range(2):
        for c in range(4):
            land_copy(i, c).wait_send()
    for cp in stores:
        cp.wait()
    for i in range(3):
        push(ggain.at[:, pl.ds(0, shard)], gland.at[(sibling, across, diagonal)[i]], e_send.at[0], e_recv.at[(sibling, across, diagonal)[i]], {"dp": sibling}).wait_recv()
        gain_copy(i).wait_send()
    ggain_ref[...] = jnp.sum(gland[...], axis=0)
    for c in range(4):
        for which, (src, dst) in enumerate([(zslots, zland), (dslots, dland), (bsend, returned), (gsend, came_back)]):
            for_places(c, lambda q: swap(src, dst, which, q).wait_send(), lambda: None)
            if which >= 2:
                for_places(c, lambda q: swap_arrival(src, dst, which, q).wait_recv(), lambda: swap_own(src, dst, which).wait())


def expert_block(zslots, dslots, olow, gains, expert_in, expert_out):
    sources, cap, width = zslots.shape
    rows = sources * cap
    pair = 4 * cap
    hidden = expert_in.shape[2]
    everything = 4 * rows
    any_spec = pl.BlockSpec(memory_space=pl.ANY)
    vmem_spec = pl.BlockSpec(memory_space=pltpu.VMEM)
    S = jax.ShapeDtypeStruct
    big = S((2, everything, width), BF)
    V = pltpu.VMEM
    D = pltpu.SemaphoreType.DMA
    return pl.pallas_call(
        expert_kernel,
        out_shape=(
            S(zslots.shape, BF), S(zslots.shape, BF), S((8,) + olow.shape, BF), S((2, width // 4), F32),
            big, big, big, big,
        ),
        in_specs=[any_spec] * 3 + [vmem_spec] + [any_spec] * 2,
        out_specs=(any_spec, any_spec, any_spec, vmem_spec, any_spec, any_spec, any_spec, any_spec),
        scratch_shapes=[
            V((2, hidden, width), BF), V((2, hidden, width), BF),
            V((4, everything, width), BF), V((4, everything, hidden), BF), V((2, everything, hidden), F32),
            V((2, 2 * rows, width), F32), V((2, 2 * rows, 128), F32), V((2 * rows, width), F32), V((2 * rows, width), F32),
            V((4, pair, width), F32),
        ]
        + [V((16, pair, width), BF)] * 4
        + [V(zslots.shape, BF)] * 6
        + [V((2, width), F32), V((4, 2, width // 4), F32), V(olow.shape, BF)]
        + [D((16,))] * 6 + [D((8,))] * 2
        + [D((32,)), D((32,)), D((11,)), D((8,)), D((13,)), D((4,)), D((3,)), D((4,))],
        compiler_params=pltpu.CompilerParams(
            collective_id=1, has_side_effects=True, vmem_limit_bytes=62 * 1024 * 1024
        ),
        name="expert_block",
    )(zslots, dslots, olow, gains, expert_in, expert_out)


def back_kernel(
    gmix, gatt, qkv_hbm, mixed_hbm, lse_rows, normed_hbm, olow_hbm, cent, wqkv,
    dq_land, gq_land, go_land, gc_land, wsecond,
    dom, dam, qkv, mixed, normed, olow, delta, dq_acc, dqkv,
    part, f1, f3, ssum, rf1, rf3, rss, gq_own, go_own, cland, csum, cdp,
    h_send, h_recv, d_send, d_recv, p_send, p_recv, gq_send, gq_recv, go_send, go_recv, c_send, c_recv, copy_sem, q_send, q_recv,
):
    j, sibling, across, diagonal = dp_peers()
    e, zpos, xpos, beside, zs = expert_peers()
    rows, width = gmix.shape
    blk = 2 * rows
    lanes = 128
    shard = width // 4
    loads = [
        pltpu.make_async_copy(src, dst, copy_sem.at[i])
        for i, (src, dst) in enumerate([(qkv_hbm, qkv), (mixed_hbm, mixed), (olow_hbm, olow), (normed_hbm, normed)])
    ]
    for cp in loads:
        cp.start()
    peers = others(8, e)
    greet([{"expert": p} for p in peers] + [{"dp": p} for p in (sibling, across, diagonal)])

    def cols_of(s):
        return pl.ds(pl.multiple_of(s * lanes, lanes), lanes)

    def rows_of(s):
        return pl.ds(pl.multiple_of(s * rows, rows), rows)

    def head_copy(src, dst, which, dest):
        return push(src.at[:, cols_of(dest)], dst.at[rows_of(e)], h_send.at[which * 8 + dest], h_recv.at[which * 8 + e], {"expert": dest})

    def head_arrival(src, dst, which, source):
        return push(src.at[:, cols_of(source)], dst.at[rows_of(source)], h_send.at[which * 8 + source], h_recv.at[which * 8 + source], {"expert": source})

    for dest in peers:
        head_copy(gmix, dom, 0, dest).start()
    for dest in peers:
        head_copy(gatt, dam, 1, dest).start()
    for dest in peers:
        push(cent.at[dest], cland.at[e], c_send.at[dest], c_recv.at[e], {"expert": dest}).start()
    later = Weights(wqkv, shard // 2, shard // 2, wsecond, q_send, q_recv)
    later.start()
    dom[rows_of(e), :] = gmix[:, cols_of(e)]
    dam[rows_of(e), :] = gatt[:, cols_of(e)]
    cland[e] = cent[e]

    def dp_block(t, s):
        return part[pl.ds(max(t - 1, 0) * lanes, lanes), pl.ds(pl.multiple_of(s * shard, shard), shard)]

    def dp_copy(kind, t):
        if kind == 0:
            return push(f1.at[t], rf1.at[t], p_send.at[t * 3], p_recv.at[t * 3], {"dp": sibling})
        if kind == 1:
            return push(f3.at[t], rf3.at[t], p_send.at[t * 3 + 1], p_recv.at[t * 3 + 1], {"dp": sibling})
        return push(ssum.at[t], rss.at[t], p_send.at[t * 3 + 2], p_recv.at[t * 3 + 2], {"dp": across})

    def dp_sum_start(t):
        f3[t] = dp_block(t, diagonal).astype(BF)
        f1[t] = dp_block(t, sibling).astype(BF)
        dp_copy(1, t).start()
        dp_copy(0, t).start()

    def dp_sum_cross(t):
        dp_copy(1, t).wait_recv()
        ssum[t] = (dp_block(t, across) + rf3[t].astype(F32)).astype(BF)
        dp_copy(2, t).start()

    def dp_sum_end(t):
        dp_copy(0, t).wait_recv()
        dp_copy(2, t).wait_recv()
        return (dp_block(t, j) + rf1[t].astype(F32) + rss[t].astype(F32)).T.astype(BF)

    for cp in loads[:2]:
        cp.wait()
    for source in peers:
        head_arrival(gmix, dom, 0, source).wait_recv()
    left_row = lax.broadcasted_iota(jnp.int32, (8, 128), 1) < HEAD
    row_id = lax.broadcasted_iota(jnp.int32, (8, 128), 0)
    pick = jnp.where((row_id == 0) == left_row, 1.0, 0.0).astype(F32)
    delta[...] = lax.dot_general(pick, dom[...].astype(F32) * mixed[...], NT, precision=HIGH, preferred_element_type=F32)

    for source in peers:
        push(cent.at[source], cland.at[source], c_send.at[source], c_recv.at[source], {"expert": source}).wait_recv()
    csum[0] = jnp.sum(cland[...], axis=0)

    def c_copy(i):
        s = (sibling, across, diagonal)[i]
        return push(csum.at[0, :, pl.ds(pl.multiple_of(s * shard, shard), shard)], cdp.at[j], c_send.at[8 + i], c_recv.at[8 + j], {"dp": s})

    def c_arrival(s):
        return push(csum.at[0, :, pl.ds(0, shard)], cdp.at[s], c_send.at[8], c_recv.at[8 + s], {"dp": sibling})

    for i in range(3):
        c_copy(i).start()
    cdp[j] = csum[0, :, pl.ds(pl.multiple_of(j * shard, shard), shard)]

    left = lane_masks(blk)
    dq_acc[...] = jnp.zeros_like(dq_acc)

    def d_copy(dest):
        return push(dqkv.at[pl.ds(dest * rows, rows)], dq_land.at[e], d_send.at[dest], d_recv.at[e], {"expert": dest})

    for b in range(4):
        at = pl.ds(b * blk, blk)
        tail = pl.ds(b * blk, 8 * rows - b * blk)
        qs = qkv[tail, 0:lanes]
        dos = dom[tail, :]
        keys = qkv[at, lanes : 2 * lanes].astype(F32) * (HEAD ** -0.5)
        vals = qkv[at, 2 * lanes : 3 * lanes]
        dks, dvs = [], []
        for h in range(2):
            mask = left if h == 0 else jnp.logical_not(left)
            k_h = jnp.where(mask, keys, 0.0).astype(BF)
            v_h = jnp.where(mask, vals.astype(F32), 0.0).astype(BF)
            sc = lax.dot_general(k_h, qs, NT, preferred_element_type=F32)
            pr = jnp.exp(sc - lse_rows[h : h + 1, tail])
            dp = lax.dot_general(v_h, dos, NT, preferred_element_type=F32)
            ds = (pr * (dp - delta[h : h + 1, tail])).astype(BF)
            dvs.append(jnp.dot(pr.astype(BF), dos, preferred_element_type=F32))
            dks.append(jnp.dot(ds, qs, preferred_element_type=F32))
            dq_acc[tail, :] += lax.dot_general(ds, k_h, TN, preferred_element_type=F32)
        dqkv[at, 0:lanes] = dq_acc[at, :].astype(BF)
        dqkv[at, lanes : 2 * lanes] = (jnp.where(left, dks[0], dks[1]) * (HEAD ** -0.5)).astype(BF)
        dqkv[at, 2 * lanes : 3 * lanes] = jnp.where(left, dvs[0], dvs[1]).astype(BF)
        for dest in (2 * b, 2 * b + 1):
            @pl.when(dest != e)
            def _():
                d_copy(dest).start()

            @pl.when(dest == e)
            def _():
                pltpu.make_async_copy(dqkv.at[pl.ds(dest * rows, rows)], dq_land.at[dest], copy_sem.at[4]).start()
        if b == 0:
            loads[2].wait()
            for source in peers:
                head_arrival(gatt, dam, 1, source).wait_recv()
            part[0:lanes, :] = lax.dot_general(dam[...], olow[...], TN, preferred_element_type=F32)
            dp_sum_start(0)
            dp_sum_cross(0)
        if b == 1:
            go_own[...] = dp_sum_end(0)
            gos = Spread(go_own, go_land, go_send, go_recv, 1)
            gos.start()
            own_go = pltpu.make_async_copy(go_own, go_land.at[e], copy_sem.at[5])
            own_go.start()
            for s in (sibling, across, diagonal):
                c_arrival(s).wait_recv()
            csum[1, :, 0:shard] = jnp.sum(cdp[...], axis=0)
            for dest in peers:
                push(csum.at[1, :, pl.ds(0, shard)], gc_land.at[e], c_send.at[12 + dest], c_recv.at[12 + e], {"expert": dest}).start()
            own_gc = pltpu.make_async_copy(csum.at[1, :, pl.ds(0, shard)], gc_land.at[e], copy_sem.at[6])
            own_gc.start()
    loads[3].wait()
    gqs = Spread(gq_own, gq_land, gq_send, gq_recv, 3)
    for g in range(3):
        at = pl.ds(g * lanes, lanes)
        part[at, :] = lax.dot_general(dqkv[:, at], normed[...], TN, preferred_element_type=F32)
        dp_sum_start(g + 1)
        if g > 0:
            dp_sum_cross(g)
    dp_sum_cross(3)
    gos.step(1)
    for g in range(3):
        gq_own[pl.ds(g * shard, shard), :] = dp_sum_end(g + 1)
        gqs.start_chunk(g)
    own_gq = pltpu.make_async_copy(gq_own, gq_land.at[e], copy_sem.at[7])
    own_gq.start()
    gos.step(2)
    later.relay()
    gqs.step(1)
    gos.step(3)
    gqs.step(2)
    gqs.step(3)
    for zz in range(4):
        gos.wait_beside(zz)
        gqs.wait_beside(zz)
    gos.drain()
    gqs.drain()
    later.drain()
    for source in range(8):
        @pl.when(source != e)
        def _():
            push(dqkv.at[pl.ds(0, rows)], dq_land.at[source], d_send.at[source], d_recv.at[source], {"expert": source}).wait_recv()
            d_copy(source).wait_send()
            push(csum.at[1, :, pl.ds(0, shard)], gc_land.at[source], c_send.at[12 + source], c_recv.at[12 + source], {"expert": source}).wait()

        @pl.when(source == e)
        def _():
            pltpu.make_async_copy(dqkv.at[pl.ds(0, rows)], dq_land.at[source], copy_sem.at[4]).wait()
    for dest in peers:
        head_copy(gmix, dom, 0, dest).wait_send()
        head_copy(gatt, dam, 1, dest).wait_send()
        push(cent.at[dest], cland.at[e], c_send.at[dest], c_recv.at[e], {"expert": dest}).wait_send()
    for i in range(3):
        c_copy(i).wait_send()
        for t in range(4):
            dp_copy(i, t).wait_send()
    for cp in (own_go, own_gc, own_gq):
        cp.wait()


def back_block(gmix, gatt, qkv, mixed, lse_rows, normed, olow_full, cent, qkv_weight):
    rows, width = gmix.shape
    seq = 8 * rows
    shard = width // 4
    any_spec = pl.BlockSpec(memory_space=pl.ANY)
    vmem_spec = pl.BlockSpec(memory_space=pltpu.VMEM)
    S = jax.ShapeDtypeStruct
    V = pltpu.VMEM
    D = pltpu.SemaphoreType.DMA
    return pl.pallas_call(
        back_kernel,
        out_shape=(
            S((8, rows, 384), BF), S((8, 3 * shard, 128), BF), S((8, shard, 128), BF), S((8, 1, shard), F32),
            S((4, shard // 2, 3 * width), BF),
        ),
        in_specs=[vmem_spec, vmem_spec, any_spec, any_spec, vmem_spec, any_spec, any_spec, vmem_spec, any_spec],
        out_specs=(any_spec,) * 5,
        scratch_shapes=[
            V((seq, 128), BF), V((seq, 128), BF), V((seq, 384), BF), V((seq, 128), F32), V((seq, width), BF), V((seq, width), BF),
            V((8, seq), F32), V((seq, 128), F32), V((seq, 384), BF),
            V((384, width), F32),
        ]
        + [V((4, 128, shard), BF)] * 6
        + [
            V((3 * shard, 128), BF), V((shard, 128), BF), V((8, 1, width), F32), V((2, 1, width), F32), V((4, 1, shard), F32),
            D((16,)), D((16,)), D((8,)), D((8,)), D((12,)), D((12,)), D((33,)), D((24,)), D((11,)), D((8,)), D((20,)), D((20,)), D((9,)), D((3,)), D((4,)),
        ],
        compiler_params=pltpu.CompilerParams(collective_id=3, has_side_effects=True, vmem_limit_bytes=56 * 1024 * 1024),
        name="back_block",
    )(gmix, gatt, qkv, mixed, lse_rows, normed, olow_full, cent, qkv_weight)


def final_kernel(
    dq_hbm, wfirst, wsecond, tok_hbm, gain_col, gres_hbm, gq_hbm, go_hbm, wqkv_hbm, gc_land, gain_part,
    n_hbm, h_hbm, df_hbm, du_hbm,
    gtok_hbm, gqkv_hbm, gout_hbm, gnorm, gcent, ggain, gein, geout,
    n, h, df, du, tile_in, tile_out, dq_land, w, tok, gres, gq_land, go_land, wqkv,
    dqkv, dnorm, gtok, gqkv, gout, small_sum,
    load_sem, tile_sem, store_sem,
):
    rows, width = tok.shape
    shard = wqkv.shape[0]
    half = shard // 2
    tiles = width // TILE

    def load(i, src, dst):
        cp = pltpu.make_async_copy(src, dst, load_sem.at[i])
        cp.start()
        return cp

    pairs = []
    for i, (src, dst) in enumerate([(du_hbm, du), (n_hbm, n), (h_hbm, h), (df_hbm, df)]):
        pairs.append([load(2 * i + k, src.at[k], dst.at[k]) for k in range(2)])
    first = [load(8, dq_hbm, dq_land), load(9, gq_hbm, gq_land), load(10, go_hbm, go_land), load(11, wqkv_hbm, wqkv)]
    rest = [load(12, tok_hbm, tok), load(13, gres_hbm, gres)]
    me = lax.axis_index("dp")
    for i in range(1, 4):
        s = lax.rem(me + i, 4)
        rest.append(load(12 + 2 * i, wfirst.at[s], w.at[s, pl.ds(0, half)]))
        rest.append(load(13 + 2 * i, wsecond.at[s], w.at[s, pl.ds(half, half)]))
    rest.append(load(20, wqkv_hbm, w.at[me]))

    def tile_copy(stage, out, base, k, t):
        at = pl.ds(pl.multiple_of(t * TILE, TILE), TILE)
        return pltpu.make_async_copy(stage.at[k, at], out.at[k, at], tile_sem.at[(base + k) * tiles + t])

    for base, left, right, stage, out, waits in (
        (0, du, n, tile_in, gein, pairs[:2]), (2, h, df, tile_out, geout, pairs[2:]),
    ):
        for k in range(2):
            for pair in waits:
                pair[k].wait()

            def tile(t, c):
                at = pl.ds(pl.multiple_of(t * TILE, TILE), TILE)
                stage[k, at, :] = lax.dot_general(left[k, :, at], right[k], TN, preferred_element_type=F32)
                tile_copy(stage, out, base, k, t).start()
                return c

            lax.fori_loop(0, tiles, tile, 0)
    for cp in first:
        cp.wait()
    for s in range(8):
        for i in range(3):
            at = pl.ds(i * width + s * 128, 128)
            dqkv[:, at] = dq_land[s, :, pl.ds(i * 128, 128)]
            gqkv[:, at] = gq_land[s, pl.ds(i * shard, shard), :].astype(F32)
        gout[:, pl.ds(s * 128, 128)] = go_land[s].astype(F32)
    stores = [
        pltpu.make_async_copy(gqkv, gqkv_hbm, store_sem.at[0]),
        pltpu.make_async_copy(gout, gout_hbm, store_sem.at[1]),
    ]
    for cp in stores:
        cp.start()
    for cp in rest:
        cp.wait()
    for s in range(4):
        dnorm[:, pl.ds(s * shard, shard)] = lax.dot_general(dqkv[...], w[s], NT, preferred_element_type=F32)
    gain = jnp.concatenate([gain_col[s : s + 1, :] for s in range(4)], axis=1)

    def norm_rows(t, c):
        at = pl.ds(pl.multiple_of(t * 32, 32), 32)
        v = tok[at, :].astype(F32)
        center = v - mean_last(v)
        inverse = lax.rsqrt(mean_last(center * center) + EPS)
        unit = center * inverse
        a = dnorm[at, :] * gain
        gtok[at, :] = gres[at, :] + inverse * (a - mean_last(a) - unit * mean_last(a * unit))
        return c

    lax.fori_loop(0, rows // 32, norm_rows, 0)
    stores.append(pltpu.make_async_copy(gtok, gtok_hbm, store_sem.at[2]))
    stores[2].start()
    small_sum[...] = jnp.zeros_like(small_sum)

    def add(t, c):
        at = pl.ds(pl.multiple_of(t * 256, 256), 256)
        prod = gqkv[:, at] * wqkv[:, at].astype(F32)
        small_sum[...] += prod[:, :128] + prod[:, 128:]
        return c

    lax.fori_loop(0, 3 * width // 256, add, 0)
    own_gain = gain_col[pl.ds(me, 1), :]
    sums = lax.dot_general(jnp.ones((8, 128), F32), small_sum[...], NT, precision=HIGH, preferred_element_type=F32)
    gnorm[...] = sums[0:1] / own_gain
    for s in range(8):
        gcent[s : s + 1, :] = gc_land[s]
    ggain[...] = gain_part[...]
    for cp in stores:
        cp.wait()
    for k in range(2):
        for t in range(tiles):
            tile_copy(tile_in, gein, 0, k, t).wait()
            tile_copy(tile_out, geout, 2, k, t).wait()


def final_block(dq_land, wfirst, wsecond, tokens, gain_col, grad_resid, gq_land, go_land, qkv_weight, gc_land, gain_part, n, h, df, du):
    rows, width = tokens.shape
    shard = width // 4
    hidden = h.shape[2]
    any_spec = pl.BlockSpec(memory_space=pl.ANY)
    vmem_spec = pl.BlockSpec(memory_space=pltpu.VMEM)
    S = jax.ShapeDtypeStruct
    V = pltpu.VMEM
    D = pltpu.SemaphoreType.DMA
    return pl.pallas_call(
        final_kernel,
        out_shape=(
            S((rows, width), F32), S((shard, 3 * width), F32), S((shard, width), F32), S((1, shard), F32),
            S((8, shard), F32), S((2, shard), F32), S((2, hidden, width), F32), S((2, hidden, width), F32),
        ),
        in_specs=[any_spec] * 4 + [vmem_spec] + [any_spec] * 4 + [vmem_spec] * 2 + [any_spec] * 4,
        out_specs=(any_spec,) * 3 + (vmem_spec,) * 3 + (any_spec,) * 2,
        scratch_shapes=[V(n.shape, BF), V(h.shape, BF), V(df.shape, BF), V(du.shape, BF)]
        + [V((2, hidden, width), F32)] * 2
        + [
            V(dq_land.shape, BF), V((4, shard, 3 * width), BF), V((rows, width), BF), V((rows, width), F32),
            V(gq_land.shape, BF), V(go_land.shape, BF), V((shard, 3 * width), BF),
            V((rows, 3 * width), BF), V((rows, width), F32), V((rows, width), F32),
            V((shard, 3 * width), F32), V((shard, width), F32), V((shard, 128), F32),
            D((21,)), D((16,)), D((3,)),
        ],
        compiler_params=pltpu.CompilerParams(vmem_limit_bytes=58 * 1024 * 1024),
        name="final_block",
    )(dq_land, wfirst, wsecond, tokens, gain_col, grad_resid, gq_land, go_land, qkv_weight, gc_land, gain_part, n, h, df, du)


def on_device_split(
    tokens,
    norm_gain,
    qkv_weight,
    out_weight,
    centroids,
    expert_gain,
    expert_in,
    expert_out,
    routes,
    cotangent,
):
    rows, width = tokens.shape
    experts = lax.axis_size("expert")
    capacity = max(2, 3 * rows // (2 * experts))
    slots = experts * capacity
    shard = width // 4
    olow, normed_all, qkv, mixed, wout_full, wfirst, lse_rows, gain_col, gains, centroid_full = front_block(
        tokens, norm_gain[None], expert_gain, centroids, qkv_weight, out_weight
    )
    inputs = tokens.astype(F32)
    residual = inputs + jnp.dot(olow, wout_full, preferred_element_type=F32)
    route_ids = routes[:, 0]
    chosen = (route_ids[:, None] == jnp.arange(experts, dtype=jnp.int32)[None, :]).astype(BF)
    centroid_rows = jnp.dot(chosen, centroid_full, preferred_element_type=F32)
    gate = jax.nn.sigmoid(jnp.sum(residual * centroid_rows, axis=-1))
    before = jnp.tril(jnp.ones((rows, rows), BF), -1)
    rank = jnp.sum(jnp.dot(before, chosen, preferred_element_type=F32) * chosen.astype(F32), axis=-1)
    target = route_ids * capacity + rank.astype(jnp.int32)
    place = (jnp.arange(slots, dtype=jnp.int32)[:, None] == target[None, :]).astype(BF)
    grad_out = cotangent.astype(F32)
    sent = jnp.concatenate([residual.astype(BF), (gate[:, None] * grad_out).astype(BF)], axis=1)
    spread = jnp.dot(place, sent, preferred_element_type=F32).astype(BF)
    returned, came_back, olow_full, gain_part, n_rows, h_rows, df_rows, du_rows = expert_block(
        spread[:, :width].reshape(experts, capacity, width),
        spread[:, width:].reshape(experts, capacity, width),
        olow,
        gains,
        expert_in,
        expert_out,
    )
    branch_tok = lax.dot_general(place, returned.reshape(slots, width), TN, preferred_element_type=F32)
    block_out = (residual + gate[:, None] * branch_tok).astype(BF)
    grad_logit = jnp.sum(grad_out * branch_tok, axis=-1) * gate * (1.0 - gate)
    grad_centroid = jnp.dot(chosen.astype(F32).T, grad_logit[:, None] * residual, precision=HIGH)
    back_rows = lax.dot_general(place, came_back.reshape(slots, width), TN, preferred_element_type=F32)
    grad_resid = grad_out + grad_logit[:, None] * centroid_rows + back_rows
    grad_attended = grad_resid.astype(BF)
    grad_mixed = lax.dot_general(grad_attended, wout_full, NT, preferred_element_type=F32).astype(BF)
    dq_land, gq_land, go_land, gc_land, wsecond = back_block(
        grad_mixed, grad_attended, qkv, mixed, lse_rows, normed_all,
        olow_full.reshape(experts * rows, width), grad_centroid[:, None, :], qkv_weight,
    )
    grad_tokens, grad_qkv, grad_out_weight, grad_norm_gain, grad_centroids, grad_gain, grad_expert_in, grad_expert_out = final_block(
        dq_land, wfirst, wsecond, tokens, gain_col, grad_resid, gq_land, go_land, qkv_weight, gc_land, gain_part,
        n_rows, h_rows, df_rows, du_rows,
    )
    return (
        block_out,
        grad_tokens,
        grad_norm_gain[0],
        grad_qkv,
        grad_out_weight,
        grad_centroids,
        grad_gain[None],
        grad_expert_in[None],
        grad_expert_out[None],
    )


def on_device(
    tokens,
    norm_gain,
    qkv_weight,
    out_weight,
    centroids,
    expert_gain,
    expert_in,
    expert_out,
    routes,
    cotangent,
):
    model_width = tokens.shape[1]
    local_rows = tokens.shape[0]
    experts = lax.axis_size("expert")
    capacity = max(2, 3 * local_rows // (2 * experts))
    slot_total = experts * capacity
    first_pos = lax.axis_index("expert") * local_rows
    scale = HEAD ** (-0.5)
    gain_full, qkv_full, out_full, centroid_full, expert_gain_full = fetch_dense(
        norm_gain, qkv_weight, out_weight, centroids, expert_gain
    )
    inputs = tokens.astype(jnp.float32)
    unit_attn, inverse_attn, normed_attn = normalize(inputs, gain_full.astype(jnp.float32))
    normed_low = normed_attn.astype(jnp.bfloat16)
    projected = jnp.dot(normed_low, qkv_full, preferred_element_type=jnp.float32).astype(
        jnp.bfloat16
    )
    queries = projected[:, :model_width]
    keyset = projected[:, model_width : 2 * model_width]
    values = projected[:, 2 * model_width :]
    query_heads = split_heads(queries)
    key_heads = split_heads(keyset)
    value_heads = split_heads(values)
    query_block = (first_pos + jnp.arange(local_rows, dtype=jnp.int32)) // BLOCK
    last_block = (first_pos + local_rows - 1) // BLOCK
    start_state = (
        jnp.zeros((local_rows, HEADS, HEAD), jnp.float32),
        jnp.full((HEADS, local_rows), NEGATIVE, jnp.float32),
        jnp.zeros((HEADS, local_rows), jnp.float32),
    )
    key_piece = lax.all_gather(keyset, "expert", axis=0, tiled=True)
    value_piece = lax.all_gather(values, "expert", axis=0, tiled=True)
    amount = key_piece.shape[0]

    def update(current):
        accumulated, highest, totals = current
        scores = (
            jnp.einsum(
                "qhd,khd->hqk",
                query_heads,
                split_heads(key_piece),
                preferred_element_type=jnp.float32,
            )
            * scale
        )
        piece_block = jnp.arange(amount, dtype=jnp.int32) // BLOCK
        visible = (piece_block[None, :] <= query_block[:, None])[None]
        scores = jnp.where(visible, scores, NEGATIVE)
        new_high = jnp.maximum(highest, jnp.max(scores, axis=-1))
        factor = jnp.exp(highest - new_high)
        weights = jnp.where(visible, jnp.exp(scores - new_high[:, :, None]), 0.0)
        totals = jnp.sum(weights, axis=-1)
        accumulated = accumulated * factor.T[:, :, None] + jnp.einsum(
            "hqk,khd->qhd",
            weights.astype(jnp.bfloat16),
            split_heads(value_piece),
            preferred_element_type=jnp.float32,
        )
        return (accumulated, new_high, totals)

    accumulated, highest, totals = lax.cond(
        jnp.int32(0) // BLOCK <= last_block, update, keep_state, start_state
    )
    mixed_heads = accumulated / totals.T[:, :, None]
    log_total = (highest + jnp.log(totals)).T
    mixed_low = mixed_heads.reshape(local_rows, model_width).astype(jnp.bfloat16)
    residual = inputs + jnp.dot(mixed_low, out_full, preferred_element_type=jnp.float32)
    route_ids = routes[:, 0]
    chosen = route_ids[:, None] == jnp.arange(experts, dtype=jnp.int32)[None, :]
    centroid_rows = jnp.dot(
        chosen.astype(jnp.bfloat16), centroid_full, preferred_element_type=jnp.float32
    )
    gate_value = jax.nn.sigmoid(jnp.sum(residual * centroid_rows, axis=-1))
    chosen_int = chosen.astype(jnp.int32)
    slot_index = jnp.sum((jnp.cumsum(chosen_int, axis=0) - 1) * chosen_int, axis=-1)
    target = route_ids * capacity + slot_index
    arrived = lax.all_to_all(
        send_slots(residual.astype(jnp.bfloat16), target, experts, capacity),
        "expert",
        split_axis=0,
        concat_axis=0,
        tiled=True,
    )
    expert_state = arrived.reshape(slot_total, model_width).astype(jnp.float32)
    gains_here = expert_gain_full[0].astype(jnp.float32)
    total_change = jnp.zeros_like(expert_state)
    stored = []
    for sublayer in range(2):
        unit_rows, inverse, normed = normalize(expert_state, gains_here[sublayer])
        normed_rows = normed.astype(jnp.bfloat16)
        first_full, second_full = (expert_in[0, sublayer], expert_out[0, sublayer])
        left_rows = spread_rows(normed_rows)
        hidden_pre = jnp.einsum(
            "rd,fd->rf", left_rows, first_full, preferred_element_type=jnp.float32
        )
        hidden_act, slope_pull = jax.vjp(exact_gelu, hidden_pre)
        hidden_low = hidden_act.astype(jnp.bfloat16)
        change = sum_rows(partial(row_product, hidden_low, second_full), slot_total)
        expert_state = expert_state + change
        total_change = total_change + change
        stored.append((unit_rows, inverse, left_rows, hidden_low, slope_pull))
    branch_low = total_change.astype(jnp.bfloat16)
    returned = lax.all_to_all(
        branch_low.reshape(experts, capacity, model_width),
        "expert",
        split_axis=0,
        concat_axis=0,
        tiled=True,
    )
    branch_tok = returned.reshape(slot_total, model_width)[target].astype(jnp.float32)
    block_out = (residual + gate_value[:, None] * branch_tok).astype(jnp.bfloat16)
    gain_full, qkv_full, out_full, centroid_full, expert_gain_full = fetch_dense(
        norm_gain, qkv_weight, out_weight, centroids, expert_gain
    )
    gains_here = expert_gain_full[0].astype(jnp.float32)
    grad_out = cotangent.astype(jnp.float32)
    grad_logit = jnp.sum(grad_out * branch_tok, axis=-1) * gate_value * (1.0 - gate_value)
    grad_centroid = jnp.dot(
        chosen.astype(jnp.float32).T, grad_logit[:, None] * residual, precision=HIGH
    )
    grad_resid = grad_out + grad_logit[:, None] * centroid_rows
    grad_branch = (gate_value[:, None] * grad_out).astype(jnp.bfloat16)
    branch_grads = lax.all_to_all(
        send_slots(grad_branch, target, experts, capacity),
        "expert",
        split_axis=0,
        concat_axis=0,
        tiled=True,
    )
    grad_change = branch_grads.reshape(slot_total, model_width).astype(jnp.float32)
    grad_state = jnp.zeros_like(grad_change)
    gain_grads = [None, None]
    first_grads = [None, None]
    second_grads = [None, None]
    for sublayer in (1, 0):
        unit_rows, inverse, left_rows, hidden_low, slope_pull = stored[sublayer]
        grad_rows_low = (grad_change + grad_state).astype(jnp.bfloat16)
        first_full, second_full = (expert_in[0, sublayer], expert_out[0, sublayer])
        grad_rows = spread_rows(grad_rows_low)
        grad_hidden = jnp.einsum(
            "rd,fd->rf", grad_rows, second_full, preferred_element_type=jnp.float32
        )
        grad_pre = slope_pull(grad_hidden)[0].astype(jnp.bfloat16)
        grad_first = jnp.einsum(
            "rf,rd->fd", grad_pre, left_rows, preferred_element_type=jnp.float32
        )
        grad_second = jnp.einsum(
            "rf,rd->fd", hidden_low, grad_rows, preferred_element_type=jnp.float32
        )
        grad_normed = sum_rows(partial(row_product, grad_pre, first_full), slot_total)
        grad_input, gain_grad = norm_backward(grad_normed, unit_rows, inverse, gains_here[sublayer])
        grad_state = grad_state + grad_input
        gain_grads[sublayer] = gain_grad
        first_grads[sublayer] = grad_first
        second_grads[sublayer] = grad_second
    came_back = lax.all_to_all(
        grad_state.astype(jnp.bfloat16).reshape(experts, capacity, model_width),
        "expert",
        split_axis=0,
        concat_axis=0,
        tiled=True,
    )
    grad_resid = grad_resid + came_back.reshape(slot_total, model_width)[target].astype(jnp.float32)
    grad_attended = grad_resid.astype(jnp.bfloat16)
    grad_out_weight = jnp.einsum(
        "rd,re->de", mixed_low, grad_attended, preferred_element_type=jnp.float32
    )
    grad_mixed = jnp.einsum(
        "re,de->rd", grad_attended, out_full, preferred_element_type=jnp.float32
    ).astype(jnp.bfloat16)
    grad_heads = split_heads(grad_mixed)
    delta_rows = jnp.sum(grad_heads.astype(jnp.float32) * mixed_heads, axis=-1)
    zero_heads = jnp.zeros((local_rows, HEADS, HEAD), jnp.float32)
    running = (zero_heads, zero_heads, zero_heads)
    offset = jnp.int32(0)
    fold_key_piece = lax.all_gather(keyset, "expert", axis=0, tiled=True)
    fold_value_piece = lax.all_gather(values, "expert", axis=0, tiled=True)
    query_piece = lax.all_gather(queries, "expert", axis=0, tiled=True)
    grad_piece = lax.all_gather(grad_mixed, "expert", axis=0, tiled=True)
    log_piece = lax.all_gather(log_total.astype(jnp.bfloat16), "expert", axis=0, tiled=True).astype(
        jnp.float32
    )
    delta_piece = lax.all_gather(
        delta_rows.astype(jnp.bfloat16), "expert", axis=0, tiled=True
    ).astype(jnp.float32)
    fold_amount = fold_key_piece.shape[0]
    piece_block = jnp.arange(fold_amount, dtype=jnp.int32) // BLOCK

    def to_queries(current):
        grad_query, grad_key, grad_value = current
        piece_keys = split_heads(fold_key_piece)
        scores = (
            jnp.einsum("qhd,khd->hqk", query_heads, piece_keys, preferred_element_type=jnp.float32)
            * scale
        )
        visible = (piece_block[None, :] <= query_block[:, None])[None]
        weights = jnp.where(visible, jnp.exp(scores - log_total.T[:, :, None]), 0.0)
        grad_weights = jnp.einsum(
            "qhd,khd->hqk",
            grad_heads,
            split_heads(fold_value_piece),
            preferred_element_type=jnp.float32,
        )
        grad_scores = (weights * (grad_weights - delta_rows.T[:, :, None])).astype(jnp.bfloat16)
        grad_query = (
            jnp.einsum("hqk,khd->qhd", grad_scores, piece_keys, preferred_element_type=jnp.float32)
            * scale
        )
        return (grad_query, grad_key, grad_value)

    def to_keys(current):
        grad_query, grad_key, grad_value = current
        piece_queries = split_heads(query_piece)
        piece_grads = split_heads(grad_piece)
        scores = (
            jnp.einsum("qhd,khd->hqk", piece_queries, key_heads, preferred_element_type=jnp.float32)
            * scale
        )
        visible = (query_block[None, :] <= piece_block[:, None])[None]
        weights = jnp.where(visible, jnp.exp(scores - log_piece.T[:, :, None]), 0.0)
        grad_weights = jnp.einsum(
            "qhd,khd->hqk", piece_grads, value_heads, preferred_element_type=jnp.float32
        )
        grad_scores = (weights * (grad_weights - delta_piece.T[:, :, None])).astype(jnp.bfloat16)
        grad_key = (
            grad_key
            + jnp.einsum(
                "hqk,qhd->khd", grad_scores, piece_queries, preferred_element_type=jnp.float32
            )
            * scale
        )
        grad_value = grad_value + jnp.einsum(
            "hqk,qhd->khd",
            weights.astype(jnp.bfloat16),
            piece_grads,
            preferred_element_type=jnp.float32,
        )
        return (grad_query, grad_key, grad_value)

    running = lax.cond(offset // BLOCK <= last_block, to_queries, keep_state, running)
    grad_query, grad_key, grad_value = lax.cond(
        query_block[0] <= (offset + fold_amount - 1) // BLOCK, to_keys, keep_state, running
    )
    grad_qkv_rows = jnp.concatenate(
        [
            grad_query.reshape(local_rows, model_width),
            grad_key.reshape(local_rows, model_width),
            grad_value.reshape(local_rows, model_width),
        ],
        axis=1,
    ).astype(jnp.bfloat16)
    grad_qkv = jnp.einsum(
        "rd,re->de", normed_low, grad_qkv_rows, preferred_element_type=jnp.float32
    )
    grad_normed_attn = jnp.einsum(
        "re,de->rd", grad_qkv_rows, qkv_full, preferred_element_type=jnp.float32
    )
    grad_input_attn, attn_gain_grad = norm_backward(
        grad_normed_attn, unit_attn, inverse_attn, gain_full.astype(jnp.float32)
    )
    grad_tokens = grad_resid + grad_input_attn
    expert_gain_grad = jnp.stack(gain_grads)[None]
    gain_share, qkv_share, out_share, centroid_share, expert_gain_share = (
        lax.psum_scatter(
            attn_gain_grad.astype(jnp.bfloat16), "dp", scatter_dimension=0, tiled=True
        ).astype(jnp.float32),
        lax.psum_scatter(
            grad_qkv.astype(jnp.bfloat16), "dp", scatter_dimension=0, tiled=True
        ).astype(jnp.float32),
        lax.psum_scatter(
            grad_out_weight.astype(jnp.bfloat16), "dp", scatter_dimension=0, tiled=True
        ).astype(jnp.float32),
        lax.psum_scatter(
            grad_centroid.astype(jnp.bfloat16), "dp", scatter_dimension=1, tiled=True
        ).astype(jnp.float32),
        lax.psum_scatter(
            expert_gain_grad.astype(jnp.bfloat16), "dp", scatter_dimension=2, tiled=True
        ).astype(jnp.float32),
    )
    gain_total, qkv_total, out_total, centroid_total = (
        lax.psum(gain_share.astype(jnp.bfloat16), "expert").astype(jnp.float32),
        lax.psum(qkv_share.astype(jnp.bfloat16), "expert").astype(jnp.float32),
        lax.psum(out_share.astype(jnp.bfloat16), "expert").astype(jnp.float32),
        lax.psum(centroid_share.astype(jnp.bfloat16), "expert").astype(jnp.float32),
    )
    grad_expert_in = jnp.stack(first_grads)[None]
    grad_expert_out = jnp.stack(second_grads)[None]
    return (
        block_out,
        grad_tokens,
        gain_total,
        qkv_total,
        out_total,
        centroid_total,
        expert_gain_share,
        grad_expert_in,
        grad_expert_out,
    )


def solution(mesh):
    in_specs = (
        P(("dp", "expert"), None),
        P("dp"),
        P("dp", None),
        P("dp", None),
        P(None, "dp"),
        P("expert", None, "dp"),
        P("expert", None, "dp", None),
        P("expert", None, "dp", None),
        P(("dp", "expert"), None),
        P(("dp", "expert"), None),
    )
    out_specs = (
        P(("dp", "expert"), None),
        P(("dp", "expert"), None),
        P("dp"),
        P("dp", None),
        P("dp", None),
        P(None, "dp"),
        P("expert", None, "dp"),
        P("expert", None, "dp", None),
        P("expert", None, "dp", None),
    )
    split = mesh.shape["dp"] == 4 and mesh.shape["expert"] == 8
    return jax.shard_map(
        on_device_split if split else on_device, mesh=mesh, in_specs=in_specs, out_specs=out_specs, check_vma=False
    )
```

```python
from functools import partial

import jax
import jax.numpy as jnp
from jax import lax
from jax.experimental import pallas as pl
from jax.experimental.pallas import tpu as pltpu
from jax.sharding import PartitionSpec as P

HEADS = 16
HEAD = 64
BLOCK = 256


EPS = 1e-05
NEGATIVE = -1e30
HIGH = lax.Precision.HIGHEST


def normalize(inputs, gain_row):
    centered = inputs - jnp.mean(inputs, axis=-1, keepdims=True)
    inverse = lax.rsqrt(jnp.mean(centered * centered, axis=-1, keepdims=True) + EPS)
    unit_rows = centered * inverse
    return (unit_rows, inverse, unit_rows * gain_row)


def norm_backward(grad_normed, unit_rows, inverse, gain_row):
    grad_unit = grad_normed * gain_row
    first_mean = jnp.mean(grad_unit, axis=-1, keepdims=True)
    second_mean = jnp.mean(grad_unit * unit_rows, axis=-1, keepdims=True)
    grad_input = inverse * (grad_unit - first_mean - unit_rows * second_mean)
    return (grad_input, jnp.sum(grad_normed * unit_rows, axis=0))


def split_heads(matrix):
    return matrix.reshape(matrix.shape[0], HEADS, HEAD)


def exact_gelu(inputs):
    return jax.nn.gelu(inputs, approximate=False)


def keep_state(current):
    return current


def row_product(left_rows, right_matrix, offset, amount):
    return jnp.dot(left_rows, right_matrix, preferred_element_type=jnp.float32)


def fetch_dense(norm_gain, qkv_weight, out_weight, centroids, expert_gain):
    return (
        lax.all_gather(norm_gain, "dp", axis=0, tiled=True),
        lax.all_gather(qkv_weight, "dp", axis=0, tiled=True),
        lax.all_gather(out_weight, "dp", axis=0, tiled=True),
        lax.all_gather(centroids, "dp", axis=1, tiled=True),
        lax.all_gather(expert_gain, "dp", axis=2, tiled=True),
    )


def spread_rows(rows_low):
    return lax.all_gather(rows_low, "dp", axis=0, tiled=True)


def sum_rows(term, amount):
    return lax.psum_scatter(
        term(jnp.int32(0), amount * lax.axis_size("dp")).astype(jnp.bfloat16),
        "dp",
        scatter_dimension=0,
        tiled=True,
    ).astype(jnp.float32)


def send_slots(rows_low, target, experts, capacity):
    buffer_rows = (
        jnp.zeros((experts * capacity, rows_low.shape[1]), rows_low.dtype).at[target].set(rows_low)
    )
    return buffer_rows.reshape(experts, capacity, rows_low.shape[1])


BF = jnp.bfloat16
F32 = jnp.float32
NT = (((1,), (1,)), ((), ()))
TN = (((0,), (0,)), ((), ()))
TILE = 256
MESH_ID = pl.DeviceIdType.MESH


def mean_last(v):
    return jnp.mean(v, axis=-1, keepdims=True)


def dp_peers():
    me = lax.axis_index("dp")
    sibling = me + 1 - 2 * lax.rem(me, 2)
    across = lax.rem(me + 2, 4)
    diagonal = lax.rem(sibling + 2, 4)
    return me, sibling, across, diagonal


def expert_peers():
    me = lax.axis_index("expert")
    z, x = me // 2, lax.rem(me, 2)
    beside = me + 1 - 2 * x
    near = z + 1 - 2 * lax.rem(z, 2)
    low, high = lax.rem(z, 2), z // 2
    inner = low + high - 2 * low * high
    flip, turn = 3 - z, lax.rem(z + 2, 4)
    second = inner * flip + (1 - inner) * turn
    third = inner * turn + (1 - inner) * flip
    return me, z, x, beside, (near, second, third)


def greet(targets):
    barrier = pltpu.get_barrier_semaphore()
    for target in targets:
        pl.semaphore_signal(barrier, inc=1, device_id=target, device_id_type=MESH_ID)
    pl.semaphore_wait(barrier, len(targets))


def others(n, me):
    return [lax.rem(me + d, n) for d in range(1, n)]


def push(src, dst, send, recv, target):
    return pltpu.make_async_remote_copy(
        src_ref=src, dst_ref=dst, send_sem=send, recv_sem=recv, device_id=target, device_id_type=MESH_ID
    )


class Spread:
    def __init__(self, own_src, slots, send, recv, chunks):
        self.me, self.z, self.x, self.beside, self.zs = expert_peers()
        self.own_src, self.slots, self.send, self.recv, self.chunks = own_src, slots, send, recv, chunks
        self.part = own_src.shape[0] // chunks

    def rows(self, c):
        return pl.ds(c * self.part, self.part)

    def own(self, way, c):
        peer = self.beside if way == 0 else 2 * (self.z + (1 if way == 1 else -1)) + self.x
        return push(
            self.own_src.at[self.rows(c)], self.slots.at[self.me, self.rows(c)],
            self.send.at[way * self.chunks + c], self.recv.at[self.me * self.chunks + c], {"expert": peer},
        )

    def slot(self, s, c, base, peer):
        block = self.slots.at[s, self.rows(c)]
        return push(block, block, self.send.at[base * self.chunks + c], self.recv.at[s * self.chunks + c], {"expert": peer})

    def own_all(self, act, chunks):
        for way in range(3):
            for c in chunks:
                if way == 0:
                    act(self.own(way, c))
                else:
                    @pl.when(self.z < 3 if way == 1 else self.z > 0)
                    def _():
                        act(self.own(way, c))

    def start(self):
        self.own_all(lambda cp: cp.start(), range(self.chunks))

    def start_chunk(self, c):
        self.own_all(lambda cp: cp.start(), (c,))

    def each(self, d, act):
        for sign in (-1, 1):
            zz = self.z + sign * d
            onward = self.z - sign

            @pl.when(jnp.logical_and(zz >= 0, zz <= 3))
            def _():
                s = 2 * zz + self.x
                for c in range(self.chunks):
                    act(s, zz, onward, c)

    def step(self, d):
        def act(s, zz, onward, c):
            self.slot(s, c, 0, self.beside).wait_recv()

            @pl.when(jnp.logical_and(onward >= 0, onward <= 3))
            def _():
                self.slot(s, c, 7 + zz, 2 * onward + self.x).start()

            self.slot(s, c, 3 + zz, self.beside).start()

        self.each(d, act)

    def wait_beside(self, zz):
        for c in range(self.chunks):
            self.slot(2 * zz + 1 - self.x, c, 0, self.beside).wait_recv()

    def drain(self):
        self.own_all(lambda cp: cp.wait_send(), range(self.chunks))

        def act(s, zz, onward, c):
            @pl.when(jnp.logical_and(onward >= 0, onward <= 3))
            def _():
                self.slot(s, c, 7 + zz, 2 * onward + self.x).wait_send()

            self.slot(s, c, 3 + zz, self.beside).wait_send()

        for d in (1, 2, 3):
            self.each(d, act)


class Weights:
    def __init__(self, src, first, rows, full, send, recv):
        self.j, self.sibling, self.across, self.diagonal = dp_peers()
        self.src, self.full, self.send, self.recv = src.at[pl.ds(first, rows)], full, send, recv

    def copy(self, kind):
        if kind == 2:
            block = self.full.at[self.across]
            return push(block, block, self.send.at[2], self.recv.at[self.across], {"dp": self.sibling})
        peer = self.sibling if kind == 0 else self.across
        return push(self.src, self.full.at[self.j], self.send.at[kind], self.recv.at[self.j], {"dp": peer})

    def start(self):
        self.copy(1).start()
        self.copy(0).start()

    def arrival(self, s):
        return push(self.src, self.full.at[s], self.send.at[0], self.recv.at[s], {"dp": self.sibling})

    def relay(self):
        self.arrival(self.across).wait_recv()
        self.copy(2).start()

    def drain(self):
        self.arrival(self.sibling).wait_recv()
        self.arrival(self.diagonal).wait_recv()
        for kind in range(3):
            self.copy(kind).wait_send()


def lane_masks(rows):
    lane = lax.broadcasted_iota(jnp.int32, (rows, 128), 1)
    return lane < HEAD


def front_kernel(
    tok, norm_gain, expert_gain, centroids, wqkv, wout,
    olow, normed_out, qkv_out, mixed_out, wout_full, wfirst, lse_rows, gain_col, gains, cent_full,
    held, wblk, normed, qkv, mixed, mixed_low, gain, bounce, small, smalls,
    tok_send, tok_recv, w_send, w_recv, o_send, o_recv, copy_sem, q_send, q_recv,
):
    j, sibling, across, diagonal = dp_peers()
    e, z, x, beside, zs = expert_peers()
    rows, width = tok.shape
    shard = wqkv.shape[0]
    lanes = 128

    def mine(s):
        return pl.ds(pl.multiple_of(s * shard, shard), shard)

    mycols = pl.ds(pl.multiple_of(e * lanes, lanes), lanes)
    own_tok = pltpu.make_async_copy(tok, held.at[e], copy_sem.at[0])
    own_tok.start()
    own_w = [
        pltpu.make_async_copy(
            wqkv.at[:, pl.ds(pl.multiple_of(i * width + e * lanes, lanes), lanes)],
            wblk.at[mine(j), pl.ds(i * lanes, lanes)],
            copy_sem.at[1 + i],
        )
        for i in range(3)
    ]
    for cp in own_w:
        cp.start()
    own_out = pltpu.make_async_copy(wout, bounce, copy_sem.at[4])
    own_out.start()
    small[...] = jnp.concatenate(
        [norm_gain[...], expert_gain[0], jnp.zeros((5, shard), BF), centroids[...]], axis=0
    )
    smalls[j] = small[...]
    greet([{"expert": p} for p in others(8, e)] + [{"dp": p} for p in (sibling, across, diagonal)])

    toks = Spread(tok, held, tok_send, tok_recv, 2)
    toks.start()
    later = Weights(wqkv, 0, shard // 2, wfirst, q_send, q_recv)
    for cp in own_w:
        cp.wait()

    def w_copy(kind):
        if kind == 0:
            return push(wblk.at[mine(j)], wblk.at[mine(j)], w_send.at[0], w_recv.at[j], {"dp": sibling})
        if kind == 1:
            return push(wblk.at[mine(j)], wblk.at[mine(j)], w_send.at[1], w_recv.at[j], {"dp": across})
        return push(wblk.at[mine(across)], wblk.at[mine(across)], w_send.at[2], w_recv.at[across], {"dp": sibling})

    def w_arrival(s):
        return push(wblk.at[mine(s)], wblk.at[mine(s)], w_send.at[0], w_recv.at[s], {"dp": sibling})

    def s_copy(i):
        return push(small, smalls.at[j], w_send.at[3 + i], w_recv.at[4 + j], {"dp": (sibling, across, diagonal)[i]})

    def s_arrival(s):
        return push(small, smalls.at[s], w_send.at[3], w_recv.at[4 + s], {"dp": sibling})

    def out_copy(kind):
        if kind == 0:
            return push(wout, wout_full.at[mine(j)], w_send.at[6], w_recv.at[8 + j], {"dp": sibling})
        if kind == 1:
            return push(wout, wout_full.at[mine(j)], w_send.at[7], w_recv.at[8 + j], {"dp": across})
        return push(wout_full.at[mine(across)], wout_full.at[mine(across)], w_send.at[8], w_recv.at[8 + across], {"dp": sibling})

    def out_arrival(s):
        return push(wout, wout_full.at[mine(s)], w_send.at[6], w_recv.at[8 + s], {"dp": sibling})

    for i in range(3):
        s_copy(i).start()
    w_copy(1).start()
    w_copy(0).start()
    out_copy(1).start()
    out_copy(0).start()
    later.start()
    own_out.wait()
    keep_out = pltpu.make_async_copy(bounce, wout_full.at[mine(j)], copy_sem.at[4])
    keep_out.start()
    for s in (sibling, across, diagonal):
        s_arrival(s).wait_recv()
    for s in range(4):
        at = pl.ds(s * shard, shard)
        block = smalls[s].astype(F32)
        gain[:, at] = block[0:1]
        gain_col[s : s + 1, :] = block[0:1]
        gains[:, at] = block[1:3]
        cent_full[:, at] = smalls[s, 8:16, :]
    w_arrival(across).wait_recv()
    w_copy(2).start()
    w_arrival(sibling).wait_recv()
    w_arrival(diagonal).wait_recv()

    def project(zz):
        base = zz * 2 * rows
        for xx in range(2):
            def norm_rows(t, c):
                rs = pl.ds(pl.multiple_of(t * 64, 64), 64)
                v = held[2 * zz + xx, rs, :].astype(F32)
                center = v - mean_last(v)
                inverse = lax.rsqrt(mean_last(center * center) + EPS)
                at = pl.ds(pl.multiple_of(base + xx * rows + t * 64, 64), 64)
                normed[at, :] = (center * inverse * gain[...]).astype(BF)
                return c
            lax.fori_loop(0, rows // 64, norm_rows, 0)
        at = pl.ds(pl.multiple_of(base, 2 * rows), 2 * rows)
        qkv[at, :] = jnp.dot(normed[at, :], wblk[...], preferred_element_type=F32).astype(BF)

    own_tok.wait()
    toks.step(1)
    toks.wait_beside(z)
    project(z)
    toks.step(2)
    toks.wait_beside(zs[0])
    project(zs[0])
    toks.step(3)
    out_arrival(across).wait_recv()
    out_copy(2).start()
    toks.wait_beside(zs[1])
    project(zs[1])
    toks.wait_beside(zs[2])
    project(zs[2])
    stores = [
        pltpu.make_async_copy(normed, normed_out, copy_sem.at[0]),
        pltpu.make_async_copy(qkv, qkv_out, copy_sem.at[1]),
    ]
    for cp in stores:
        cp.start()

    def o_copy(dest):
        return push(mixed_low.at[pl.ds(dest * rows, rows)], olow.at[:, mycols], o_send.at[dest], o_recv.at[e], {"expert": dest})

    def o_own(dest):
        return pltpu.make_async_copy(mixed_low.at[pl.ds(dest * rows, rows)], olow.at[:, mycols], copy_sem.at[5])

    left = lane_masks(2 * rows)
    for b in (3, 2, 1, 0):
        qs = qkv[pl.ds(b * 2 * rows, 2 * rows), 0:lanes]
        keys = qkv[0 : (b + 1) * 2 * rows, lanes : 2 * lanes]
        vals = qkv[0 : (b + 1) * 2 * rows, 2 * lanes : 3 * lanes]
        outs, logs = [], []
        for h in range(2):
            mask = left if h == 0 else jnp.logical_not(left)
            q_h = jnp.where(mask, qs.astype(F32) * (HEAD ** -0.5), 0.0).astype(BF)
            sc = lax.dot_general(q_h, keys, NT, preferred_element_type=F32)
            top = jnp.max(sc, axis=-1, keepdims=True)
            pr = jnp.exp(sc - top)
            tot = jnp.sum(pr, axis=-1, keepdims=True)
            outs.append(jnp.dot(pr.astype(BF), vals, preferred_element_type=F32) / tot)
            logs.append(top + jnp.log(tot))
        at = pl.ds(b * 2 * rows, 2 * rows)
        res = jnp.where(left, outs[0], outs[1])
        mixed[at, :] = res
        mixed_low[at, :] = res.astype(BF)
        turned = jnp.where(left, logs[0], logs[1]).T
        lse_rows[0:1, at] = turned[0:1]
        lse_rows[1:2, at] = turned[HEAD : HEAD + 1]
        for dest in (2 * b, 2 * b + 1):
            @pl.when(dest != e)
            def _():
                o_copy(dest).start()

            @pl.when(dest == e)
            def _():
                o_own(dest).start()
    more = [
        pltpu.make_async_copy(mixed, mixed_out, copy_sem.at[2]),
    ]
    for cp in more:
        cp.start()
    for dest in range(8):
        @pl.when(dest != e)
        def _():
            push(mixed_low.at[pl.ds(0, rows)], olow.at[:, pl.ds(dest * lanes, lanes)], o_send.at[dest], o_recv.at[dest], {"expert": dest}).wait_recv()
            o_copy(dest).wait_send()

        @pl.when(dest == e)
        def _():
            o_own(dest).wait()
    later.relay()
    for s in (sibling, diagonal):
        out_arrival(s).wait_recv()
    toks.drain()
    later.drain()
    for i in range(3):
        w_copy(i).wait_send()
        s_copy(i).wait_send()
        out_copy(i).wait_send()
    keep_out.wait()
    for cp in stores + more:
        cp.wait()


def front_block(tokens, norm_gain, expert_gain, centroids, qkv_weight, out_weight):
    rows, width = tokens.shape
    seq = 8 * rows
    shard = qkv_weight.shape[0]
    any_spec = pl.BlockSpec(memory_space=pl.ANY)
    vmem_spec = pl.BlockSpec(memory_space=pltpu.VMEM)
    V = pltpu.VMEM
    D = pltpu.SemaphoreType.DMA
    S = jax.ShapeDtypeStruct
    return pl.pallas_call(
        front_kernel,
        out_shape=(
            S((rows, width), BF), S((seq, width), BF), S((seq, 384), BF), S((seq, 128), F32),
            S((width, width), BF), S((4, shard // 2, 3 * width), BF),
            S((2, seq), F32), S((4, shard), F32), S((2, width), F32), S((8, width), BF),
        ),
        in_specs=[any_spec, vmem_spec, vmem_spec, vmem_spec, any_spec, any_spec],
        out_specs=(any_spec,) * 6 + (vmem_spec,) * 4,
        scratch_shapes=[
            V((8, rows, width), BF), V((width, 384), BF), V((seq, width), BF), V((seq, 384), BF),
            V((seq, 128), F32), V((seq, 128), BF), V((1, width), F32), V((shard, width), BF),
            V((16, shard), BF), V((4, 16, shard), BF),
            D((22,)), D((16,)), D((9,)), D((12,)), D((8,)), D((8,)), D((8,)), D((3,)), D((4,)),
        ],
        compiler_params=pltpu.CompilerParams(collective_id=2, has_side_effects=True, vmem_limit_bytes=56 * 1024 * 1024),
        name="front_block",
    )(tokens, norm_gain, expert_gain, centroids, qkv_weight, out_weight)


def expert_kernel(
    zslots, dslots, olow, gain_ref, w1_hbm, w2_hbm,
    returned, came_back, olow_full, ggain_ref, n_out, h_out, df_out, du_out,
    w1, w2, x, hid, gpr, unit_s, inv_s, state, total, own, f1, rf1, ssum, rss,
    zland, dland, zfar, dfar, bsend, gsend, ggain, gland, olow_held,
    x_send, x_recv, f_send, f_recv, s_send, s_recv, l_send, l_recv,
    a_send, a_recv, g_send, g_recv, copy_sem, own_sem, e_send, e_recv,
):
    cap, width = zslots.shape[1:]
    quarter = 2 * cap
    pair = 2 * quarter
    chunk = 2 * pair
    tiles = width // TILE
    shard = width // 4
    j, sibling, across, diagonal = dp_peers()
    e, zpos, xpos, beside, zs = expert_peers()
    mine = pl.multiple_of((j // 2) * quarter, 16)
    theirs = pl.multiple_of((1 - j // 2) * quarter, 16)

    loads = []
    for i, (src, dst) in enumerate(
        [(w1_hbm.at[0, 0], w1.at[0]), (w2_hbm.at[0, 0], w2.at[0]),
         (w1_hbm.at[0, 1], w1.at[1]), (w2_hbm.at[0, 1], w2.at[1])]
    ):
        cp = pltpu.make_async_copy(src, dst, copy_sem.at[i])
        cp.start()
        loads.append(cp)
    zx = (zpos, zs[0], lax.rem(zpos + 2, 4), 3 - zpos)

    def peer_at(q):
        return 2 * zx[q // 2] + q % 2

    def seat(q):
        return 2 * (q // 2) + xpos

    greet([{"expert": p} for p in others(8, e)] + [{"dp": p} for p in (sibling, across, diagonal)])

    def swap(src, dst, which, q):
        peer = peer_at(q)
        if which < 2:
            return push(src.at[peer], dst.at[seat(q)], a_send.at[which * 8 + q], a_recv.at[which * 8 + seat(q)], {"expert": peer})
        return push(src.at[q], dst.at[e], a_send.at[which * 8 + q], a_recv.at[which * 8 + seat(q)], {"expert": peer})

    def swap_arrival(src, dst, which, q):
        peer = peer_at(q)
        if which < 2:
            return push(src.at[peer], dst.at[q], a_send.at[which * 8 + q], a_recv.at[which * 8 + q], {"expert": peer})
        return push(src.at[q], dst.at[peer], a_send.at[which * 8 + q], a_recv.at[which * 8 + q], {"expert": peer})

    def swap_own(src, dst, which):
        if which < 2:
            return pltpu.make_async_copy(src.at[e], dst.at[xpos], own_sem.at[which])
        return pltpu.make_async_copy(src.at[xpos], dst.at[e], own_sem.at[which])

    def for_places(c, act, here):
        for q in (2 * c, 2 * c + 1):
            if q >= 2:
                act(q)
            else:
                @pl.when(xpos != q)
                def _():
                    act(q)

                @pl.when(xpos == q)
                def _():
                    here()

    for which, (src, dst) in enumerate([(zslots, zland), (dslots, dland)]):
        for c in ((1, 2, 3, 0) if which == 0 else (3, 2, 1, 0)):
            for_places(c, lambda q: swap(src, dst, which, q).start(), lambda: swap_own(src, dst, which).start())
    olows = Spread(olow, olow_full, g_send, g_recv, 1)
    take_o = pltpu.make_async_copy(olow, olow_held, copy_sem.at[12])
    take_o.start()
    own_o = pltpu.make_async_copy(olow_held, olow_full.at[e], copy_sem.at[12])
    layer_of = (0, 1, 1, 0)
    order = [(p, c if p < 2 else 3 - c) for p in range(4) for c in range(4)]

    def place(p, c):
        return order.index((p, c)) % 4

    def my_half(c):
        return pl.ds(c * chunk, pair)

    def x_copy(p, c):
        q = 4 * p + c
        return push(x.at[p, my_half(c)], x.at[p, pl.ds(c * chunk + pair, pair)], x_send.at[q], x_recv.at[q], {"dp": sibling})

    def f_copy(q, cols):
        return push(f1.at[q, :, cols], rf1.at[q, :, cols], f_send.at[q], f_recv.at[q], {"dp": sibling})

    def s_copy(p, c, arrives=False):
        q = 4 * p + c
        if p in (0, 2):
            return push(ssum.at[q], rss.at[q], s_send.at[q], s_recv.at[q], {"dp": across})
        at = pl.ds(mine if arrives else theirs, quarter)
        return push(ssum.at[q, at], rss.at[q, at], s_send.at[q], s_recv.at[q], {"dp": across})

    def land_copy(which, c):
        src, dst = (zland, zfar) if which == 0 else (dland, dfar)
        at = pl.ds(2 * c, 2)
        return push(src.at[at], dst.at[at], l_send.at[4 * which + c], l_recv.at[4 * which + c], {"dp": across})

    def forward(which, c):
        src, dst = (zslots, zland) if which == 0 else (dslots, dland)
        for_places(c, lambda q: swap_arrival(src, dst, which, q).wait_recv(), lambda: swap_own(src, dst, which).wait())
        land_copy(which, c).start()

    def both(buf, c):
        return jnp.concatenate([buf[2 * c].astype(F32), buf[2 * c + 1].astype(F32)], axis=0)

    def by_rows(act):
        def step(t, carry):
            act(pl.multiple_of(t * 32, 32))
            return carry
        lax.fori_loop(0, pair // 32, step, 0)

    def norm_rows(p, c, read):
        def act(t):
            v = read(t)
            center = v - mean_last(v)
            inverse = lax.rsqrt(mean_last(center * center) + EPS)
            unit = center * inverse
            rs = pl.ds(c * pair + t, 32)
            unit_s[p, rs, :] = unit
            inv_s[p, rs, :] = jnp.broadcast_to(inverse, (32, 128))
            x[p, pl.ds(c * chunk + t, 32), :] = (unit * gain_ref[pl.ds(p, 1), :]).astype(BF)
        by_rows(act)
        x_copy(p, c).start()

    def begin(c):
        land_copy(0, c).wait_recv()
        state[pl.ds(c * pair + mine, quarter), :] = both(zland, c)
        state[pl.ds(c * pair + theirs, quarter), :] = both(zfar, c)
        norm_rows(0, c, lambda t: state[pl.ds(c * pair + t, 32), :])

    def begin_back(c):
        land_copy(1, c).wait_recv()
        x[2, pl.ds(c * chunk + mine, quarter), :] = both(dland, c).astype(BF)
        x[2, pl.ds(c * chunk + theirs, quarter), :] = both(dfar, c).astype(BF)
        x_copy(2, c).start()

    def up(p, c):
        k = layer_of[p]
        base = pl.ds(c * chunk, chunk)
        left_w = w1 if p < 2 else w2
        x_copy(p, c).wait_recv()

        def gelu(t, pre):
            cols = pl.ds(pl.multiple_of(t * TILE, TILE), TILE)
            cdf = 0.5 * (1.0 + lax.erf(pre * (0.5 ** 0.5)))
            pdf = jnp.exp(-0.5 * pre * pre) * 0.3989422804014327
            hid[k, base, cols] = (pre * cdf).astype(BF)
            gpr[k, base, cols] = cdf + pre * pdf

        def product(t):
            cols = pl.ds(pl.multiple_of(t * TILE, TILE), TILE)
            return lax.dot_general(x[p, base, :], left_w[k, cols, :], NT, preferred_element_type=F32)

        def step(t, carry):
            if p < 2:
                gelu(t, product(t))
            else:
                cols = pl.ds(pl.multiple_of(t * TILE, TILE), TILE)
                hid[2 + k, base, cols] = (product(t) * gpr[k, base, cols]).astype(BF)
            return carry

        lax.fori_loop(0, tiles, step, 0)

    def down(p, c):
        k = layer_of[p]
        base = pl.ds(c * chunk, chunk)
        right_w = w2 if p < 2 else w1
        q = 4 * p + c

        def step(t, carry):
            cols = pl.ds(pl.multiple_of(t * TILE, TILE), TILE)
            res = jnp.dot(hid[k if p < 2 else 2 + k, base, :], right_w[k, :, cols], preferred_element_type=F32)
            own[place(p, c), :, cols] = res[:pair]
            f1[q, :, cols] = res[pair:].astype(BF)
            f_copy(q, cols).start()
            return carry

        lax.fori_loop(0, tiles, step, 0)

    everything = pl.ds(0, width)

    def send_sum(p, c):
        q = 4 * p + c
        f_copy(q, everything).wait_recv()

        def act(t):
            rs = pl.ds(t, 32)
            v = own[place(p, c), rs, :] + rf1[q, rs, :].astype(F32)
            own[place(p, c), rs, :] = v
            ssum[q, rs, :] = v.astype(BF)
        by_rows(act)
        s_copy(p, c).start()

    def give_back(buf, dst, which, c, v):
        for i in range(2):
            buf[2 * c + i] = v[i * cap : (i + 1) * cap].astype(BF)
        for_places(c, lambda q: swap(buf, dst, which, q).start(), lambda: swap_own(buf, dst, which).start())

    def add_gain(k, c, part):
        if c == 3:
            ggain[pl.ds(k, 1), :] = part
        else:
            ggain[pl.ds(k, 1), :] = ggain[pl.ds(k, 1), :] + part

    def norm_back(k, got, rs):
        unit = unit_s[k, rs, :]
        a = got * gain_ref[pl.ds(k, 1), :]
        back = inv_s[k, rs, :][:, :1] * (a - mean_last(a) - unit * mean_last(a * unit))
        return back, jnp.sum(got * unit, axis=0, keepdims=True)

    def finish(p, c):
        k = layer_of[p]
        q = 4 * p + c
        s_copy(p, c, True).wait_recv()
        if p == 0:
            def read(t):
                rs = pl.ds(c * pair + t, 32)
                got = own[place(p, c), pl.ds(t, 32), :] + rss[q, pl.ds(t, 32), :].astype(F32)
                total[rs, :] = got
                return state[rs, :] + got
            norm_rows(1, c, read)
        elif p == 2:
            def step(i, part):
                t = pl.multiple_of(i * 32, 32)
                rs = pl.ds(c * pair + t, 32)
                got = own[place(p, c), pl.ds(t, 32), :] + rss[q, pl.ds(t, 32), :].astype(F32)
                back, add = norm_back(1, got, rs)
                state[rs, :] = back
                at = pl.ds(c * chunk + t, 32)
                x[3, at, :] = (x[2, at, :].astype(F32) + back).astype(BF)
                return part + add
            part = lax.fori_loop(0, pair // 32, step, jnp.zeros((1, width), F32))
            x_copy(3, c).start()
            add_gain(1, c, 0.5 * part)
        else:
            at = pl.ds(mine, quarter)
            rs = pl.ds(c * pair + mine, quarter)
            got = own[place(p, c), at, :] + rss[q, at, :].astype(F32)
            if p == 1:
                give_back(bsend, returned, 2, c, total[rs, :] + got)
            else:
                back, part = norm_back(0, got, rs)
                give_back(gsend, came_back, 3, c, state[rs, :] + back)
                add_gain(0, c, part)

    stores = []

    def store(i, src, dst):
        cp = pltpu.make_async_copy(src, dst, copy_sem.at[4 + i])
        cp.start()
        stores.append(cp)

    def gain_copy(i):
        s = (sibling, across, diagonal)[i]
        return push(ggain.at[:, pl.ds(pl.multiple_of(s * shard, shard), shard)], gland.at[j], e_send.at[i], e_recv.at[j], {"dp": s})

    forward(0, 0)
    forward(0, 1)
    begin(0)
    loads[0].wait()
    loads[1].wait()
    for t, (p, c) in enumerate(order):
        if t == 4:
            loads[2].wait()
            loads[3].wait()
        up(p, c)
        if t > 0:
            send_sum(*order[t - 1])
        if t < 2:
            forward(0, t + 2)
        down(p, c)
        if 2 <= t < 6:
            forward(1, 5 - t)
        if t < 3:
            begin(t + 1)
        if t >= 2:
            finish(*order[t - 2])
        if 5 <= t < 9:
            begin_back(8 - t)
        if t == 2:
            olows.start()
            take_o.wait()
            own_o.start()
        if t in (5, 8, 11):
            olows.step((t - 2) // 3)
        if t % 4 == 3:
            k = layer_of[p]
            if p < 2:
                store(p * 2, x.at[p], n_out.at[k])
                store(p * 2 + 1, hid.at[k], h_out.at[k])
            else:
                store(p * 2, x.at[p], df_out.at[k])
                store(p * 2 + 1, hid.at[2 + k], du_out.at[k])
    send_sum(*order[15])
    finish(*order[14])
    finish(*order[15])
    for i in range(3):
        gain_copy(i).start()
    gland[j] = ggain[:, pl.ds(pl.multiple_of(j * shard, shard), shard)]
    own_o.wait()
    for zz in range(4):
        olows.wait_beside(zz)
    olows.drain()
    for p in range(4):
        for c in range(4):
            x_copy(p, c).wait_send()
            f_copy(4 * p + c, everything).wait_send()
            s_copy(p, c).wait_send()
    for i in range(2):
        for c in range(4):
            land_copy(i, c).wait_send()
    for cp in stores:
        cp.wait()
    for i in range(3):
        push(ggain.at[:, pl.ds(0, shard)], gland.at[(sibling, across, diagonal)[i]], e_send.at[0], e_recv.at[(sibling, across, diagonal)[i]], {"dp": sibling}).wait_recv()
        gain_copy(i).wait_send()
    ggain_ref[...] = jnp.sum(gland[...], axis=0)
    for c in range(4):
        for which, (src, dst) in enumerate([(zslots, zland), (dslots, dland), (bsend, returned), (gsend, came_back)]):
            for_places(c, lambda q: swap(src, dst, which, q).wait_send(), lambda: None)
            if which >= 2:
                for_places(c, lambda q: swap_arrival(src, dst, which, q).wait_recv(), lambda: swap_own(src, dst, which).wait())


def expert_block(zslots, dslots, olow, gains, expert_in, expert_out):
    sources, cap, width = zslots.shape
    rows = sources * cap
    pair = 4 * cap
    hidden = expert_in.shape[2]
    everything = 4 * rows
    any_spec = pl.BlockSpec(memory_space=pl.ANY)
    vmem_spec = pl.BlockSpec(memory_space=pltpu.VMEM)
    S = jax.ShapeDtypeStruct
    big = S((2, everything, width), BF)
    V = pltpu.VMEM
    D = pltpu.SemaphoreType.DMA
    return pl.pallas_call(
        expert_kernel,
        out_shape=(
            S(zslots.shape, BF), S(zslots.shape, BF), S((8,) + olow.shape, BF), S((2, width // 4), F32),
            big, big, big, big,
        ),
        in_specs=[any_spec] * 3 + [vmem_spec] + [any_spec] * 2,
        out_specs=(any_spec, any_spec, any_spec, vmem_spec, any_spec, any_spec, any_spec, any_spec),
        scratch_shapes=[
            V((2, hidden, width), BF), V((2, hidden, width), BF),
            V((4, everything, width), BF), V((4, everything, hidden), BF), V((2, everything, hidden), F32),
            V((2, 2 * rows, width), F32), V((2, 2 * rows, 128), F32), V((2 * rows, width), F32), V((2 * rows, width), F32),
            V((4, pair, width), F32),
        ]
        + [V((16, pair, width), BF)] * 4
        + [V(zslots.shape, BF)] * 6
        + [V((2, width), F32), V((4, 2, width // 4), F32), V(olow.shape, BF)]
        + [D((16,))] * 6 + [D((8,))] * 2
        + [D((32,)), D((32,)), D((11,)), D((8,)), D((13,)), D((4,)), D((3,)), D((4,))],
        compiler_params=pltpu.CompilerParams(
            collective_id=1, has_side_effects=True, vmem_limit_bytes=62 * 1024 * 1024
        ),
        name="expert_block",
    )(zslots, dslots, olow, gains, expert_in, expert_out)


def back_kernel(
    gmix, gatt, qkv_hbm, mixed_hbm, lse_rows, normed_hbm, olow_hbm, cent, wqkv, wfirst_hbm,
    dnorm_hbm, gq_land, go_land, gc_land,
    dom, dam, qkv, mixed, normed, olow, delta, dq_acc, dqkv,
    part, f1, f3, ssum, rf1, rf3, rss, gq_own, go_own, cland, csum, cdp,
    h_send, h_recv, d_send, d_recv, p_send, p_recv, gq_send, gq_recv, go_send, go_recv, c_send, c_recv, copy_sem, q_send, q_recv,
    dq_land, wfirst, wsecond, dq_rows, dnorm, n_sem,
):
    j, sibling, across, diagonal = dp_peers()
    e, zpos, xpos, beside, zs = expert_peers()
    rows, width = gmix.shape
    blk = 2 * rows
    lanes = 128
    shard = width // 4
    loads = [
        pltpu.make_async_copy(src, dst, copy_sem.at[i])
        for i, (src, dst) in enumerate([(qkv_hbm, qkv), (mixed_hbm, mixed), (olow_hbm, olow), (normed_hbm, normed)])
    ]
    for cp in loads:
        cp.start()
    half = shard // 2
    weights = [
        pltpu.make_async_copy(wqkv.at[pl.ds(0, half)], wfirst.at[j], n_sem.at[0]),
        pltpu.make_async_copy(wqkv.at[pl.ds(half, half)], wsecond.at[j], n_sem.at[1]),
    ]
    for i in range(1, 4):
        s = lax.rem(j + i, 4)
        weights.append(pltpu.make_async_copy(wfirst_hbm.at[s], wfirst.at[s], n_sem.at[1 + i]))
    for cp in weights:
        cp.start()
    peers = others(8, e)
    greet([{"expert": p} for p in peers] + [{"dp": p} for p in (sibling, across, diagonal)])

    def cols_of(s):
        return pl.ds(pl.multiple_of(s * lanes, lanes), lanes)

    def rows_of(s):
        return pl.ds(pl.multiple_of(s * rows, rows), rows)

    def head_copy(src, dst, which, dest):
        return push(src.at[:, cols_of(dest)], dst.at[rows_of(e)], h_send.at[which * 8 + dest], h_recv.at[which * 8 + e], {"expert": dest})

    def head_arrival(src, dst, which, source):
        return push(src.at[:, cols_of(source)], dst.at[rows_of(source)], h_send.at[which * 8 + source], h_recv.at[which * 8 + source], {"expert": source})

    for dest in peers:
        head_copy(gmix, dom, 0, dest).start()
    for dest in peers:
        head_copy(gatt, dam, 1, dest).start()
    for dest in peers:
        push(cent.at[dest], cland.at[e], c_send.at[dest], c_recv.at[e], {"expert": dest}).start()
    later = Weights(wqkv, shard // 2, shard // 2, wsecond, q_send, q_recv)
    later.start()
    dom[rows_of(e), :] = gmix[:, cols_of(e)]
    dam[rows_of(e), :] = gatt[:, cols_of(e)]
    cland[e] = cent[e]

    def dp_block(t, s):
        return part[pl.ds(max(t - 1, 0) * lanes, lanes), pl.ds(pl.multiple_of(s * shard, shard), shard)]

    def dp_copy(kind, t):
        if kind == 0:
            return push(f1.at[t], rf1.at[t], p_send.at[t * 3], p_recv.at[t * 3], {"dp": sibling})
        if kind == 1:
            return push(f3.at[t], rf3.at[t], p_send.at[t * 3 + 1], p_recv.at[t * 3 + 1], {"dp": sibling})
        return push(ssum.at[t], rss.at[t], p_send.at[t * 3 + 2], p_recv.at[t * 3 + 2], {"dp": across})

    def dp_sum_start(t):
        f3[t] = dp_block(t, diagonal).astype(BF)
        f1[t] = dp_block(t, sibling).astype(BF)
        dp_copy(1, t).start()
        dp_copy(0, t).start()

    def dp_sum_cross(t):
        dp_copy(1, t).wait_recv()
        ssum[t] = (dp_block(t, across) + rf3[t].astype(F32)).astype(BF)
        dp_copy(2, t).start()

    def dp_sum_end(t):
        dp_copy(0, t).wait_recv()
        dp_copy(2, t).wait_recv()
        return (dp_block(t, j) + rf1[t].astype(F32) + rss[t].astype(F32)).T.astype(BF)

    for cp in loads[:2]:
        cp.wait()
    for source in peers:
        head_arrival(gmix, dom, 0, source).wait_recv()
    left_row = lax.broadcasted_iota(jnp.int32, (8, 128), 1) < HEAD
    row_id = lax.broadcasted_iota(jnp.int32, (8, 128), 0)
    pick = jnp.where((row_id == 0) == left_row, 1.0, 0.0).astype(F32)
    delta[...] = lax.dot_general(pick, dom[...].astype(F32) * mixed[...], NT, precision=HIGH, preferred_element_type=F32)

    for source in peers:
        push(cent.at[source], cland.at[source], c_send.at[source], c_recv.at[source], {"expert": source}).wait_recv()
    csum[0] = jnp.sum(cland[...], axis=0)

    def c_copy(i):
        s = (sibling, across, diagonal)[i]
        return push(csum.at[0, :, pl.ds(pl.multiple_of(s * shard, shard), shard)], cdp.at[j], c_send.at[8 + i], c_recv.at[8 + j], {"dp": s})

    def c_arrival(s):
        return push(csum.at[0, :, pl.ds(0, shard)], cdp.at[s], c_send.at[8], c_recv.at[8 + s], {"dp": sibling})

    for i in range(3):
        c_copy(i).start()
    cdp[j] = csum[0, :, pl.ds(pl.multiple_of(j * shard, shard), shard)]

    left = lane_masks(blk)
    dq_acc[...] = jnp.zeros_like(dq_acc)

    def d_copy(dest):
        return push(dqkv.at[pl.ds(dest * rows, rows)], dq_land.at[e], d_send.at[dest], d_recv.at[e], {"expert": dest})

    for b in range(4):
        at = pl.ds(b * blk, blk)
        tail = pl.ds(b * blk, 8 * rows - b * blk)
        qs = qkv[tail, 0:lanes]
        dos = dom[tail, :]
        keys = qkv[at, lanes : 2 * lanes].astype(F32) * (HEAD ** -0.5)
        vals = qkv[at, 2 * lanes : 3 * lanes]
        dks, dvs = [], []
        for h in range(2):
            mask = left if h == 0 else jnp.logical_not(left)
            k_h = jnp.where(mask, keys, 0.0).astype(BF)
            v_h = jnp.where(mask, vals.astype(F32), 0.0).astype(BF)
            sc = lax.dot_general(k_h, qs, NT, preferred_element_type=F32)
            pr = jnp.exp(sc - lse_rows[h : h + 1, tail])
            dp = lax.dot_general(v_h, dos, NT, preferred_element_type=F32)
            ds = (pr * (dp - delta[h : h + 1, tail])).astype(BF)
            dvs.append(jnp.dot(pr.astype(BF), dos, preferred_element_type=F32))
            dks.append(jnp.dot(ds, qs, preferred_element_type=F32))
            dq_acc[tail, :] += lax.dot_general(ds, k_h, TN, preferred_element_type=F32)
        dqkv[at, 0:lanes] = dq_acc[at, :].astype(BF)
        dqkv[at, lanes : 2 * lanes] = (jnp.where(left, dks[0], dks[1]) * (HEAD ** -0.5)).astype(BF)
        dqkv[at, 2 * lanes : 3 * lanes] = jnp.where(left, dvs[0], dvs[1]).astype(BF)
        for dest in (2 * b, 2 * b + 1):
            @pl.when(dest != e)
            def _():
                d_copy(dest).start()

            @pl.when(dest == e)
            def _():
                dq_land[dest] = dqkv[pl.ds(dest * rows, rows), :]
        if b == 0:
            loads[2].wait()
            for source in peers:
                head_arrival(gatt, dam, 1, source).wait_recv()
            part[0:lanes, :] = lax.dot_general(dam[...], olow[...], TN, preferred_element_type=F32)
            dp_sum_start(0)
            dp_sum_cross(0)
        if b == 1:
            go_own[...] = dp_sum_end(0)
            gos = Spread(go_own, go_land, go_send, go_recv, 1)
            gos.start()
            own_go = pltpu.make_async_copy(go_own, go_land.at[e], copy_sem.at[5])
            own_go.start()
            for s in (sibling, across, diagonal):
                c_arrival(s).wait_recv()
            csum[1, :, 0:shard] = jnp.sum(cdp[...], axis=0)
            for dest in peers:
                push(csum.at[1, :, pl.ds(0, shard)], gc_land.at[e], c_send.at[12 + dest], c_recv.at[12 + e], {"expert": dest}).start()
            own_gc = pltpu.make_async_copy(csum.at[1, :, pl.ds(0, shard)], gc_land.at[e], copy_sem.at[6])
            own_gc.start()
    loads[3].wait()
    later.relay()
    gqs = Spread(gq_own, gq_land, gq_send, gq_recv, 3)
    for g in range(3):
        at = pl.ds(g * lanes, lanes)
        part[at, :] = lax.dot_general(dqkv[:, at], normed[...], TN, preferred_element_type=F32)
        dp_sum_start(g + 1)
        if g > 0:
            dp_sum_cross(g)
    dp_sum_cross(3)
    gos.step(1)
    for g in range(3):
        gq_own[pl.ds(g * shard, shard), :] = dp_sum_end(g + 1)
        gqs.start_chunk(g)
    own_gq = pltpu.make_async_copy(gq_own, gq_land.at[e], copy_sem.at[7])
    own_gq.start()
    gos.step(2)
    gqs.step(1)
    gos.step(3)
    later.drain()
    for cp in weights:
        cp.wait()
    for source in peers:
        push(dqkv.at[pl.ds(0, rows)], dq_land.at[source], d_send.at[source], d_recv.at[source], {"expert": source}).wait_recv()
    for s in range(8):
        for i in range(3):
            dq_rows[:, pl.ds(i * width + s * lanes, lanes)] = dq_land[s, :, pl.ds(i * lanes, lanes)]
    gqs.step(2)
    for s in range(4):
        for side, w in enumerate((wfirst, wsecond)):
            at = pl.ds(s * shard + side * half, half)
            dnorm[:, at] = lax.dot_general(dq_rows[...], w[s], NT, preferred_element_type=F32)
    own_dnorm = pltpu.make_async_copy(dnorm, dnorm_hbm, copy_sem.at[4])
    own_dnorm.start()
    gqs.step(3)
    for zz in range(4):
        gos.wait_beside(zz)
        gqs.wait_beside(zz)
    gos.drain()
    gqs.drain()
    own_dnorm.wait()
    for source in range(8):
        @pl.when(source != e)
        def _():
            d_copy(source).wait_send()
            push(csum.at[1, :, pl.ds(0, shard)], gc_land.at[source], c_send.at[12 + source], c_recv.at[12 + source], {"expert": source}).wait()

    for dest in peers:
        head_copy(gmix, dom, 0, dest).wait_send()
        head_copy(gatt, dam, 1, dest).wait_send()
        push(cent.at[dest], cland.at[e], c_send.at[dest], c_recv.at[e], {"expert": dest}).wait_send()
    for i in range(3):
        c_copy(i).wait_send()
        for t in range(4):
            dp_copy(i, t).wait_send()
    for cp in (own_go, own_gc, own_gq):
        cp.wait()


def back_block(gmix, gatt, qkv, mixed, lse_rows, normed, olow_full, cent, qkv_weight, wfirst):
    rows, width = gmix.shape
    seq = 8 * rows
    shard = width // 4
    any_spec = pl.BlockSpec(memory_space=pl.ANY)
    vmem_spec = pl.BlockSpec(memory_space=pltpu.VMEM)
    S = jax.ShapeDtypeStruct
    V = pltpu.VMEM
    D = pltpu.SemaphoreType.DMA
    return pl.pallas_call(
        back_kernel,
        out_shape=(
            S((rows, width), F32), S((8, 3 * shard, 128), BF), S((8, shard, 128), BF), S((8, 1, shard), F32),
        ),
        in_specs=[vmem_spec, vmem_spec, any_spec, any_spec, vmem_spec, any_spec, any_spec, vmem_spec, any_spec, any_spec],
        out_specs=(any_spec,) * 4,
        scratch_shapes=[
            V((seq, 128), BF), V((seq, 128), BF), V((seq, 384), BF), V((seq, 128), F32), V((seq, width), BF), V((seq, width), BF),
            V((8, seq), F32), V((seq, 128), F32), V((seq, 384), BF),
            V((384, width), F32),
        ]
        + [V((4, 128, shard), BF)] * 6
        + [
            V((3 * shard, 128), BF), V((shard, 128), BF), V((8, 1, width), F32), V((2, 1, width), F32), V((4, 1, shard), F32),
            D((16,)), D((16,)), D((8,)), D((8,)), D((12,)), D((12,)), D((33,)), D((24,)), D((11,)), D((8,)), D((20,)), D((20,)), D((9,)), D((3,)), D((4,)),
            V((8, rows, 384), BF), V((4, shard // 2, 3 * width), BF), V((4, shard // 2, 3 * width), BF),
            V((rows, 3 * width), BF), V((rows, width), F32), D((5,)),
        ],
        compiler_params=pltpu.CompilerParams(collective_id=3, has_side_effects=True, vmem_limit_bytes=56 * 1024 * 1024),
        name="back_block",
    )(gmix, gatt, qkv, mixed, lse_rows, normed, olow_full, cent, qkv_weight, wfirst)


def final_kernel(
    dnorm_hbm, tok_hbm, gain_col, gres_hbm, gq_hbm, go_hbm, wqkv_hbm, gc_land, gain_part,
    n_hbm, h_hbm, df_hbm, du_hbm,
    gtok_hbm, gqkv_hbm, gout_hbm, gnorm, gcent, ggain, gein, geout,
    n, h, df, du, tile_in, tile_out, dnorm, tok, gres, gq_land, go_land, wqkv,
    gtok, gqkv, gout, small_sum,
    load_sem, tile_sem, store_sem,
):
    rows, width = tok.shape
    shard = wqkv.shape[0]
    tiles = width // TILE

    def load(i, src, dst):
        cp = pltpu.make_async_copy(src, dst, load_sem.at[i])
        cp.start()
        return cp

    pairs = []
    for i, (src, dst) in enumerate([(du_hbm, du), (n_hbm, n), (h_hbm, h), (df_hbm, df)]):
        pairs.append([load(2 * i + k, src.at[k], dst.at[k]) for k in range(2)])
    first = [load(8, dnorm_hbm, dnorm), load(9, gq_hbm, gq_land), load(10, go_hbm, go_land), load(11, wqkv_hbm, wqkv)]
    rest = [load(12, tok_hbm, tok), load(13, gres_hbm, gres)]
    me = lax.axis_index("dp")

    def tile_copy(stage, out, base, k, t):
        at = pl.ds(pl.multiple_of(t * TILE, TILE), TILE)
        return pltpu.make_async_copy(stage.at[k, at], out.at[k, at], tile_sem.at[(base + k) * tiles + t])

    for base, left, right, stage, out, waits in (
        (0, du, n, tile_in, gein, pairs[:2]), (2, h, df, tile_out, geout, pairs[2:]),
    ):
        for k in range(2):
            for pair in waits:
                pair[k].wait()

            def tile(t, c):
                at = pl.ds(pl.multiple_of(t * TILE, TILE), TILE)
                stage[k, at, :] = lax.dot_general(left[k, :, at], right[k], TN, preferred_element_type=F32)
                tile_copy(stage, out, base, k, t).start()
                return c

            lax.fori_loop(0, tiles, tile, 0)
    for cp in first:
        cp.wait()
    for s in range(8):
        for i in range(3):
            at = pl.ds(i * width + s * 128, 128)
            gqkv[:, at] = gq_land[s, pl.ds(i * shard, shard), :].astype(F32)
        gout[:, pl.ds(s * 128, 128)] = go_land[s].astype(F32)
    stores = [
        pltpu.make_async_copy(gqkv, gqkv_hbm, store_sem.at[0]),
        pltpu.make_async_copy(gout, gout_hbm, store_sem.at[1]),
    ]
    for cp in stores:
        cp.start()
    for cp in rest:
        cp.wait()
    gain = jnp.concatenate([gain_col[s : s + 1, :] for s in range(4)], axis=1)

    def norm_rows(t, c):
        at = pl.ds(pl.multiple_of(t * 32, 32), 32)
        v = tok[at, :].astype(F32)
        center = v - mean_last(v)
        inverse = lax.rsqrt(mean_last(center * center) + EPS)
        unit = center * inverse
        a = dnorm[at, :] * gain
        gtok[at, :] = gres[at, :] + inverse * (a - mean_last(a) - unit * mean_last(a * unit))
        return c

    lax.fori_loop(0, rows // 32, norm_rows, 0)
    stores.append(pltpu.make_async_copy(gtok, gtok_hbm, store_sem.at[2]))
    stores[2].start()
    small_sum[...] = jnp.zeros_like(small_sum)

    def add(t, c):
        at = pl.ds(pl.multiple_of(t * 256, 256), 256)
        prod = gqkv[:, at] * wqkv[:, at].astype(F32)
        small_sum[...] += prod[:, :128] + prod[:, 128:]
        return c

    lax.fori_loop(0, 3 * width // 256, add, 0)
    own_gain = gain_col[pl.ds(me, 1), :]
    sums = lax.dot_general(jnp.ones((8, 128), F32), small_sum[...], NT, precision=HIGH, preferred_element_type=F32)
    gnorm[...] = sums[0:1] / own_gain
    for s in range(8):
        gcent[s : s + 1, :] = gc_land[s]
    ggain[...] = gain_part[...]
    for cp in stores:
        cp.wait()
    for k in range(2):
        for t in range(tiles):
            tile_copy(tile_in, gein, 0, k, t).wait()
            tile_copy(tile_out, geout, 2, k, t).wait()


def final_block(dnorm, tokens, gain_col, grad_resid, gq_land, go_land, qkv_weight, gc_land, gain_part, n, h, df, du):
    rows, width = tokens.shape
    shard = width // 4
    hidden = h.shape[2]
    any_spec = pl.BlockSpec(memory_space=pl.ANY)
    vmem_spec = pl.BlockSpec(memory_space=pltpu.VMEM)
    S = jax.ShapeDtypeStruct
    V = pltpu.VMEM
    D = pltpu.SemaphoreType.DMA
    return pl.pallas_call(
        final_kernel,
        out_shape=(
            S((rows, width), F32), S((shard, 3 * width), F32), S((shard, width), F32), S((1, shard), F32),
            S((8, shard), F32), S((2, shard), F32), S((2, hidden, width), F32), S((2, hidden, width), F32),
        ),
        in_specs=[any_spec] * 2 + [vmem_spec] + [any_spec] * 4 + [vmem_spec] * 2 + [any_spec] * 4,
        out_specs=(any_spec,) * 3 + (vmem_spec,) * 3 + (any_spec,) * 2,
        scratch_shapes=[V(n.shape, BF), V(h.shape, BF), V(df.shape, BF), V(du.shape, BF)]
        + [V((2, hidden, width), F32)] * 2
        + [
            V((rows, width), F32), V((rows, width), BF), V((rows, width), F32),
            V(gq_land.shape, BF), V(go_land.shape, BF), V((shard, 3 * width), BF),
            V((rows, width), F32),
            V((shard, 3 * width), F32), V((shard, width), F32), V((shard, 128), F32),
            D((14,)), D((16,)), D((3,)),
        ],
        compiler_params=pltpu.CompilerParams(vmem_limit_bytes=58 * 1024 * 1024),
        name="final_block",
    )(dnorm, tokens, gain_col, grad_resid, gq_land, go_land, qkv_weight, gc_land, gain_part, n, h, df, du)


def on_device_split(
    tokens,
    norm_gain,
    qkv_weight,
    out_weight,
    centroids,
    expert_gain,
    expert_in,
    expert_out,
    routes,
    cotangent,
):
    rows, width = tokens.shape
    experts = lax.axis_size("expert")
    capacity = max(2, 3 * rows // (2 * experts))
    slots = experts * capacity
    shard = width // 4
    olow, normed_all, qkv, mixed, wout_full, wfirst, lse_rows, gain_col, gains, centroid_full = front_block(
        tokens, norm_gain[None], expert_gain, centroids, qkv_weight, out_weight
    )
    inputs = tokens.astype(F32)
    residual = inputs + jnp.dot(olow, wout_full, preferred_element_type=F32)
    route_ids = routes[:, 0]
    chosen = (route_ids[:, None] == jnp.arange(experts, dtype=jnp.int32)[None, :]).astype(BF)
    centroid_rows = jnp.dot(chosen, centroid_full, preferred_element_type=F32)
    gate = jax.nn.sigmoid(jnp.sum(residual * centroid_rows, axis=-1))
    before = jnp.tril(jnp.ones((rows, rows), BF), -1)
    rank = jnp.sum(jnp.dot(before, chosen, preferred_element_type=F32) * chosen.astype(F32), axis=-1)
    target = route_ids * capacity + rank.astype(jnp.int32)
    place = (jnp.arange(slots, dtype=jnp.int32)[:, None] == target[None, :]).astype(BF)
    grad_out = cotangent.astype(F32)
    sent = jnp.concatenate([residual.astype(BF), (gate[:, None] * grad_out).astype(BF)], axis=1)
    spread = jnp.dot(place, sent, preferred_element_type=F32).astype(BF)
    returned, came_back, olow_full, gain_part, n_rows, h_rows, df_rows, du_rows = expert_block(
        spread[:, :width].reshape(experts, capacity, width),
        spread[:, width:].reshape(experts, capacity, width),
        olow,
        gains,
        expert_in,
        expert_out,
    )
    branch_tok = lax.dot_general(place, returned.reshape(slots, width), TN, preferred_element_type=F32)
    block_out = (residual + gate[:, None] * branch_tok).astype(BF)
    grad_logit = jnp.sum(grad_out * branch_tok, axis=-1) * gate * (1.0 - gate)
    grad_centroid = jnp.dot(chosen.astype(F32).T, grad_logit[:, None] * residual, precision=HIGH)
    back_rows = lax.dot_general(place, came_back.reshape(slots, width), TN, preferred_element_type=F32)
    grad_resid = grad_out + grad_logit[:, None] * centroid_rows + back_rows
    grad_attended = grad_resid.astype(BF)
    grad_mixed = lax.dot_general(grad_attended, wout_full, NT, preferred_element_type=F32).astype(BF)
    dnormed, gq_land, go_land, gc_land = back_block(
        grad_mixed, grad_attended, qkv, mixed, lse_rows, normed_all,
        olow_full.reshape(experts * rows, width), grad_centroid[:, None, :], qkv_weight, wfirst,
    )
    grad_tokens, grad_qkv, grad_out_weight, grad_norm_gain, grad_centroids, grad_gain, grad_expert_in, grad_expert_out = final_block(
        dnormed, tokens, gain_col, grad_resid, gq_land, go_land, qkv_weight, gc_land, gain_part,
        n_rows, h_rows, df_rows, du_rows,
    )
    return (
        block_out,
        grad_tokens,
        grad_norm_gain[0],
        grad_qkv,
        grad_out_weight,
        grad_centroids,
        grad_gain[None],
        grad_expert_in[None],
        grad_expert_out[None],
    )


def on_device(
    tokens,
    norm_gain,
    qkv_weight,
    out_weight,
    centroids,
    expert_gain,
    expert_in,
    expert_out,
    routes,
    cotangent,
):
    model_width = tokens.shape[1]
    local_rows = tokens.shape[0]
    experts = lax.axis_size("expert")
    capacity = max(2, 3 * local_rows // (2 * experts))
    slot_total = experts * capacity
    first_pos = lax.axis_index("expert") * local_rows
    scale = HEAD ** (-0.5)
    gain_full, qkv_full, out_full, centroid_full, expert_gain_full = fetch_dense(
        norm_gain, qkv_weight, out_weight, centroids, expert_gain
    )
    inputs = tokens.astype(jnp.float32)
    unit_attn, inverse_attn, normed_attn = normalize(inputs, gain_full.astype(jnp.float32))
    normed_low = normed_attn.astype(jnp.bfloat16)
    projected = jnp.dot(normed_low, qkv_full, preferred_element_type=jnp.float32).astype(
        jnp.bfloat16
    )
    queries = projected[:, :model_width]
    keyset = projected[:, model_width : 2 * model_width]
    values = projected[:, 2 * model_width :]
    query_heads = split_heads(queries)
    key_heads = split_heads(keyset)
    value_heads = split_heads(values)
    query_block = (first_pos + jnp.arange(local_rows, dtype=jnp.int32)) // BLOCK
    last_block = (first_pos + local_rows - 1) // BLOCK
    start_state = (
        jnp.zeros((local_rows, HEADS, HEAD), jnp.float32),
        jnp.full((HEADS, local_rows), NEGATIVE, jnp.float32),
        jnp.zeros((HEADS, local_rows), jnp.float32),
    )
    key_piece = lax.all_gather(keyset, "expert", axis=0, tiled=True)
    value_piece = lax.all_gather(values, "expert", axis=0, tiled=True)
    amount = key_piece.shape[0]

    def update(current):
        accumulated, highest, totals = current
        scores = (
            jnp.einsum(
                "qhd,khd->hqk",
                query_heads,
                split_heads(key_piece),
                preferred_element_type=jnp.float32,
            )
            * scale
        )
        piece_block = jnp.arange(amount, dtype=jnp.int32) // BLOCK
        visible = (piece_block[None, :] <= query_block[:, None])[None]
        scores = jnp.where(visible, scores, NEGATIVE)
        new_high = jnp.maximum(highest, jnp.max(scores, axis=-1))
        factor = jnp.exp(highest - new_high)
        weights = jnp.where(visible, jnp.exp(scores - new_high[:, :, None]), 0.0)
        totals = jnp.sum(weights, axis=-1)
        accumulated = accumulated * factor.T[:, :, None] + jnp.einsum(
            "hqk,khd->qhd",
            weights.astype(jnp.bfloat16),
            split_heads(value_piece),
            preferred_element_type=jnp.float32,
        )
        return (accumulated, new_high, totals)

    accumulated, highest, totals = lax.cond(
        jnp.int32(0) // BLOCK <= last_block, update, keep_state, start_state
    )
    mixed_heads = accumulated / totals.T[:, :, None]
    log_total = (highest + jnp.log(totals)).T
    mixed_low = mixed_heads.reshape(local_rows, model_width).astype(jnp.bfloat16)
    residual = inputs + jnp.dot(mixed_low, out_full, preferred_element_type=jnp.float32)
    route_ids = routes[:, 0]
    chosen = route_ids[:, None] == jnp.arange(experts, dtype=jnp.int32)[None, :]
    centroid_rows = jnp.dot(
        chosen.astype(jnp.bfloat16), centroid_full, preferred_element_type=jnp.float32
    )
    gate_value = jax.nn.sigmoid(jnp.sum(residual * centroid_rows, axis=-1))
    chosen_int = chosen.astype(jnp.int32)
    slot_index = jnp.sum((jnp.cumsum(chosen_int, axis=0) - 1) * chosen_int, axis=-1)
    target = route_ids * capacity + slot_index
    arrived = lax.all_to_all(
        send_slots(residual.astype(jnp.bfloat16), target, experts, capacity),
        "expert",
        split_axis=0,
        concat_axis=0,
        tiled=True,
    )
    expert_state = arrived.reshape(slot_total, model_width).astype(jnp.float32)
    gains_here = expert_gain_full[0].astype(jnp.float32)
    total_change = jnp.zeros_like(expert_state)
    stored = []
    for sublayer in range(2):
        unit_rows, inverse, normed = normalize(expert_state, gains_here[sublayer])
        normed_rows = normed.astype(jnp.bfloat16)
        first_full, second_full = (expert_in[0, sublayer], expert_out[0, sublayer])
        left_rows = spread_rows(normed_rows)
        hidden_pre = jnp.einsum(
            "rd,fd->rf", left_rows, first_full, preferred_element_type=jnp.float32
        )
        hidden_act, slope_pull = jax.vjp(exact_gelu, hidden_pre)
        hidden_low = hidden_act.astype(jnp.bfloat16)
        change = sum_rows(partial(row_product, hidden_low, second_full), slot_total)
        expert_state = expert_state + change
        total_change = total_change + change
        stored.append((unit_rows, inverse, left_rows, hidden_low, slope_pull))
    branch_low = total_change.astype(jnp.bfloat16)
    returned = lax.all_to_all(
        branch_low.reshape(experts, capacity, model_width),
        "expert",
        split_axis=0,
        concat_axis=0,
        tiled=True,
    )
    branch_tok = returned.reshape(slot_total, model_width)[target].astype(jnp.float32)
    block_out = (residual + gate_value[:, None] * branch_tok).astype(jnp.bfloat16)
    gain_full, qkv_full, out_full, centroid_full, expert_gain_full = fetch_dense(
        norm_gain, qkv_weight, out_weight, centroids, expert_gain
    )
    gains_here = expert_gain_full[0].astype(jnp.float32)
    grad_out = cotangent.astype(jnp.float32)
    grad_logit = jnp.sum(grad_out * branch_tok, axis=-1) * gate_value * (1.0 - gate_value)
    grad_centroid = jnp.dot(
        chosen.astype(jnp.float32).T, grad_logit[:, None] * residual, precision=HIGH
    )
    grad_resid = grad_out + grad_logit[:, None] * centroid_rows
    grad_branch = (gate_value[:, None] * grad_out).astype(jnp.bfloat16)
    branch_grads = lax.all_to_all(
        send_slots(grad_branch, target, experts, capacity),
        "expert",
        split_axis=0,
        concat_axis=0,
        tiled=True,
    )
    grad_change = branch_grads.reshape(slot_total, model_width).astype(jnp.float32)
    grad_state = jnp.zeros_like(grad_change)
    gain_grads = [None, None]
    first_grads = [None, None]
    second_grads = [None, None]
    for sublayer in (1, 0):
        unit_rows, inverse, left_rows, hidden_low, slope_pull = stored[sublayer]
        grad_rows_low = (grad_change + grad_state).astype(jnp.bfloat16)
        first_full, second_full = (expert_in[0, sublayer], expert_out[0, sublayer])
        grad_rows = spread_rows(grad_rows_low)
        grad_hidden = jnp.einsum(
            "rd,fd->rf", grad_rows, second_full, preferred_element_type=jnp.float32
        )
        grad_pre = slope_pull(grad_hidden)[0].astype(jnp.bfloat16)
        grad_first = jnp.einsum(
            "rf,rd->fd", grad_pre, left_rows, preferred_element_type=jnp.float32
        )
        grad_second = jnp.einsum(
            "rf,rd->fd", hidden_low, grad_rows, preferred_element_type=jnp.float32
        )
        grad_normed = sum_rows(partial(row_product, grad_pre, first_full), slot_total)
        grad_input, gain_grad = norm_backward(grad_normed, unit_rows, inverse, gains_here[sublayer])
        grad_state = grad_state + grad_input
        gain_grads[sublayer] = gain_grad
        first_grads[sublayer] = grad_first
        second_grads[sublayer] = grad_second
    came_back = lax.all_to_all(
        grad_state.astype(jnp.bfloat16).reshape(experts, capacity, model_width),
        "expert",
        split_axis=0,
        concat_axis=0,
        tiled=True,
    )
    grad_resid = grad_resid + came_back.reshape(slot_total, model_width)[target].astype(jnp.float32)
    grad_attended = grad_resid.astype(jnp.bfloat16)
    grad_out_weight = jnp.einsum(
        "rd,re->de", mixed_low, grad_attended, preferred_element_type=jnp.float32
    )
    grad_mixed = jnp.einsum(
        "re,de->rd", grad_attended, out_full, preferred_element_type=jnp.float32
    ).astype(jnp.bfloat16)
    grad_heads = split_heads(grad_mixed)
    delta_rows = jnp.sum(grad_heads.astype(jnp.float32) * mixed_heads, axis=-1)
    zero_heads = jnp.zeros((local_rows, HEADS, HEAD), jnp.float32)
    running = (zero_heads, zero_heads, zero_heads)
    offset = jnp.int32(0)
    fold_key_piece = lax.all_gather(keyset, "expert", axis=0, tiled=True)
    fold_value_piece = lax.all_gather(values, "expert", axis=0, tiled=True)
    query_piece = lax.all_gather(queries, "expert", axis=0, tiled=True)
    grad_piece = lax.all_gather(grad_mixed, "expert", axis=0, tiled=True)
    log_piece = lax.all_gather(log_total.astype(jnp.bfloat16), "expert", axis=0, tiled=True).astype(
        jnp.float32
    )
    delta_piece = lax.all_gather(
        delta_rows.astype(jnp.bfloat16), "expert", axis=0, tiled=True
    ).astype(jnp.float32)
    fold_amount = fold_key_piece.shape[0]
    piece_block = jnp.arange(fold_amount, dtype=jnp.int32) // BLOCK

    def to_queries(current):
        grad_query, grad_key, grad_value = current
        piece_keys = split_heads(fold_key_piece)
        scores = (
            jnp.einsum("qhd,khd->hqk", query_heads, piece_keys, preferred_element_type=jnp.float32)
            * scale
        )
        visible = (piece_block[None, :] <= query_block[:, None])[None]
        weights = jnp.where(visible, jnp.exp(scores - log_total.T[:, :, None]), 0.0)
        grad_weights = jnp.einsum(
            "qhd,khd->hqk",
            grad_heads,
            split_heads(fold_value_piece),
            preferred_element_type=jnp.float32,
        )
        grad_scores = (weights * (grad_weights - delta_rows.T[:, :, None])).astype(jnp.bfloat16)
        grad_query = (
            jnp.einsum("hqk,khd->qhd", grad_scores, piece_keys, preferred_element_type=jnp.float32)
            * scale
        )
        return (grad_query, grad_key, grad_value)

    def to_keys(current):
        grad_query, grad_key, grad_value = current
        piece_queries = split_heads(query_piece)
        piece_grads = split_heads(grad_piece)
        scores = (
            jnp.einsum("qhd,khd->hqk", piece_queries, key_heads, preferred_element_type=jnp.float32)
            * scale
        )
        visible = (query_block[None, :] <= piece_block[:, None])[None]
        weights = jnp.where(visible, jnp.exp(scores - log_piece.T[:, :, None]), 0.0)
        grad_weights = jnp.einsum(
            "qhd,khd->hqk", piece_grads, value_heads, preferred_element_type=jnp.float32
        )
        grad_scores = (weights * (grad_weights - delta_piece.T[:, :, None])).astype(jnp.bfloat16)
        grad_key = (
            grad_key
            + jnp.einsum(
                "hqk,qhd->khd", grad_scores, piece_queries, preferred_element_type=jnp.float32
            )
            * scale
        )
        grad_value = grad_value + jnp.einsum(
            "hqk,qhd->khd",
            weights.astype(jnp.bfloat16),
            piece_grads,
            preferred_element_type=jnp.float32,
        )
        return (grad_query, grad_key, grad_value)

    running = lax.cond(offset // BLOCK <= last_block, to_queries, keep_state, running)
    grad_query, grad_key, grad_value = lax.cond(
        query_block[0] <= (offset + fold_amount - 1) // BLOCK, to_keys, keep_state, running
    )
    grad_qkv_rows = jnp.concatenate(
        [
            grad_query.reshape(local_rows, model_width),
            grad_key.reshape(local_rows, model_width),
            grad_value.reshape(local_rows, model_width),
        ],
        axis=1,
    ).astype(jnp.bfloat16)
    grad_qkv = jnp.einsum(
        "rd,re->de", normed_low, grad_qkv_rows, preferred_element_type=jnp.float32
    )
    grad_normed_attn = jnp.einsum(
        "re,de->rd", grad_qkv_rows, qkv_full, preferred_element_type=jnp.float32
    )
    grad_input_attn, attn_gain_grad = norm_backward(
        grad_normed_attn, unit_attn, inverse_attn, gain_full.astype(jnp.float32)
    )
    grad_tokens = grad_resid + grad_input_attn
    expert_gain_grad = jnp.stack(gain_grads)[None]
    gain_share, qkv_share, out_share, centroid_share, expert_gain_share = (
        lax.psum_scatter(
            attn_gain_grad.astype(jnp.bfloat16), "dp", scatter_dimension=0, tiled=True
        ).astype(jnp.float32),
        lax.psum_scatter(
            grad_qkv.astype(jnp.bfloat16), "dp", scatter_dimension=0, tiled=True
        ).astype(jnp.float32),
        lax.psum_scatter(
            grad_out_weight.astype(jnp.bfloat16), "dp", scatter_dimension=0, tiled=True
        ).astype(jnp.float32),
        lax.psum_scatter(
            grad_centroid.astype(jnp.bfloat16), "dp", scatter_dimension=1, tiled=True
        ).astype(jnp.float32),
        lax.psum_scatter(
            expert_gain_grad.astype(jnp.bfloat16), "dp", scatter_dimension=2, tiled=True
        ).astype(jnp.float32),
    )
    gain_total, qkv_total, out_total, centroid_total = (
        lax.psum(gain_share.astype(jnp.bfloat16), "expert").astype(jnp.float32),
        lax.psum(qkv_share.astype(jnp.bfloat16), "expert").astype(jnp.float32),
        lax.psum(out_share.astype(jnp.bfloat16), "expert").astype(jnp.float32),
        lax.psum(centroid_share.astype(jnp.bfloat16), "expert").astype(jnp.float32),
    )
    grad_expert_in = jnp.stack(first_grads)[None]
    grad_expert_out = jnp.stack(second_grads)[None]
    return (
        block_out,
        grad_tokens,
        gain_total,
        qkv_total,
        out_total,
        centroid_total,
        expert_gain_share,
        grad_expert_in,
        grad_expert_out,
    )


def solution(mesh):
    in_specs = (
        P(("dp", "expert"), None),
        P("dp"),
        P("dp", None),
        P("dp", None),
        P(None, "dp"),
        P("expert", None, "dp"),
        P("expert", None, "dp", None),
        P("expert", None, "dp", None),
        P(("dp", "expert"), None),
        P(("dp", "expert"), None),
    )
    out_specs = (
        P(("dp", "expert"), None),
        P(("dp", "expert"), None),
        P("dp"),
        P("dp", None),
        P("dp", None),
        P(None, "dp"),
        P("expert", None, "dp"),
        P("expert", None, "dp", None),
        P("expert", None, "dp", None),
    )
    split = mesh.shape["dp"] == 4 and mesh.shape["expert"] == 8
    return jax.shard_map(
        on_device_split if split else on_device, mesh=mesh, in_specs=in_specs, out_specs=out_specs, check_vma=False
    )
```

```python
from functools import partial

import jax
import jax.numpy as jnp
from jax import lax
from jax.experimental import pallas as pl
from jax.experimental.pallas import tpu as pltpu
from jax.sharding import PartitionSpec as P

HEADS = 16
HEAD = 64
BLOCK = 256


EPS = 1e-05
NEGATIVE = -1e30
HIGH = lax.Precision.HIGHEST


def normalize(inputs, gain_row):
    centered = inputs - jnp.mean(inputs, axis=-1, keepdims=True)
    inverse = lax.rsqrt(jnp.mean(centered * centered, axis=-1, keepdims=True) + EPS)
    unit_rows = centered * inverse
    return (unit_rows, inverse, unit_rows * gain_row)


def norm_backward(grad_normed, unit_rows, inverse, gain_row):
    grad_unit = grad_normed * gain_row
    first_mean = jnp.mean(grad_unit, axis=-1, keepdims=True)
    second_mean = jnp.mean(grad_unit * unit_rows, axis=-1, keepdims=True)
    grad_input = inverse * (grad_unit - first_mean - unit_rows * second_mean)
    return (grad_input, jnp.sum(grad_normed * unit_rows, axis=0))


def split_heads(matrix):
    return matrix.reshape(matrix.shape[0], HEADS, HEAD)


def exact_gelu(inputs):
    return jax.nn.gelu(inputs, approximate=False)


def keep_state(current):
    return current


def row_product(left_rows, right_matrix, offset, amount):
    return jnp.dot(left_rows, right_matrix, preferred_element_type=jnp.float32)


def fetch_dense(norm_gain, qkv_weight, out_weight, centroids, expert_gain):
    return (
        lax.all_gather(norm_gain, "dp", axis=0, tiled=True),
        lax.all_gather(qkv_weight, "dp", axis=0, tiled=True),
        lax.all_gather(out_weight, "dp", axis=0, tiled=True),
        lax.all_gather(centroids, "dp", axis=1, tiled=True),
        lax.all_gather(expert_gain, "dp", axis=2, tiled=True),
    )


def spread_rows(rows_low):
    return lax.all_gather(rows_low, "dp", axis=0, tiled=True)


def sum_rows(term, amount):
    return lax.psum_scatter(
        term(jnp.int32(0), amount * lax.axis_size("dp")).astype(jnp.bfloat16),
        "dp",
        scatter_dimension=0,
        tiled=True,
    ).astype(jnp.float32)


def send_slots(rows_low, target, experts, capacity):
    buffer_rows = (
        jnp.zeros((experts * capacity, rows_low.shape[1]), rows_low.dtype).at[target].set(rows_low)
    )
    return buffer_rows.reshape(experts, capacity, rows_low.shape[1])


BF = jnp.bfloat16
F32 = jnp.float32
NT = (((1,), (1,)), ((), ()))
TN = (((0,), (0,)), ((), ()))
TILE = 256
MESH_ID = pl.DeviceIdType.MESH


def mean_last(v):
    return jnp.mean(v, axis=-1, keepdims=True)


def dp_peers():
    me = lax.axis_index("dp")
    sibling = me + 1 - 2 * lax.rem(me, 2)
    across = lax.rem(me + 2, 4)
    diagonal = lax.rem(sibling + 2, 4)
    return me, sibling, across, diagonal


def expert_peers():
    me = lax.axis_index("expert")
    z, x = me // 2, lax.rem(me, 2)
    beside = me + 1 - 2 * x
    near = z + 1 - 2 * lax.rem(z, 2)
    low, high = lax.rem(z, 2), z // 2
    inner = low + high - 2 * low * high
    flip, turn = 3 - z, lax.rem(z + 2, 4)
    second = inner * flip + (1 - inner) * turn
    third = inner * turn + (1 - inner) * flip
    return me, z, x, beside, (near, second, third)


def greet(targets):
    barrier = pltpu.get_barrier_semaphore()
    for target in targets:
        pl.semaphore_signal(barrier, inc=1, device_id=target, device_id_type=MESH_ID)
    pl.semaphore_wait(barrier, len(targets))


def others(n, me):
    return [lax.rem(me + d, n) for d in range(1, n)]


def push(src, dst, send, recv, target):
    return pltpu.make_async_remote_copy(
        src_ref=src, dst_ref=dst, send_sem=send, recv_sem=recv, device_id=target, device_id_type=MESH_ID
    )


class Spread:
    def __init__(self, own_src, slots, send, recv, chunks):
        self.me, self.z, self.x, self.beside, self.zs = expert_peers()
        self.own_src, self.slots, self.send, self.recv, self.chunks = own_src, slots, send, recv, chunks
        self.part = own_src.shape[0] // chunks

    def rows(self, c):
        return pl.ds(c * self.part, self.part)

    def own(self, way, c):
        peer = self.beside if way == 0 else 2 * (self.z + (1 if way == 1 else -1)) + self.x
        return push(
            self.own_src.at[self.rows(c)], self.slots.at[self.me, self.rows(c)],
            self.send.at[way * self.chunks + c], self.recv.at[self.me * self.chunks + c], {"expert": peer},
        )

    def slot(self, s, c, base, peer):
        block = self.slots.at[s, self.rows(c)]
        return push(block, block, self.send.at[base * self.chunks + c], self.recv.at[s * self.chunks + c], {"expert": peer})

    def own_all(self, act, chunks):
        for way in range(3):
            for c in chunks:
                if way == 0:
                    act(self.own(way, c))
                else:
                    @pl.when(self.z < 3 if way == 1 else self.z > 0)
                    def _():
                        act(self.own(way, c))

    def start(self):
        self.own_all(lambda cp: cp.start(), range(self.chunks))

    def start_chunk(self, c):
        self.own_all(lambda cp: cp.start(), (c,))

    def each(self, d, act):
        for sign in (-1, 1):
            zz = self.z + sign * d
            onward = self.z - sign

            @pl.when(jnp.logical_and(zz >= 0, zz <= 3))
            def _():
                s = 2 * zz + self.x
                for c in range(self.chunks):
                    act(s, zz, onward, c)

    def step(self, d):
        def act(s, zz, onward, c):
            self.slot(s, c, 0, self.beside).wait_recv()

            @pl.when(jnp.logical_and(onward >= 0, onward <= 3))
            def _():
                self.slot(s, c, 7 + zz, 2 * onward + self.x).start()

            self.slot(s, c, 3 + zz, self.beside).start()

        self.each(d, act)

    def wait_beside(self, zz):
        for c in range(self.chunks):
            self.slot(2 * zz + 1 - self.x, c, 0, self.beside).wait_recv()

    def drain(self):
        self.own_all(lambda cp: cp.wait_send(), range(self.chunks))

        def act(s, zz, onward, c):
            @pl.when(jnp.logical_and(onward >= 0, onward <= 3))
            def _():
                self.slot(s, c, 7 + zz, 2 * onward + self.x).wait_send()

            self.slot(s, c, 3 + zz, self.beside).wait_send()

        for d in (1, 2, 3):
            self.each(d, act)


class Weights:
    def __init__(self, src, first, rows, full, send, recv):
        self.j, self.sibling, self.across, self.diagonal = dp_peers()
        self.src, self.full, self.send, self.recv = src.at[pl.ds(first, rows)], full, send, recv

    def copy(self, kind):
        if kind == 2:
            block = self.full.at[self.across]
            return push(block, block, self.send.at[2], self.recv.at[self.across], {"dp": self.sibling})
        peer = self.sibling if kind == 0 else self.across
        return push(self.src, self.full.at[self.j], self.send.at[kind], self.recv.at[self.j], {"dp": peer})

    def start(self):
        self.copy(1).start()
        self.copy(0).start()

    def arrival(self, s):
        return push(self.src, self.full.at[s], self.send.at[0], self.recv.at[s], {"dp": self.sibling})

    def relay(self):
        self.arrival(self.across).wait_recv()
        self.copy(2).start()

    def drain(self):
        self.arrival(self.sibling).wait_recv()
        self.arrival(self.diagonal).wait_recv()
        for kind in range(3):
            self.copy(kind).wait_send()


def lane_masks(rows):
    lane = lax.broadcasted_iota(jnp.int32, (rows, 128), 1)
    return lane < HEAD


def front_kernel(
    tok, norm_gain, expert_gain, centroids, wqkv, wout,
    olow, normed_out, qkv_out, mixed_out, wout_full, wfirst, lse_rows, gain_col, gains, cent_full,
    held, wblk, normed, qkv, mixed, mixed_low, gain, bounce, small, smalls,
    tok_send, tok_recv, w_send, w_recv, o_send, o_recv, copy_sem, q_send, q_recv,
):
    j, sibling, across, diagonal = dp_peers()
    e, z, x, beside, zs = expert_peers()
    rows, width = tok.shape
    shard = wqkv.shape[0]
    lanes = 128

    def mine(s):
        return pl.ds(pl.multiple_of(s * shard, shard), shard)

    mycols = pl.ds(pl.multiple_of(e * lanes, lanes), lanes)
    own_tok = pltpu.make_async_copy(tok, held.at[e], copy_sem.at[0])
    own_tok.start()
    own_w = [
        pltpu.make_async_copy(
            wqkv.at[:, pl.ds(pl.multiple_of(i * width + e * lanes, lanes), lanes)],
            wblk.at[mine(j), pl.ds(i * lanes, lanes)],
            copy_sem.at[1 + i],
        )
        for i in range(3)
    ]
    for cp in own_w:
        cp.start()
    own_out = pltpu.make_async_copy(wout, bounce, copy_sem.at[4])
    own_out.start()
    small[...] = jnp.concatenate(
        [norm_gain[...], expert_gain[0], jnp.zeros((5, shard), BF), centroids[...]], axis=0
    )
    smalls[j] = small[...]
    greet([{"expert": p} for p in others(8, e)] + [{"dp": p} for p in (sibling, across, diagonal)])

    toks = Spread(tok, held, tok_send, tok_recv, 2)
    toks.start()
    later = Weights(wqkv, 0, shard // 2, wfirst, q_send, q_recv)
    for cp in own_w:
        cp.wait()

    def w_copy(kind):
        if kind == 0:
            return push(wblk.at[mine(j)], wblk.at[mine(j)], w_send.at[0], w_recv.at[j], {"dp": sibling})
        if kind == 1:
            return push(wblk.at[mine(j)], wblk.at[mine(j)], w_send.at[1], w_recv.at[j], {"dp": across})
        return push(wblk.at[mine(across)], wblk.at[mine(across)], w_send.at[2], w_recv.at[across], {"dp": sibling})

    def w_arrival(s):
        return push(wblk.at[mine(s)], wblk.at[mine(s)], w_send.at[0], w_recv.at[s], {"dp": sibling})

    def s_copy(i):
        return push(small, smalls.at[j], w_send.at[3 + i], w_recv.at[4 + j], {"dp": (sibling, across, diagonal)[i]})

    def s_arrival(s):
        return push(small, smalls.at[s], w_send.at[3], w_recv.at[4 + s], {"dp": sibling})

    def out_copy(kind):
        if kind == 0:
            return push(wout, wout_full.at[mine(j)], w_send.at[6], w_recv.at[8 + j], {"dp": sibling})
        if kind == 1:
            return push(wout, wout_full.at[mine(j)], w_send.at[7], w_recv.at[8 + j], {"dp": across})
        return push(wout_full.at[mine(across)], wout_full.at[mine(across)], w_send.at[8], w_recv.at[8 + across], {"dp": sibling})

    def out_arrival(s):
        return push(wout, wout_full.at[mine(s)], w_send.at[6], w_recv.at[8 + s], {"dp": sibling})

    for i in range(3):
        s_copy(i).start()
    w_copy(1).start()
    w_copy(0).start()
    out_copy(1).start()
    out_copy(0).start()
    later.start()
    own_out.wait()
    keep_out = pltpu.make_async_copy(bounce, wout_full.at[mine(j)], copy_sem.at[4])
    keep_out.start()
    for s in (sibling, across, diagonal):
        s_arrival(s).wait_recv()
    for s in range(4):
        at = pl.ds(s * shard, shard)
        block = smalls[s].astype(F32)
        gain[:, at] = block[0:1]
        gain_col[s : s + 1, :] = block[0:1]
        gains[:, at] = block[1:3]
        cent_full[:, at] = smalls[s, 8:16, :]
    w_arrival(across).wait_recv()
    w_copy(2).start()
    w_arrival(sibling).wait_recv()
    w_arrival(diagonal).wait_recv()

    def project(zz):
        base = zz * 2 * rows
        for xx in range(2):
            def norm_rows(t, c):
                rs = pl.ds(pl.multiple_of(t * 64, 64), 64)
                v = held[2 * zz + xx, rs, :].astype(F32)
                center = v - mean_last(v)
                inverse = lax.rsqrt(mean_last(center * center) + EPS)
                at = pl.ds(pl.multiple_of(base + xx * rows + t * 64, 64), 64)
                normed[at, :] = (center * inverse * gain[...]).astype(BF)
                return c
            lax.fori_loop(0, rows // 64, norm_rows, 0)
        at = pl.ds(pl.multiple_of(base, 2 * rows), 2 * rows)
        qkv[at, :] = jnp.dot(normed[at, :], wblk[...], preferred_element_type=F32).astype(BF)

    own_tok.wait()
    toks.step(1)
    toks.wait_beside(z)
    project(z)
    toks.step(2)
    toks.wait_beside(zs[0])
    project(zs[0])
    toks.step(3)
    out_arrival(across).wait_recv()
    out_copy(2).start()
    toks.wait_beside(zs[1])
    project(zs[1])
    toks.wait_beside(zs[2])
    project(zs[2])
    stores = [
        pltpu.make_async_copy(normed, normed_out, copy_sem.at[0]),
        pltpu.make_async_copy(qkv, qkv_out, copy_sem.at[1]),
    ]
    for cp in stores:
        cp.start()

    def o_copy(dest):
        return push(mixed_low.at[pl.ds(dest * rows, rows)], olow.at[:, mycols], o_send.at[dest], o_recv.at[e], {"expert": dest})

    def o_own(dest):
        return pltpu.make_async_copy(mixed_low.at[pl.ds(dest * rows, rows)], olow.at[:, mycols], copy_sem.at[5])

    left = lane_masks(2 * rows)
    for b in (3, 2, 1, 0):
        qs = qkv[pl.ds(b * 2 * rows, 2 * rows), 0:lanes]
        keys = qkv[0 : (b + 1) * 2 * rows, lanes : 2 * lanes]
        vals = qkv[0 : (b + 1) * 2 * rows, 2 * lanes : 3 * lanes]
        outs, logs = [], []
        for h in range(2):
            mask = left if h == 0 else jnp.logical_not(left)
            q_h = jnp.where(mask, qs.astype(F32) * (HEAD ** -0.5), 0.0).astype(BF)
            sc = lax.dot_general(q_h, keys, NT, preferred_element_type=F32)
            top = jnp.max(sc, axis=-1, keepdims=True)
            pr = jnp.exp(sc - top)
            tot = jnp.sum(pr, axis=-1, keepdims=True)
            outs.append(jnp.dot(pr.astype(BF), vals, preferred_element_type=F32) / tot)
            logs.append(top + jnp.log(tot))
        at = pl.ds(b * 2 * rows, 2 * rows)
        res = jnp.where(left, outs[0], outs[1])
        mixed[at, :] = res
        mixed_low[at, :] = res.astype(BF)
        turned = jnp.where(left, logs[0], logs[1]).T
        lse_rows[0:1, at] = turned[0:1]
        lse_rows[1:2, at] = turned[HEAD : HEAD + 1]
        for dest in (2 * b, 2 * b + 1):
            @pl.when(dest != e)
            def _():
                o_copy(dest).start()

            @pl.when(dest == e)
            def _():
                o_own(dest).start()
    more = [
        pltpu.make_async_copy(mixed, mixed_out, copy_sem.at[2]),
    ]
    for cp in more:
        cp.start()
    for dest in range(8):
        @pl.when(dest != e)
        def _():
            push(mixed_low.at[pl.ds(0, rows)], olow.at[:, pl.ds(dest * lanes, lanes)], o_send.at[dest], o_recv.at[dest], {"expert": dest}).wait_recv()
            o_copy(dest).wait_send()

        @pl.when(dest == e)
        def _():
            o_own(dest).wait()
    later.relay()
    for s in (sibling, diagonal):
        out_arrival(s).wait_recv()
    toks.drain()
    later.drain()
    for i in range(3):
        w_copy(i).wait_send()
        s_copy(i).wait_send()
        out_copy(i).wait_send()
    keep_out.wait()
    for cp in stores + more:
        cp.wait()


def front_block(tokens, norm_gain, expert_gain, centroids, qkv_weight, out_weight):
    rows, width = tokens.shape
    seq = 8 * rows
    shard = qkv_weight.shape[0]
    any_spec = pl.BlockSpec(memory_space=pl.ANY)
    vmem_spec = pl.BlockSpec(memory_space=pltpu.VMEM)
    V = pltpu.VMEM
    D = pltpu.SemaphoreType.DMA
    S = jax.ShapeDtypeStruct
    return pl.pallas_call(
        front_kernel,
        out_shape=(
            S((rows, width), BF), S((seq, width), BF), S((seq, 384), BF), S((seq, 128), F32),
            S((width, width), BF), S((4, shard // 2, 3 * width), BF),
            S((2, seq), F32), S((4, shard), F32), S((2, width), F32), S((8, width), BF),
        ),
        in_specs=[any_spec, vmem_spec, vmem_spec, vmem_spec, any_spec, any_spec],
        out_specs=(any_spec,) * 6 + (vmem_spec,) * 4,
        scratch_shapes=[
            V((8, rows, width), BF), V((width, 384), BF), V((seq, width), BF), V((seq, 384), BF),
            V((seq, 128), F32), V((seq, 128), BF), V((1, width), F32), V((shard, width), BF),
            V((16, shard), BF), V((4, 16, shard), BF),
            D((22,)), D((16,)), D((9,)), D((12,)), D((8,)), D((8,)), D((8,)), D((3,)), D((4,)),
        ],
        compiler_params=pltpu.CompilerParams(collective_id=2, has_side_effects=True, vmem_limit_bytes=56 * 1024 * 1024),
        name="front_block",
    )(tokens, norm_gain, expert_gain, centroids, qkv_weight, out_weight)


def expert_kernel(
    zslots, dslots, olow, gain_ref, w1_hbm, w2_hbm,
    returned, came_back, olow_full, ggain_ref, n_out, h_out, df_out, du_out,
    w1, w2, x, hid, gpr, unit_s, inv_s, state, total, own, f1, rf1, ssum, rss,
    zland, dland, zfar, dfar, bsend, gsend, ggain, gland, olow_held,
    x_send, x_recv, f_send, f_recv, s_send, s_recv, l_send, l_recv,
    a_send, a_recv, g_send, g_recv, copy_sem, own_sem, e_send, e_recv,
):
    cap, width = zslots.shape[1:]
    quarter = 2 * cap
    pair = 2 * quarter
    chunk = 2 * pair
    tiles = width // TILE
    shard = width // 4
    j, sibling, across, diagonal = dp_peers()
    e, zpos, xpos, beside, zs = expert_peers()
    mine = pl.multiple_of((j // 2) * quarter, 16)
    theirs = pl.multiple_of((1 - j // 2) * quarter, 16)

    loads = []
    for i, (src, dst) in enumerate(
        [(w1_hbm.at[0, 0], w1.at[0]), (w2_hbm.at[0, 0], w2.at[0]),
         (w1_hbm.at[0, 1], w1.at[1]), (w2_hbm.at[0, 1], w2.at[1])]
    ):
        cp = pltpu.make_async_copy(src, dst, copy_sem.at[i])
        cp.start()
        loads.append(cp)
    zx = (zpos, zs[0], lax.rem(zpos + 2, 4), 3 - zpos)

    def peer_at(q):
        return 2 * zx[q // 2] + q % 2

    def seat(q):
        return 2 * (q // 2) + xpos

    greet([{"expert": p} for p in others(8, e)] + [{"dp": p} for p in (sibling, across, diagonal)])

    def swap(src, dst, which, q):
        peer = peer_at(q)
        if which < 2:
            return push(src.at[peer], dst.at[seat(q)], a_send.at[which * 8 + q], a_recv.at[which * 8 + seat(q)], {"expert": peer})
        return push(src.at[q], dst.at[e], a_send.at[which * 8 + q], a_recv.at[which * 8 + seat(q)], {"expert": peer})

    def swap_arrival(src, dst, which, q):
        peer = peer_at(q)
        if which < 2:
            return push(src.at[peer], dst.at[q], a_send.at[which * 8 + q], a_recv.at[which * 8 + q], {"expert": peer})
        return push(src.at[q], dst.at[peer], a_send.at[which * 8 + q], a_recv.at[which * 8 + q], {"expert": peer})

    def swap_own(src, dst, which):
        if which < 2:
            return pltpu.make_async_copy(src.at[e], dst.at[xpos], own_sem.at[which])
        return pltpu.make_async_copy(src.at[xpos], dst.at[e], own_sem.at[which])

    def for_places(c, act, here):
        for q in (2 * c, 2 * c + 1):
            if q >= 2:
                act(q)
            else:
                @pl.when(xpos != q)
                def _():
                    act(q)

                @pl.when(xpos == q)
                def _():
                    here()

    for which, (src, dst) in enumerate([(zslots, zland), (dslots, dland)]):
        for c in ((1, 2, 3, 0) if which == 0 else (3, 2, 1, 0)):
            for_places(c, lambda q: swap(src, dst, which, q).start(), lambda: swap_own(src, dst, which).start())
    olows = Spread(olow, olow_full, g_send, g_recv, 1)
    take_o = pltpu.make_async_copy(olow, olow_held, copy_sem.at[12])
    take_o.start()
    own_o = pltpu.make_async_copy(olow_held, olow_full.at[e], copy_sem.at[12])
    layer_of = (0, 1, 1, 0)
    order = [(p, c if p < 2 else 3 - c) for p in range(4) for c in range(4)]

    def place(p, c):
        return order.index((p, c)) % 4

    def my_half(c):
        return pl.ds(c * chunk, pair)

    def x_copy(p, c):
        q = 4 * p + c
        return push(x.at[p, my_half(c)], x.at[p, pl.ds(c * chunk + pair, pair)], x_send.at[q], x_recv.at[q], {"dp": sibling})

    def f_copy(q, cols):
        return push(f1.at[q, :, cols], rf1.at[q, :, cols], f_send.at[q], f_recv.at[q], {"dp": sibling})

    def s_copy(p, c, arrives=False):
        q = 4 * p + c
        if p in (0, 2):
            return push(ssum.at[q], rss.at[q], s_send.at[q], s_recv.at[q], {"dp": across})
        at = pl.ds(mine if arrives else theirs, quarter)
        return push(ssum.at[q, at], rss.at[q, at], s_send.at[q], s_recv.at[q], {"dp": across})

    def land_copy(which, c):
        src, dst = (zland, zfar) if which == 0 else (dland, dfar)
        at = pl.ds(2 * c, 2)
        return push(src.at[at], dst.at[at], l_send.at[4 * which + c], l_recv.at[4 * which + c], {"dp": across})

    def forward(which, c):
        src, dst = (zslots, zland) if which == 0 else (dslots, dland)
        for_places(c, lambda q: swap_arrival(src, dst, which, q).wait_recv(), lambda: swap_own(src, dst, which).wait())
        land_copy(which, c).start()

    def both(buf, c):
        return jnp.concatenate([buf[2 * c].astype(F32), buf[2 * c + 1].astype(F32)], axis=0)

    def by_rows(act):
        def step(t, carry):
            act(pl.multiple_of(t * 32, 32))
            return carry
        lax.fori_loop(0, pair // 32, step, 0)

    def norm_rows(p, c, read):
        def act(t):
            v = read(t)
            center = v - mean_last(v)
            inverse = lax.rsqrt(mean_last(center * center) + EPS)
            unit = center * inverse
            rs = pl.ds(c * pair + t, 32)
            unit_s[p, rs, :] = unit
            inv_s[p, rs, :] = jnp.broadcast_to(inverse, (32, 128))
            x[p, pl.ds(c * chunk + t, 32), :] = (unit * gain_ref[pl.ds(p, 1), :]).astype(BF)
        by_rows(act)
        x_copy(p, c).start()

    def begin(c):
        land_copy(0, c).wait_recv()
        state[pl.ds(c * pair + mine, quarter), :] = both(zland, c)
        state[pl.ds(c * pair + theirs, quarter), :] = both(zfar, c)
        norm_rows(0, c, lambda t: state[pl.ds(c * pair + t, 32), :])

    def begin_back(c):
        land_copy(1, c).wait_recv()
        x[2, pl.ds(c * chunk + mine, quarter), :] = both(dland, c).astype(BF)
        x[2, pl.ds(c * chunk + theirs, quarter), :] = both(dfar, c).astype(BF)
        x_copy(2, c).start()

    def up(p, c):
        k = layer_of[p]
        base = pl.ds(c * chunk, chunk)
        left_w = w1 if p < 2 else w2
        x_copy(p, c).wait_recv()

        def gelu(t, pre):
            cols = pl.ds(pl.multiple_of(t * TILE, TILE), TILE)
            cdf = 0.5 * (1.0 + lax.erf(pre * (0.5 ** 0.5)))
            pdf = jnp.exp(-0.5 * pre * pre) * 0.3989422804014327
            hid[k, base, cols] = (pre * cdf).astype(BF)
            gpr[k, base, cols] = cdf + pre * pdf

        def product(t):
            cols = pl.ds(pl.multiple_of(t * TILE, TILE), TILE)
            return lax.dot_general(x[p, base, :], left_w[k, cols, :], NT, preferred_element_type=F32)

        def step(t, carry):
            if p < 2:
                gelu(t, product(t))
            else:
                cols = pl.ds(pl.multiple_of(t * TILE, TILE), TILE)
                hid[2 + k, base, cols] = (product(t) * gpr[k, base, cols]).astype(BF)
            return carry

        lax.fori_loop(0, tiles, step, 0)

    def down(p, c):
        k = layer_of[p]
        base = pl.ds(c * chunk, chunk)
        right_w = w2 if p < 2 else w1
        q = 4 * p + c

        def step(t, carry):
            cols = pl.ds(pl.multiple_of(t * TILE, TILE), TILE)
            res = jnp.dot(hid[k if p < 2 else 2 + k, base, :], right_w[k, :, cols], preferred_element_type=F32)
            own[place(p, c), :, cols] = res[:pair]
            f1[q, :, cols] = res[pair:].astype(BF)
            f_copy(q, cols).start()
            return carry

        lax.fori_loop(0, tiles, step, 0)

    everything = pl.ds(0, width)

    def send_sum(p, c):
        q = 4 * p + c
        f_copy(q, everything).wait_recv()

        def act(t):
            rs = pl.ds(t, 32)
            v = own[place(p, c), rs, :] + rf1[q, rs, :].astype(F32)
            own[place(p, c), rs, :] = v
            ssum[q, rs, :] = v.astype(BF)
        by_rows(act)
        s_copy(p, c).start()

    def give_back(buf, dst, which, c, v):
        for i in range(2):
            buf[2 * c + i] = v[i * cap : (i + 1) * cap].astype(BF)
        for_places(c, lambda q: swap(buf, dst, which, q).start(), lambda: swap_own(buf, dst, which).start())

    def add_gain(k, c, part):
        if c == 3:
            ggain[pl.ds(k, 1), :] = part
        else:
            ggain[pl.ds(k, 1), :] = ggain[pl.ds(k, 1), :] + part

    def norm_back(k, got, rs):
        unit = unit_s[k, rs, :]
        a = got * gain_ref[pl.ds(k, 1), :]
        back = inv_s[k, rs, :][:, :1] * (a - mean_last(a) - unit * mean_last(a * unit))
        return back, jnp.sum(got * unit, axis=0, keepdims=True)

    def finish(p, c):
        k = layer_of[p]
        q = 4 * p + c
        s_copy(p, c, True).wait_recv()
        if p == 0:
            def read(t):
                rs = pl.ds(c * pair + t, 32)
                got = own[place(p, c), pl.ds(t, 32), :] + rss[q, pl.ds(t, 32), :].astype(F32)
                total[rs, :] = got
                return state[rs, :] + got
            norm_rows(1, c, read)
        elif p == 2:
            def step(i, part):
                t = pl.multiple_of(i * 32, 32)
                rs = pl.ds(c * pair + t, 32)
                got = own[place(p, c), pl.ds(t, 32), :] + rss[q, pl.ds(t, 32), :].astype(F32)
                back, add = norm_back(1, got, rs)
                state[rs, :] = back
                at = pl.ds(c * chunk + t, 32)
                x[3, at, :] = (x[2, at, :].astype(F32) + back).astype(BF)
                return part + add
            part = lax.fori_loop(0, pair // 32, step, jnp.zeros((1, width), F32))
            x_copy(3, c).start()
            add_gain(1, c, 0.5 * part)
        else:
            at = pl.ds(mine, quarter)
            rs = pl.ds(c * pair + mine, quarter)
            got = own[place(p, c), at, :] + rss[q, at, :].astype(F32)
            if p == 1:
                give_back(bsend, returned, 2, c, total[rs, :] + got)
            else:
                back, part = norm_back(0, got, rs)
                give_back(gsend, came_back, 3, c, state[rs, :] + back)
                add_gain(0, c, part)

    stores = []

    def store(i, src, dst):
        cp = pltpu.make_async_copy(src, dst, copy_sem.at[4 + i])
        cp.start()
        stores.append(cp)

    def gain_copy(i):
        s = (sibling, across, diagonal)[i]
        return push(ggain.at[:, pl.ds(pl.multiple_of(s * shard, shard), shard)], gland.at[j], e_send.at[i], e_recv.at[j], {"dp": s})

    forward(0, 0)
    forward(0, 1)
    begin(0)
    loads[0].wait()
    loads[1].wait()
    for t, (p, c) in enumerate(order):
        if t == 4:
            loads[2].wait()
            loads[3].wait()
        up(p, c)
        if t > 0:
            send_sum(*order[t - 1])
        if t < 2:
            forward(0, t + 2)
        down(p, c)
        if 2 <= t < 6:
            forward(1, 5 - t)
        if t < 3:
            begin(t + 1)
        if t >= 2:
            finish(*order[t - 2])
        if 5 <= t < 9:
            begin_back(8 - t)
        if t == 2:
            olows.start()
            take_o.wait()
            own_o.start()
        if t in (5, 8, 11):
            olows.step((t - 2) // 3)
        if t % 4 == 3:
            k = layer_of[p]
            if p < 2:
                store(p * 2, x.at[p], n_out.at[k])
                store(p * 2 + 1, hid.at[k], h_out.at[k])
            else:
                store(p * 2, x.at[p], df_out.at[k])
                store(p * 2 + 1, hid.at[2 + k], du_out.at[k])
    send_sum(*order[15])
    finish(*order[14])
    finish(*order[15])
    for i in range(3):
        gain_copy(i).start()
    gland[j] = ggain[:, pl.ds(pl.multiple_of(j * shard, shard), shard)]
    own_o.wait()
    for zz in range(4):
        olows.wait_beside(zz)
    olows.drain()
    for p in range(4):
        for c in range(4):
            x_copy(p, c).wait_send()
            f_copy(4 * p + c, everything).wait_send()
            s_copy(p, c).wait_send()
    for i in range(2):
        for c in range(4):
            land_copy(i, c).wait_send()
    for cp in stores:
        cp.wait()
    for i in range(3):
        push(ggain.at[:, pl.ds(0, shard)], gland.at[(sibling, across, diagonal)[i]], e_send.at[0], e_recv.at[(sibling, across, diagonal)[i]], {"dp": sibling}).wait_recv()
        gain_copy(i).wait_send()
    ggain_ref[...] = jnp.sum(gland[...], axis=0)
    for c in range(4):
        for which, (src, dst) in enumerate([(zslots, zland), (dslots, dland), (bsend, returned), (gsend, came_back)]):
            for_places(c, lambda q: swap(src, dst, which, q).wait_send(), lambda: None)
            if which >= 2:
                for_places(c, lambda q: swap_arrival(src, dst, which, q).wait_recv(), lambda: swap_own(src, dst, which).wait())


def expert_block(zslots, dslots, olow, gains, expert_in, expert_out):
    sources, cap, width = zslots.shape
    rows = sources * cap
    pair = 4 * cap
    hidden = expert_in.shape[2]
    everything = 4 * rows
    any_spec = pl.BlockSpec(memory_space=pl.ANY)
    vmem_spec = pl.BlockSpec(memory_space=pltpu.VMEM)
    S = jax.ShapeDtypeStruct
    big = S((2, everything, width), BF)
    V = pltpu.VMEM
    D = pltpu.SemaphoreType.DMA
    return pl.pallas_call(
        expert_kernel,
        out_shape=(
            S(zslots.shape, BF), S(zslots.shape, BF), S((8,) + olow.shape, BF), S((2, width // 4), F32),
            big, big, big, big,
        ),
        in_specs=[any_spec] * 3 + [vmem_spec] + [any_spec] * 2,
        out_specs=(any_spec, any_spec, any_spec, vmem_spec, any_spec, any_spec, any_spec, any_spec),
        scratch_shapes=[
            V((2, hidden, width), BF), V((2, hidden, width), BF),
            V((4, everything, width), BF), V((4, everything, hidden), BF), V((2, everything, hidden), F32),
            V((2, 2 * rows, width), F32), V((2, 2 * rows, 128), F32), V((2 * rows, width), F32), V((2 * rows, width), F32),
            V((4, pair, width), F32),
        ]
        + [V((16, pair, width), BF)] * 4
        + [V(zslots.shape, BF)] * 6
        + [V((2, width), F32), V((4, 2, width // 4), F32), V(olow.shape, BF)]
        + [D((16,))] * 6 + [D((8,))] * 2
        + [D((32,)), D((32,)), D((11,)), D((8,)), D((13,)), D((4,)), D((3,)), D((4,))],
        compiler_params=pltpu.CompilerParams(
            collective_id=1, has_side_effects=True, vmem_limit_bytes=62 * 1024 * 1024
        ),
        name="expert_block",
    )(zslots, dslots, olow, gains, expert_in, expert_out)


def back_kernel(
    gmix, gatt, qkv_hbm, mixed_hbm, lse_rows, normed_hbm, olow_hbm, cent, wqkv, wfirst_hbm, n_hbm, h_hbm, df_hbm, du_hbm,
    dnorm_hbm, gq_land, go_land, gc_land, grads_hbm,
    dom, dam, qkv, mixed, normed, olow, delta, dq_acc, dqkv,
    part, f1, f3, ssum, rf1, rf3, rss, gq_own, go_own, cland, csum, cdp,
    h_send, h_recv, d_send, d_recv, p_send, p_recv, gq_send, gq_recv, go_send, go_recv, c_send, c_recv, copy_sem, q_send, q_recv,
    dq_land, wfirst, wsecond, dq_rows, dnorm, n_sem,
    lefts, rights, grads, m_sem, t_sem,
):
    j, sibling, across, diagonal = dp_peers()
    e, zpos, xpos, beside, zs = expert_peers()
    rows, width = gmix.shape
    blk = 2 * rows
    lanes = 128
    shard = width // 4
    loads = [
        pltpu.make_async_copy(src, dst, copy_sem.at[i])
        for i, (src, dst) in enumerate([(qkv_hbm, qkv), (mixed_hbm, mixed), (olow_hbm, olow), (normed_hbm, normed)])
    ]
    for cp in loads:
        cp.start()
    half = shard // 2
    weights = [
        pltpu.make_async_copy(wqkv.at[pl.ds(0, half)], wfirst.at[j], n_sem.at[0]),
        pltpu.make_async_copy(wqkv.at[pl.ds(half, half)], wsecond.at[j], n_sem.at[1]),
    ]
    for i in range(1, 4):
        s = lax.rem(j + i, 4)
        weights.append(pltpu.make_async_copy(wfirst_hbm.at[s], wfirst.at[s], n_sem.at[1 + i]))
    operands = []
    for i in range(4):
        k = i % 2
        left, right = (du_hbm, n_hbm) if i < 2 else (h_hbm, df_hbm)
        operands.append(pltpu.make_async_copy(left.at[k], lefts.at[i], m_sem.at[2 * i]))
        operands.append(pltpu.make_async_copy(right.at[k], rights.at[i], m_sem.at[2 * i + 1]))
    for cp in operands + weights:
        cp.start()
    peers = others(8, e)
    greet([{"expert": p} for p in peers] + [{"dp": p} for p in (sibling, across, diagonal)])

    tiles = width // TILE

    def grad_copy(i):
        at = pl.ds(pl.multiple_of(i % tiles * TILE, TILE), TILE)
        return pltpu.make_async_copy(grads.at[i // tiles, at], grads_hbm.at[i // tiles, at], t_sem.at[i])

    def grad_tiles(first, last):
        for cp in operands[2 * ((first + tiles - 1) // tiles) : 2 * ((last + tiles - 1) // tiles)]:
            cp.wait()

        def tile(i, c):
            at = pl.ds(pl.multiple_of(i % tiles * TILE, TILE), TILE)
            res = lax.dot_general(lefts[i // tiles, :, at], rights[i // tiles], TN, preferred_element_type=F32)
            grads[i // tiles, at, :] = res.astype(BF)
            grad_copy(i).start()
            return c

        lax.fori_loop(first, last, tile, 0)

    def cols_of(s):
        return pl.ds(pl.multiple_of(s * lanes, lanes), lanes)

    def rows_of(s):
        return pl.ds(pl.multiple_of(s * rows, rows), rows)

    def head_copy(src, dst, which, dest):
        return push(src.at[:, cols_of(dest)], dst.at[rows_of(e)], h_send.at[which * 8 + dest], h_recv.at[which * 8 + e], {"expert": dest})

    def head_arrival(src, dst, which, source):
        return push(src.at[:, cols_of(source)], dst.at[rows_of(source)], h_send.at[which * 8 + source], h_recv.at[which * 8 + source], {"expert": source})

    for dest in peers:
        head_copy(gmix, dom, 0, dest).start()
    for dest in peers:
        head_copy(gatt, dam, 1, dest).start()
    for dest in peers:
        push(cent.at[dest], cland.at[e], c_send.at[dest], c_recv.at[e], {"expert": dest}).start()
    later = Weights(wqkv, shard // 2, shard // 2, wsecond, q_send, q_recv)
    later.start()
    dom[rows_of(e), :] = gmix[:, cols_of(e)]
    dam[rows_of(e), :] = gatt[:, cols_of(e)]
    cland[e] = cent[e]

    def dp_block(t, s):
        return part[pl.ds(max(t - 1, 0) * lanes, lanes), pl.ds(pl.multiple_of(s * shard, shard), shard)]

    def dp_copy(kind, t):
        if kind == 0:
            return push(f1.at[t], rf1.at[t], p_send.at[t * 3], p_recv.at[t * 3], {"dp": sibling})
        if kind == 1:
            return push(f3.at[t], rf3.at[t], p_send.at[t * 3 + 1], p_recv.at[t * 3 + 1], {"dp": sibling})
        return push(ssum.at[t], rss.at[t], p_send.at[t * 3 + 2], p_recv.at[t * 3 + 2], {"dp": across})

    def dp_sum_start(t):
        f3[t] = dp_block(t, diagonal).astype(BF)
        f1[t] = dp_block(t, sibling).astype(BF)
        dp_copy(1, t).start()
        dp_copy(0, t).start()

    def dp_sum_cross(t):
        dp_copy(1, t).wait_recv()
        ssum[t] = (dp_block(t, across) + rf3[t].astype(F32)).astype(BF)
        dp_copy(2, t).start()

    def dp_sum_end(t):
        dp_copy(0, t).wait_recv()
        dp_copy(2, t).wait_recv()
        return (dp_block(t, j) + rf1[t].astype(F32) + rss[t].astype(F32)).T.astype(BF)

    for cp in loads[:2]:
        cp.wait()
    grad_tiles(0, 6)
    for source in peers:
        head_arrival(gmix, dom, 0, source).wait_recv()
    left_row = lax.broadcasted_iota(jnp.int32, (8, 128), 1) < HEAD
    row_id = lax.broadcasted_iota(jnp.int32, (8, 128), 0)
    pick = jnp.where((row_id == 0) == left_row, 1.0, 0.0).astype(F32)
    delta[...] = lax.dot_general(pick, dom[...].astype(F32) * mixed[...], NT, precision=HIGH, preferred_element_type=F32)

    for source in peers:
        push(cent.at[source], cland.at[source], c_send.at[source], c_recv.at[source], {"expert": source}).wait_recv()
    csum[0] = jnp.sum(cland[...], axis=0)

    def c_copy(i):
        s = (sibling, across, diagonal)[i]
        return push(csum.at[0, :, pl.ds(pl.multiple_of(s * shard, shard), shard)], cdp.at[j], c_send.at[8 + i], c_recv.at[8 + j], {"dp": s})

    def c_arrival(s):
        return push(csum.at[0, :, pl.ds(0, shard)], cdp.at[s], c_send.at[8], c_recv.at[8 + s], {"dp": sibling})

    for i in range(3):
        c_copy(i).start()
    cdp[j] = csum[0, :, pl.ds(pl.multiple_of(j * shard, shard), shard)]

    left = lane_masks(blk)
    dq_acc[...] = jnp.zeros_like(dq_acc)

    def d_copy(dest):
        return push(dqkv.at[pl.ds(dest * rows, rows)], dq_land.at[e], d_send.at[dest], d_recv.at[e], {"expert": dest})

    for b in range(4):
        at = pl.ds(b * blk, blk)
        tail = pl.ds(b * blk, 8 * rows - b * blk)
        qs = qkv[tail, 0:lanes]
        dos = dom[tail, :]
        keys = qkv[at, lanes : 2 * lanes].astype(F32) * (HEAD ** -0.5)
        vals = qkv[at, 2 * lanes : 3 * lanes]
        dks, dvs = [], []
        for h in range(2):
            mask = left if h == 0 else jnp.logical_not(left)
            k_h = jnp.where(mask, keys, 0.0).astype(BF)
            v_h = jnp.where(mask, vals.astype(F32), 0.0).astype(BF)
            sc = lax.dot_general(k_h, qs, NT, preferred_element_type=F32)
            pr = jnp.exp(sc - lse_rows[h : h + 1, tail])
            dp = lax.dot_general(v_h, dos, NT, preferred_element_type=F32)
            ds = (pr * (dp - delta[h : h + 1, tail])).astype(BF)
            dvs.append(jnp.dot(pr.astype(BF), dos, preferred_element_type=F32))
            dks.append(jnp.dot(ds, qs, preferred_element_type=F32))
            dq_acc[tail, :] += lax.dot_general(ds, k_h, TN, preferred_element_type=F32)
        dqkv[at, 0:lanes] = dq_acc[at, :].astype(BF)
        dqkv[at, lanes : 2 * lanes] = (jnp.where(left, dks[0], dks[1]) * (HEAD ** -0.5)).astype(BF)
        dqkv[at, 2 * lanes : 3 * lanes] = jnp.where(left, dvs[0], dvs[1]).astype(BF)
        for dest in (2 * b, 2 * b + 1):
            @pl.when(dest != e)
            def _():
                d_copy(dest).start()

            @pl.when(dest == e)
            def _():
                dq_land[dest] = dqkv[pl.ds(dest * rows, rows), :]
        if b == 0:
            loads[2].wait()
            for source in peers:
                head_arrival(gatt, dam, 1, source).wait_recv()
            part[0:lanes, :] = lax.dot_general(dam[...], olow[...], TN, preferred_element_type=F32)
            dp_sum_start(0)
            dp_sum_cross(0)
        if b == 1:
            go_own[...] = dp_sum_end(0)
            gos = Spread(go_own, go_land, go_send, go_recv, 1)
            gos.start()
            own_go = pltpu.make_async_copy(go_own, go_land.at[e], copy_sem.at[5])
            own_go.start()
            for s in (sibling, across, diagonal):
                c_arrival(s).wait_recv()
            csum[1, :, 0:shard] = jnp.sum(cdp[...], axis=0)
            for dest in peers:
                push(csum.at[1, :, pl.ds(0, shard)], gc_land.at[e], c_send.at[12 + dest], c_recv.at[12 + e], {"expert": dest}).start()
            own_gc = pltpu.make_async_copy(csum.at[1, :, pl.ds(0, shard)], gc_land.at[e], copy_sem.at[6])
            own_gc.start()
    loads[3].wait()
    later.relay()
    gqs = Spread(gq_own, gq_land, gq_send, gq_recv, 3)
    for g in range(3):
        at = pl.ds(g * lanes, lanes)
        part[at, :] = lax.dot_general(dqkv[:, at], normed[...], TN, preferred_element_type=F32)
        dp_sum_start(g + 1)
        if g > 0:
            dp_sum_cross(g)
    dp_sum_cross(3)
    gos.step(1)
    grad_tiles(6, 9)
    for g in range(3):
        gq_own[pl.ds(g * shard, shard), :] = dp_sum_end(g + 1)
        gqs.start_chunk(g)
    own_gq = pltpu.make_async_copy(gq_own, gq_land.at[e], copy_sem.at[7])
    own_gq.start()
    gos.step(2)
    grad_tiles(9, 12)
    gqs.step(1)
    gos.step(3)
    grad_tiles(12, 16)
    later.drain()
    for cp in weights:
        cp.wait()
    for source in peers:
        push(dqkv.at[pl.ds(0, rows)], dq_land.at[source], d_send.at[source], d_recv.at[source], {"expert": source}).wait_recv()
    for s in range(8):
        for i in range(3):
            dq_rows[:, pl.ds(i * width + s * lanes, lanes)] = dq_land[s, :, pl.ds(i * lanes, lanes)]
    gqs.step(2)
    for s in range(4):
        for side, w in enumerate((wfirst, wsecond)):
            at = pl.ds(s * shard + side * half, half)
            dnorm[:, at] = lax.dot_general(dq_rows[...], w[s], NT, preferred_element_type=F32)
    own_dnorm = pltpu.make_async_copy(dnorm, dnorm_hbm, copy_sem.at[4])
    own_dnorm.start()
    gqs.step(3)
    for zz in range(4):
        gos.wait_beside(zz)
        gqs.wait_beside(zz)
    gos.drain()
    gqs.drain()
    own_dnorm.wait()
    for i in range(4 * tiles):
        grad_copy(i).wait()
    for source in range(8):
        @pl.when(source != e)
        def _():
            d_copy(source).wait_send()
            push(csum.at[1, :, pl.ds(0, shard)], gc_land.at[source], c_send.at[12 + source], c_recv.at[12 + source], {"expert": source}).wait()

    for dest in peers:
        head_copy(gmix, dom, 0, dest).wait_send()
        head_copy(gatt, dam, 1, dest).wait_send()
        push(cent.at[dest], cland.at[e], c_send.at[dest], c_recv.at[e], {"expert": dest}).wait_send()
    for i in range(3):
        c_copy(i).wait_send()
        for t in range(4):
            dp_copy(i, t).wait_send()
    for cp in (own_go, own_gc, own_gq):
        cp.wait()


def back_block(gmix, gatt, qkv, mixed, lse_rows, normed, olow_full, cent, qkv_weight, wfirst, n, h, df, du):
    rows, width = gmix.shape
    seq = 8 * rows
    shard = width // 4
    any_spec = pl.BlockSpec(memory_space=pl.ANY)
    vmem_spec = pl.BlockSpec(memory_space=pltpu.VMEM)
    S = jax.ShapeDtypeStruct
    V = pltpu.VMEM
    D = pltpu.SemaphoreType.DMA
    return pl.pallas_call(
        back_kernel,
        out_shape=(
            S((rows, width), F32), S((8, 3 * shard, 128), BF), S((8, shard, 128), BF), S((8, 1, shard), F32),
            S((4, width, width), BF),
        ),
        in_specs=[vmem_spec, vmem_spec, any_spec, any_spec, vmem_spec, any_spec, any_spec, vmem_spec] + [any_spec] * 6,
        out_specs=(any_spec,) * 5,
        scratch_shapes=[
            V((seq, 128), BF), V((seq, 128), BF), V((seq, 384), BF), V((seq, 128), F32), V((seq, width), BF), V((seq, width), BF),
            V((8, seq), F32), V((seq, 128), F32), V((seq, 384), BF),
            V((384, width), F32),
        ]
        + [V((4, 128, shard), BF)] * 6
        + [
            V((3 * shard, 128), BF), V((shard, 128), BF), V((8, 1, width), F32), V((2, 1, width), F32), V((4, 1, shard), F32),
            D((16,)), D((16,)), D((8,)), D((8,)), D((12,)), D((12,)), D((33,)), D((24,)), D((11,)), D((8,)), D((20,)), D((20,)), D((9,)), D((3,)), D((4,)),
            V((8, rows, 384), BF), V((4, shard // 2, 3 * width), BF), V((4, shard // 2, 3 * width), BF),
            V((rows, 3 * width), BF), V((rows, width), F32), D((5,)),
            V((4,) + h.shape[1:], BF), V((4,) + n.shape[1:], BF), V((4, width, width), BF), D((8,)), D((16,)),
        ],
        compiler_params=pltpu.CompilerParams(collective_id=3, has_side_effects=True, vmem_limit_bytes=56 * 1024 * 1024),
        name="back_block",
    )(gmix, gatt, qkv, mixed, lse_rows, normed, olow_full, cent, qkv_weight, wfirst, n, h, df, du)


def final_kernel(
    dnorm_hbm, tok_hbm, gain_col, gres_hbm, gq_hbm, go_hbm, wqkv_hbm, gc_land, gain_part,
    grads_hbm,
    gtok_hbm, gqkv_hbm, gout_hbm, gnorm, gcent, ggain, gein, geout,
    grads, wide, dnorm, tok, gres, gq_land, go_land, wqkv,
    gtok, gqkv, gout, small_sum,
    load_sem, tile_sem, store_sem,
):
    rows, width = tok.shape
    shard = wqkv.shape[0]
    tiles = width // TILE

    def load(i, src, dst):
        cp = pltpu.make_async_copy(src, dst, load_sem.at[i])
        cp.start()
        return cp

    parts = [load(i, grads_hbm.at[i], grads.at[i]) for i in range(4)]
    first = [load(8, dnorm_hbm, dnorm), load(9, gq_hbm, gq_land), load(10, go_hbm, go_land), load(11, wqkv_hbm, wqkv)]
    rest = [load(12, tok_hbm, tok), load(13, gres_hbm, gres)]
    me = lax.axis_index("dp")

    def grad_copy(i, t):
        out = gein if i < 2 else geout
        at = pl.ds(pl.multiple_of(t * TILE, TILE), TILE)
        return pltpu.make_async_copy(wide.at[i, at], out.at[i % 2, at], tile_sem.at[i * tiles + t])

    for i in range(4):
        parts[i].wait()

        def tile(t, c):
            at = pl.ds(pl.multiple_of(t * TILE, TILE), TILE)
            wide[i, at, :] = grads[i, at, :].astype(F32)
            grad_copy(i, t).start()
            return c

        lax.fori_loop(0, tiles, tile, 0)
    for cp in first:
        cp.wait()
    for s in range(8):
        for i in range(3):
            at = pl.ds(i * width + s * 128, 128)
            gqkv[:, at] = gq_land[s, pl.ds(i * shard, shard), :].astype(F32)
        gout[:, pl.ds(s * 128, 128)] = go_land[s].astype(F32)
    stores = [
        pltpu.make_async_copy(gqkv, gqkv_hbm, store_sem.at[0]),
        pltpu.make_async_copy(gout, gout_hbm, store_sem.at[1]),
    ]
    for cp in stores:
        cp.start()
    for cp in rest:
        cp.wait()
    gain = jnp.concatenate([gain_col[s : s + 1, :] for s in range(4)], axis=1)

    def norm_rows(t, c):
        at = pl.ds(pl.multiple_of(t * 32, 32), 32)
        v = tok[at, :].astype(F32)
        center = v - mean_last(v)
        inverse = lax.rsqrt(mean_last(center * center) + EPS)
        unit = center * inverse
        a = dnorm[at, :] * gain
        gtok[at, :] = gres[at, :] + inverse * (a - mean_last(a) - unit * mean_last(a * unit))
        return c

    lax.fori_loop(0, rows // 32, norm_rows, 0)
    stores.append(pltpu.make_async_copy(gtok, gtok_hbm, store_sem.at[2]))
    stores[2].start()
    small_sum[...] = jnp.zeros_like(small_sum)

    def add(t, c):
        at = pl.ds(pl.multiple_of(t * 256, 256), 256)
        prod = gqkv[:, at] * wqkv[:, at].astype(F32)
        small_sum[...] += prod[:, :128] + prod[:, 128:]
        return c

    lax.fori_loop(0, 3 * width // 256, add, 0)
    own_gain = gain_col[pl.ds(me, 1), :]
    sums = lax.dot_general(jnp.ones((8, 128), F32), small_sum[...], NT, precision=HIGH, preferred_element_type=F32)
    gnorm[...] = sums[0:1] / own_gain
    for s in range(8):
        gcent[s : s + 1, :] = gc_land[s]
    ggain[...] = gain_part[...]
    for cp in stores:
        cp.wait()
    for i in range(4):
        for t in range(tiles):
            grad_copy(i, t).wait()


def final_block(dnorm, tokens, gain_col, grad_resid, gq_land, go_land, qkv_weight, gc_land, gain_part, grads):
    rows, width = tokens.shape
    shard = width // 4
    hidden = grads.shape[1]
    any_spec = pl.BlockSpec(memory_space=pl.ANY)
    vmem_spec = pl.BlockSpec(memory_space=pltpu.VMEM)
    S = jax.ShapeDtypeStruct
    V = pltpu.VMEM
    D = pltpu.SemaphoreType.DMA
    return pl.pallas_call(
        final_kernel,
        out_shape=(
            S((rows, width), F32), S((shard, 3 * width), F32), S((shard, width), F32), S((1, shard), F32),
            S((8, shard), F32), S((2, shard), F32), S((2, hidden, width), F32), S((2, hidden, width), F32),
        ),
        in_specs=[any_spec] * 2 + [vmem_spec] + [any_spec] * 4 + [vmem_spec] * 2 + [any_spec],
        out_specs=(any_spec,) * 3 + (vmem_spec,) * 3 + (any_spec,) * 2,
        scratch_shapes=[
            V(grads.shape, BF), V(grads.shape, F32),
            V((rows, width), F32), V((rows, width), BF), V((rows, width), F32),
            V(gq_land.shape, BF), V(go_land.shape, BF), V((shard, 3 * width), BF),
            V((rows, width), F32),
            V((shard, 3 * width), F32), V((shard, width), F32), V((shard, 128), F32),
            D((14,)), D((16,)), D((3,)),
        ],
        compiler_params=pltpu.CompilerParams(vmem_limit_bytes=58 * 1024 * 1024),
        name="final_block",
    )(dnorm, tokens, gain_col, grad_resid, gq_land, go_land, qkv_weight, gc_land, gain_part, grads)


def on_device_split(
    tokens,
    norm_gain,
    qkv_weight,
    out_weight,
    centroids,
    expert_gain,
    expert_in,
    expert_out,
    routes,
    cotangent,
):
    rows, width = tokens.shape
    experts = lax.axis_size("expert")
    capacity = max(2, 3 * rows // (2 * experts))
    slots = experts * capacity
    shard = width // 4
    olow, normed_all, qkv, mixed, wout_full, wfirst, lse_rows, gain_col, gains, centroid_full = front_block(
        tokens, norm_gain[None], expert_gain, centroids, qkv_weight, out_weight
    )
    inputs = tokens.astype(F32)
    residual = inputs + jnp.dot(olow, wout_full, preferred_element_type=F32)
    route_ids = routes[:, 0]
    chosen = (route_ids[:, None] == jnp.arange(experts, dtype=jnp.int32)[None, :]).astype(BF)
    centroid_rows = jnp.dot(chosen, centroid_full, preferred_element_type=F32)
    gate = jax.nn.sigmoid(jnp.sum(residual * centroid_rows, axis=-1))
    before = jnp.tril(jnp.ones((rows, rows), BF), -1)
    rank = jnp.sum(jnp.dot(before, chosen, preferred_element_type=F32) * chosen.astype(F32), axis=-1)
    target = route_ids * capacity + rank.astype(jnp.int32)
    place = (jnp.arange(slots, dtype=jnp.int32)[:, None] == target[None, :]).astype(BF)
    grad_out = cotangent.astype(F32)
    sent = jnp.concatenate([residual.astype(BF), (gate[:, None] * grad_out).astype(BF)], axis=1)
    spread = jnp.dot(place, sent, preferred_element_type=F32).astype(BF)
    returned, came_back, olow_full, gain_part, n_rows, h_rows, df_rows, du_rows = expert_block(
        spread[:, :width].reshape(experts, capacity, width),
        spread[:, width:].reshape(experts, capacity, width),
        olow,
        gains,
        expert_in,
        expert_out,
    )
    branch_tok = lax.dot_general(place, returned.reshape(slots, width), TN, preferred_element_type=F32)
    block_out = (residual + gate[:, None] * branch_tok).astype(BF)
    grad_logit = jnp.sum(grad_out * branch_tok, axis=-1) * gate * (1.0 - gate)
    grad_centroid = jnp.dot(chosen.astype(F32).T, grad_logit[:, None] * residual, precision=HIGH)
    back_rows = lax.dot_general(place, came_back.reshape(slots, width), TN, preferred_element_type=F32)
    grad_resid = grad_out + grad_logit[:, None] * centroid_rows + back_rows
    grad_attended = grad_resid.astype(BF)
    grad_mixed = lax.dot_general(grad_attended, wout_full, NT, preferred_element_type=F32).astype(BF)
    dnormed, gq_land, go_land, gc_land, expert_grads = back_block(
        grad_mixed, grad_attended, qkv, mixed, lse_rows, normed_all,
        olow_full.reshape(experts * rows, width), grad_centroid[:, None, :], qkv_weight, wfirst,
        n_rows, h_rows, df_rows, du_rows,
    )
    grad_tokens, grad_qkv, grad_out_weight, grad_norm_gain, grad_centroids, grad_gain, grad_expert_in, grad_expert_out = final_block(
        dnormed, tokens, gain_col, grad_resid, gq_land, go_land, qkv_weight, gc_land, gain_part,
        expert_grads,
    )
    return (
        block_out,
        grad_tokens,
        grad_norm_gain[0],
        grad_qkv,
        grad_out_weight,
        grad_centroids,
        grad_gain[None],
        grad_expert_in[None],
        grad_expert_out[None],
    )


def on_device(
    tokens,
    norm_gain,
    qkv_weight,
    out_weight,
    centroids,
    expert_gain,
    expert_in,
    expert_out,
    routes,
    cotangent,
):
    model_width = tokens.shape[1]
    local_rows = tokens.shape[0]
    experts = lax.axis_size("expert")
    capacity = max(2, 3 * local_rows // (2 * experts))
    slot_total = experts * capacity
    first_pos = lax.axis_index("expert") * local_rows
    scale = HEAD ** (-0.5)
    gain_full, qkv_full, out_full, centroid_full, expert_gain_full = fetch_dense(
        norm_gain, qkv_weight, out_weight, centroids, expert_gain
    )
    inputs = tokens.astype(jnp.float32)
    unit_attn, inverse_attn, normed_attn = normalize(inputs, gain_full.astype(jnp.float32))
    normed_low = normed_attn.astype(jnp.bfloat16)
    projected = jnp.dot(normed_low, qkv_full, preferred_element_type=jnp.float32).astype(
        jnp.bfloat16
    )
    queries = projected[:, :model_width]
    keyset = projected[:, model_width : 2 * model_width]
    values = projected[:, 2 * model_width :]
    query_heads = split_heads(queries)
    key_heads = split_heads(keyset)
    value_heads = split_heads(values)
    query_block = (first_pos + jnp.arange(local_rows, dtype=jnp.int32)) // BLOCK
    last_block = (first_pos + local_rows - 1) // BLOCK
    start_state = (
        jnp.zeros((local_rows, HEADS, HEAD), jnp.float32),
        jnp.full((HEADS, local_rows), NEGATIVE, jnp.float32),
        jnp.zeros((HEADS, local_rows), jnp.float32),
    )
    key_piece = lax.all_gather(keyset, "expert", axis=0, tiled=True)
    value_piece = lax.all_gather(values, "expert", axis=0, tiled=True)
    amount = key_piece.shape[0]

    def update(current):
        accumulated, highest, totals = current
        scores = (
            jnp.einsum(
                "qhd,khd->hqk",
                query_heads,
                split_heads(key_piece),
                preferred_element_type=jnp.float32,
            )
            * scale
        )
        piece_block = jnp.arange(amount, dtype=jnp.int32) // BLOCK
        visible = (piece_block[None, :] <= query_block[:, None])[None]
        scores = jnp.where(visible, scores, NEGATIVE)
        new_high = jnp.maximum(highest, jnp.max(scores, axis=-1))
        factor = jnp.exp(highest - new_high)
        weights = jnp.where(visible, jnp.exp(scores - new_high[:, :, None]), 0.0)
        totals = jnp.sum(weights, axis=-1)
        accumulated = accumulated * factor.T[:, :, None] + jnp.einsum(
            "hqk,khd->qhd",
            weights.astype(jnp.bfloat16),
            split_heads(value_piece),
            preferred_element_type=jnp.float32,
        )
        return (accumulated, new_high, totals)

    accumulated, highest, totals = lax.cond(
        jnp.int32(0) // BLOCK <= last_block, update, keep_state, start_state
    )
    mixed_heads = accumulated / totals.T[:, :, None]
    log_total = (highest + jnp.log(totals)).T
    mixed_low = mixed_heads.reshape(local_rows, model_width).astype(jnp.bfloat16)
    residual = inputs + jnp.dot(mixed_low, out_full, preferred_element_type=jnp.float32)
    route_ids = routes[:, 0]
    chosen = route_ids[:, None] == jnp.arange(experts, dtype=jnp.int32)[None, :]
    centroid_rows = jnp.dot(
        chosen.astype(jnp.bfloat16), centroid_full, preferred_element_type=jnp.float32
    )
    gate_value = jax.nn.sigmoid(jnp.sum(residual * centroid_rows, axis=-1))
    chosen_int = chosen.astype(jnp.int32)
    slot_index = jnp.sum((jnp.cumsum(chosen_int, axis=0) - 1) * chosen_int, axis=-1)
    target = route_ids * capacity + slot_index
    arrived = lax.all_to_all(
        send_slots(residual.astype(jnp.bfloat16), target, experts, capacity),
        "expert",
        split_axis=0,
        concat_axis=0,
        tiled=True,
    )
    expert_state = arrived.reshape(slot_total, model_width).astype(jnp.float32)
    gains_here = expert_gain_full[0].astype(jnp.float32)
    total_change = jnp.zeros_like(expert_state)
    stored = []
    for sublayer in range(2):
        unit_rows, inverse, normed = normalize(expert_state, gains_here[sublayer])
        normed_rows = normed.astype(jnp.bfloat16)
        first_full, second_full = (expert_in[0, sublayer], expert_out[0, sublayer])
        left_rows = spread_rows(normed_rows)
        hidden_pre = jnp.einsum(
            "rd,fd->rf", left_rows, first_full, preferred_element_type=jnp.float32
        )
        hidden_act, slope_pull = jax.vjp(exact_gelu, hidden_pre)
        hidden_low = hidden_act.astype(jnp.bfloat16)
        change = sum_rows(partial(row_product, hidden_low, second_full), slot_total)
        expert_state = expert_state + change
        total_change = total_change + change
        stored.append((unit_rows, inverse, left_rows, hidden_low, slope_pull))
    branch_low = total_change.astype(jnp.bfloat16)
    returned = lax.all_to_all(
        branch_low.reshape(experts, capacity, model_width),
        "expert",
        split_axis=0,
        concat_axis=0,
        tiled=True,
    )
    branch_tok = returned.reshape(slot_total, model_width)[target].astype(jnp.float32)
    block_out = (residual + gate_value[:, None] * branch_tok).astype(jnp.bfloat16)
    gain_full, qkv_full, out_full, centroid_full, expert_gain_full = fetch_dense(
        norm_gain, qkv_weight, out_weight, centroids, expert_gain
    )
    gains_here = expert_gain_full[0].astype(jnp.float32)
    grad_out = cotangent.astype(jnp.float32)
    grad_logit = jnp.sum(grad_out * branch_tok, axis=-1) * gate_value * (1.0 - gate_value)
    grad_centroid = jnp.dot(
        chosen.astype(jnp.float32).T, grad_logit[:, None] * residual, precision=HIGH
    )
    grad_resid = grad_out + grad_logit[:, None] * centroid_rows
    grad_branch = (gate_value[:, None] * grad_out).astype(jnp.bfloat16)
    branch_grads = lax.all_to_all(
        send_slots(grad_branch, target, experts, capacity),
        "expert",
        split_axis=0,
        concat_axis=0,
        tiled=True,
    )
    grad_change = branch_grads.reshape(slot_total, model_width).astype(jnp.float32)
    grad_state = jnp.zeros_like(grad_change)
    gain_grads = [None, None]
    first_grads = [None, None]
    second_grads = [None, None]
    for sublayer in (1, 0):
        unit_rows, inverse, left_rows, hidden_low, slope_pull = stored[sublayer]
        grad_rows_low = (grad_change + grad_state).astype(jnp.bfloat16)
        first_full, second_full = (expert_in[0, sublayer], expert_out[0, sublayer])
        grad_rows = spread_rows(grad_rows_low)
        grad_hidden = jnp.einsum(
            "rd,fd->rf", grad_rows, second_full, preferred_element_type=jnp.float32
        )
        grad_pre = slope_pull(grad_hidden)[0].astype(jnp.bfloat16)
        grad_first = jnp.einsum(
            "rf,rd->fd", grad_pre, left_rows, preferred_element_type=jnp.float32
        )
        grad_second = jnp.einsum(
            "rf,rd->fd", hidden_low, grad_rows, preferred_element_type=jnp.float32
        )
        grad_normed = sum_rows(partial(row_product, grad_pre, first_full), slot_total)
        grad_input, gain_grad = norm_backward(grad_normed, unit_rows, inverse, gains_here[sublayer])
        grad_state = grad_state + grad_input
        gain_grads[sublayer] = gain_grad
        first_grads[sublayer] = grad_first
        second_grads[sublayer] = grad_second
    came_back = lax.all_to_all(
        grad_state.astype(jnp.bfloat16).reshape(experts, capacity, model_width),
        "expert",
        split_axis=0,
        concat_axis=0,
        tiled=True,
    )
    grad_resid = grad_resid + came_back.reshape(slot_total, model_width)[target].astype(jnp.float32)
    grad_attended = grad_resid.astype(jnp.bfloat16)
    grad_out_weight = jnp.einsum(
        "rd,re->de", mixed_low, grad_attended, preferred_element_type=jnp.float32
    )
    grad_mixed = jnp.einsum(
        "re,de->rd", grad_attended, out_full, preferred_element_type=jnp.float32
    ).astype(jnp.bfloat16)
    grad_heads = split_heads(grad_mixed)
    delta_rows = jnp.sum(grad_heads.astype(jnp.float32) * mixed_heads, axis=-1)
    zero_heads = jnp.zeros((local_rows, HEADS, HEAD), jnp.float32)
    running = (zero_heads, zero_heads, zero_heads)
    offset = jnp.int32(0)
    fold_key_piece = lax.all_gather(keyset, "expert", axis=0, tiled=True)
    fold_value_piece = lax.all_gather(values, "expert", axis=0, tiled=True)
    query_piece = lax.all_gather(queries, "expert", axis=0, tiled=True)
    grad_piece = lax.all_gather(grad_mixed, "expert", axis=0, tiled=True)
    log_piece = lax.all_gather(log_total.astype(jnp.bfloat16), "expert", axis=0, tiled=True).astype(
        jnp.float32
    )
    delta_piece = lax.all_gather(
        delta_rows.astype(jnp.bfloat16), "expert", axis=0, tiled=True
    ).astype(jnp.float32)
    fold_amount = fold_key_piece.shape[0]
    piece_block = jnp.arange(fold_amount, dtype=jnp.int32) // BLOCK

    def to_queries(current):
        grad_query, grad_key, grad_value = current
        piece_keys = split_heads(fold_key_piece)
        scores = (
            jnp.einsum("qhd,khd->hqk", query_heads, piece_keys, preferred_element_type=jnp.float32)
            * scale
        )
        visible = (piece_block[None, :] <= query_block[:, None])[None]
        weights = jnp.where(visible, jnp.exp(scores - log_total.T[:, :, None]), 0.0)
        grad_weights = jnp.einsum(
            "qhd,khd->hqk",
            grad_heads,
            split_heads(fold_value_piece),
            preferred_element_type=jnp.float32,
        )
        grad_scores = (weights * (grad_weights - delta_rows.T[:, :, None])).astype(jnp.bfloat16)
        grad_query = (
            jnp.einsum("hqk,khd->qhd", grad_scores, piece_keys, preferred_element_type=jnp.float32)
            * scale
        )
        return (grad_query, grad_key, grad_value)

    def to_keys(current):
        grad_query, grad_key, grad_value = current
        piece_queries = split_heads(query_piece)
        piece_grads = split_heads(grad_piece)
        scores = (
            jnp.einsum("qhd,khd->hqk", piece_queries, key_heads, preferred_element_type=jnp.float32)
            * scale
        )
        visible = (query_block[None, :] <= piece_block[:, None])[None]
        weights = jnp.where(visible, jnp.exp(scores - log_piece.T[:, :, None]), 0.0)
        grad_weights = jnp.einsum(
            "qhd,khd->hqk", piece_grads, value_heads, preferred_element_type=jnp.float32
        )
        grad_scores = (weights * (grad_weights - delta_piece.T[:, :, None])).astype(jnp.bfloat16)
        grad_key = (
            grad_key
            + jnp.einsum(
                "hqk,qhd->khd", grad_scores, piece_queries, preferred_element_type=jnp.float32
            )
            * scale
        )
        grad_value = grad_value + jnp.einsum(
            "hqk,qhd->khd",
            weights.astype(jnp.bfloat16),
            piece_grads,
            preferred_element_type=jnp.float32,
        )
        return (grad_query, grad_key, grad_value)

    running = lax.cond(offset // BLOCK <= last_block, to_queries, keep_state, running)
    grad_query, grad_key, grad_value = lax.cond(
        query_block[0] <= (offset + fold_amount - 1) // BLOCK, to_keys, keep_state, running
    )
    grad_qkv_rows = jnp.concatenate(
        [
            grad_query.reshape(local_rows, model_width),
            grad_key.reshape(local_rows, model_width),
            grad_value.reshape(local_rows, model_width),
        ],
        axis=1,
    ).astype(jnp.bfloat16)
    grad_qkv = jnp.einsum(
        "rd,re->de", normed_low, grad_qkv_rows, preferred_element_type=jnp.float32
    )
    grad_normed_attn = jnp.einsum(
        "re,de->rd", grad_qkv_rows, qkv_full, preferred_element_type=jnp.float32
    )
    grad_input_attn, attn_gain_grad = norm_backward(
        grad_normed_attn, unit_attn, inverse_attn, gain_full.astype(jnp.float32)
    )
    grad_tokens = grad_resid + grad_input_attn
    expert_gain_grad = jnp.stack(gain_grads)[None]
    gain_share, qkv_share, out_share, centroid_share, expert_gain_share = (
        lax.psum_scatter(
            attn_gain_grad.astype(jnp.bfloat16), "dp", scatter_dimension=0, tiled=True
        ).astype(jnp.float32),
        lax.psum_scatter(
            grad_qkv.astype(jnp.bfloat16), "dp", scatter_dimension=0, tiled=True
        ).astype(jnp.float32),
        lax.psum_scatter(
            grad_out_weight.astype(jnp.bfloat16), "dp", scatter_dimension=0, tiled=True
        ).astype(jnp.float32),
        lax.psum_scatter(
            grad_centroid.astype(jnp.bfloat16), "dp", scatter_dimension=1, tiled=True
        ).astype(jnp.float32),
        lax.psum_scatter(
            expert_gain_grad.astype(jnp.bfloat16), "dp", scatter_dimension=2, tiled=True
        ).astype(jnp.float32),
    )
    gain_total, qkv_total, out_total, centroid_total = (
        lax.psum(gain_share.astype(jnp.bfloat16), "expert").astype(jnp.float32),
        lax.psum(qkv_share.astype(jnp.bfloat16), "expert").astype(jnp.float32),
        lax.psum(out_share.astype(jnp.bfloat16), "expert").astype(jnp.float32),
        lax.psum(centroid_share.astype(jnp.bfloat16), "expert").astype(jnp.float32),
    )
    grad_expert_in = jnp.stack(first_grads)[None]
    grad_expert_out = jnp.stack(second_grads)[None]
    return (
        block_out,
        grad_tokens,
        gain_total,
        qkv_total,
        out_total,
        centroid_total,
        expert_gain_share,
        grad_expert_in,
        grad_expert_out,
    )


def solution(mesh):
    in_specs = (
        P(("dp", "expert"), None),
        P("dp"),
        P("dp", None),
        P("dp", None),
        P(None, "dp"),
        P("expert", None, "dp"),
        P("expert", None, "dp", None),
        P("expert", None, "dp", None),
        P(("dp", "expert"), None),
        P(("dp", "expert"), None),
    )
    out_specs = (
        P(("dp", "expert"), None),
        P(("dp", "expert"), None),
        P("dp"),
        P("dp", None),
        P("dp", None),
        P(None, "dp"),
        P("expert", None, "dp"),
        P("expert", None, "dp", None),
        P("expert", None, "dp", None),
    )
    split = mesh.shape["dp"] == 4 and mesh.shape["expert"] == 8
    return jax.shard_map(
        on_device_split if split else on_device, mesh=mesh, in_specs=in_specs, out_specs=out_specs, check_vma=False
    )
```
